32 devices in a mesh: seq: 8 (over y, x, core), fsdp: 4 (over z).
Axes of the slice: x: 2, y: 2, z: 4, core: 2. Of those that a mesh axis runs over, the one named last changes fastest.
Arguments:
- tokens: bfloat16 [4, 2048, 1536], P('fsdp', 'seq'), may hold values from -6 to 6
- segment_ids: int32 [4, 2048], P('fsdp'), may hold values from 0 to 7, never falling along the last dimension, each value on 1 to 512 neighbouring positions
- cotangent: bfloat16 [4, 2048, 1536], P('fsdp', 'seq'), may hold values from -6 to 6
- w_in: bfloat16 [1536, 6448], P('fsdp'), may hold values from -0.15625 to 0.15625
- w_out: bfloat16 [3072, 1536], P('fsdp'), may hold values from -0.109375 to 0.109375
- conv_w: bfloat16 [4, 3328], P(None, 'fsdp'), may hold values from -3 to 3
- conv_b: bfloat16 [3328], P('fsdp'), may hold values from -1.5 to 1.5
- a_log: bfloat16 [48], P('fsdp'), may hold values from -3 to 1.5
- dt_bias: bfloat16 [48], P('fsdp'), may hold values from -5.5 to -3
- d_skip: bfloat16 [48], P('fsdp'), may hold values from 0.5 to 1.5
- norm_w: bfloat16 [1536], P('fsdp'), may hold values from 0.5 to 1.5
- gate_w: bfloat16 [3072], P('fsdp'), may hold values from 0.5 to 1.5
Outputs:
- layer_out: bfloat16 [4, 2048, 1536], P('fsdp', 'seq')
- token_grad: float32 [4, 2048, 1536], P('fsdp', 'seq')
- w_in_grad: float32 [1536, 6448], P('fsdp')
- w_out_grad: float32 [3072, 1536], P('fsdp')
- conv_w_grad: float32 [4, 3328], P(None, 'fsdp')
- conv_b_grad: float32 [3328], P('fsdp')
- a_log_grad: float32 [48], P('fsdp')
- dt_bias_grad: float32 [48], P('fsdp')
- d_skip_grad: float32 [48], P('fsdp')
- norm_w_grad: float32 [1536], P('fsdp')
- gate_w_grad: float32 [3072], P('fsdp')
The draws below stay inside these ranges and needn't reach their ends.
Inputs may be any that keep to these rules, and one draw needn't show every extreme that they name: `segment_ids`: in each sequence the ids never fall from one token to the next, start at 0 and take every value; each document has 1 to 512 tokens and one has exactly 512.
All inputs are finite; a program needn't handle non-finite values.
Results may differ from the reference program's by a relative error of at most 0.011.
Values may be sent and summed in bfloat16 or wider, within the bound.
A program may use at most 320 MiB of HBM per device.

```python
import math
import jax
import jax.numpy as jnp
import numpy as np
from jax import lax

D = 1536
DI = 3072
HEADDIM = 64
STATE = 128
CONV = 4
SPAN = 256
HEADS = 48
CHAN = 3328
WIDTH = 6448
LENGTH = 2048
SEQS = 4
DOC_MOST = 512
DOCS = 8


def levels(own_key, dims, cuts, least, top_value):
    loudness = 1.0
    for dim, shards_of in cuts:
        steps = jax.random.uniform(jax.random.fold_in(jax.random.fold_in(own_key, 6), dim), (shards_of,), jnp.float32, least / len(cuts), top_value / len(cuts))
        loudness = loudness * jnp.repeat(jnp.exp(steps), dims[dim] // shards_of).reshape((-1,) + (1,) * (len(dims) - 1 - dim))
    return loudness


def profile(amount, total, most, slope):
    weights = [(1 << 20) // math.isqrt(grade ** slope) + 1 for grade in range(2, amount + 1)]
    rest, given = total - most - (amount - 1), [1] * (amount - 1)
    while rest > 0:
        free = [i for i in range(amount - 1) if given[i] < most]
        mass, remaining = sum([weights[i] for i in free]), rest
        for i in free:
            more = min(most - given[i], max(1, remaining * weights[i] // mass), rest)
            given[i] = given[i] + more
            rest = rest - more
    return np.array([most] + given)


def ragged_sizes(own_key, amount, total, bound, lean):
    if amount == 2:
        one = jax.random.randint(own_key, (), max(1, total - bound), min(bound, total - 1) + 1)
        return jnp.stack([one, total - one])
    sizes = jnp.asarray(profile(amount, total, bound, lean), jnp.int32)
    twos = (amount - 1) // 2
    donor, taker = sizes[1:1 + 2 * twos:2], sizes[2:2 + 2 * twos:2]
    room = jnp.minimum(donor - 1, bound - taker)
    moved = jax.random.randint(jax.random.fold_in(own_key, 1), (twos,), 0, 1 << 20) % (room + 1)
    sizes = sizes.at[1:1 + 2 * twos:2].set(donor - moved).at[2:2 + 2 * twos:2].set(taker + moved)
    return sizes[jax.random.permutation(jax.random.fold_in(own_key, 2), amount)]


def scatter_about(rng, shape, scale, most, pieces=(), dtype=jnp.bfloat16):
    factor_of = levels(rng, shape, pieces, -0.22, 0.18) if pieces else 1.0
    array = jax.random.normal(rng, shape, jnp.float32) * scale * factor_of
    return jnp.minimum(jnp.maximum(array, -most), most).astype(dtype)


def setup_inputs(seed: int = 0) -> dict:
    streams_of = jax.random.split(jax.random.key(seed), 13)
    tokens = scatter_about(streams_of[0], (SEQS, LENGTH, D), 1.0, 6.0, ((0, 4), (1, 8)))
    segment_ids = jax.vmap(lambda own: jnp.searchsorted(jnp.cumsum(ragged_sizes(own, DOCS, LENGTH, DOC_MOST, 0)), jnp.arange(LENGTH), side="right"))(jax.random.split(streams_of[1], SEQS)).reshape((SEQS, LENGTH)).astype(jnp.int32)
    cotangent = scatter_about(streams_of[2], (SEQS, LENGTH, D), 1.0, 6.0, ((0, 4), (1, 8)))
    w_in = scatter_about(streams_of[3], (D, WIDTH), D ** -0.5, 0.15625, ((0, 4),))
    w_out = scatter_about(streams_of[4], (DI, D), DI ** -0.5, 0.109375, ((0, 4),))
    conv_w = scatter_about(streams_of[5], (CONV, CHAN), CONV ** -0.5, 3.0, ((1, 4),))
    conv_b = scatter_about(streams_of[6], (CHAN,), 0.3, 1.5, ((0, 4),))
    a_log = jnp.clip(-3.0 + 4.5 * jax.random.uniform(streams_of[7], (HEADS,), jnp.float32) ** levels(streams_of[7], (HEADS,), ((0, 4),), -0.2, 0.2), -3.0, 1.5).astype(jnp.bfloat16)
    dt_bias = jnp.clip(-5.5 + 2.5 * jax.random.uniform(streams_of[8], (HEADS,), jnp.float32) ** levels(streams_of[8], (HEADS,), ((0, 4),), -0.2, 0.2), -5.5, -3.0).astype(jnp.bfloat16)
    d_skip = jnp.clip(0.5 + 1.0 * jax.random.uniform(streams_of[9], (HEADS,), jnp.float32) ** levels(streams_of[9], (HEADS,), ((0, 4),), -0.2, 0.2), 0.5, 1.5).astype(jnp.bfloat16)
    norm_w = jnp.clip(1.0 + 0.1 * jax.random.normal(streams_of[10], (D,), jnp.float32), 0.5, 1.5).astype(jnp.bfloat16)
    gate_w = jnp.clip(1.0 + 0.1 * jax.random.normal(streams_of[11], (DI,), jnp.float32), 0.5, 1.5).astype(jnp.bfloat16)
    return {"tokens": tokens, "segment_ids": segment_ids, "cotangent": cotangent, "w_in": w_in, "w_out": w_out, "conv_w": conv_w, "conv_b": conv_b, "a_log": a_log, "dt_bias": dt_bias, "d_skip": d_skip, "norm_w": norm_w, "gate_w": gate_w}


EPSILON = 1e-05
HIGHEST = lax.Precision.HIGHEST

@jax.custom_vjp
def low(v):
    return lax.optimization_barrier(v.astype(jnp.bfloat16)).astype(jnp.float32)

@jax.custom_vjp
def low_back(v):
    return v

def low_keep(v):
    return (low(v), None)

def low_pass(kept, grad):
    return (grad,)

def back_keep(v):
    return (v, None)

def back_low(kept, grad):
    return (low(grad),)
low.defvjp(low_keep, low_pass)
low_back.defvjp(back_keep, back_low)

def ssd_block(state_now, block_in):
    x_block, b_block, c_block, step_block, decay_block, id_block, before = block_in
    cum_decay = jnp.cumsum(decay_block, axis=0)
    cum_heads = cum_decay.T
    block_len = cum_decay.shape[0]
    places = jnp.arange(block_len)
    causal_mask = (places[:, None] >= places[None, :]) & (id_block[:, None] == id_block[None, :])
    gap_decay = cum_heads[:, :, None] - cum_heads[:, None, :]
    decay_map = jnp.exp(jnp.where(causal_mask[None], gap_decay, 0.0)) * causal_mask[None].astype(jnp.float32)
    scores = jnp.dot(c_block, b_block.T, precision=HIGHEST)
    mixing = scores[None] * decay_map * step_block.T[:, None, :]
    inner_out = jnp.einsum('hts,shp->thp', mixing, x_block, precision=HIGHEST)
    keep_flag = (id_block == before).astype(jnp.float32)
    carry_weight = keep_flag[:, None] * jnp.exp(cum_decay)
    carried = carry_weight[:, :, None] * jnp.einsum('tn,hpn->thp', c_block, state_now, precision=HIGHEST)
    same_last = (id_block == id_block[-1]).astype(jnp.float32)
    weights = jnp.exp(cum_decay[-1][None, :] - cum_decay) * step_block * same_last[:, None]
    fresh_state = jnp.einsum('sh,shp,sn->hpn', weights, x_block, b_block, precision=HIGHEST)
    new_state = fresh_state + (keep_flag[-1] * jnp.exp(cum_decay[-1]))[:, None, None] * state_now
    return (new_state, inner_out + carried)

def layer(inputs, w_in, w_out, conv_w, conv_b, a_log, dt_bias, d_skip, norm_w, gate_w, seg_ids):
    length = inputs.shape[0]
    normed = inputs * lax.rsqrt(lax.optimization_barrier(jnp.mean(inputs * inputs, axis=-1, keepdims=True)) + EPSILON) * norm_w
    normed = low(normed)
    projected = low(low_back(jnp.dot(normed, w_in, precision=HIGHEST)))
    gate_z = projected[:, :DI]
    conv_in = projected[:, DI:DI + CHAN]
    dt_raw = projected[:, DI + CHAN:]
    conv_out = conv_b + conv_w[CONV - 1] * conv_in
    for offset in range(1, CONV):
        shifted = jnp.concatenate([jnp.zeros((offset, CHAN), jnp.float32), conv_in[:-offset]], axis=0)
        ids_shift = jnp.concatenate([jnp.full((offset,), -1, jnp.int32), seg_ids[:-offset]], axis=0)
        same_doc = (ids_shift == seg_ids).astype(jnp.float32)
        conv_out = conv_out + conv_w[CONV - 1 - offset] * shifted * same_doc[:, None]
    activated = jax.nn.silu(conv_out)
    x_heads = activated[:, :DI].reshape(length, HEADS, HEADDIM)
    b_rows = activated[:, DI:DI + STATE]
    c_rows = activated[:, DI + STATE:]
    step_size = jax.nn.softplus(dt_raw + dt_bias)
    log_decay = -step_size * jnp.exp(a_log)
    blocks = length // SPAN
    before_ids = jnp.concatenate([jnp.full((1,), -1, jnp.int32), seg_ids[:-1]], axis=0)[::SPAN]
    scan_in = (x_heads.reshape(blocks, SPAN, HEADS, HEADDIM), b_rows.reshape(blocks, SPAN, STATE), c_rows.reshape(blocks, SPAN, STATE), step_size.reshape(blocks, SPAN, HEADS), log_decay.reshape(blocks, SPAN, HEADS), seg_ids.reshape(blocks, SPAN), before_ids)
    start_state = jnp.zeros((HEADS, HEADDIM, STATE), jnp.float32)
    final_state, ssd_blocks = lax.scan(jax.checkpoint(ssd_block), start_state, scan_in)
    ssd_out = ssd_blocks.reshape(length, HEADS, HEADDIM) + d_skip[:, None] * x_heads
    gated = ssd_out.reshape(length, DI) * jax.nn.silu(gate_z)
    normed_out = gated * lax.rsqrt(lax.optimization_barrier(jnp.mean(gated * gated, axis=-1, keepdims=True)) + EPSILON) * gate_w
    normed_out = low(normed_out)
    return inputs + jnp.dot(normed_out, w_out, precision=HIGHEST)

def reference(tokens, segment_ids, cotangent, w_in, w_out, conv_w, conv_b, a_log, dt_bias, d_skip, norm_w, gate_w):
    params = tuple((param.astype(jnp.float32) for param in (w_in, w_out, conv_w, conv_b, a_log, dt_bias, d_skip, norm_w, gate_w)))

    def per_sequence(grad_sum, seq_item):
        seq_tokens, seg_ids, seq_cot = seq_item

        def forward(inputs, *weights):
            return layer(inputs, *weights, seg_ids)
        result, pull_back = jax.vjp(forward, seq_tokens.astype(jnp.float32), *params)
        grads = pull_back(seq_cot.astype(jnp.float32))
        grad_sum = tuple((left + right for left, right in zip(grad_sum, grads[1:])))
        return (grad_sum, (result.astype(jnp.bfloat16), grads[0]))
    zero_grads = tuple((jnp.zeros_like(param) for param in params))
    grad_sum, (layer_outs, input_grads) = lax.scan(per_sequence, zero_grads, (tokens, segment_ids, cotangent))
    return (layer_outs, input_grads) + grad_sum
```

```python
import jax
import jax.numpy as jnp
from jax import lax
from jax.experimental import pallas as pl
from jax.experimental.pallas import tpu as pltpu
from jax.sharding import PartitionSpec as P

DI = 3072
HEADDIM = 64
STATE = 128
CONV = 4
SPAN = 256
HEADS = 48
D = 1536
CHAN = 3328


EPSILON = 1e-05
HIGHEST = lax.Precision.HIGHEST


def passed_along(value, axis, steps):
    count = lax.axis_size(axis)
    first, last = (max(0, -steps), min(count, count - steps))
    return lax.ppermute(value, axis, [(source, source + steps) for source in range(first, last)])


def shortened(array):

    def short(part):
        return part.astype(jnp.bfloat16) if part.dtype == jnp.float32 else part

    return jax.tree.map(short, array)


def block_masks(ids_blocks, before_ids):
    block_len = ids_blocks.shape[1]
    places = jnp.arange(block_len)
    causal_mask = (places[:, None] >= places[None, :])[None] & (
        ids_blocks[:, :, None] == ids_blocks[:, None, :]
    )
    keep_flag = (ids_blocks == before_ids[:, None]).astype(jnp.float32)
    same_last = (ids_blocks == ids_blocks[:, -1:]).astype(jnp.float32)
    return (causal_mask, keep_flag, same_last)


def local_states(x_heads, b_rows, step_size, log_decay, same_last, keep_flag):
    cum_decay = jnp.cumsum(log_decay, axis=1)
    last_cum = cum_decay[:, -1]
    weights = jnp.exp(last_cum[:, None, :] - cum_decay) * step_size * same_last[:, :, None]
    fresh_state = jnp.einsum("csh,cshp,csn->chpn", weights, x_heads, b_rows, precision=HIGHEST)
    passing = keep_flag[:, -1:] * jnp.exp(last_cum)
    total_state = jnp.zeros_like(fresh_state[0])
    total_decay = jnp.ones_like(passing[0])
    total_state = fresh_state[0] + passing[0][:, None, None] * total_state
    total_decay = total_decay * passing[0]
    return (fresh_state, passing, total_state, total_decay)


def local_output(x_heads, b_rows, c_rows, step_size, log_decay, incoming, causal_mask, keep_flag):
    cum_decay = jnp.cumsum(log_decay, axis=1)
    cum_heads = jnp.swapaxes(cum_decay, 1, 2)
    gap_decay = cum_heads[:, :, :, None] - cum_heads[:, :, None, :]
    head_mask = causal_mask[:, None]
    decay_map = jnp.exp(jnp.where(head_mask, gap_decay, 0.0)) * head_mask.astype(jnp.float32)
    scores = jnp.einsum("ctn,csn->cts", c_rows, b_rows, precision=HIGHEST)
    mixing = scores[:, None] * decay_map * jnp.swapaxes(step_size, 1, 2)[:, :, None, :]
    inner_out = jnp.einsum("chts,cshp->cthp", mixing, x_heads, precision=HIGHEST)
    starts = [incoming]
    start_states = jnp.stack(starts)
    carried = jnp.einsum("ctn,chpn->cthp", c_rows, start_states, precision=HIGHEST)
    carried = carried * (keep_flag[:, :, None] * jnp.exp(cum_decay))[..., None]
    return inner_out + carried


def on_device(
    tokens,
    segment_ids,
    cotangent,
    w_in,
    w_out,
    conv_w,
    conv_b,
    a_log,
    dt_bias,
    d_skip,
    norm_w,
    gate_w,
):
    gathered = (
        lax.all_gather(w_in, "fsdp", axis=0, tiled=True),
        lax.all_gather(w_out, "fsdp", axis=0, tiled=True),
        lax.all_gather(conv_w, "fsdp", axis=1, tiled=True),
        lax.all_gather(conv_b, "fsdp", axis=0, tiled=True),
        lax.all_gather(a_log, "fsdp", axis=0, tiled=True),
        lax.all_gather(dt_bias, "fsdp", axis=0, tiled=True),
        lax.all_gather(d_skip, "fsdp", axis=0, tiled=True),
        lax.all_gather(norm_w, "fsdp", axis=0, tiled=True),
        lax.all_gather(gate_w, "fsdp", axis=0, tiled=True),
    )
    (
        w_in_full,
        w_out_full,
        conv_full,
        bias_full,
        a_log_full,
        dt_bias_full,
        skip_full,
        norm_full,
        gate_full,
    ) = gathered
    inputs = tokens[0].astype(jnp.float32)
    length = inputs.shape[0]
    norm_gain = norm_full.astype(jnp.float32)
    scale_in = lax.rsqrt(jnp.mean(inputs * inputs, axis=-1, keepdims=True) + EPSILON)
    normed = (inputs * scale_in * norm_gain).astype(jnp.bfloat16)
    projected = jnp.dot(normed, w_in_full, preferred_element_type=jnp.float32).astype(jnp.bfloat16)
    gate_z = projected[:, :DI].astype(jnp.float32)
    conv_in = projected[:, DI : DI + CHAN]
    dt_raw = projected[:, DI + CHAN :].astype(jnp.float32)
    first_row = lax.axis_index("seq") * length
    id_row = jnp.concatenate([jnp.full((CONV - 1,), -1, jnp.int32), segment_ids[0]], axis=0)
    ids_pad = lax.dynamic_slice_in_dim(id_row, first_row, length + CONV - 1)
    ids_own = ids_pad[CONV - 1 :]
    left_edge = passed_along(conv_in[length - (CONV - 1) :], "seq", 1)
    padded = jnp.concatenate([left_edge, conv_in], axis=0).astype(jnp.float32)
    kernel = conv_full.astype(jnp.float32)
    conv_out = jnp.zeros((length, CHAN), jnp.float32) + bias_full.astype(jnp.float32)
    same_docs = []
    for offset in range(CONV):
        same_doc = (ids_pad[offset : offset + length] == ids_own).astype(jnp.float32)
        same_docs.append(same_doc)
        conv_out = conv_out + kernel[offset] * padded[offset : offset + length] * same_doc[:, None]
    activated = jax.nn.silu(conv_out)
    blocks = length // SPAN
    x_heads = activated[:, :DI].reshape(blocks, SPAN, HEADS, HEADDIM)
    b_rows = activated[:, DI : DI + STATE].reshape(blocks, SPAN, STATE)
    c_rows = activated[:, DI + STATE :].reshape(blocks, SPAN, STATE)
    dt_bias_f = dt_bias_full.astype(jnp.float32)
    decay_rate = jnp.exp(a_log_full.astype(jnp.float32))
    step_flat = jax.nn.softplus(dt_raw + dt_bias_f)
    step_size = step_flat.reshape(blocks, SPAN, HEADS)
    log_decay = (-step_flat * decay_rate).reshape(blocks, SPAN, HEADS)
    ids_blocks = ids_own.reshape(blocks, SPAN)
    before_ids = ids_pad[CONV - 2 : CONV - 2 + length : SPAN]
    causal_mask, keep_flag, same_last = block_masks(ids_blocks, before_ids)

    def state_part(heads_in, rows_b, steps_in, decay_in):
        return local_states(heads_in, rows_b, steps_in, decay_in, same_last, keep_flag)

    (fresh_state, passing, total_state, total_decay), state_pull = jax.vjp(
        state_part, x_heads, b_rows, step_size, log_decay
    )

    def pass_forward(turn_index, received):
        return passed_along(
            (total_state + total_decay[:, None, None] * received).astype(jnp.bfloat16), "seq", 1
        ).astype(jnp.float32)

    incoming = lax.fori_loop(0, lax.axis_size("seq") - 1, pass_forward, jnp.zeros_like(total_state))

    def output_part(
        heads_in, rows_b, rows_c, steps_in, decay_in, fresh_in, passing_in, incoming_in
    ):
        return local_output(
            heads_in, rows_b, rows_c, steps_in, decay_in, incoming_in, causal_mask, keep_flag
        )

    ssd_out, output_pull = jax.vjp(
        output_part, x_heads, b_rows, c_rows, step_size, log_decay, fresh_state, passing, incoming
    )
    skip_heads = skip_full.astype(jnp.float32)
    y_full = (ssd_out + skip_heads[:, None] * x_heads).reshape(length, DI)
    silu_z = jax.nn.silu(gate_z)
    gated = y_full * silu_z
    scale_out = lax.rsqrt(jnp.mean(gated * gated, axis=-1, keepdims=True) + EPSILON)
    gate_gain = gate_full.astype(jnp.float32)
    normed_out = (gated * scale_out * gate_gain).astype(jnp.bfloat16)
    branch = jnp.dot(normed_out, w_out_full, preferred_element_type=jnp.float32)
    layer_out = (inputs + branch).astype(jnp.bfloat16)[None]
    grad_out = cotangent[0]
    d_w_out = lax.dot_general(
        normed_out, grad_out, (((0,), (0,)), ((), ())), preferred_element_type=jnp.float32
    )
    d_normed_out = lax.dot_general(
        grad_out, w_out_full, (((1,), (1,)), ((), ())), preferred_element_type=jnp.float32
    )
    d_gate_w = jnp.sum(d_normed_out * gated * scale_out, axis=0)
    along_out = d_normed_out * gate_gain
    cube_out = scale_out * scale_out * scale_out
    d_gated = scale_out * along_out - gated * cube_out * jnp.mean(
        along_out * gated, axis=-1, keepdims=True
    )
    d_y = d_gated * silu_z
    sig_z = jax.nn.sigmoid(gate_z)
    d_gate_z = d_gated * y_full * sig_z * (1.0 + gate_z * (1.0 - sig_z))
    d_ssd = d_y.reshape(blocks, SPAN, HEADS, HEADDIM)
    d_skip_grad = jnp.sum(d_ssd * x_heads, axis=(0, 1, 3))
    dx_out, db_out, dc_out, dstep_out, ddecay_out, d_fresh, d_passing, d_incoming = output_pull(
        d_ssd
    )

    def pass_backward(turn_index, received):
        return passed_along(d_incoming + total_decay[:, None, None] * received, "seq", -1)

    d_total = lax.fori_loop(0, lax.axis_size("seq") - 1, pass_backward, jnp.zeros_like(d_incoming))
    d_total_decay = jnp.sum(d_total * incoming, axis=(1, 2))
    dx_state, db_state, dstep_state, ddecay_state = state_pull(
        (d_fresh, d_passing, d_total, d_total_decay)
    )
    d_x = dx_out + dx_state + skip_heads[:, None] * d_ssd
    d_b = db_out + db_state
    d_log = (ddecay_out + ddecay_state).reshape(length, HEADS)
    d_step = (dstep_out + dstep_state).reshape(length, HEADS) - d_log * decay_rate
    d_a_log = -jnp.sum(d_log * step_flat, axis=0) * decay_rate
    d_dt_raw = d_step * jax.nn.sigmoid(dt_raw + dt_bias_f)
    d_dt_bias = jnp.sum(d_dt_raw, axis=0)
    d_act = jnp.concatenate(
        [d_x.reshape(length, DI), d_b.reshape(length, STATE), dc_out.reshape(length, STATE)], axis=1
    )
    sig_conv = jax.nn.sigmoid(conv_out)
    d_conv = d_act * sig_conv * (1.0 + conv_out * (1.0 - sig_conv))
    d_conv_b = jnp.sum(d_conv, axis=0)
    kernel_rows = []
    d_padded = jnp.zeros((length + CONV - 1, CHAN), jnp.float32)
    for offset in range(CONV):
        masked = d_conv * same_docs[offset][:, None]
        kernel_rows.append(jnp.sum(masked * padded[offset : offset + length], axis=0))
        d_padded = d_padded + jnp.pad(
            kernel[offset] * masked, ((offset, CONV - 1 - offset), (0, 0))
        )
    d_kernel = jnp.stack(kernel_rows)
    d_edge = passed_along(shortened(d_padded[: CONV - 1]), "seq", -1)
    d_conv_in = d_padded[CONV - 1 :] + jnp.pad(d_edge, ((length - (CONV - 1), 0), (0, 0)))
    d_projected = jnp.concatenate([d_gate_z, d_conv_in, d_dt_raw], axis=1).astype(jnp.bfloat16)
    d_normed = lax.dot_general(
        d_projected, w_in_full, (((1,), (1,)), ((), ())), preferred_element_type=jnp.float32
    )
    d_norm_w = jnp.sum(d_normed * inputs * scale_in, axis=0)
    along_in = d_normed * norm_gain
    cube_in = scale_in * scale_in * scale_in
    d_inputs = (
        scale_in * along_in
        - inputs * cube_in * jnp.mean(along_in * inputs, axis=-1, keepdims=True)
        + grad_out.astype(jnp.float32)
    )
    d_w_in = lax.dot_general(
        normed, d_projected, (((0,), (0,)), ((), ())), preferred_element_type=jnp.float32
    )
    weight_grads = (
        d_w_in,
        d_w_out,
        d_kernel,
        d_conv_b,
        d_a_log,
        d_dt_bias,
        d_skip_grad,
        d_norm_w,
        d_gate_w,
    )
    shares = tuple(
        (
            lax.psum_scatter(weight_grads[0], "fsdp", scatter_dimension=0, tiled=True),
            lax.psum_scatter(weight_grads[1], "fsdp", scatter_dimension=0, tiled=True),
            lax.psum_scatter(weight_grads[2], "fsdp", scatter_dimension=1, tiled=True),
            lax.psum_scatter(weight_grads[3], "fsdp", scatter_dimension=0, tiled=True),
            lax.psum_scatter(weight_grads[4], "fsdp", scatter_dimension=0, tiled=True),
            lax.psum_scatter(weight_grads[5], "fsdp", scatter_dimension=0, tiled=True),
            lax.psum_scatter(weight_grads[6], "fsdp", scatter_dimension=0, tiled=True),
            lax.psum_scatter(weight_grads[7], "fsdp", scatter_dimension=0, tiled=True),
            lax.psum_scatter(weight_grads[8], "fsdp", scatter_dimension=0, tiled=True),
        )
    )
    totals = lax.psum(shares, "seq")
    return (layer_out, d_inputs[None]) + tuple(totals)


F32 = jnp.float32
BF = jnp.bfloat16
BLK = 256
TEAM = 8
HPD = HEADS // TEAM
CH = HPD * HEADDIM
NZ, NX, NB, ND = CH, CH, 2 * STATE, 128
COLS = NZ + NX + NB + ND
CONVC = NX + NB
TAIL = CONV - 1


def dot(a, b):
    return lax.dot_general(a, b, (((1,), (0,)), ((), ())), preferred_element_type=F32)


def dot_nt(a, b):
    return lax.dot_general(a, b, (((1,), (1,)), ((), ())), preferred_element_type=F32)


def dot_tn(a, b):
    return lax.dot_general(a, b, (((0,), (0,)), ((), ())), preferred_element_type=F32)


def dot_exact(a, b):
    return lax.dot_general(
        a, b, (((1,), (0,)), ((), ())), precision=HIGHEST, preferred_element_type=F32
    )


def iota(shape, dim):
    return lax.broadcasted_iota(jnp.int32, shape, dim)


def split_dot(a, b):
    high = a.astype(BF)
    low = (a - high.astype(F32)).astype(BF)
    return dot(high, b) + dot(low, b)


def spread():
    return (iota((128, CH), 1) // HEADDIM == iota((128, CH), 0)).astype(BF)


def gather_heads():
    return (iota((CH, 128), 0) // HEADDIM == iota((CH, 128), 1)).astype(BF)


def lower_tri():
    return (iota((BLK, BLK), 0) >= iota((BLK, BLK), 1)).astype(F32)


def softplus(v):
    return jnp.maximum(v, 0.0) + jnp.log1p(jnp.exp(-jnp.abs(v)))


def sigmoid(v):
    return 1.0 / (1.0 + jnp.exp(-v))


def conv_taps(cbuf, cw, tok):
    out = cw[CONV : CONV + 1, :] + cw[CONV - 1 : CONV, :] * cbuf[8 : 8 + BLK, :]
    for back in range(1, CONV):
        term = cw[CONV - 1 - back : CONV - back, :] * cbuf[8 - back : 8 - back + BLK, :]
        out = out + term * tok[:, back : back + 1]
    return out


def pair_select(left, right):
    return jnp.where(iota(left.shape, 1) % 128 < HEADDIM, left, right)


def fwd_kernel(
    u_ref, g_ref, w_ref, wo_ref, nw_ref, cw_ref, hp_ref, cp_ref, tok_ref, idr_ref,
    nrm_ref, proj_ref, halo_ref, ssd_ref, dno_ref, st_ref, stat_ref, br_ref,
    cbuf, state,
):
    step_id = pl.program_id(0)

    @pl.when(step_id == 0)
    def _():
        state[...] = jnp.zeros_like(state)
        cbuf[0:8, :] = jnp.zeros((8, CONVC), F32)

    u = u_ref[...].astype(F32)
    scale = lax.rsqrt(jnp.mean(u * u, axis=1, keepdims=True) + EPSILON)
    nrm = (u * scale * nw_ref[...]).astype(BF)
    nrm_ref[...] = nrm
    proj = dot(nrm, w_ref[...]).astype(BF)
    proj_ref[...] = proj
    cbuf[8 : 8 + BLK, :] = proj[:, NZ : NZ + CONVC].astype(F32)
    tok = tok_ref[...]
    halo_ref[0] = cbuf[0:8, :]
    conv_out = conv_taps(cbuf, cw_ref[...], tok)
    cbuf[0:8, :] = cbuf[BLK : BLK + 8, :]
    act = conv_out * sigmoid(conv_out)
    x = act[:, :CH]
    bm = act[:, CH : CH + STATE].astype(BF)
    cm = act[:, CH + STATE :].astype(BF)
    hp = hp_ref[...]
    step = softplus(proj[:, NZ + CONVC :].astype(F32) + hp[0:1, :])
    cum = dot_exact(lower_tri(), -step * hp[1:2, :])
    cum_t = cum.T
    mask = (iota((BLK, BLK), 0) >= iota((BLK, BLK), 1)) & (tok[:, 0:1] == idr_ref[0, 0:1, :])
    gm = jnp.where(mask, dot_nt(cm, bm), 0.0)
    ex = spread()
    xs = (x * split_dot(step, ex)).astype(BF)
    parts = []
    for pair in range(HPD // 2):
        xp = xs[:, 128 * pair : 128 * pair + 128]
        both = []
        for h in (2 * pair, 2 * pair + 1):
            decay = jnp.exp(jnp.minimum(cum[:, h : h + 1] - cum_t[h : h + 1, :], 0.0))
            both.append(dot((gm * decay).astype(BF), xp))
        parts.append(pair_select(*both))
    inner = jnp.concatenate(parts, axis=1)
    old = state[...]
    st_ref[0] = old
    keep = tok[:, 7:8]
    carried = split_dot(keep * jnp.exp(cum), ex) * dot(cm, old.astype(BF))
    last = cum[BLK - 1 : BLK, :]
    weights = jnp.exp(last - cum) * step * tok[:, 8:9]
    through = split_dot(jnp.broadcast_to(keep[BLK - 1 :, :] * jnp.exp(last), (8, 128)), ex)[0:1, :]
    state[...] = dot_tn(bm, (x * split_dot(weights, ex)).astype(BF)) + through * old
    cp = cp_ref[...]
    ssd = inner + carried + cp[1:2, :] * x
    ssd_ref[...] = ssd
    z = proj[:, :NZ].astype(F32)
    gated = ssd * (z * sigmoid(z))
    br_ref[...] = dot((gated * cp[0:1, :]).astype(BF), wo_ref[...]).astype(BF)
    dno = dot_nt(g_ref[...], wo_ref[...])
    dno_ref[...] = dno
    ss = jnp.sum(gated * gated, axis=1, keepdims=True)
    sa = jnp.sum(dno * cp[0:1, :] * gated, axis=1, keepdims=True)
    lane = iota((BLK, 128), 1)
    stat_ref[...] = jnp.where(lane == 0, ss, jnp.where(lane == 1, sa, 0.0))


def bwd_kernel(
    nrm_ref, g_ref, proj_ref, halo_ref, ssd_ref, dno_ref, st_ref, stat_ref, w_ref,
    nw_ref, cw_ref, hp_ref, cp_ref, tok_ref, idr_ref,
    no_ref, dproj_ref, dn_ref, cg_ref, hg_ref, cpg_ref, nwg_ref,
    cbuf, dcbuf, dstate,
):
    step_id = pl.program_id(0)

    @pl.when(step_id == 0)
    def _():
        dstate[...] = jnp.zeros_like(dstate)
        dcbuf[BLK : BLK + 8, :] = jnp.zeros((8, CONVC), F32)
        cg_ref[...] = jnp.zeros_like(cg_ref)
        hg_ref[...] = jnp.zeros_like(hg_ref)
        cpg_ref[...] = jnp.zeros_like(cpg_ref)
        nwg_ref[...] = jnp.zeros_like(nwg_ref)

    proj = proj_ref[...]
    tok = tok_ref[...]
    cw = cw_ref[...]
    hp = hp_ref[...]
    cp = cp_ref[...]
    gate_w = cp[0:1, :]
    z = proj[:, :NZ].astype(F32)
    sig_z = sigmoid(z)
    silu_z = z * sig_z
    ssd = ssd_ref[...]
    dno = dno_ref[...]
    stat = stat_ref[...]
    s2 = lax.rsqrt(stat[:, 0:1] * (1.0 / DI) + EPSILON)
    mean_ag = stat[:, 1:2] * (1.0 / DI)
    gated = ssd * silu_z
    gs = gated * s2
    no_ref[...] = (gs * gate_w).astype(BF)
    d_gate_w = jnp.sum(dno * gs, axis=0, keepdims=True)
    d_gated = s2 * (dno * gate_w) - gated * (s2 * s2 * s2 * mean_ag)
    dy = d_gated * silu_z
    dz = d_gated * ssd * sig_z * (1.0 + z * (1.0 - sig_z))
    cbuf[0:8, :] = halo_ref[0]
    cbuf[8 : 8 + BLK, :] = proj[:, NZ : NZ + CONVC].astype(F32)
    conv_out = conv_taps(cbuf, cw, tok)
    sig_c = sigmoid(conv_out)
    act = conv_out * sig_c
    x = act[:, :CH]
    bm = act[:, CH : CH + STATE].astype(BF)
    cm_f = act[:, CH + STATE :]
    cm = cm_f.astype(BF)
    dt_in = proj[:, NZ + CONVC :].astype(F32) + hp[0:1, :]
    step = softplus(dt_in)
    rate = hp[1:2, :]
    tri = lower_tri()
    cum = dot_exact(tri, -step * rate)
    cum_t = cum.T
    mask = (iota((BLK, BLK), 0) >= iota((BLK, BLK), 1)) & (tok[:, 0:1] == idr_ref[0, 0:1, :])
    gm = jnp.where(mask, dot_nt(cm, bm), 0.0)
    ex = spread()
    gh = gather_heads()
    step_x = split_dot(step, ex)
    xs = (x * step_x).astype(BF)
    dyb = dy.astype(BF)
    dyt = dy.T.astype(BF)
    lane = iota((BLK, 128), 1)
    dg = jnp.zeros((BLK, BLK), F32)
    row_sums = jnp.zeros((BLK, 128), F32)
    col_sums = []
    e_rows = []
    for h in range(HPD):
        pair = h // 2
        decay = jnp.exp(jnp.minimum(cum[:, h : h + 1] - cum_t[h : h + 1, :], 0.0))
        mixed = gm * decay
        half = jnp.where((lane < HEADDIM) == (h % 2 == 0), dyb[:, 128 * pair : 128 * pair + 128], 0)
        dms = dot_nt(half.astype(BF), xs[:, 128 * pair : 128 * pair + 128])
        product = dms * mixed
        row_sums = jnp.where(lane == h, jnp.sum(product, axis=1, keepdims=True), row_sums)
        col_sums.append(jnp.sum(product, axis=0, keepdims=True))
        dg = dg + dms * decay
        e_rows.append(dot(dyt[HEADDIM * h : HEADDIM * h + HEADDIM, :], mixed.astype(BF)))
    dg = jnp.where(mask, dg, 0.0).astype(BF)
    e = jnp.concatenate(e_rows, axis=0).T
    col_sums.append(jnp.zeros((128 - HPD, BLK), F32))
    col = jnp.concatenate(col_sums, axis=0).T
    keep = tok[:, 7:8]
    same_last = tok[:, 8:9]
    old = st_ref[0]
    old_b = old.astype(BF)
    dnew = dstate[...]
    dnew_b = dnew.astype(BF)
    carry_w = keep * jnp.exp(cum)
    carry_x = split_dot(carry_w, ex)
    dyk = (dy * carry_x).astype(BF)
    carried = dot(cm, old_b)
    last = cum[BLK - 1 : BLK, :]
    fade = jnp.exp(last - cum) * same_last
    weights = fade * step
    weights_x = split_dot(weights, ex)
    zt = dot(bm, dnew_b)
    xw = (x * weights_x).astype(BF)
    through = keep[BLK - 1 :, :] * jnp.exp(last)
    through_x = split_dot(jnp.broadcast_to(through, (8, 128)), ex)[0:1, :]
    k_term = split_dot(dy * carry_x * carried, gh)
    r_term = split_dot(x * zt, gh)
    q_term = split_dot(x * e, gh)
    pass_term = jnp.sum(old * dnew, axis=0, keepdims=True) * through_x
    pass_h = split_dot(jnp.broadcast_to(pass_term, (8, CH)), gh)[0:1, :]
    wr = weights * r_term
    d_cum = row_sums - col + k_term - wr
    d_last = jnp.sum(wr, axis=0, keepdims=True) + pass_h
    d_cum = d_cum + jnp.where(iota((BLK, 128), 0) == BLK - 1, d_last, 0.0)
    upper = (iota((BLK, BLK), 0) <= iota((BLK, BLK), 1)).astype(F32)
    d_log = dot_exact(upper, d_cum)
    d_step = q_term + fade * r_term - d_log * rate
    d_a = -jnp.sum(d_log * step, axis=0, keepdims=True) * rate
    d_dt = d_step * sigmoid(dt_in)
    d_bias = jnp.sum(d_dt, axis=0, keepdims=True)
    dstate[...] = dot_tn(cm, dyk) + through_x * dnew
    dx = step_x * e + weights_x * zt + cp[1:2, :] * dy
    d_skip = jnp.sum(dy * x, axis=0, keepdims=True)
    dc = dot(dg, bm) + dot_nt(dyk, old_b)
    db = dot(cm_f.T.astype(BF), dg).T + dot_nt(xw, dnew_b)
    d_act = jnp.concatenate([dx, db, dc], axis=1)
    d_conv = d_act * (sig_c * (1.0 + conv_out * (1.0 - sig_c)))
    dcbuf[0:BLK, :] = d_conv
    d_in = cw[CONV - 1 : CONV, :] * d_conv
    cg = [None] * CONV
    cg[CONV - 1] = jnp.sum(d_conv * cbuf[8 : 8 + BLK, :], axis=0, keepdims=True)
    for back in range(1, CONV):
        tap = CONV - 1 - back
        cg[tap] = jnp.sum(
            d_conv * (cbuf[8 - back : 8 - back + BLK, :] * tok[:, back : back + 1]),
            axis=0, keepdims=True,
        )
        d_in = d_in + cw[tap : tap + 1, :] * (
            dcbuf[back : back + BLK, :] * tok[:, 3 + back : 4 + back]
        )
    dcbuf[BLK : BLK + 8, :] = dcbuf[0:8, :]
    d_b = jnp.sum(d_conv, axis=0, keepdims=True)
    cg_ref[...] += jnp.concatenate(cg + [d_b, jnp.zeros((3, CONVC), F32)], axis=0)
    hg_ref[...] += jnp.concatenate([d_a, d_bias, jnp.zeros((6, 128), F32)], axis=0)
    cpg_ref[...] += jnp.concatenate([d_gate_w, d_skip, jnp.zeros((6, CH), F32)], axis=0)
    dproj = jnp.concatenate([dz, d_in, d_dt], axis=1).astype(BF)
    dproj_ref[...] = dproj
    dn = dot_nt(dproj, w_ref[...])
    dn_ref[...] = dn.astype(BF)
    nwg_ref[0:1, :] += jnp.sum(dn * nrm_ref[...].astype(F32), axis=0, keepdims=True) / nw_ref[...]


def whole(shape):
    return pl.BlockSpec(shape, lambda i: (0,) * len(shape), pipeline_mode=pl.Buffered(1))


def forward_call(u, g, w, wo, nw, cw, hp, cp, tok, idr):
    n = u.shape[0]
    blocks = n // BLK
    rows = lambda c: pl.BlockSpec((BLK, c), lambda i: (i, 0))
    cube = lambda a, b: pl.BlockSpec((1, a, b), lambda i: (i, 0, 0))
    sds = jax.ShapeDtypeStruct
    return pl.pallas_call(
        fwd_kernel,
        grid=(blocks,),
        in_specs=[rows(D), rows(D), whole((D, COLS)), whole((CH, D)), whole((1, D)),
                  whole((8, CONVC)), whole((8, 128)), whole((8, CH)), rows(128), cube(8, BLK)],
        out_specs=[rows(D), rows(COLS), cube(8, CONVC), rows(CH), rows(CH), cube(STATE, CH),
                   rows(128), rows(D)],
        out_shape=[sds((n, D), BF), sds((n, COLS), BF), sds((blocks, 8, CONVC), F32),
                   sds((n, CH), F32), sds((n, CH), F32), sds((blocks, STATE, CH), F32),
                   sds((n, 128), F32), sds((n, D), BF)],
        scratch_shapes=[pltpu.VMEM((BLK + 8, CONVC), F32), pltpu.VMEM((STATE, CH), F32)],
        compiler_params=pltpu.CompilerParams(vmem_limit_bytes=56 << 20),
    )(u, g, w, wo, nw, cw, hp, cp, tok, idr)


def backward_call(nrm, g, proj, halo, ssd, dno, st, stat, w, nw, cw, hp, cp, tok, idr):
    n = nrm.shape[0]
    blocks = n // BLK
    back = blocks - 1
    rows = lambda c: pl.BlockSpec((BLK, c), lambda i: (back - i, 0))
    cube = lambda a, b: pl.BlockSpec((1, a, b), lambda i: (back - i, 0, 0))
    keepb = lambda a, b: pl.BlockSpec((a, b), lambda i: (0, 0))
    sds = jax.ShapeDtypeStruct
    return pl.pallas_call(
        bwd_kernel,
        grid=(blocks,),
        in_specs=[rows(D), rows(D), rows(COLS), cube(8, CONVC), rows(CH), rows(CH),
                  cube(STATE, CH), rows(128), whole((D, COLS)), whole((1, D)), whole((8, CONVC)),
                  whole((8, 128)), whole((8, CH)), rows(128), cube(8, BLK)],
        out_specs=[rows(CH), rows(COLS), rows(D), keepb(8, CONVC), keepb(8, 128), keepb(8, CH),
                   keepb(8, D)],
        out_shape=[sds((n, CH), BF), sds((n, COLS), BF), sds((n, D), BF), sds((8, CONVC), F32),
                   sds((8, 128), F32), sds((8, CH), F32), sds((8, D), F32)],
        scratch_shapes=[pltpu.VMEM((BLK + 8, CONVC), F32), pltpu.VMEM((BLK + 8, CONVC), F32),
                        pltpu.VMEM((STATE, CH), F32)],
        compiler_params=pltpu.CompilerParams(vmem_limit_bytes=56 << 20),
    )(nrm, g, proj, halo, ssd, dno, st, stat, w, nw, cw, hp, cp, tok, idr)


def token_info(ids_full, first, n):
    length = ids_full.shape[0]
    pad = jnp.concatenate(
        [jnp.full((8,), -1, jnp.int32), ids_full, jnp.full((8,), -2, jnp.int32)]
    )
    window = lax.dynamic_slice_in_dim(pad, first, n + 16)
    own = window[8 : 8 + n]
    blocks = own.reshape(-1, BLK)
    before = window[7 : 7 + n].reshape(-1, BLK)[:, :1]
    cols = [own]
    for back in range(1, CONV):
        cols.append((window[8 - back : 8 - back + n] == own))
    for ahead in range(1, CONV):
        cols.append((window[8 + ahead : 8 + ahead + n] == own))
    cols.append((blocks == before).reshape(-1))
    cols.append((blocks == blocks[:, -1:]).reshape(-1))
    table = jnp.stack([c.astype(F32) for c in cols], axis=1)
    tok = jnp.pad(table, ((0, 0), (0, 128 - table.shape[1])))
    idr = jnp.broadcast_to(own.astype(F32).reshape(-1, 1, BLK), (n // BLK, 8, BLK))
    return tok, idr


def on_team(
    tokens, segment_ids, cotangent, w_in, w_out, conv_w, conv_b, a_log, dt_bias, d_skip,
    norm_w, gate_w,
):
    place = lax.axis_index("seq")
    depth = lax.axis_index("fsdp")
    shards = lax.axis_size("fsdp")
    n = tokens.shape[1] * TEAM
    ch0 = place * CH
    cut = lambda a, start, size: lax.dynamic_slice_in_dim(a, start, size, a.ndim - 1)
    w_shard = jnp.concatenate(
        [cut(w_in, ch0, CH), cut(w_in, DI + ch0, CH), w_in[:, 2 * DI : 2 * DI + NB],
         jnp.pad(cut(w_in, DI + CHAN + place * HPD, HPD), ((0, 0), (0, ND - HPD)))], axis=1)
    w_loc = lax.all_gather(w_shard, "fsdp", axis=0, tiled=True)
    rows_out = w_out.shape[0]
    holder = ch0 // rows_out
    w_out_mine = lax.dynamic_slice_in_dim(w_out, ch0 - holder * rows_out, CH, 0)
    wo_loc = lax.psum(jnp.where(depth == holder, w_out_mine, 0), "fsdp")
    small = jnp.concatenate([conv_w.reshape(-1), conv_b, a_log, dt_bias, d_skip, norm_w, gate_w])
    small = lax.all_gather(small, "fsdp", axis=0, tiled=False).astype(F32)
    sizes = [conv_w.size, conv_b.size, a_log.size, dt_bias.size, d_skip.size, norm_w.size, gate_w.size]
    offs = [0]
    for size in sizes:
        offs.append(offs[-1] + size)
    part = [small[:, offs[i] : offs[i + 1]] for i in range(7)]
    taps = part[0].reshape(shards, CONV, -1).transpose(1, 0, 2).reshape(CONV, CHAN)
    bias, alog, dtb, skip, normw, gatew = [p.reshape(1, -1) for p in part[1:]]
    conv_all = jnp.concatenate([taps, bias, jnp.zeros((3, CHAN), F32)], axis=0)
    cw = jnp.concatenate([cut(conv_all, ch0, CH), conv_all[:, DI:]], axis=1)
    heads = jnp.concatenate([dtb, jnp.exp(alog), jnp.zeros((6, HEADS), F32)], axis=0)
    hp = cut(heads, place * HPD, HPD)
    hp = jnp.concatenate(
        [hp, jnp.where(jnp.arange(8)[:, None] == 0, -100.0, 0.0) * jnp.ones((8, 128 - HPD), F32)], axis=1)
    cp = jnp.concatenate([gatew, jnp.repeat(skip, HEADDIM, axis=1), jnp.zeros((6, DI), F32)], axis=0)
    cp = cut(cp, ch0, CH)
    tok, idr = token_info(segment_ids[0], 0, n)
    u_own, g_own = tokens[0], cotangent[0]
    u = lax.all_gather(u_own, "seq", axis=0, tiled=True)
    g = lax.all_gather(g_own, "seq", axis=0, tiled=True)
    nrm, proj, halo, ssd, dno, st, stat, br = forward_call(
        u, g, w_loc, wo_loc, normw, cw, hp, cp, tok, idr)
    stat = lax.psum(stat, "seq")
    no, dproj, dn, cg, hg, cpg, nwg = backward_call(
        nrm, g, proj, halo, ssd, dno, st, stat, w_loc, normw, cw, hp, cp, tok, idr)
    branch = lax.psum_scatter(br, "seq", scatter_dimension=0, tiled=True).astype(F32)
    d_normed = lax.psum_scatter(dn, "seq", scatter_dimension=0, tiled=True).astype(F32)
    ss = lax.dynamic_slice_in_dim(stat[:, 0:1], place * BLK, BLK, 0)
    uf = u_own.astype(F32)
    layer_out = (uf + branch * lax.rsqrt(ss / DI + EPSILON)).astype(BF)
    s1 = lax.rsqrt(jnp.mean(uf * uf, axis=1, keepdims=True) + EPSILON)
    along = d_normed * normw
    token_grad = g_own.astype(F32) + s1 * along - uf * (s1 * s1 * s1) * jnp.mean(along * uf, axis=1, keepdims=True)
    wig = dot_tn(nrm, dproj).astype(BF)
    wog = dot_tn(no, g).astype(BF)
    wig = lax.psum_scatter(wig, "fsdp", scatter_dimension=0, tiled=True)
    bc = lax.psum(wig[:, NZ + NX : NZ + NX + NB].astype(F32), "seq")
    own_cols = jnp.concatenate([wig[:, : NZ + NX], wig[:, NZ + NX + NB :]], axis=1)
    allc = lax.all_gather(own_cols, "seq", axis=0, tiled=False).astype(F32)
    flat = lambda a: a.transpose(1, 0, 2).reshape(a.shape[1], -1)
    w_in_grad = jnp.concatenate(
        [flat(allc[:, :, :CH]), flat(allc[:, :, CH : 2 * CH]), bc,
         flat(allc[:, :, 2 * CH : 2 * CH + HPD])], axis=1)
    wog_z = lax.psum(wog, "fsdp")
    wog_all = lax.all_gather(wog_z, "seq", axis=0, tiled=True)
    w_out_grad = lax.dynamic_slice_in_dim(wog_all, depth * rows_out, rows_out, 0).astype(F32)
    spot = lambda a, width, size: lax.dynamic_update_slice_in_dim(
        jnp.zeros(a.shape[:-1] + (width,), F32), a, place * size, a.ndim - 1)
    convg = jnp.concatenate([spot(cg[:5, :CH], DI, CH), cg[:5, CH:]], axis=1)
    headg = spot(hg[:2, :HPD], HEADS, HPD)
    chang = spot(cpg[:2], DI, CH)
    convg, headg, chang, normg = lax.psum((convg, headg, chang, nwg[0]), ("seq", "fsdp"))
    mine = lambda a, size: cut(a, depth * size, size)
    conv_wg = mine(convg[:4], CHAN // shards)
    conv_bg = mine(convg[4], CHAN // shards)
    ag = mine(headg[0], HEADS // shards)
    dg = mine(headg[1], HEADS // shards)
    sg = mine(chang[1].reshape(HEADS, HEADDIM).sum(axis=1), HEADS // shards)
    gg = mine(chang[0], DI // shards)
    ng = mine(normg, D // shards)
    return (layer_out[None], token_grad[None], w_in_grad, w_out_grad, conv_wg, conv_bg, ag, dg, sg, ng, gg)


def solution(mesh):
    body = on_team if mesh.shape["seq"] == TEAM else on_device
    return jax.shard_map(
        body,
        mesh=mesh,
        in_specs=(
            P("fsdp", "seq", None),
            P("fsdp", None),
            P("fsdp", "seq", None),
            P("fsdp", None),
            P("fsdp", None),
            P(None, "fsdp"),
            P("fsdp"),
            P("fsdp"),
            P("fsdp"),
            P("fsdp"),
            P("fsdp"),
            P("fsdp"),
        ),
        out_specs=(
            P("fsdp", "seq", None),
            P("fsdp", "seq", None),
            P("fsdp", None),
            P("fsdp", None),
            P(None, "fsdp"),
            P("fsdp"),
            P("fsdp"),
            P("fsdp"),
            P("fsdp"),
            P("fsdp"),
            P("fsdp"),
        ),
        check_vma=False,
    )
```

```python
import jax
import jax.numpy as jnp
from jax import lax
from jax.experimental import pallas as pl
from jax.experimental.pallas import tpu as pltpu
from jax.sharding import PartitionSpec as P

DI = 3072
HEADDIM = 64
STATE = 128
CONV = 4
SPAN = 256
HEADS = 48
D = 1536
WIDTH = 6448
CHAN = 3328


EPSILON = 1e-05
HIGHEST = lax.Precision.HIGHEST


def passed_along(value, axis, steps):
    count = lax.axis_size(axis)
    first, last = (max(0, -steps), min(count, count - steps))
    return lax.ppermute(value, axis, [(source, source + steps) for source in range(first, last)])


def shortened(array):

    def short(part):
        return part.astype(jnp.bfloat16) if part.dtype == jnp.float32 else part

    return jax.tree.map(short, array)


def block_masks(ids_blocks, before_ids):
    block_len = ids_blocks.shape[1]
    places = jnp.arange(block_len)
    causal_mask = (places[:, None] >= places[None, :])[None] & (
        ids_blocks[:, :, None] == ids_blocks[:, None, :]
    )
    keep_flag = (ids_blocks == before_ids[:, None]).astype(jnp.float32)
    same_last = (ids_blocks == ids_blocks[:, -1:]).astype(jnp.float32)
    return (causal_mask, keep_flag, same_last)


def local_states(x_heads, b_rows, step_size, log_decay, same_last, keep_flag):
    cum_decay = jnp.cumsum(log_decay, axis=1)
    last_cum = cum_decay[:, -1]
    weights = jnp.exp(last_cum[:, None, :] - cum_decay) * step_size * same_last[:, :, None]
    fresh_state = jnp.einsum("csh,cshp,csn->chpn", weights, x_heads, b_rows, precision=HIGHEST)
    passing = keep_flag[:, -1:] * jnp.exp(last_cum)
    total_state = jnp.zeros_like(fresh_state[0])
    total_decay = jnp.ones_like(passing[0])
    total_state = fresh_state[0] + passing[0][:, None, None] * total_state
    total_decay = total_decay * passing[0]
    return (fresh_state, passing, total_state, total_decay)


def local_output(x_heads, b_rows, c_rows, step_size, log_decay, incoming, causal_mask, keep_flag):
    cum_decay = jnp.cumsum(log_decay, axis=1)
    cum_heads = jnp.swapaxes(cum_decay, 1, 2)
    gap_decay = cum_heads[:, :, :, None] - cum_heads[:, :, None, :]
    head_mask = causal_mask[:, None]
    decay_map = jnp.exp(jnp.where(head_mask, gap_decay, 0.0)) * head_mask.astype(jnp.float32)
    scores = jnp.einsum("ctn,csn->cts", c_rows, b_rows, precision=HIGHEST)
    mixing = scores[:, None] * decay_map * jnp.swapaxes(step_size, 1, 2)[:, :, None, :]
    inner_out = jnp.einsum("chts,cshp->cthp", mixing, x_heads, precision=HIGHEST)
    starts = [incoming]
    start_states = jnp.stack(starts)
    carried = jnp.einsum("ctn,chpn->cthp", c_rows, start_states, precision=HIGHEST)
    carried = carried * (keep_flag[:, :, None] * jnp.exp(cum_decay))[..., None]
    return inner_out + carried


def on_device(
    tokens,
    segment_ids,
    cotangent,
    w_in,
    w_out,
    conv_w,
    conv_b,
    a_log,
    dt_bias,
    d_skip,
    norm_w,
    gate_w,
):
    gathered = (
        lax.all_gather(w_in, "fsdp", axis=0, tiled=True),
        lax.all_gather(w_out, "fsdp", axis=0, tiled=True),
        lax.all_gather(conv_w, "fsdp", axis=1, tiled=True),
        lax.all_gather(conv_b, "fsdp", axis=0, tiled=True),
        lax.all_gather(a_log, "fsdp", axis=0, tiled=True),
        lax.all_gather(dt_bias, "fsdp", axis=0, tiled=True),
        lax.all_gather(d_skip, "fsdp", axis=0, tiled=True),
        lax.all_gather(norm_w, "fsdp", axis=0, tiled=True),
        lax.all_gather(gate_w, "fsdp", axis=0, tiled=True),
    )
    (
        w_in_full,
        w_out_full,
        conv_full,
        bias_full,
        a_log_full,
        dt_bias_full,
        skip_full,
        norm_full,
        gate_full,
    ) = gathered
    inputs = tokens[0].astype(jnp.float32)
    length = inputs.shape[0]
    norm_gain = norm_full.astype(jnp.float32)
    scale_in = lax.rsqrt(jnp.mean(inputs * inputs, axis=-1, keepdims=True) + EPSILON)
    normed = (inputs * scale_in * norm_gain).astype(jnp.bfloat16)
    projected = jnp.dot(normed, w_in_full, preferred_element_type=jnp.float32).astype(jnp.bfloat16)
    gate_z = projected[:, :DI].astype(jnp.float32)
    conv_in = projected[:, DI : DI + CHAN]
    dt_raw = projected[:, DI + CHAN :].astype(jnp.float32)
    first_row = lax.axis_index("seq") * length
    id_row = jnp.concatenate([jnp.full((CONV - 1,), -1, jnp.int32), segment_ids[0]], axis=0)
    ids_pad = lax.dynamic_slice_in_dim(id_row, first_row, length + CONV - 1)
    ids_own = ids_pad[CONV - 1 :]
    left_edge = passed_along(conv_in[length - (CONV - 1) :], "seq", 1)
    padded = jnp.concatenate([left_edge, conv_in], axis=0).astype(jnp.float32)
    kernel = conv_full.astype(jnp.float32)
    conv_out = jnp.zeros((length, CHAN), jnp.float32) + bias_full.astype(jnp.float32)
    same_docs = []
    for offset in range(CONV):
        same_doc = (ids_pad[offset : offset + length] == ids_own).astype(jnp.float32)
        same_docs.append(same_doc)
        conv_out = conv_out + kernel[offset] * padded[offset : offset + length] * same_doc[:, None]
    activated = jax.nn.silu(conv_out)
    blocks = length // SPAN
    x_heads = activated[:, :DI].reshape(blocks, SPAN, HEADS, HEADDIM)
    b_rows = activated[:, DI : DI + STATE].reshape(blocks, SPAN, STATE)
    c_rows = activated[:, DI + STATE :].reshape(blocks, SPAN, STATE)
    dt_bias_f = dt_bias_full.astype(jnp.float32)
    decay_rate = jnp.exp(a_log_full.astype(jnp.float32))
    step_flat = jax.nn.softplus(dt_raw + dt_bias_f)
    step_size = step_flat.reshape(blocks, SPAN, HEADS)
    log_decay = (-step_flat * decay_rate).reshape(blocks, SPAN, HEADS)
    ids_blocks = ids_own.reshape(blocks, SPAN)
    before_ids = ids_pad[CONV - 2 : CONV - 2 + length : SPAN]
    causal_mask, keep_flag, same_last = block_masks(ids_blocks, before_ids)

    def state_part(heads_in, rows_b, steps_in, decay_in):
        return local_states(heads_in, rows_b, steps_in, decay_in, same_last, keep_flag)

    (fresh_state, passing, total_state, total_decay), state_pull = jax.vjp(
        state_part, x_heads, b_rows, step_size, log_decay
    )

    def pass_forward(turn_index, received):
        return passed_along(
            (total_state + total_decay[:, None, None] * received).astype(jnp.bfloat16), "seq", 1
        ).astype(jnp.float32)

    incoming = lax.fori_loop(0, lax.axis_size("seq") - 1, pass_forward, jnp.zeros_like(total_state))

    def output_part(
        heads_in, rows_b, rows_c, steps_in, decay_in, fresh_in, passing_in, incoming_in
    ):
        return local_output(
            heads_in, rows_b, rows_c, steps_in, decay_in, incoming_in, causal_mask, keep_flag
        )

    ssd_out, output_pull = jax.vjp(
        output_part, x_heads, b_rows, c_rows, step_size, log_decay, fresh_state, passing, incoming
    )
    skip_heads = skip_full.astype(jnp.float32)
    y_full = (ssd_out + skip_heads[:, None] * x_heads).reshape(length, DI)
    silu_z = jax.nn.silu(gate_z)
    gated = y_full * silu_z
    scale_out = lax.rsqrt(jnp.mean(gated * gated, axis=-1, keepdims=True) + EPSILON)
    gate_gain = gate_full.astype(jnp.float32)
    normed_out = (gated * scale_out * gate_gain).astype(jnp.bfloat16)
    branch = jnp.dot(normed_out, w_out_full, preferred_element_type=jnp.float32)
    layer_out = (inputs + branch).astype(jnp.bfloat16)[None]
    grad_out = cotangent[0]
    d_w_out = lax.dot_general(
        normed_out, grad_out, (((0,), (0,)), ((), ())), preferred_element_type=jnp.float32
    )
    d_normed_out = lax.dot_general(
        grad_out, w_out_full, (((1,), (1,)), ((), ())), preferred_element_type=jnp.float32
    )
    d_gate_w = jnp.sum(d_normed_out * gated * scale_out, axis=0)
    along_out = d_normed_out * gate_gain
    cube_out = scale_out * scale_out * scale_out
    d_gated = scale_out * along_out - gated * cube_out * jnp.mean(
        along_out * gated, axis=-1, keepdims=True
    )
    d_y = d_gated * silu_z
    sig_z = jax.nn.sigmoid(gate_z)
    d_gate_z = d_gated * y_full * sig_z * (1.0 + gate_z * (1.0 - sig_z))
    d_ssd = d_y.reshape(blocks, SPAN, HEADS, HEADDIM)
    d_skip_grad = jnp.sum(d_ssd * x_heads, axis=(0, 1, 3))
    dx_out, db_out, dc_out, dstep_out, ddecay_out, d_fresh, d_passing, d_incoming = output_pull(
        d_ssd
    )

    def pass_backward(turn_index, received):
        return passed_along(d_incoming + total_decay[:, None, None] * received, "seq", -1)

    d_total = lax.fori_loop(0, lax.axis_size("seq") - 1, pass_backward, jnp.zeros_like(d_incoming))
    d_total_decay = jnp.sum(d_total * incoming, axis=(1, 2))
    dx_state, db_state, dstep_state, ddecay_state = state_pull(
        (d_fresh, d_passing, d_total, d_total_decay)
    )
    d_x = dx_out + dx_state + skip_heads[:, None] * d_ssd
    d_b = db_out + db_state
    d_log = (ddecay_out + ddecay_state).reshape(length, HEADS)
    d_step = (dstep_out + dstep_state).reshape(length, HEADS) - d_log * decay_rate
    d_a_log = -jnp.sum(d_log * step_flat, axis=0) * decay_rate
    d_dt_raw = d_step * jax.nn.sigmoid(dt_raw + dt_bias_f)
    d_dt_bias = jnp.sum(d_dt_raw, axis=0)
    d_act = jnp.concatenate(
        [d_x.reshape(length, DI), d_b.reshape(length, STATE), dc_out.reshape(length, STATE)], axis=1
    )
    sig_conv = jax.nn.sigmoid(conv_out)
    d_conv = d_act * sig_conv * (1.0 + conv_out * (1.0 - sig_conv))
    d_conv_b = jnp.sum(d_conv, axis=0)
    kernel_rows = []
    d_padded = jnp.zeros((length + CONV - 1, CHAN), jnp.float32)
    for offset in range(CONV):
        masked = d_conv * same_docs[offset][:, None]
        kernel_rows.append(jnp.sum(masked * padded[offset : offset + length], axis=0))
        d_padded = d_padded + jnp.pad(
            kernel[offset] * masked, ((offset, CONV - 1 - offset), (0, 0))
        )
    d_kernel = jnp.stack(kernel_rows)
    d_edge = passed_along(shortened(d_padded[: CONV - 1]), "seq", -1)
    d_conv_in = d_padded[CONV - 1 :] + jnp.pad(d_edge, ((length - (CONV - 1), 0), (0, 0)))
    d_projected = jnp.concatenate([d_gate_z, d_conv_in, d_dt_raw], axis=1).astype(jnp.bfloat16)
    d_normed = lax.dot_general(
        d_projected, w_in_full, (((1,), (1,)), ((), ())), preferred_element_type=jnp.float32
    )
    d_norm_w = jnp.sum(d_normed * inputs * scale_in, axis=0)
    along_in = d_normed * norm_gain
    cube_in = scale_in * scale_in * scale_in
    d_inputs = (
        scale_in * along_in
        - inputs * cube_in * jnp.mean(along_in * inputs, axis=-1, keepdims=True)
        + grad_out.astype(jnp.float32)
    )
    d_w_in = lax.dot_general(
        normed, d_projected, (((0,), (0,)), ((), ())), preferred_element_type=jnp.float32
    )
    weight_grads = (
        d_w_in,
        d_w_out,
        d_kernel,
        d_conv_b,
        d_a_log,
        d_dt_bias,
        d_skip_grad,
        d_norm_w,
        d_gate_w,
    )
    shares = tuple(
        (
            lax.psum_scatter(weight_grads[0], "fsdp", scatter_dimension=0, tiled=True),
            lax.psum_scatter(weight_grads[1], "fsdp", scatter_dimension=0, tiled=True),
            lax.psum_scatter(weight_grads[2], "fsdp", scatter_dimension=1, tiled=True),
            lax.psum_scatter(weight_grads[3], "fsdp", scatter_dimension=0, tiled=True),
            lax.psum_scatter(weight_grads[4], "fsdp", scatter_dimension=0, tiled=True),
            lax.psum_scatter(weight_grads[5], "fsdp", scatter_dimension=0, tiled=True),
            lax.psum_scatter(weight_grads[6], "fsdp", scatter_dimension=0, tiled=True),
            lax.psum_scatter(weight_grads[7], "fsdp", scatter_dimension=0, tiled=True),
            lax.psum_scatter(weight_grads[8], "fsdp", scatter_dimension=0, tiled=True),
        )
    )
    totals = lax.psum(shares, "seq")
    return (layer_out, d_inputs[None]) + tuple(totals)


F32 = jnp.float32
BF = jnp.bfloat16
BLK = 256
TEAM = 8
HPD = HEADS // TEAM
CH = HPD * HEADDIM
NZ, NX, NB, ND = CH, CH, 2 * STATE, 64
COLS = NZ + NX + NB + ND
REST = NX + NB + ND
CONVC = NX + NB
TAIL = CONV - 1


def dot(a, b):
    return lax.dot_general(a, b, (((1,), (0,)), ((), ())), preferred_element_type=F32)


def dot_nt(a, b):
    return lax.dot_general(a, b, (((1,), (1,)), ((), ())), preferred_element_type=F32)


def dot_tn(a, b):
    return lax.dot_general(a, b, (((0,), (0,)), ((), ())), preferred_element_type=F32)


def dot_exact(a, b):
    return lax.dot_general(
        a, b, (((1,), (0,)), ((), ())), precision=HIGHEST, preferred_element_type=F32
    )


def iota(shape, dim):
    return lax.broadcasted_iota(jnp.int32, shape, dim)


def split_dot(a, b):
    high = a.astype(BF)
    low = (a - high.astype(F32)).astype(BF)
    return dot(high, b) + dot(low, b)


def spread():
    return (iota((128, CH), 1) // HEADDIM == iota((128, CH), 0)).astype(BF)


def gather_heads():
    return (iota((CH, 128), 0) // HEADDIM == iota((CH, 128), 1)).astype(BF)


def lower_tri():
    return (iota((BLK, BLK), 0) >= iota((BLK, BLK), 1)).astype(F32)


def softplus(v):
    return jnp.maximum(v, 0.0) + jnp.log1p(jnp.exp(-jnp.abs(v)))


def sigmoid(v):
    return 1.0 / (1.0 + jnp.exp(-v))


def conv_taps(cbuf, cw, tok):
    out = cw[CONV : CONV + 1, :] + cw[CONV - 1 : CONV, :] * cbuf[8 : 8 + BLK, :]
    for back in range(1, CONV):
        term = cw[CONV - 1 - back : CONV - back, :] * cbuf[8 - back : 8 - back + BLK, :]
        out = out + term * tok[:, back : back + 1]
    return out


def pair_select(left, right):
    return jnp.where(iota(left.shape, 1) % 128 < HEADDIM, left, right)


def head_of(slot, chip, core):
    first = 12 * slot + 3 * chip + 2 * core
    second = 12 * (core + 2 * (slot - 4)) + 3 * chip + 1
    return first, second


def pick_heads():
    seq = lax.axis_index("seq")
    chip, core = lax.div(seq, 2), lax.rem(seq, 2)
    slot = iota((128, 128), 1)
    first, second = head_of(slot, chip, core)
    head = jnp.where(slot < 4, first, jnp.where(slot < HPD, second, -1))
    return (iota((128, 128), 0) == head).astype(BF)


def own_heads(par, dt_cols):
    pick = pick_heads()
    pair = jnp.concatenate([par[5:6, CH : CH + 128], par[5:6, CH + 128 :], jnp.zeros((6, 128), F32)], axis=0)
    pair = dot(pair.astype(BF), pick)
    wide = jnp.concatenate([dt_cols, jnp.zeros((BLK, 128 - ND), BF)], axis=1)
    return jnp.exp(pair[1:2, :]), dot(wide, pick) + pair[0:1, :], iota((BLK, 128), 1) < HPD, pick


def norm_gain(par):
    return jnp.concatenate([par[7 + i : 8 + i, :512] for i in range(3)], axis=1)


def row_sum(q):
    high = q.astype(BF)
    low = (q - high.astype(F32)).astype(BF)
    ones = jnp.ones((8, q.shape[1]), BF)
    return (dot_nt(ones, high) + dot_nt(ones, low))[0:1, :]


def scan_forward(j, nrm, w_v, par, tok, idr, cbuf, state, projc_ref, st_ref, ssd_v):
    rows = pl.ds(pl.multiple_of(BLK * j, BLK), BLK)
    proj = dot_nt(nrm, w_v[NZ:, :]).astype(BF)
    projc_ref[...] = proj
    cbuf[8 : 8 + BLK, :] = proj[:, :CONVC].astype(F32)
    conv_out = conv_taps(cbuf, par, tok)
    cbuf[0:8, :] = cbuf[BLK : BLK + 8, :]
    act = conv_out * sigmoid(conv_out)
    x = act[:, :CH]
    bm = act[:, CH : CH + STATE].astype(BF)
    cm = act[:, CH + STATE :].astype(BF)
    rate, dt_in, own, pick = own_heads(par, proj[:, CONVC:])
    step = jnp.where(own, softplus(dt_in), 0.0)
    cum = dot_exact(lower_tri(), -step * rate)
    cum_t = cum.T
    mask = (iota((BLK, BLK), 0) >= iota((BLK, BLK), 1)) & (tok[:, 0:1] == idr)
    gm = jnp.where(mask, dot_nt(cm, bm), 0.0)
    ex = spread()
    xs = (x * split_dot(step, ex)).astype(BF)
    parts = []
    for pair in range(HPD // 2):
        xp = xs[:, 128 * pair : 128 * pair + 128]
        both = []
        for h in (2 * pair, 2 * pair + 1):
            decay = jnp.exp(jnp.minimum(cum[:, h : h + 1] - cum_t[h : h + 1, :], 0.0))
            both.append(dot((gm * decay).astype(BF), xp))
        parts.append(pair_select(*both))
    inner = jnp.concatenate(parts, axis=1)
    old = state[...]
    st_ref[0] = old
    keep = tok[:, 7:8]
    carried = split_dot(keep * jnp.exp(cum), ex) * dot(cm, old.astype(BF))
    last = cum[BLK - 1 : BLK, :]
    weights = jnp.exp(last - cum) * step * tok[:, 8:9]
    through = split_dot(jnp.broadcast_to(keep[BLK - 1 :, :] * jnp.exp(last), (8, 128)), ex)[0:1, :]
    state[...] = dot_tn(bm, (x * split_dot(weights, ex)).astype(BF)) + through * old
    ssd_v[rows, :] = inner + carried + par[6:7, :CH] * x


def gate_forward(j, nrm_v, g_v, w_v, wo_v, par, ssd_v, projz_ref, ssd_ref, dno_ref, br_ref, stat_v):
    rows = pl.ds(pl.multiple_of(BLK * j, BLK), BLK)
    projz = dot_nt(nrm_v[rows, :], w_v[:NZ, :]).astype(BF)
    projz_ref[...] = projz
    ssd = ssd_v[rows, :]
    ssd_ref[...] = ssd
    z = projz.astype(F32)
    gate_w = par[5:6, :CH]
    gated = ssd * (z * sigmoid(z))
    br_ref[...] = dot((gated * gate_w).astype(BF), wo_v[...]).astype(BF)
    dno = dot_nt(g_v[rows, :], wo_v[...])
    dno_ref[...] = dno
    stat_v[pl.ds(j, 1), 0:BLK] = row_sum(gated * gated)
    stat_v[pl.ds(j, 1), BLK : 2 * BLK] = row_sum(dno * gate_w * gated)


def gate_backward(j, z, ssd, dno, stat, gate_w, not_v, dy_v, dz_v, dzt_v, small_v):
    rows = pl.ds(pl.multiple_of(BLK * j, BLK), BLK)
    sig_z = sigmoid(z)
    silu_z = z * sig_z
    stat = jnp.where(iota((128, BLK), 0) == 0, stat[:, :BLK], stat[:, BLK:]).T
    s2 = lax.rsqrt(stat[:, 0:1] * (1.0 / DI) + EPSILON)
    mean_ag = stat[:, 1:2] * (1.0 / DI)
    gated = ssd * silu_z
    gs = gated * s2
    not_v[:, rows] = (gs * gate_w).T.astype(BF)
    d_gated = s2 * (dno * gate_w) - gated * (s2 * s2 * s2 * mean_ag)
    dy_v[rows, :] = d_gated * silu_z
    dz = d_gated * ssd * sig_z * (1.0 + z * (1.0 - sig_z))
    dz_v[rows, :] = dz.astype(BF)
    dzt_v[:, rows] = dz.T.astype(BF)
    small_v[5:6, :CH] += jnp.sum(dno * gs, axis=0, keepdims=True)


def scan_backward(proj, halo, tok, idr, old, par, dy, cbuf, dcbuf, dstate, small_v):
    cbuf[0:8, :] = halo[8:16, :CONVC].astype(F32)
    cbuf[8 : 8 + BLK, :] = proj[:, :CONVC].astype(F32)
    conv_out = conv_taps(cbuf, par, tok)
    sig_c = sigmoid(conv_out)
    act = conv_out * sig_c
    x = act[:, :CH]
    bm = act[:, CH : CH + STATE].astype(BF)
    cm_f = act[:, CH + STATE :]
    cm = cm_f.astype(BF)
    rate, dt_in, own, pick = own_heads(par, proj[:, CONVC:])
    step = jnp.where(own, softplus(dt_in), 0.0)
    cum = dot_exact(lower_tri(), -step * rate)
    cum_t = cum.T
    mask = (iota((BLK, BLK), 0) >= iota((BLK, BLK), 1)) & (tok[:, 0:1] == idr)
    gm = jnp.where(mask, dot_nt(cm, bm), 0.0)
    ex = spread()
    gh = gather_heads()
    step_x = split_dot(step, ex)
    xs = (x * step_x).astype(BF)
    dyb = dy.astype(BF)
    dyt = dy.T.astype(BF)
    lane = iota((BLK, 128), 1)
    dg = jnp.zeros((BLK, BLK), F32)
    row_sums = jnp.zeros((BLK, 128), F32)
    col_sums = []
    e_rows = []
    for h in range(HPD):
        pair = h // 2
        decay = jnp.exp(jnp.minimum(cum[:, h : h + 1] - cum_t[h : h + 1, :], 0.0))
        mixed = gm * decay
        half = jnp.where((lane < HEADDIM) == (h % 2 == 0), dyb[:, 128 * pair : 128 * pair + 128], 0)
        dms = dot_nt(half.astype(BF), xs[:, 128 * pair : 128 * pair + 128])
        product = dms * mixed
        row_sums = jnp.where(lane == h, jnp.sum(product, axis=1, keepdims=True), row_sums)
        col_sums.append(jnp.sum(product, axis=0, keepdims=True))
        dg = dg + dms * decay
        e_rows.append(dot(dyt[HEADDIM * h : HEADDIM * h + HEADDIM, :], mixed.astype(BF)))
    dg = jnp.where(mask, dg, 0.0).astype(BF)
    e = jnp.concatenate(e_rows, axis=0).T
    col_sums.append(jnp.zeros((128 - HPD, BLK), F32))
    col = jnp.concatenate(col_sums, axis=0).T
    keep = tok[:, 7:8]
    old_b = old.astype(BF)
    dnew = dstate[...]
    dnew_b = dnew.astype(BF)
    carry_x = split_dot(keep * jnp.exp(cum), ex)
    dyk_f = dy * carry_x
    dyk = dyk_f.astype(BF)
    carried = dot(cm, old_b)
    last = cum[BLK - 1 : BLK, :]
    fade = jnp.exp(last - cum) * tok[:, 8:9]
    weights = fade * step
    weights_x = split_dot(weights, ex)
    zt = dot(bm, dnew_b)
    xw = (x * weights_x).astype(BF)
    through = keep[BLK - 1 :, :] * jnp.exp(last)
    through_x = split_dot(jnp.broadcast_to(through, (8, 128)), ex)[0:1, :]
    k_term = split_dot(dyk_f * carried, gh)
    r_term = split_dot(x * zt, gh)
    q_term = split_dot(x * e, gh)
    pass_term = jnp.sum(old * dnew, axis=0, keepdims=True) * through_x
    pass_h = split_dot(jnp.broadcast_to(pass_term, (8, CH)), gh)[0:1, :]
    wr = weights * r_term
    d_cum = row_sums - col + k_term - wr
    d_last = jnp.sum(wr, axis=0, keepdims=True) + pass_h
    d_cum = d_cum + jnp.where(iota((BLK, 128), 0) == BLK - 1, d_last, 0.0)
    upper = (iota((BLK, BLK), 0) <= iota((BLK, BLK), 1)).astype(F32)
    d_log = dot_exact(upper, d_cum)
    d_step = q_term + fade * r_term - d_log * rate
    d_a = -jnp.sum(d_log * step, axis=0, keepdims=True) * rate
    d_dt = jnp.where(own, d_step * sigmoid(dt_in), 0.0)
    heads = jnp.concatenate([d_a, jnp.sum(d_dt, axis=0, keepdims=True), jnp.zeros((6, 128), F32)], axis=0)
    high = heads.astype(BF)
    heads = dot_nt(high, pick) + dot_nt((heads - high.astype(F32)).astype(BF), pick)
    d_dt = dot_nt(d_dt.astype(BF), pick)
    dstate[...] = dot_tn(cm, dyk) + through_x * dnew
    dx = step_x * e + weights_x * zt + par[6:7, :CH] * dy
    dc = dot(dg, bm) + dot_nt(dyk, old_b)
    db = dot(cm_f.T.astype(BF), dg).T + dot_nt(xw, dnew_b)
    d_act = jnp.concatenate([dx, db, dc], axis=1)
    d_conv = d_act * (sig_c * (1.0 + conv_out * (1.0 - sig_c)))
    dcbuf[0:BLK, :] = d_conv
    d_in = par[CONV - 1 : CONV, :] * d_conv
    cg = [None] * CONV
    cg[CONV - 1] = jnp.sum(d_conv * cbuf[8 : 8 + BLK, :], axis=0, keepdims=True)
    for back in range(1, CONV):
        tap = CONV - 1 - back
        cg[tap] = jnp.sum(
            d_conv * (cbuf[8 - back : 8 - back + BLK, :] * tok[:, back : back + 1]),
            axis=0, keepdims=True,
        )
        d_in = d_in + par[tap : tap + 1, :] * (
            dcbuf[back : back + BLK, :] * tok[:, 3 + back : 4 + back]
        )
    dcbuf[BLK : BLK + 8, :] = dcbuf[0:8, :]
    small_v[0:CONV, :] += jnp.concatenate(cg, axis=0)
    small_v[CONV : CONV + 1, :] += jnp.sum(d_conv, axis=0, keepdims=True)
    small_v[5:6, CH:] += jnp.concatenate([heads[0:1, :], heads[1:2, :]], axis=1)
    small_v[6:7, :CH] += jnp.sum(dy * x, axis=0, keepdims=True)
    return jnp.concatenate([d_in, d_dt[:, :ND]], axis=1)


def token_info(ids_full, first, n):
    length = ids_full.shape[0]
    pad = jnp.concatenate(
        [jnp.full((8,), -1, jnp.int32), ids_full, jnp.full((8,), -2, jnp.int32)]
    )
    window = lax.dynamic_slice_in_dim(pad, first, n + 16)
    own = window[8 : 8 + n]
    blocks = own.reshape(-1, BLK)
    before = window[7 : 7 + n].reshape(-1, BLK)[:, :1]
    cols = [own]
    for back in range(1, CONV):
        cols.append((window[8 - back : 8 - back + n] == own))
    for ahead in range(1, CONV):
        cols.append((window[8 + ahead : 8 + ahead + n] == own))
    cols.append((blocks == before).reshape(-1))
    cols.append((blocks == blocks[:, -1:]).reshape(-1))
    table = jnp.stack([c.astype(F32) for c in cols], axis=1)
    tok = jnp.pad(table, ((0, 0), (0, 128 - table.shape[1])))
    idr = jnp.broadcast_to(own.astype(F32).reshape(-1, 1, BLK), (n // BLK, 8, BLK))
    return tok, idr


CHIPS = TEAM // 2
DEPTH = 4
KROWS = D // DEPTH
BCD = NB + ND
HALF = BCD // 2


def places():
    seq = lax.axis_index("seq")
    return seq, lax.div(seq, 2), lax.rem(seq, 2), lax.axis_index("fsdp")


def send(src, dst, send_sem, recv_sem, device):
    return pltpu.make_async_remote_copy(
        src_ref=src, dst_ref=dst, send_sem=send_sem, recv_sem=recv_sem,
        device_id=device, device_id_type=pl.DeviceIdType.MESH,
    )


def greet(devices):
    barrier = pltpu.get_barrier_semaphore()
    for device in devices:
        pl.semaphore_signal(
            barrier, inc=1, device_id=device, device_id_type=pl.DeviceIdType.MESH
        )
    pl.semaphore_wait(barrier, len(devices))


def forward_kernel(
    tok_ref, cot_ref, win_ref, bcd_ref, wout_ref, small_ref, info_ref, idr_ref,
    nrm_ref, projc_ref, projz_ref, st_ref, ssd_ref, dno_ref, br_ref, stat_ref, par_ref, w_ref, g_ref,
    u_v, g_v, w_v, wo_v, smalls, ssd_v, cbuf, state, stat_v, stat_in,
    loc, t_send, t_recv, f_send, f_recv, z_send, z_recv, b_send, b_recv, s_send, s_recv, r_send, r_recv,
):
    i = pl.program_id(0)
    seq, chip, core, z = places()
    sib = {"seq": 2 * chip + 1 - core}
    peer = lambda k: {"seq": 2 * lax.rem(chip + k, CHIPS) + core}
    under = lambda k: {"fsdp": lax.rem(z + k, DEPTH)}
    around = lambda k: {"seq": lax.rem(seq + k, TEAM)}
    behind = lambda k: lax.rem(chip + CHIPS - k, CHIPS)
    block = lambda s: pl.ds(pl.multiple_of(BLK * s, BLK), BLK)
    lanes = lambda o: pl.ds(pl.multiple_of(KROWS * o, KROWS), KROWS)
    half = pl.ds(pl.multiple_of(NZ + NX + HALF * core, 16), HALF)
    has = [z < DEPTH - 1, z > 0]
    heads = [head_of(n, chip, core)[n // 4] for n in range(HPD)]
    piece = lambda n: pl.ds(pl.multiple_of(HEADDIM * n, HEADDIM), HEADDIM)

    def token_copy(n, k):
        src, dst = ((tok_ref, u_v), (cot_ref, g_v))[n]
        return send(src, dst.at[block(seq)], t_send.at[n, k], t_recv.at[n, k], sib if k == 0 else peer(k))

    def token_next(n, k):
        ref = (u_v, g_v)[n].at[block(2 * behind(k) + core)]
        return send(ref, ref, f_send.at[n, k], f_recv.at[n, k], sib)

    def place(p, o):
        if p < 3:
            return w_v.at[(pl.ds(NZ, NX), half, pl.ds(0, NZ))[p], lanes(o)]
        return wo_v.at[piece(o if p == 3 else DEPTH + lax.div(o, 2))]

    def hop(p, side, dist):
        o = z - dist if side == 0 else z + dist
        there = {"fsdp": z + 1} if side == 0 else {"fsdp": z - 1}
        return send(place(p, o), place(p, o), z_send.at[p, side, dist], z_recv.at[p, side, dist], there)

    def got(p, side, dist):
        o = z - dist - 1 if side == 0 else z + dist + 1
        there = {"fsdp": z + 1} if side == 0 else {"fsdp": z - 1}
        return send(place(p, o), place(p, o), z_send.at[p, side, dist], z_recv.at[p, side, dist], there)

    def share(side, dist):
        o = z - dist - 1 if side == 0 else z + dist + 1
        return send(place(1, o), place(1, o), b_send.at[side, dist], b_recv.at[side, dist], sib)

    def exists(p, side, hops):
        o = z - hops if side == 0 else z + hops
        there = (o >= 0) if side == 0 else (o < DEPTH)
        return there & (lax.rem(o + DEPTH, 2) == core) if p == 4 else there

    def small_copy(k):
        return send(small_ref, smalls.at[z], s_send.at[k], s_recv.at[k], under(k))

    def stat_copy(k):
        return send(stat_v, stat_in.at[k], r_send.at[k], r_recv.at[k], around(k))

    def local_copies():
        pairs = [(tok_ref, u_v.at[block(seq)]), (cot_ref, g_v.at[block(seq)]), (small_ref, smalls.at[z])]
        return [pltpu.make_async_copy(src, dst, loc.at[n]) for n, (src, dst) in enumerate(pairs)]

    def own_weights():
        pairs = [(bcd_ref, w_v.at[pl.ds(NZ + NX, BCD), lanes(z)], 3)]
        for n in range(HPD):
            row = HEADDIM * heads[n]
            pairs.append((win_ref.at[pl.ds(pl.multiple_of(row, HEADDIM), HEADDIM)],
                          w_v.at[piece(n), lanes(z)], 4 + n))
            pairs.append((win_ref.at[pl.ds(pl.multiple_of(DI + row, HEADDIM), HEADDIM)],
                          w_v.at[piece(HPD + n), lanes(z)], 10 + n))
        pairs.append((wout_ref.at[piece(3 * chip + 2 * core)], place(3, z), 16))
        return [pltpu.make_async_copy(src, dst, loc.at[n]) for src, dst, n in pairs]

    def own_extra():
        return pltpu.make_async_copy(wout_ref.at[piece(3 * chip + 1)], place(4, z), loc.at[17])

    def pass_on(parts, dist):
        for p in parts:
            for side in range(2):

                @pl.when(exists(p, side, dist + 1))
                def _():
                    got(p, side, dist).wait_recv()
                    if p == 1:
                        share(side, dist).start()

                if dist < DEPTH - 2:

                    @pl.when(exists(p, side, dist + 1) & has[side])
                    def _():
                        hop(p, side, dist + 1).start()

    def start_own(parts):
        for p in parts:
            for side in range(2):

                @pl.when(exists(p, side, 0) & has[side])
                def _():
                    hop(p, side, 0).start()

    @pl.when(i == 0)
    def _():
        greet([around(k) for k in range(1, TEAM)] + [under(k) for k in range(1, DEPTH)])
        for k in range(1, DEPTH):
            small_copy(k).start()
        for k in range(CHIPS):
            token_copy(0, k).start()
        for copy in own_weights() + local_copies():
            copy.start()

        @pl.when(lax.rem(z, 2) == core)
        def _():
            own_extra().start()

        for copy in own_weights():
            copy.wait()
        start_own((0, 1))
        state[...] = jnp.zeros_like(state)
        cbuf[0:8, :] = jnp.zeros((8, CONVC), F32)
        pass_on((0, 1), 0)
        pass_on((0, 1), 1)
        start_own((2,))
        for k in range(1, CHIPS):
            token_copy(0, k).wait_recv()
            token_next(0, k).start()
        for k in range(CHIPS):
            token_copy(1, k).start()
        pass_on((0, 1), 2)
        token_copy(0, 0).wait_recv()
        for k in range(1, CHIPS):
            token_next(0, k).wait()
        for k in range(1, DEPTH):
            small_copy(k).wait()
        for copy in local_copies():
            copy.wait()
        for side in range(2):
            for dist in range(DEPTH - 1):

                @pl.when(exists(1, side, dist + 1))
                def _():
                    share(side, dist).wait()

        total = smalls[0].astype(F32)
        for o in range(1, DEPTH):
            total = total + smalls[o].astype(F32)
        par_ref[...] = total

    @pl.when(i == 1)
    def _():
        @pl.when(lax.rem(z, 2) == core)
        def _():
            own_extra().wait()

        pass_on((2,), 0)
        start_own((3, 4))

    @pl.when(i == 3)
    def _():
        pass_on((2,), 1)

    @pl.when(i == 5)
    def _():
        pass_on((3, 4), 0)

    @pl.when(i == 7)
    def _():
        pass_on((3, 4), 1)

    @pl.when(i == TEAM)
    def _():
        pass_on((2, 3, 4), 2)
        for k in range(1, CHIPS):
            token_copy(1, k).wait_recv()
            token_next(1, k).start()
        token_copy(1, 0).wait_recv()
        for k in range(1, CHIPS):
            token_next(1, k).wait()
        pltpu.make_async_copy(w_v, w_ref, loc.at[18]).start()
        pltpu.make_async_copy(g_v, g_ref, loc.at[19]).start()

    par = par_ref[...]

    @pl.when(i < TEAM)
    def _():
        u = u_v[block(i), :].astype(F32)
        scale = lax.rsqrt(jnp.mean(u * u, axis=1, keepdims=True) + EPSILON)
        nrm = (u * scale * norm_gain(par)).astype(BF)
        nrm_ref[...] = nrm
        u_v[block(i), :] = nrm
        scan_forward(i, nrm, w_v, par, info_ref[...], idr_ref[0, 0:1, :], cbuf, state,
                     projc_ref, st_ref, ssd_v)

    @pl.when(i >= TEAM)
    def _():
        gate_forward(i - TEAM, u_v, g_v, w_v, wo_v, par, ssd_v, projz_ref, ssd_ref, dno_ref,
                     br_ref, stat_v)

    @pl.when(i == 2 * TEAM - 1)
    def _():
        for k in range(1, TEAM):
            stat_copy(k).start()
        total = stat_v[...]
        for k in range(1, TEAM):
            stat_copy(k).wait_recv()
            total = total + stat_in[k]
        stat_ref[...] = total
        for k in range(1, TEAM):
            stat_copy(k).wait_send()
        for n in range(2):
            for k in range(CHIPS):
                token_copy(n, k).wait_send()
        for side in range(2):
            for dist in range(DEPTH - 1):
                for p in range(5):

                    @pl.when(exists(p, side, dist) & has[side])
                    def _():
                        hop(p, side, dist).wait_send()

        pltpu.make_async_copy(w_v, w_ref, loc.at[18]).wait()
        pltpu.make_async_copy(g_v, g_ref, loc.at[19]).wait()


def forward_call(tok, cot, win, bcd, wout, small, info, idr):
    n = tok.shape[0] * TEAM
    any_space = pl.BlockSpec(memory_space=pl.ANY)
    sds = jax.ShapeDtypeStruct
    dma = pltpu.SemaphoreType.DMA
    one = lambda i: jnp.minimum(i, TEAM - 1)
    two = lambda i: jnp.maximum(i - TEAM, 0)
    rows = lambda c, turn: pl.BlockSpec((BLK, c), lambda i: (turn(i), 0))
    cube = lambda a, b: pl.BlockSpec((1, a, b), lambda i: (one(i), 0, 0))
    fixed = lambda a, b: pl.BlockSpec((a, b), lambda i: (0, 0))
    return pl.pallas_call(
        forward_kernel,
        grid=(2 * TEAM,),
        in_specs=[any_space] * 6 + [rows(128, one), cube(8, BLK)],
        out_specs=[rows(D, one), rows(REST, one), rows(NZ, two), cube(STATE, CH), rows(CH, two),
                   rows(CH, two), rows(D, two), fixed(TEAM, 2 * BLK), fixed(16, CONVC), any_space,
                   any_space],
        out_shape=[sds((n, D), BF), sds((n, REST), BF), sds((n, NZ), BF), sds((TEAM, STATE, CH), F32),
                   sds((n, CH), F32), sds((n, CH), F32), sds((n, D), BF), sds((TEAM, 2 * BLK), F32),
                   sds((16, CONVC), F32), sds((COLS, D), BF), sds((n, D), BF)],
        scratch_shapes=[pltpu.VMEM((n, D), BF), pltpu.VMEM((n, D), BF), pltpu.VMEM((COLS, D), BF),
                        pltpu.VMEM((CH, D), BF), pltpu.VMEM((DEPTH, 16, CONVC), BF),
                        pltpu.VMEM((n, CH), F32), pltpu.VMEM((BLK + 8, CONVC), F32),
                        pltpu.VMEM((STATE, CH), F32), pltpu.VMEM((TEAM, 2 * BLK), F32),
                        pltpu.VMEM((TEAM, TEAM, 2 * BLK), F32),
                        dma((20,)), dma((2, CHIPS)), dma((2, CHIPS)), dma((2, CHIPS)),
                        dma((2, CHIPS)), dma((5, 2, DEPTH - 1)), dma((5, 2, DEPTH - 1)),
                        dma((2, DEPTH - 1)), dma((2, DEPTH - 1)),
                        dma((DEPTH,)), dma((DEPTH,)), dma((TEAM,)), dma((TEAM,))],
        compiler_params=pltpu.CompilerParams(
            collective_id=0, has_side_effects=True, vmem_limit_bytes=60 << 20),
    )(tok, cot, win, bcd, wout, small, info, idr)


def backward_kernel(
    tok_ref, cot_ref, nrm_ref, br_ref, w_ref, g_ref,
    projz_ref, ssd_ref, dno_ref, stat_ref, par_ref, projc_ref, halo_ref, st_ref, info_ref, idr_ref,
    out_ref, tg_ref, wig_ref, wog_ref, smalls_ref,
    nrm_v, g_v, w_v, not_v, dz_v, dzt_v, dy_v, rest_v, wig_v, wog_v, bcd_v, bcd_in,
    zz_in, zx_in, zb_in, zw_in, zs_in, gz_v, gx_v, gb_v, gw_v, gb_in, gt_v, ob_v, rb_v, rr_v, rd_v,
    tok_v, cot_v, small_v, small_s, cbuf, dcbuf, dstate,
    loc, b_send, b_recv, p_send, p_recv, d_send, d_recv, q_send, q_recv, z_send, z_recv,
    a_send, a_recv, f_send, f_recv, h_send, h_recv, free,
):
    i = pl.program_id(0)
    seq, chip, core, z = places()
    sib = {"seq": 2 * chip + 1 - core}
    peer = lambda k: {"seq": 2 * lax.rem(chip + k, CHIPS) + core}
    under = lambda k: {"fsdp": lax.rem(z + k, DEPTH)}
    around = lambda k: {"seq": lax.rem(seq + k, TEAM)}
    behind = lambda k: lax.rem(chip + CHIPS - k, CHIPS)
    block = lambda s: pl.ds(pl.multiple_of(BLK * s, BLK), BLK)
    lanes = lambda o: pl.ds(pl.multiple_of(KROWS * o, KROWS), KROWS)
    piece = lambda n: pl.ds(pl.multiple_of(HEADDIM * n, HEADDIM), HEADDIM)
    half = lambda c: pl.ds(pl.multiple_of(HALF * c, 16), HALF)
    extra = lambda o: lax.rem(o, 2) == core
    n_all = HEADDIM * HPD
    give = lambda c: g_v.at[block(c)]
    hold = lambda c: g_v.at[block(CHIPS + c)]

    def load(n):
        pairs = [(nrm_ref, nrm_v), (g_ref, g_v), (w_ref, w_v), (tok_ref, tok_v), (cot_ref, cot_v)]
        return pltpu.make_async_copy(pairs[n][0], pairs[n][1], loc.at[n])

    def load_own(c):
        return pltpu.make_async_copy(br_ref.at[block(2 * c + core)], ob_v.at[c], loc.at[5 + c])

    def br_pair(c):
        return send(br_ref.at[block(2 * c + 1 - core)], rb_v.at[c], b_send.at[c], b_recv.at[c], sib)

    def br_push(k):
        return send(ob_v.at[lax.rem(chip + k, CHIPS)], rr_v.at[k - 1], p_send.at[k], p_recv.at[k], peer(k))

    def dn_pair(c):
        return send(give(c), rb_v.at[c], d_send.at[c], d_recv.at[c], sib)

    def dn_push(c):
        k = lax.rem(c + CHIPS - chip, CHIPS)
        return send(hold(c), rd_v.at[k - 1], q_send.at[k], q_recv.at[k], {"seq": 2 * c + core})

    def dn_pushed(k):
        return send(hold(0), rd_v.at[k - 1], q_send.at[k], q_recv.at[k], peer(k))

    def down(n, k):
        o = lax.rem(z + k, DEPTH)
        src, dst = [
            (wig_v.at[:, lanes(o)], zz_in.at[k - 1]),
            (wig_v.at[:, lanes(o)], zx_in.at[k - 1]),
            (bcd_v.at[half(core), lanes(o)], zb_in.at[k - 1]),
            (wog_v.at[piece(o)], zw_in.at[k - 1, 0:HEADDIM]),
            (wog_v.at[piece(DEPTH + lax.div(o, 2))], zw_in.at[k - 1, HEADDIM:]),
            (small_v, zs_in.at[k - 1]),
        ][n]
        return send(src, dst, z_send.at[n, k], z_recv.at[n, k], under(k))

    def bcd_pair():
        return send(bcd_v.at[half(1 - core)], bcd_in, h_send.at[0], h_recv.at[0], sib)

    def bcd_push(k):
        return send(gb_v, gb_in.at[k - 1], a_send.at[4, k], a_recv.at[4, k], peer(k))

    def bcd_back():
        return send(gt_v.at[core], gt_v.at[core], h_send.at[1], h_recv.at[1], sib)

    def parts(n, c, cr):
        if n < 2:
            base = n * DI // HEADDIM
            src = (gz_v, gx_v)[n]
            return [(src.at[piece(s)], wig_ref.at[piece(base + head_of(s, c, cr)[s // 4])]) for s in range(HPD)]
        if n == 2:
            return [(gw_v.at[0:HEADDIM], wog_ref.at[piece(3 * c + 2 * cr)])]
        if n == 3:
            return [(gw_v.at[HEADDIM:], wog_ref.at[piece(3 * c + 1)])]
        return [(small_s, smalls_ref.at[2 * c + cr])]

    def all_of(n):
        if n < 2:
            return wig_ref.at[pl.ds(n * DI, n_all)]
        return parts(n, 0, 0)[0][1]

    def ag(n, k):
        where = sib if k == 0 else peer(k)
        return [send(src, dst, a_send.at[n, k], a_recv.at[n, k], where) for src, dst in parts(n, chip, core)]

    def ag_wait(n, k):
        return send(all_of(n), all_of(n), a_send.at[n, k], a_recv.at[n, k], sib)

    def ag_next(n, k):
        return [send(dst, dst, f_send.at[n, k], f_recv.at[n, k], sib) for _, dst in parts(n, behind(k), core)]

    def ag_next_wait(n, k):
        return send(all_of(n), all_of(n), f_send.at[n, k], f_recv.at[n, k], sib)

    def ag_own(n):
        return [pltpu.make_async_copy(src, dst, loc.at[9 + n]) for src, dst in parts(n, chip, core)]

    def ag_own_wait(n):
        return pltpu.make_async_copy(all_of(n), all_of(n), loc.at[9 + n])

    def ag_start(n):
        for k in range(1, CHIPS):
            for copy in ag(n, k):
                copy.start()
        for copy in ag(n, 0) + ag_own(n):
            copy.start()

    def ag_forward(n):
        for k in range(1, CHIPS):
            ag_wait(n, k).wait_recv()
            for copy in ag_next(n, k):
                copy.start()

    def ag_finish(n):
        ag_wait(n, 0).wait_recv()
        for k in range(CHIPS):
            ag_wait(n, k).wait_send()
        for k in range(1, CHIPS):
            ag_next_wait(n, k).wait()
        ag_own_wait(n).wait()

    def reduce_z(own, arrived):
        total = own.astype(F32)
        for k in range(1, DEPTH):
            total = total + arrived[k - 1].astype(F32)
        return total

    @pl.when(i == 0)
    def _():
        greet([around(k) for k in range(1, TEAM)] + [under(k) for k in range(1, DEPTH)])
        for c in range(CHIPS):
            br_pair(c).start()
            load_own(c).start()
        for n in range(5):
            load(n).start()
        small_v[...] = jnp.zeros_like(small_v)
        dstate[...] = jnp.zeros_like(dstate)
        dcbuf[BLK : BLK + 8, :] = jnp.zeros((8, CONVC), F32)

    @pl.when(i < TEAM)
    def _():
        gate_backward(i, projz_ref[...].astype(F32), ssd_ref[...], dno_ref[...],
                      stat_ref[pl.ds(i, 1), :], par_ref[5:6, :CH], not_v, dy_v, dz_v, dzt_v, small_v)

    @pl.when(i == 1)
    def _():
        for c in range(CHIPS):
            load_own(c).wait()
            br_pair(c).wait_recv()
            ob_v[c] = (ob_v[c].astype(F32) + rb_v[c].astype(F32)).astype(BF)
        for k in range(1, CHIPS):
            br_push(k).start()
        pl.semaphore_signal(free, inc=1, device_id=sib, device_id_type=pl.DeviceIdType.MESH)

    @pl.when(i == TEAM)
    def _():
        pl.semaphore_wait(free, 1)
        for n in range(5):
            load(n).wait()

        @pl.loop(0, D // 256)
        def _(n):
            cols = pl.ds(pl.multiple_of(256 * n, 256), 256)
            wig_v[:, cols] = dot(dzt_v[...], nrm_v[:, cols]).astype(BF)

        for k in range(1, DEPTH):
            down(0, k).start()

        @pl.loop(0, D // 256)
        def _(n):
            cols = pl.ds(pl.multiple_of(256 * n, 256), 256)
            wog_v[:, cols] = dot(not_v[...], g_v[:, cols]).astype(BF)

        for k in range(1, DEPTH):
            down(3, k).start()

            @pl.when(extra(z + k))
            def _():
                down(4, k).start()

    def combine(c):
        dn_pair(c).wait_recv()
        hold(c)[...] = (hold(c)[...].astype(F32) + rb_v[c].astype(F32)).astype(BF)

        @pl.when(chip != c)
        def _():
            dn_push(c).start()

    for c in range(CHIPS - 1, 0, -1):

        @pl.when(i == TEAM + 1 + 2 * (CHIPS - c))
        def _():
            combine(c)

    @pl.when((i > TEAM) & (i <= 2 * TEAM))
    def _():
        j = 2 * TEAM - i
        rows = block(j)
        d_rest = scan_backward(projc_ref[...], halo_ref[...], info_ref[...], idr_ref[0, 0:1, :], st_ref[0],
                               par_ref[...], dy_v[rows, :], cbuf, dcbuf, dstate, small_v)
        rest_v[:, rows] = d_rest.T.astype(BF)
        dn = dot(dz_v[rows, :], w_v[:NZ, :]) + dot(d_rest.astype(BF), w_v[NZ:, :])
        part = jnp.sum(dn * nrm_v[rows, :].astype(F32), axis=0, keepdims=True)
        for n in range(3):
            small_v[7 + n : 8 + n, :512] += part[:, 512 * n : 512 * n + 512]
        dn = dn.astype(BF)
        c = lax.div(j, 2)

        @pl.when(lax.rem(j, 2) == core)
        def _():
            hold(c)[...] = dn

        @pl.when(lax.rem(j, 2) != core)
        def _():
            give(c)[...] = dn
            dn_pair(c).start()

    @pl.when(i == 2 * TEAM - 1)
    def _():
        for k in range(1, CHIPS):
            br_push(k).wait_recv()
        total = ob_v[chip].astype(F32)
        for k in range(1, CHIPS):
            total = total + rr_v[k - 1].astype(F32)
        stat = stat_ref[pl.ds(seq, 1), 0:BLK]
        stat = jnp.broadcast_to(stat, (128, BLK)).T
        s2 = lax.rsqrt(stat[:, 0:1] * (1.0 / DI) + EPSILON)
        out_ref[...] = (tok_v[...].astype(F32) + total * s2).astype(BF)

    @pl.when(i == 2 * TEAM)
    def _():
        for k in range(1, DEPTH):
            down(0, k).wait_recv()
        gz_v[...] = reduce_z(wig_v[:, lanes(z)], [zz_in[k - 1] for k in range(1, DEPTH)]).astype(BF)
        ag_start(0)

    @pl.when(i == 2 * TEAM + 1)
    def _():
        for n in range(3):
            small_v[7 + n : 8 + n, :512] = small_v[7 + n : 8 + n, :512] / par_ref[7 + n : 8 + n, :512]
        for k in range(1, DEPTH):
            down(5, k).start()
        combine(0)

        @pl.loop(0, D // 256)
        def _(n):
            cols = pl.ds(pl.multiple_of(256 * n, 256), 256)
            bcd_v[:, cols] = dot(rest_v[NX:, :], nrm_v[:, cols]).astype(BF)

        bcd_pair().start()
        for k in range(1, DEPTH):
            down(0, k).wait_send()

        @pl.loop(0, D // 256)
        def _(n):
            cols = pl.ds(pl.multiple_of(256 * n, 256), 256)
            wig_v[:, cols] = dot(rest_v[:NX, :], nrm_v[:, cols]).astype(BF)

        for k in range(1, DEPTH):
            down(1, k).start()
        bcd_pair().wait_recv()
        bcd_v[half(core), :] = (bcd_v[half(core), :].astype(F32) + bcd_in[...].astype(F32)).astype(BF)
        for k in range(1, DEPTH):
            down(2, k).start()
        for k in range(1, DEPTH):
            down(3, k).wait_recv()
        gw_v[0:HEADDIM, :] = reduce_z(wog_v[piece(z), :], [zw_in[k - 1, 0:HEADDIM] for k in range(1, DEPTH)]).astype(BF)
        ag_start(2)

        @pl.when(extra(z))
        def _():
            for k in range(1, DEPTH):
                down(4, k).wait_recv()
            gw_v[HEADDIM:, :] = reduce_z(
                wog_v[piece(DEPTH + lax.div(z, 2)), :], [zw_in[k - 1, HEADDIM:] for k in range(1, DEPTH)]).astype(BF)
            ag_start(3)

        for k in range(1, DEPTH):
            down(5, k).wait_recv()
        small_s[...] = reduce_z(small_v[...], [zs_in[k - 1] for k in range(1, DEPTH)])
        ag_start(5)
        ag_forward(0)
        for k in range(1, CHIPS):
            dn_pushed(k).wait_recv()
        total = hold(chip)[...].astype(F32)
        for k in range(1, CHIPS):
            total = total + rd_v[k - 1].astype(F32)
        uf = tok_v[...].astype(F32)
        along = total * norm_gain(par_ref[...])
        s1 = lax.rsqrt(jnp.mean(uf * uf, axis=1, keepdims=True) + EPSILON)
        tg_ref[...] = cot_v[...].astype(F32) + s1 * along - uf * (
            s1 * s1 * s1 * jnp.mean(along * uf, axis=1, keepdims=True))
        for k in range(1, DEPTH):
            down(1, k).wait_recv()
        gx_v[...] = reduce_z(wig_v[:, lanes(z)], [zx_in[k - 1] for k in range(1, DEPTH)]).astype(BF)
        ag_start(1)
        for k in range(1, DEPTH):
            down(2, k).wait_recv()
        gb_v[...] = reduce_z(bcd_v[half(core), lanes(z)], [zb_in[k - 1] for k in range(1, DEPTH)]).astype(BF)
        for k in range(1, CHIPS):
            bcd_push(k).start()
        ag_forward(2)

        @pl.when(extra(z))
        def _():
            ag_forward(3)

        ag_forward(5)
        for k in range(1, CHIPS):
            bcd_push(k).wait_recv()
        total = gb_v[...].astype(F32)
        for k in range(1, CHIPS):
            total = total + gb_in[k - 1].astype(F32)
        gt_v[core] = total.astype(BF)
        bcd_back().start()
        ag_forward(1)
        bcd_back().wait()
        last = [
            pltpu.make_async_copy(gt_v.at[0], wig_ref.at[pl.ds(2 * DI, HALF)], loc.at[15]),
            pltpu.make_async_copy(gt_v.at[1, 0 : WIDTH - 2 * DI - HALF],
                                  wig_ref.at[pl.ds(2 * DI + HALF, WIDTH - 2 * DI - HALF)], loc.at[16])]
        for copy in last:
            copy.start()
        for n in (0, 1, 2, 5):
            ag_finish(n)

        @pl.when(extra(z))
        def _():
            for k in range(CHIPS):
                ag_wait(3, k).wait_send()
            for k in range(1, CHIPS):
                ag_next_wait(3, k).wait_send()
            ag_own_wait(3).wait()

        @pl.when(jnp.logical_not(extra(z)))
        def _():
            ag_wait(3, 0).wait_recv()
            for k in range(1, CHIPS):
                ag_next_wait(3, k).wait_recv()

        for c in range(CHIPS):
            br_pair(c).wait_send()
            dn_pair(c).wait_send()
        for k in range(1, CHIPS):
            br_push(k).wait_send()
            dn_pushed(k).wait_send()
            bcd_push(k).wait_send()
        for k in range(1, DEPTH):
            for n in (1, 2, 3, 5):
                down(n, k).wait_send()

            @pl.when(extra(z + k))
            def _():
                down(4, k).wait_send()

        bcd_pair().wait_send()
        for copy in last:
            copy.wait()


def backward_call(tok, cot, nrm, br, w, g, projz, ssd, dno, stat, par, projc, st, info, idr):
    n = nrm.shape[0]
    any_space = pl.BlockSpec(memory_space=pl.ANY)
    sds = jax.ShapeDtypeStruct
    dma = pltpu.SemaphoreType.DMA
    one = lambda i: jnp.minimum(i, TEAM - 1)
    two = lambda i: jnp.clip(2 * TEAM - i, 0, TEAM - 1)
    rows = lambda c, turn: pl.BlockSpec((BLK, c), lambda i: (turn(i), 0))
    cube = lambda a, b: pl.BlockSpec((1, a, b), lambda i: (two(i), 0, 0))
    fixed = lambda a, b: pl.BlockSpec((a, b), lambda i: (0, 0), pipeline_mode=pl.Buffered(1))
    vm = pltpu.VMEM
    return pl.pallas_call(
        backward_kernel,
        grid=(2 * TEAM + 2,),
        in_specs=[any_space] * 6 + [
            rows(NZ, one), rows(CH, one), rows(CH, one), fixed(TEAM, 2 * BLK), fixed(16, CONVC), rows(REST, two),
            pl.BlockSpec((16, REST), lambda i: (jnp.maximum(16 * two(i) - 1, 0), 0)),
            cube(STATE, CH), rows(128, two), cube(8, BLK)],
        out_specs=[fixed(BLK, D), fixed(BLK, D), any_space, any_space, any_space],
        out_shape=[sds((BLK, D), BF), sds((BLK, D), F32), sds((WIDTH, KROWS), BF),
                   sds((DI // DEPTH, D), BF), sds((TEAM, 16, CONVC), F32)],
        scratch_shapes=[
            vm((n, D), BF), vm((n, D), BF), vm((COLS, D), BF), vm((CH, n), BF), vm((n, CH), BF), vm((CH, n), BF),
            vm((n, CH), F32), vm((REST, n), BF), vm((CH, D), BF), vm((CH, D), BF), vm((BCD, D), BF),
            vm((HALF, D), BF),
            vm((DEPTH - 1, CH, KROWS), BF), vm((DEPTH - 1, CH, KROWS), BF), vm((DEPTH - 1, HALF, KROWS), BF),
            vm((DEPTH - 1, 2 * HEADDIM, D), BF), vm((DEPTH - 1, 16, CONVC), F32), vm((CH, KROWS), BF), vm((CH, KROWS), BF),
            vm((HALF, KROWS), BF), vm((2 * HEADDIM, D), BF), vm((CHIPS - 1, HALF, KROWS), BF), vm((2, HALF, KROWS), BF),
            vm((CHIPS, BLK, D), BF), vm((CHIPS, BLK, D), BF), vm((CHIPS - 1, BLK, D), BF), vm((CHIPS - 1, BLK, D), BF),
            vm((BLK, D), BF), vm((BLK, D), BF), vm((16, CONVC), F32), vm((16, CONVC), F32),
            vm((BLK + 8, CONVC), F32), vm((BLK + 8, CONVC), F32), vm((STATE, CH), F32),
            dma((17,)), dma((CHIPS,)), dma((CHIPS,)), dma((CHIPS,)), dma((CHIPS,)), dma((CHIPS,)), dma((CHIPS,)),
            dma((CHIPS,)), dma((CHIPS,)), dma((6, DEPTH)), dma((6, DEPTH)),
            dma((6, CHIPS)), dma((6, CHIPS)), dma((6, CHIPS)), dma((6, CHIPS)), dma((2,)), dma((2,)),
            pltpu.SemaphoreType.REGULAR],
        compiler_params=pltpu.CompilerParams(
            collective_id=1, has_side_effects=True, vmem_limit_bytes=63 << 20),
    )(tok, cot, nrm, br, w, g, projz, ssd, dno, stat, par, projc, projc, st, info, idr)


def on_team(
    tokens, segment_ids, cotangent, w_in, w_out, conv_w, conv_b, a_log, dt_bias, d_skip,
    norm_w, gate_w,
):
    place = lax.axis_index("seq")
    chip, core = place // 2, place % 2
    depth = lax.axis_index("fsdp")
    shards = DEPTH
    n = tokens.shape[1] * TEAM
    w_t = w_in.T
    bcd = jnp.pad(w_t[2 * DI :], ((0, BCD - (WIDTH - 2 * DI)), (0, 0)))

    def put(a, whole_size):
        return lax.dynamic_update_slice_in_dim(
            jnp.zeros(a.shape[:-1] + (whole_size,), BF), a, depth * a.shape[-1], a.ndim - 1)

    def own_part(a):
        a = a.reshape(a.shape[0], 4, 12, HEADDIM)
        a = lax.dynamic_slice_in_dim(a, 3 * chip, 3, 2)
        first = lax.dynamic_index_in_dim(a, 2 * core, 2, keepdims=False)
        second = a[:, :, 1].reshape(-1, 2, 2, HEADDIM)
        second = lax.dynamic_index_in_dim(second, core, 2, keepdims=False)
        return jnp.concatenate([first, second], axis=1).reshape(a.shape[0], CH)

    wide = lambda a, size: jnp.pad(a, (0, size - a.shape[0]))
    conv_rows = put(jnp.concatenate([conv_w, conv_b[None]], axis=0), CHAN)
    chan_rows = own_part(jnp.concatenate(
        [conv_rows[:, :DI], put(gate_w, DI)[None], jnp.repeat(put(d_skip, HEADS), HEADDIM)[None]], axis=0))
    heads_row = jnp.concatenate([wide(put(dt_bias, HEADS), 128), wide(put(a_log, HEADS), 128)])
    side = jnp.concatenate([conv_rows[:, DI:], heads_row[None], jnp.zeros((1, NB), BF)], axis=0)
    gain_rows = jnp.pad(put(norm_w, D).reshape(3, D // 3), ((0, 0), (0, CONVC - D // 3)))
    small = jnp.concatenate(
        [jnp.concatenate([chan_rows, side], axis=1), gain_rows, jnp.zeros((6, CONVC), BF)], axis=0)
    tok, idr = token_info(segment_ids[0], 0, n)
    u_own, g_own = tokens[0], cotangent[0]
    nrm, projc, projz, st, ssd, dno, br, stat, par, w_loc, g = forward_call(
        u_own, g_own, w_t, bcd, w_out, small, tok, idr)
    layer_out, token_grad, wig, wog, smalls = backward_call(
        u_own, g_own, nrm, br, w_loc, g, projz, ssd, dno, stat, par, projc, st, tok, idr)
    w_in_grad = wig.astype(F32).T
    w_out_grad = wog.astype(F32)
    parts = smalls[:, :7, :CH].reshape(CHIPS, 2, 7, HPD, HEADDIM)
    first = parts[:, :, :, :4].transpose(1, 2, 3, 0, 4)
    second = parts[:, :, :, 4:].transpose(2, 3, 1, 0, 4).reshape(7, 4, CHIPS, HEADDIM)
    chang = jnp.stack([first[0], second, first[1]], axis=3).reshape(7, DI)
    sideg = jnp.sum(smalls[:, :6, CH:], axis=0)
    normg = jnp.sum(smalls[:, 7:10, :512], axis=0).reshape(D)
    convg = jnp.concatenate([chang[:5], sideg[:5]], axis=1)
    mine = lambda a: lax.dynamic_slice_in_dim(a, depth * (a.shape[-1] // shards), a.shape[-1] // shards, a.ndim - 1)
    convg = mine(convg)
    skipg = jnp.sum(chang[6].reshape(HEADS, HEADDIM), axis=1)
    return (layer_out[None], token_grad[None], w_in_grad, w_out_grad, convg[:4], convg[4],
            mine(sideg[5, :HEADS]), mine(sideg[5, 128 : 128 + HEADS]), mine(skipg), mine(normg), mine(chang[5]))


def solution(mesh):
    body = on_team if (mesh.shape["seq"], mesh.shape["fsdp"]) == (TEAM, DEPTH) else on_device
    return jax.shard_map(
        body,
        mesh=mesh,
        in_specs=(
            P("fsdp", "seq", None),
            P("fsdp", None),
            P("fsdp", "seq", None),
            P("fsdp", None),
            P("fsdp", None),
            P(None, "fsdp"),
            P("fsdp"),
            P("fsdp"),
            P("fsdp"),
            P("fsdp"),
            P("fsdp"),
            P("fsdp"),
        ),
        out_specs=(
            P("fsdp", "seq", None),
            P("fsdp", "seq", None),
            P("fsdp", None),
            P("fsdp", None),
            P(None, "fsdp"),
            P("fsdp"),
            P("fsdp"),
            P("fsdp"),
            P("fsdp"),
            P("fsdp"),
            P("fsdp"),
        ),
        check_vma=False,
    )
```

```python
import jax
import jax.numpy as jnp
from jax import lax
from jax.experimental import pallas as pl
from jax.experimental.pallas import tpu as pltpu
from jax.sharding import PartitionSpec as P

DI = 3072
HEADDIM = 64
STATE = 128
CONV = 4
SPAN = 256
HEADS = 48
D = 1536
WIDTH = 6448
CHAN = 3328


EPSILON = 1e-05
HIGHEST = lax.Precision.HIGHEST


def passed_along(value, axis, steps):
    count = lax.axis_size(axis)
    first, last = (max(0, -steps), min(count, count - steps))
    return lax.ppermute(value, axis, [(source, source + steps) for source in range(first, last)])


def shortened(array):

    def short(part):
        return part.astype(jnp.bfloat16) if part.dtype == jnp.float32 else part

    return jax.tree.map(short, array)


def block_masks(ids_blocks, before_ids):
    block_len = ids_blocks.shape[1]
    places = jnp.arange(block_len)
    causal_mask = (places[:, None] >= places[None, :])[None] & (
        ids_blocks[:, :, None] == ids_blocks[:, None, :]
    )
    keep_flag = (ids_blocks == before_ids[:, None]).astype(jnp.float32)
    same_last = (ids_blocks == ids_blocks[:, -1:]).astype(jnp.float32)
    return (causal_mask, keep_flag, same_last)


def local_states(x_heads, b_rows, step_size, log_decay, same_last, keep_flag):
    cum_decay = jnp.cumsum(log_decay, axis=1)
    last_cum = cum_decay[:, -1]
    weights = jnp.exp(last_cum[:, None, :] - cum_decay) * step_size * same_last[:, :, None]
    fresh_state = jnp.einsum("csh,cshp,csn->chpn", weights, x_heads, b_rows, precision=HIGHEST)
    passing = keep_flag[:, -1:] * jnp.exp(last_cum)
    total_state = jnp.zeros_like(fresh_state[0])
    total_decay = jnp.ones_like(passing[0])
    total_state = fresh_state[0] + passing[0][:, None, None] * total_state
    total_decay = total_decay * passing[0]
    return (fresh_state, passing, total_state, total_decay)


def local_output(x_heads, b_rows, c_rows, step_size, log_decay, incoming, causal_mask, keep_flag):
    cum_decay = jnp.cumsum(log_decay, axis=1)
    cum_heads = jnp.swapaxes(cum_decay, 1, 2)
    gap_decay = cum_heads[:, :, :, None] - cum_heads[:, :, None, :]
    head_mask = causal_mask[:, None]
    decay_map = jnp.exp(jnp.where(head_mask, gap_decay, 0.0)) * head_mask.astype(jnp.float32)
    scores = jnp.einsum("ctn,csn->cts", c_rows, b_rows, precision=HIGHEST)
    mixing = scores[:, None] * decay_map * jnp.swapaxes(step_size, 1, 2)[:, :, None, :]
    inner_out = jnp.einsum("chts,cshp->cthp", mixing, x_heads, precision=HIGHEST)
    starts = [incoming]
    start_states = jnp.stack(starts)
    carried = jnp.einsum("ctn,chpn->cthp", c_rows, start_states, precision=HIGHEST)
    carried = carried * (keep_flag[:, :, None] * jnp.exp(cum_decay))[..., None]
    return inner_out + carried


def on_device(
    tokens,
    segment_ids,
    cotangent,
    w_in,
    w_out,
    conv_w,
    conv_b,
    a_log,
    dt_bias,
    d_skip,
    norm_w,
    gate_w,
):
    gathered = (
        lax.all_gather(w_in, "fsdp", axis=0, tiled=True),
        lax.all_gather(w_out, "fsdp", axis=0, tiled=True),
        lax.all_gather(conv_w, "fsdp", axis=1, tiled=True),
        lax.all_gather(conv_b, "fsdp", axis=0, tiled=True),
        lax.all_gather(a_log, "fsdp", axis=0, tiled=True),
        lax.all_gather(dt_bias, "fsdp", axis=0, tiled=True),
        lax.all_gather(d_skip, "fsdp", axis=0, tiled=True),
        lax.all_gather(norm_w, "fsdp", axis=0, tiled=True),
        lax.all_gather(gate_w, "fsdp", axis=0, tiled=True),
    )
    (
        w_in_full,
        w_out_full,
        conv_full,
        bias_full,
        a_log_full,
        dt_bias_full,
        skip_full,
        norm_full,
        gate_full,
    ) = gathered
    inputs = tokens[0].astype(jnp.float32)
    length = inputs.shape[0]
    norm_gain = norm_full.astype(jnp.float32)
    scale_in = lax.rsqrt(jnp.mean(inputs * inputs, axis=-1, keepdims=True) + EPSILON)
    normed = (inputs * scale_in * norm_gain).astype(jnp.bfloat16)
    projected = jnp.dot(normed, w_in_full, preferred_element_type=jnp.float32).astype(jnp.bfloat16)
    gate_z = projected[:, :DI].astype(jnp.float32)
    conv_in = projected[:, DI : DI + CHAN]
    dt_raw = projected[:, DI + CHAN :].astype(jnp.float32)
    first_row = lax.axis_index("seq") * length
    id_row = jnp.concatenate([jnp.full((CONV - 1,), -1, jnp.int32), segment_ids[0]], axis=0)
    ids_pad = lax.dynamic_slice_in_dim(id_row, first_row, length + CONV - 1)
    ids_own = ids_pad[CONV - 1 :]
    left_edge = passed_along(conv_in[length - (CONV - 1) :], "seq", 1)
    padded = jnp.concatenate([left_edge, conv_in], axis=0).astype(jnp.float32)
    kernel = conv_full.astype(jnp.float32)
    conv_out = jnp.zeros((length, CHAN), jnp.float32) + bias_full.astype(jnp.float32)
    same_docs = []
    for offset in range(CONV):
        same_doc = (ids_pad[offset : offset + length] == ids_own).astype(jnp.float32)
        same_docs.append(same_doc)
        conv_out = conv_out + kernel[offset] * padded[offset : offset + length] * same_doc[:, None]
    activated = jax.nn.silu(conv_out)
    blocks = length // SPAN
    x_heads = activated[:, :DI].reshape(blocks, SPAN, HEADS, HEADDIM)
    b_rows = activated[:, DI : DI + STATE].reshape(blocks, SPAN, STATE)
    c_rows = activated[:, DI + STATE :].reshape(blocks, SPAN, STATE)
    dt_bias_f = dt_bias_full.astype(jnp.float32)
    decay_rate = jnp.exp(a_log_full.astype(jnp.float32))
    step_flat = jax.nn.softplus(dt_raw + dt_bias_f)
    step_size = step_flat.reshape(blocks, SPAN, HEADS)
    log_decay = (-step_flat * decay_rate).reshape(blocks, SPAN, HEADS)
    ids_blocks = ids_own.reshape(blocks, SPAN)
    before_ids = ids_pad[CONV - 2 : CONV - 2 + length : SPAN]
    causal_mask, keep_flag, same_last = block_masks(ids_blocks, before_ids)

    def state_part(heads_in, rows_b, steps_in, decay_in):
        return local_states(heads_in, rows_b, steps_in, decay_in, same_last, keep_flag)

    (fresh_state, passing, total_state, total_decay), state_pull = jax.vjp(
        state_part, x_heads, b_rows, step_size, log_decay
    )

    def pass_forward(turn_index, received):
        return passed_along(
            (total_state + total_decay[:, None, None] * received).astype(jnp.bfloat16), "seq", 1
        ).astype(jnp.float32)

    incoming = lax.fori_loop(0, lax.axis_size("seq") - 1, pass_forward, jnp.zeros_like(total_state))

    def output_part(
        heads_in, rows_b, rows_c, steps_in, decay_in, fresh_in, passing_in, incoming_in
    ):
        return local_output(
            heads_in, rows_b, rows_c, steps_in, decay_in, incoming_in, causal_mask, keep_flag
        )

    ssd_out, output_pull = jax.vjp(
        output_part, x_heads, b_rows, c_rows, step_size, log_decay, fresh_state, passing, incoming
    )
    skip_heads = skip_full.astype(jnp.float32)
    y_full = (ssd_out + skip_heads[:, None] * x_heads).reshape(length, DI)
    silu_z = jax.nn.silu(gate_z)
    gated = y_full * silu_z
    scale_out = lax.rsqrt(jnp.mean(gated * gated, axis=-1, keepdims=True) + EPSILON)
    gate_gain = gate_full.astype(jnp.float32)
    normed_out = (gated * scale_out * gate_gain).astype(jnp.bfloat16)
    branch = jnp.dot(normed_out, w_out_full, preferred_element_type=jnp.float32)
    layer_out = (inputs + branch).astype(jnp.bfloat16)[None]
    grad_out = cotangent[0]
    d_w_out = lax.dot_general(
        normed_out, grad_out, (((0,), (0,)), ((), ())), preferred_element_type=jnp.float32
    )
    d_normed_out = lax.dot_general(
        grad_out, w_out_full, (((1,), (1,)), ((), ())), preferred_element_type=jnp.float32
    )
    d_gate_w = jnp.sum(d_normed_out * gated * scale_out, axis=0)
    along_out = d_normed_out * gate_gain
    cube_out = scale_out * scale_out * scale_out
    d_gated = scale_out * along_out - gated * cube_out * jnp.mean(
        along_out * gated, axis=-1, keepdims=True
    )
    d_y = d_gated * silu_z
    sig_z = jax.nn.sigmoid(gate_z)
    d_gate_z = d_gated * y_full * sig_z * (1.0 + gate_z * (1.0 - sig_z))
    d_ssd = d_y.reshape(blocks, SPAN, HEADS, HEADDIM)
    d_skip_grad = jnp.sum(d_ssd * x_heads, axis=(0, 1, 3))
    dx_out, db_out, dc_out, dstep_out, ddecay_out, d_fresh, d_passing, d_incoming = output_pull(
        d_ssd
    )

    def pass_backward(turn_index, received):
        return passed_along(d_incoming + total_decay[:, None, None] * received, "seq", -1)

    d_total = lax.fori_loop(0, lax.axis_size("seq") - 1, pass_backward, jnp.zeros_like(d_incoming))
    d_total_decay = jnp.sum(d_total * incoming, axis=(1, 2))
    dx_state, db_state, dstep_state, ddecay_state = state_pull(
        (d_fresh, d_passing, d_total, d_total_decay)
    )
    d_x = dx_out + dx_state + skip_heads[:, None] * d_ssd
    d_b = db_out + db_state
    d_log = (ddecay_out + ddecay_state).reshape(length, HEADS)
    d_step = (dstep_out + dstep_state).reshape(length, HEADS) - d_log * decay_rate
    d_a_log = -jnp.sum(d_log * step_flat, axis=0) * decay_rate
    d_dt_raw = d_step * jax.nn.sigmoid(dt_raw + dt_bias_f)
    d_dt_bias = jnp.sum(d_dt_raw, axis=0)
    d_act = jnp.concatenate(
        [d_x.reshape(length, DI), d_b.reshape(length, STATE), dc_out.reshape(length, STATE)], axis=1
    )
    sig_conv = jax.nn.sigmoid(conv_out)
    d_conv = d_act * sig_conv * (1.0 + conv_out * (1.0 - sig_conv))
    d_conv_b = jnp.sum(d_conv, axis=0)
    kernel_rows = []
    d_padded = jnp.zeros((length + CONV - 1, CHAN), jnp.float32)
    for offset in range(CONV):
        masked = d_conv * same_docs[offset][:, None]
        kernel_rows.append(jnp.sum(masked * padded[offset : offset + length], axis=0))
        d_padded = d_padded + jnp.pad(
            kernel[offset] * masked, ((offset, CONV - 1 - offset), (0, 0))
        )
    d_kernel = jnp.stack(kernel_rows)
    d_edge = passed_along(shortened(d_padded[: CONV - 1]), "seq", -1)
    d_conv_in = d_padded[CONV - 1 :] + jnp.pad(d_edge, ((length - (CONV - 1), 0), (0, 0)))
    d_projected = jnp.concatenate([d_gate_z, d_conv_in, d_dt_raw], axis=1).astype(jnp.bfloat16)
    d_normed = lax.dot_general(
        d_projected, w_in_full, (((1,), (1,)), ((), ())), preferred_element_type=jnp.float32
    )
    d_norm_w = jnp.sum(d_normed * inputs * scale_in, axis=0)
    along_in = d_normed * norm_gain
    cube_in = scale_in * scale_in * scale_in
    d_inputs = (
        scale_in * along_in
        - inputs * cube_in * jnp.mean(along_in * inputs, axis=-1, keepdims=True)
        + grad_out.astype(jnp.float32)
    )
    d_w_in = lax.dot_general(
        normed, d_projected, (((0,), (0,)), ((), ())), preferred_element_type=jnp.float32
    )
    weight_grads = (
        d_w_in,
        d_w_out,
        d_kernel,
        d_conv_b,
        d_a_log,
        d_dt_bias,
        d_skip_grad,
        d_norm_w,
        d_gate_w,
    )
    shares = tuple(
        (
            lax.psum_scatter(weight_grads[0], "fsdp", scatter_dimension=0, tiled=True),
            lax.psum_scatter(weight_grads[1], "fsdp", scatter_dimension=0, tiled=True),
            lax.psum_scatter(weight_grads[2], "fsdp", scatter_dimension=1, tiled=True),
            lax.psum_scatter(weight_grads[3], "fsdp", scatter_dimension=0, tiled=True),
            lax.psum_scatter(weight_grads[4], "fsdp", scatter_dimension=0, tiled=True),
            lax.psum_scatter(weight_grads[5], "fsdp", scatter_dimension=0, tiled=True),
            lax.psum_scatter(weight_grads[6], "fsdp", scatter_dimension=0, tiled=True),
            lax.psum_scatter(weight_grads[7], "fsdp", scatter_dimension=0, tiled=True),
            lax.psum_scatter(weight_grads[8], "fsdp", scatter_dimension=0, tiled=True),
        )
    )
    totals = lax.psum(shares, "seq")
    return (layer_out, d_inputs[None]) + tuple(totals)


F32 = jnp.float32
BF = jnp.bfloat16
BLK = 256
TEAM = 8
HPD = HEADS // TEAM
CH = HPD * HEADDIM
NZ, NX, NB, ND = CH, CH, 2 * STATE, 64
COLS = NZ + NX + NB + ND
REST = NX + NB + ND
CONVC = NX + NB
TAIL = CONV - 1


def dot(a, b):
    return lax.dot_general(a, b, (((1,), (0,)), ((), ())), preferred_element_type=F32)


def dot_nt(a, b):
    return lax.dot_general(a, b, (((1,), (1,)), ((), ())), preferred_element_type=F32)


def dot_tn(a, b):
    return lax.dot_general(a, b, (((0,), (0,)), ((), ())), preferred_element_type=F32)


def dot_exact(a, b):
    return lax.dot_general(
        a, b, (((1,), (0,)), ((), ())), precision=HIGHEST, preferred_element_type=F32
    )


def iota(shape, dim):
    return lax.broadcasted_iota(jnp.int32, shape, dim)


def split_dot(a, b):
    high = a.astype(BF)
    low = (a - high.astype(F32)).astype(BF)
    return dot(high, b) + dot(low, b)


def spread():
    return (iota((128, CH), 1) // HEADDIM == iota((128, CH), 0)).astype(BF)


def gather_heads():
    return (iota((CH, 128), 0) // HEADDIM == iota((CH, 128), 1)).astype(BF)


def lower_tri():
    return (iota((BLK, BLK), 0) >= iota((BLK, BLK), 1)).astype(F32)


def softplus(v):
    return jnp.maximum(v, 0.0) + jnp.log1p(jnp.exp(-jnp.abs(v)))


def sigmoid(v):
    return 1.0 / (1.0 + jnp.exp(-v))


def conv_taps(cbuf, cw, tok):
    out = cw[CONV : CONV + 1, :] + cw[CONV - 1 : CONV, :] * cbuf[8 : 8 + BLK, :]
    for back in range(1, CONV):
        term = cw[CONV - 1 - back : CONV - back, :] * cbuf[8 - back : 8 - back + BLK, :]
        out = out + term * tok[:, back : back + 1]
    return out


def pair_select(left, right):
    return jnp.where(iota(left.shape, 1) % 128 < HEADDIM, left, right)


def head_of(slot, chip, core):
    first = 12 * slot + 3 * chip + 2 * core
    second = 12 * (core + 2 * (slot - 4)) + 3 * chip + 1
    return first, second


def pick_heads():
    seq = lax.axis_index("seq")
    chip, core = lax.div(seq, 2), lax.rem(seq, 2)
    slot = iota((128, 128), 1)
    first, second = head_of(slot, chip, core)
    head = jnp.where(slot < 4, first, jnp.where(slot < HPD, second, -1))
    return (iota((128, 128), 0) == head).astype(BF)


def own_heads(par, dt_cols):
    pick = pick_heads()
    pair = jnp.concatenate([par[5:6, CH : CH + 128], par[5:6, CH + 128 :], jnp.zeros((6, 128), F32)], axis=0)
    pair = dot(pair.astype(BF), pick)
    wide = jnp.concatenate([dt_cols, jnp.zeros((BLK, 128 - ND), BF)], axis=1)
    return jnp.exp(pair[1:2, :]), dot(wide, pick) + pair[0:1, :], iota((BLK, 128), 1) < HPD, pick


def norm_gain(par):
    return jnp.concatenate([par[7 + i : 8 + i, :512] for i in range(3)], axis=1)


def row_sum(q):
    high = q.astype(BF)
    low = (q - high.astype(F32)).astype(BF)
    ones = jnp.ones((8, q.shape[1]), BF)
    return (dot_nt(ones, high) + dot_nt(ones, low))[0:1, :]


def scan_forward(j, nrm, w_v, par, tok, idr, cbuf, state, projc_ref, st_ref, ssd_v):
    rows = pl.ds(pl.multiple_of(BLK * j, BLK), BLK)
    proj = dot_nt(nrm, w_v[NZ:, :]).astype(BF)
    projc_ref[...] = proj
    cbuf[8 : 8 + BLK, :] = proj[:, :CONVC].astype(F32)
    conv_out = conv_taps(cbuf, par, tok)
    cbuf[0:8, :] = cbuf[BLK : BLK + 8, :]
    act = conv_out * sigmoid(conv_out)
    x = act[:, :CH]
    bm = act[:, CH : CH + STATE].astype(BF)
    cm = act[:, CH + STATE :].astype(BF)
    rate, dt_in, own, pick = own_heads(par, proj[:, CONVC:])
    step = jnp.where(own, softplus(dt_in), 0.0)
    cum = dot_exact(lower_tri(), -step * rate)
    cum_t = cum.T
    mask = (iota((BLK, BLK), 0) >= iota((BLK, BLK), 1)) & (tok[:, 0:1] == idr)
    gm = jnp.where(mask, dot_nt(cm, bm), 0.0)
    ex = spread()
    xs = (x * split_dot(step, ex)).astype(BF)
    parts = []
    for pair in range(HPD // 2):
        xp = xs[:, 128 * pair : 128 * pair + 128]
        both = []
        for h in (2 * pair, 2 * pair + 1):
            decay = jnp.exp(jnp.minimum(cum[:, h : h + 1] - cum_t[h : h + 1, :], 0.0))
            both.append(dot((gm * decay).astype(BF), xp))
        parts.append(pair_select(*both))
    inner = jnp.concatenate(parts, axis=1)
    old = state[...]
    st_ref[0] = old
    keep = tok[:, 7:8]
    carried = split_dot(keep * jnp.exp(cum), ex) * dot(cm, old.astype(BF))
    last = cum[BLK - 1 : BLK, :]
    weights = jnp.exp(last - cum) * step * tok[:, 8:9]
    through = split_dot(jnp.broadcast_to(keep[BLK - 1 :, :] * jnp.exp(last), (8, 128)), ex)[0:1, :]
    state[...] = dot_tn(bm, (x * split_dot(weights, ex)).astype(BF)) + through * old
    ssd_v[rows, :] = inner + carried + par[6:7, :CH] * x


def gate_forward(j, nrm_v, g_v, w_v, wo_v, par, ssd_v, projz_ref, ssd_ref, dno_ref, br_ref, stat_v):
    rows = pl.ds(pl.multiple_of(BLK * j, BLK), BLK)
    projz = dot_nt(nrm_v[rows, :], w_v[:NZ, :]).astype(BF)
    projz_ref[...] = projz
    ssd = ssd_v[rows, :]
    ssd_ref[...] = ssd
    z = projz.astype(F32)
    gate_w = par[5:6, :CH]
    gated = ssd * (z * sigmoid(z))
    br_ref[...] = dot((gated * gate_w).astype(BF), wo_v[...]).astype(BF)
    dno = dot_nt(g_v[rows, :], wo_v[...])
    dno_ref[...] = dno
    stat_v[pl.ds(j, 1), 0:BLK] = row_sum(gated * gated)
    stat_v[pl.ds(j, 1), BLK : 2 * BLK] = row_sum(dno * gate_w * gated)


def gate_backward(j, z, ssd, dno, stat, gate_w, not_v, dy_v, dz_v, dzt_v, small_v):
    rows = pl.ds(pl.multiple_of(BLK * j, BLK), BLK)
    sig_z = sigmoid(z)
    silu_z = z * sig_z
    stat = jnp.where(iota((128, BLK), 0) == 0, stat[:, :BLK], stat[:, BLK:]).T
    s2 = lax.rsqrt(stat[:, 0:1] * (1.0 / DI) + EPSILON)
    mean_ag = stat[:, 1:2] * (1.0 / DI)
    gated = ssd * silu_z
    gs = gated * s2
    not_v[:, rows] = (gs * gate_w).T.astype(BF)
    d_gated = s2 * (dno * gate_w) - gated * (s2 * s2 * s2 * mean_ag)
    dy_v[rows, :] = d_gated * silu_z
    dz = d_gated * ssd * sig_z * (1.0 + z * (1.0 - sig_z))
    dz_v[rows, :] = dz.astype(BF)
    dzt_v[:, rows] = dz.T.astype(BF)
    small_v[5:6, :CH] += jnp.sum(dno * gs, axis=0, keepdims=True)


def scan_backward(proj, halo, tok, idr, old, par, dy, cbuf, dcbuf, dstate, small_v):
    cbuf[0:8, :] = halo[8:16, :CONVC].astype(F32)
    cbuf[8 : 8 + BLK, :] = proj[:, :CONVC].astype(F32)
    conv_out = conv_taps(cbuf, par, tok)
    sig_c = sigmoid(conv_out)
    act = conv_out * sig_c
    x = act[:, :CH]
    bm = act[:, CH : CH + STATE].astype(BF)
    cm_f = act[:, CH + STATE :]
    cm = cm_f.astype(BF)
    rate, dt_in, own, pick = own_heads(par, proj[:, CONVC:])
    step = jnp.where(own, softplus(dt_in), 0.0)
    cum = dot_exact(lower_tri(), -step * rate)
    cum_t = cum.T
    mask = (iota((BLK, BLK), 0) >= iota((BLK, BLK), 1)) & (tok[:, 0:1] == idr)
    gm = jnp.where(mask, dot_nt(cm, bm), 0.0)
    ex = spread()
    gh = gather_heads()
    step_x = split_dot(step, ex)
    xs = (x * step_x).astype(BF)
    dyb = dy.astype(BF)
    dyt = dy.T.astype(BF)
    lane = iota((BLK, 128), 1)
    dg = jnp.zeros((BLK, BLK), F32)
    row_sums = jnp.zeros((BLK, 128), F32)
    col_sums = []
    e_rows = []
    for h in range(HPD):
        pair = h // 2
        decay = jnp.exp(jnp.minimum(cum[:, h : h + 1] - cum_t[h : h + 1, :], 0.0))
        mixed = gm * decay
        half = jnp.where((lane < HEADDIM) == (h % 2 == 0), dyb[:, 128 * pair : 128 * pair + 128], 0)
        dms = dot_nt(half.astype(BF), xs[:, 128 * pair : 128 * pair + 128])
        product = dms * mixed
        row_sums = jnp.where(lane == h, jnp.sum(product, axis=1, keepdims=True), row_sums)
        col_sums.append(jnp.sum(product, axis=0, keepdims=True))
        dg = dg + dms * decay
        e_rows.append(dot(dyt[HEADDIM * h : HEADDIM * h + HEADDIM, :], mixed.astype(BF)))
    dg = jnp.where(mask, dg, 0.0).astype(BF)
    e = jnp.concatenate(e_rows, axis=0).T
    col_sums.append(jnp.zeros((128 - HPD, BLK), F32))
    col = jnp.concatenate(col_sums, axis=0).T
    keep = tok[:, 7:8]
    old_b = old.astype(BF)
    dnew = dstate[...]
    dnew_b = dnew.astype(BF)
    carry_x = split_dot(keep * jnp.exp(cum), ex)
    dyk_f = dy * carry_x
    dyk = dyk_f.astype(BF)
    carried = dot(cm, old_b)
    last = cum[BLK - 1 : BLK, :]
    fade = jnp.exp(last - cum) * tok[:, 8:9]
    weights = fade * step
    weights_x = split_dot(weights, ex)
    zt = dot(bm, dnew_b)
    xw = (x * weights_x).astype(BF)
    through = keep[BLK - 1 :, :] * jnp.exp(last)
    through_x = split_dot(jnp.broadcast_to(through, (8, 128)), ex)[0:1, :]
    k_term = split_dot(dyk_f * carried, gh)
    r_term = split_dot(x * zt, gh)
    q_term = split_dot(x * e, gh)
    pass_term = jnp.sum(old * dnew, axis=0, keepdims=True) * through_x
    pass_h = split_dot(jnp.broadcast_to(pass_term, (8, CH)), gh)[0:1, :]
    wr = weights * r_term
    d_cum = row_sums - col + k_term - wr
    d_last = jnp.sum(wr, axis=0, keepdims=True) + pass_h
    d_cum = d_cum + jnp.where(iota((BLK, 128), 0) == BLK - 1, d_last, 0.0)
    upper = (iota((BLK, BLK), 0) <= iota((BLK, BLK), 1)).astype(F32)
    d_log = dot_exact(upper, d_cum)
    d_step = q_term + fade * r_term - d_log * rate
    d_a = -jnp.sum(d_log * step, axis=0, keepdims=True) * rate
    d_dt = jnp.where(own, d_step * sigmoid(dt_in), 0.0)
    heads = jnp.concatenate([d_a, jnp.sum(d_dt, axis=0, keepdims=True), jnp.zeros((6, 128), F32)], axis=0)
    high = heads.astype(BF)
    heads = dot_nt(high, pick) + dot_nt((heads - high.astype(F32)).astype(BF), pick)
    d_dt = dot_nt(d_dt.astype(BF), pick)
    dstate[...] = dot_tn(cm, dyk) + through_x * dnew
    dx = step_x * e + weights_x * zt + par[6:7, :CH] * dy
    dc = dot(dg, bm) + dot_nt(dyk, old_b)
    db = dot(cm_f.T.astype(BF), dg).T + dot_nt(xw, dnew_b)
    d_act = jnp.concatenate([dx, db, dc], axis=1)
    d_conv = d_act * (sig_c * (1.0 + conv_out * (1.0 - sig_c)))
    dcbuf[0:BLK, :] = d_conv
    d_in = par[CONV - 1 : CONV, :] * d_conv
    cg = [None] * CONV
    cg[CONV - 1] = jnp.sum(d_conv * cbuf[8 : 8 + BLK, :], axis=0, keepdims=True)
    for back in range(1, CONV):
        tap = CONV - 1 - back
        cg[tap] = jnp.sum(
            d_conv * (cbuf[8 - back : 8 - back + BLK, :] * tok[:, back : back + 1]),
            axis=0, keepdims=True,
        )
        d_in = d_in + par[tap : tap + 1, :] * (
            dcbuf[back : back + BLK, :] * tok[:, 3 + back : 4 + back]
        )
    dcbuf[BLK : BLK + 8, :] = dcbuf[0:8, :]
    small_v[0:CONV, :] += jnp.concatenate(cg, axis=0)
    small_v[CONV : CONV + 1, :] += jnp.sum(d_conv, axis=0, keepdims=True)
    small_v[5:6, CH:] += jnp.concatenate([heads[0:1, :], heads[1:2, :]], axis=1)
    small_v[6:7, :CH] += jnp.sum(dy * x, axis=0, keepdims=True)
    return jnp.concatenate([d_in, d_dt[:, :ND]], axis=1)


def token_info(ids_full, first, n):
    length = ids_full.shape[0]
    pad = jnp.concatenate(
        [jnp.full((8,), -1, jnp.int32), ids_full, jnp.full((8,), -2, jnp.int32)]
    )
    window = lax.dynamic_slice_in_dim(pad, first, n + 16)
    own = window[8 : 8 + n]
    blocks = own.reshape(-1, BLK)
    before = window[7 : 7 + n].reshape(-1, BLK)[:, :1]
    cols = [own]
    for back in range(1, CONV):
        cols.append((window[8 - back : 8 - back + n] == own))
    for ahead in range(1, CONV):
        cols.append((window[8 + ahead : 8 + ahead + n] == own))
    cols.append((blocks == before).reshape(-1))
    cols.append((blocks == blocks[:, -1:]).reshape(-1))
    table = jnp.stack([c.astype(F32) for c in cols], axis=1)
    tok = jnp.pad(table, ((0, 0), (0, 128 - table.shape[1])))
    idr = jnp.broadcast_to(own.astype(F32).reshape(-1, 1, BLK), (n // BLK, 8, BLK))
    return tok, idr


CHIPS = TEAM // 2
DEPTH = 4
KROWS = D // DEPTH
BCD = NB + ND
HALF = BCD // 2


def places():
    seq = lax.axis_index("seq")
    return seq, lax.div(seq, 2), lax.rem(seq, 2), lax.axis_index("fsdp")


def neighbours(chip):
    return [chip, chip + 1 - 2 * lax.rem(chip, 2), lax.rem(chip + 2, CHIPS), CHIPS - 1 - chip]


def send(src, dst, send_sem, recv_sem, device):
    return pltpu.make_async_remote_copy(
        src_ref=src, dst_ref=dst, send_sem=send_sem, recv_sem=recv_sem,
        device_id=device, device_id_type=pl.DeviceIdType.MESH,
    )


def greet(devices):
    barrier = pltpu.get_barrier_semaphore()
    for device in devices:
        pl.semaphore_signal(
            barrier, inc=1, device_id=device, device_id_type=pl.DeviceIdType.MESH
        )
    pl.semaphore_wait(barrier, len(devices))


def forward_kernel(
    tok_ref, cot_ref, win_ref, bcd_ref, wout_ref, small_ref, info_ref, idr_ref,
    nrm_ref, projc_ref, projz_ref, st_ref, ssd_ref, dno_ref, br_ref, stat_ref, par_ref, w_ref, g_ref,
    u_v, g_v, w_v, wo_v, smalls, ssd_v, cbuf, state, stat_v, stat_in,
    loc, t_send, t_recv, y_send, y_recv, f_send, f_recv, z_send, z_recv, b_send, b_recv, s_send, s_recv, r_send, r_recv,
):
    i = pl.program_id(0)
    seq, chip, core, z = places()
    sib = {"seq": 2 * chip + 1 - core}
    near = neighbours(chip)
    peer = lambda k: {"seq": 2 * near[k] + core}
    under = lambda k: {"fsdp": lax.rem(z + k, DEPTH)}
    around = lambda k: {"seq": lax.rem(seq + k, TEAM)}
    block = lambda s: pl.ds(pl.multiple_of(BLK * s, BLK), BLK)
    lanes = lambda o: pl.ds(pl.multiple_of(KROWS * o, KROWS), KROWS)
    half = pl.ds(pl.multiple_of(NZ + NX + HALF * core, 16), HALF)
    has = [z < DEPTH - 1, z > 0]
    heads = [head_of(n, chip, core)[n // 4] for n in range(HPD)]
    piece = lambda n: pl.ds(pl.multiple_of(HEADDIM * n, HEADDIM), HEADDIM)

    def token_copy(n, k):
        src, dst = ((tok_ref, u_v), (cot_ref, g_v))[n]
        return send(src, dst.at[block(seq)], t_send.at[n, k], t_recv.at[n, k], sib if k == 0 else peer(k))

    def token_part(n, k, h):
        return (u_v, g_v)[n].at[pl.ds(pl.multiple_of(BLK * (2 * near[k] + core) + h * (BLK // 2), BLK // 2), BLK // 2)]

    def token_relay(n, h):
        part = token_part(n, 1 + h, h)
        return send(part, part, y_send.at[n, h], y_recv.at[n, h], peer(2 - h))

    def token_next(n, k):
        if k < 3:
            ref = (u_v, g_v)[n].at[block(2 * near[k] + core)]
        else:
            ref = token_part(n, 3, k - 3)
        return send(ref, ref, f_send.at[n, k], f_recv.at[n, k], sib)

    def token_start(n):
        for k in range(3):
            token_copy(n, k).start()

    def token_turn(n):
        for k in (1, 2):
            token_copy(n, k).wait_recv()
            token_relay(n, k - 1).start()
            token_next(n, k).start()

    def token_end(n):
        for h in range(2):
            token_relay(n, h).wait_recv()
            token_next(n, 3 + h).start()
        token_copy(n, 0).wait_recv()
        for k in range(1, 5):
            token_next(n, k).wait()
        for h in range(2):
            token_relay(n, h).wait_send()

    def place(p, o):
        if p < 3:
            return w_v.at[(pl.ds(NZ, NX), half, pl.ds(0, NZ))[p], lanes(o)]
        return wo_v.at[piece(o if p == 3 else DEPTH + lax.div(o, 2))]

    def hop(p, side, dist):
        o = z - dist if side == 0 else z + dist
        there = {"fsdp": z + 1} if side == 0 else {"fsdp": z - 1}
        return send(place(p, o), place(p, o), z_send.at[p, side, dist], z_recv.at[p, side, dist], there)

    def got(p, side, dist):
        o = z - dist - 1 if side == 0 else z + dist + 1
        there = {"fsdp": z + 1} if side == 0 else {"fsdp": z - 1}
        return send(place(p, o), place(p, o), z_send.at[p, side, dist], z_recv.at[p, side, dist], there)

    def share(side, dist):
        o = z - dist - 1 if side == 0 else z + dist + 1
        return send(place(1, o), place(1, o), b_send.at[side, dist], b_recv.at[side, dist], sib)

    def exists(p, side, hops):
        o = z - hops if side == 0 else z + hops
        there = (o >= 0) if side == 0 else (o < DEPTH)
        return there & (lax.rem(o + DEPTH, 2) == core) if p == 4 else there

    def small_copy(k):
        return send(small_ref, smalls.at[z], s_send.at[k], s_recv.at[k], under(k))

    def stat_copy(k):
        return send(stat_v, stat_in.at[k], r_send.at[k], r_recv.at[k], around(k))

    def local_copies():
        pairs = [(tok_ref, u_v.at[block(seq)]), (cot_ref, g_v.at[block(seq)]), (small_ref, smalls.at[z])]
        return [pltpu.make_async_copy(src, dst, loc.at[n]) for n, (src, dst) in enumerate(pairs)]

    def own_weights():
        pairs = [(bcd_ref, w_v.at[pl.ds(NZ + NX, BCD), lanes(z)], 3)]
        for n in range(HPD):
            row = HEADDIM * heads[n]
            pairs.append((win_ref.at[pl.ds(pl.multiple_of(row, HEADDIM), HEADDIM)],
                          w_v.at[piece(n), lanes(z)], 4 + n))
            pairs.append((win_ref.at[pl.ds(pl.multiple_of(DI + row, HEADDIM), HEADDIM)],
                          w_v.at[piece(HPD + n), lanes(z)], 10 + n))
        pairs.append((wout_ref.at[piece(3 * chip + 2 * core)], place(3, z), 16))
        return [pltpu.make_async_copy(src, dst, loc.at[n]) for src, dst, n in pairs]

    def own_extra():
        return pltpu.make_async_copy(wout_ref.at[piece(3 * chip + 1)], place(4, z), loc.at[17])

    def pass_on(parts, dist):
        for p in parts:
            for side in range(2):

                @pl.when(exists(p, side, dist + 1))
                def _():
                    got(p, side, dist).wait_recv()
                    if p == 1:
                        share(side, dist).start()

                if dist < DEPTH - 2:

                    @pl.when(exists(p, side, dist + 1) & has[side])
                    def _():
                        hop(p, side, dist + 1).start()

    def start_own(parts):
        for p in parts:
            for side in range(2):

                @pl.when(exists(p, side, 0) & has[side])
                def _():
                    hop(p, side, 0).start()

    @pl.when(i == 0)
    def _():
        greet([around(k) for k in range(1, TEAM)] + [under(k) for k in range(1, DEPTH)])
        for k in range(1, DEPTH):
            small_copy(k).start()
        token_start(0)
        for copy in own_weights() + local_copies():
            copy.start()

        @pl.when(lax.rem(z, 2) == core)
        def _():
            own_extra().start()

        for copy in own_weights():
            copy.wait()
        start_own((0, 1))
        state[...] = jnp.zeros_like(state)
        cbuf[0:8, :] = jnp.zeros((8, CONVC), F32)
        pass_on((0, 1), 0)
        token_turn(0)
        token_start(1)
        pass_on((0, 1), 1)
        start_own((2,))
        token_end(0)
        pass_on((0, 1), 2)
        for k in range(1, DEPTH):
            small_copy(k).wait()
        for copy in local_copies():
            copy.wait()
        for side in range(2):
            for dist in range(DEPTH - 1):

                @pl.when(exists(1, side, dist + 1))
                def _():
                    share(side, dist).wait()

        total = smalls[0].astype(F32)
        for o in range(1, DEPTH):
            total = total + smalls[o].astype(F32)
        par_ref[...] = total

    @pl.when(i == 1)
    def _():
        @pl.when(lax.rem(z, 2) == core)
        def _():
            own_extra().wait()

        pass_on((2,), 0)
        start_own((3, 4))

    @pl.when(i == 3)
    def _():
        pass_on((2,), 1)

    @pl.when(i == 4)
    def _():
        token_turn(1)

    @pl.when(i == 5)
    def _():
        pass_on((3, 4), 0)

    @pl.when(i == 7)
    def _():
        pass_on((3, 4), 1)

    @pl.when(i == TEAM)
    def _():
        pass_on((2, 3, 4), 2)
        token_end(1)
        pltpu.make_async_copy(w_v, w_ref, loc.at[18]).start()
        pltpu.make_async_copy(g_v, g_ref, loc.at[19]).start()

    par = par_ref[...]

    @pl.when(i < TEAM)
    def _():
        u = u_v[block(i), :].astype(F32)
        scale = lax.rsqrt(jnp.mean(u * u, axis=1, keepdims=True) + EPSILON)
        nrm = (u * scale * norm_gain(par)).astype(BF)
        nrm_ref[...] = nrm
        u_v[block(i), :] = nrm
        scan_forward(i, nrm, w_v, par, info_ref[...], idr_ref[0, 0:1, :], cbuf, state,
                     projc_ref, st_ref, ssd_v)

    @pl.when(i >= TEAM)
    def _():
        gate_forward(i - TEAM, u_v, g_v, w_v, wo_v, par, ssd_v, projz_ref, ssd_ref, dno_ref,
                     br_ref, stat_v)

    @pl.when(i == 2 * TEAM - 1)
    def _():
        for k in range(1, TEAM):
            stat_copy(k).start()
        total = stat_v[...]
        for k in range(1, TEAM):
            stat_copy(k).wait_recv()
            total = total + stat_in[k]
        stat_ref[...] = total
        for k in range(1, TEAM):
            stat_copy(k).wait_send()
        for n in range(2):
            for k in range(3):
                token_copy(n, k).wait_send()
        for side in range(2):
            for dist in range(DEPTH - 1):
                for p in range(5):

                    @pl.when(exists(p, side, dist) & has[side])
                    def _():
                        hop(p, side, dist).wait_send()

        pltpu.make_async_copy(w_v, w_ref, loc.at[18]).wait()
        pltpu.make_async_copy(g_v, g_ref, loc.at[19]).wait()


def forward_call(tok, cot, win, bcd, wout, small, info, idr):
    n = tok.shape[0] * TEAM
    any_space = pl.BlockSpec(memory_space=pl.ANY)
    sds = jax.ShapeDtypeStruct
    dma = pltpu.SemaphoreType.DMA
    one = lambda i: jnp.minimum(i, TEAM - 1)
    two = lambda i: jnp.maximum(i - TEAM, 0)
    rows = lambda c, turn: pl.BlockSpec((BLK, c), lambda i: (turn(i), 0))
    cube = lambda a, b: pl.BlockSpec((1, a, b), lambda i: (one(i), 0, 0))
    fixed = lambda a, b: pl.BlockSpec((a, b), lambda i: (0, 0))
    return pl.pallas_call(
        forward_kernel,
        grid=(2 * TEAM,),
        in_specs=[any_space] * 6 + [rows(128, one), cube(8, BLK)],
        out_specs=[rows(D, one), rows(REST, one), rows(NZ, two), cube(STATE, CH), rows(CH, two),
                   rows(CH, two), rows(D, two), fixed(TEAM, 2 * BLK), fixed(16, CONVC), any_space,
                   any_space],
        out_shape=[sds((n, D), BF), sds((n, REST), BF), sds((n, NZ), BF), sds((TEAM, STATE, CH), F32),
                   sds((n, CH), F32), sds((n, CH), F32), sds((n, D), BF), sds((TEAM, 2 * BLK), F32),
                   sds((16, CONVC), F32), sds((COLS, D), BF), sds((n, D), BF)],
        scratch_shapes=[pltpu.VMEM((n, D), BF), pltpu.VMEM((n, D), BF), pltpu.VMEM((COLS, D), BF),
                        pltpu.VMEM((CH, D), BF), pltpu.VMEM((DEPTH, 16, CONVC), BF),
                        pltpu.VMEM((n, CH), F32), pltpu.VMEM((BLK + 8, CONVC), F32),
                        pltpu.VMEM((STATE, CH), F32), pltpu.VMEM((TEAM, 2 * BLK), F32),
                        pltpu.VMEM((TEAM, TEAM, 2 * BLK), F32),
                        dma((20,)), dma((2, 3)), dma((2, 3)), dma((2, 2)), dma((2, 2)), dma((2, 5)),
                        dma((2, 5)), dma((5, 2, DEPTH - 1)), dma((5, 2, DEPTH - 1)),
                        dma((2, DEPTH - 1)), dma((2, DEPTH - 1)),
                        dma((DEPTH,)), dma((DEPTH,)), dma((TEAM,)), dma((TEAM,))],
        compiler_params=pltpu.CompilerParams(
            collective_id=0, has_side_effects=True, vmem_limit_bytes=60 << 20),
    )(tok, cot, win, bcd, wout, small, info, idr)


def backward_kernel(
    tok_ref, cot_ref, nrm_ref, br_ref, w_ref, g_ref,
    projz_ref, ssd_ref, dno_ref, stat_ref, par_ref, projc_ref, halo_ref, st_ref, info_ref, idr_ref,
    out_ref, tg_ref, wig_ref, wog_ref, smalls_ref,
    nrm_v, g_v, w_v, not_v, dz_v, dzt_v, dy_v, rest_v, wig_v, wog_v, bcd_v, bcd_in,
    zz_in, zx_in, zb_in, zw_in, zs_in, gz_v, gx_v, gb_v, gw_v, gb_in, gt_v, ob_v, rb_v, in_v, rel_v,
    tok_v, cot_v, small_v, small_s, cbuf, dcbuf, dstate,
    loc, b_send, b_recv, p_send, p_recv, d_send, d_recv, q_send, q_recv, z_send, z_recv,
    a_send, a_recv, f_send, f_recv, h_send, h_recv, free,
):
    i = pl.program_id(0)
    seq, chip, core, z = places()
    sib = {"seq": 2 * chip + 1 - core}
    near = neighbours(chip)
    peer = lambda k: {"seq": 2 * near[k] + core}
    under = lambda k: {"fsdp": lax.rem(z + k, DEPTH)}
    around = lambda k: {"seq": lax.rem(seq + k, TEAM)}
    block = lambda s: pl.ds(pl.multiple_of(BLK * s, BLK), BLK)
    lanes = lambda o: pl.ds(pl.multiple_of(KROWS * o, KROWS), KROWS)
    piece = lambda n: pl.ds(pl.multiple_of(HEADDIM * n, HEADDIM), HEADDIM)
    half = lambda c: pl.ds(pl.multiple_of(HALF * c, 16), HALF)
    extra = lambda o: lax.rem(o, 2) == core
    n_all = HEADDIM * HPD
    give = lambda c: g_v.at[block(c)]
    hold = lambda c: g_v.at[block(CHIPS + c)]

    def load(n):
        pairs = [(nrm_ref, nrm_v), (g_ref, g_v), (w_ref, w_v), (tok_ref, tok_v), (cot_ref, cot_v)]
        return pltpu.make_async_copy(pairs[n][0], pairs[n][1], loc.at[n])

    def load_own(c):
        return pltpu.make_async_copy(br_ref.at[block(2 * c + core)], ob_v.at[c], loc.at[5 + c])

    def br_pair(c):
        return send(br_ref.at[block(2 * c + 1 - core)], rb_v.at[c], b_send.at[c], b_recv.at[c], sib)

    def block_of(n, c):
        return ob_v.at[c] if n == 0 else hold(c)

    def rs(n, kind):
        h = pl.ds((0, BLK // 2, BLK // 2, 0, 0, BLK // 2)[kind], BLK // 2)
        src = block_of(n, near[(1, 1, 2, 2, 3, 3)[kind]]).at[h]
        if kind < 4:
            dst = in_v.at[n, kind // 2, h]
        else:
            dst = rel_v.at[n, 5 - kind]
        return send(src, dst, p_send.at[n, kind], p_recv.at[n, kind], peer((1, 1, 2, 2, 1, 2)[kind]))

    def rs_first(n, role):
        for kind in ((), (0,), (2,), (4, 5))[role]:
            rs(n, kind).start()

    def rs_second(n, role):
        kind, came = ((1, 5), (3, 4))[role - 1]
        rs(n, came).wait_recv()
        h = pl.ds((BLK // 2, 0)[role - 1], BLK // 2)
        ref = block_of(n, near[role]).at[h]
        ref[...] = (ref[...].astype(F32) + rel_v[n, role - 1].astype(F32)).astype(BF)
        rs(n, kind).start()

    def rs_total(n):
        for kind in range(4):
            rs(n, kind).wait_recv()
        return block_of(n, chip)[...].astype(F32) + in_v[n, 0].astype(F32) + in_v[n, 1].astype(F32)

    def dn_pair(c):
        return send(give(c), rb_v.at[c], d_send.at[c], d_recv.at[c], sib)

    def down(n, k):
        o = lax.rem(z + k, DEPTH)
        src, dst = [
            (wig_v.at[:, lanes(o)], zz_in.at[k - 1]),
            (wig_v.at[:, lanes(o)], zx_in.at[k - 1]),
            (bcd_v.at[half(core), lanes(o)], zb_in.at[k - 1]),
            (wog_v.at[piece(o)], zw_in.at[k - 1, 0:HEADDIM]),
            (wog_v.at[piece(DEPTH + lax.div(o, 2))], zw_in.at[k - 1, HEADDIM:]),
            (small_v, zs_in.at[k - 1]),
        ][n]
        return send(src, dst, z_send.at[n, k], z_recv.at[n, k], under(k))

    def bcd_pair():
        return send(bcd_v.at[half(1 - core)], bcd_in, h_send.at[0], h_recv.at[0], sib)

    def bcd_push(k):
        return send(gb_v, gb_in.at[k - 1], q_send.at[k], q_recv.at[k], peer(k))

    def bcd_back():
        return send(gt_v.at[core], gt_v.at[core], h_send.at[1], h_recv.at[1], sib)

    def parts(n, c, cr, h=None):
        if n < 2:
            base = n * DI // HEADDIM
            src = (gz_v, gx_v)[n]
            slots = range(HPD) if h is None else range(3 * h, 3 * h + 3)
            return [(src.at[piece(s)], wig_ref.at[piece(base + head_of(s, c, cr)[s // 4])]) for s in slots]
        if n < 4:
            row = HEADDIM * (3 * c + 2 * cr if n == 2 else 3 * c + 1)
            first, size = (0, HEADDIM) if h is None else (h * HEADDIM // 2, HEADDIM // 2)
            return [(gw_v.at[pl.ds(HEADDIM * (n - 2) + first, size)],
                     wog_ref.at[pl.ds(pl.multiple_of(row + first, HEADDIM // 2), size)])]
        if h is None:
            return [(small_s, smalls_ref.at[2 * c + cr])]
        return [(small_s.at[8 * h : 8 * h + 8], smalls_ref.at[2 * c + cr, 8 * h : 8 * h + 8])]

    def all_of(n, h=None):
        if n < 2:
            return wig_ref.at[pl.ds(n * DI, n_all if h is None else n_all // 2)]
        return parts(n, 0, 0, h)[0][1]

    def ag(n, k):
        if k < 3:
            return [send(src, dst, a_send.at[n, k], a_recv.at[n, k], sib if k == 0 else peer(k))
                    for src, dst in parts(n, chip, core)]
        return [send(dst, dst, a_send.at[n, k], a_recv.at[n, k], peer(5 - k))
                for _, dst in parts(n, near[k - 2], core, k - 3)]

    def ag_wait(n, k):
        ref = all_of(n, None if k < 3 else k - 3)
        return send(ref, ref, a_send.at[n, k], a_recv.at[n, k], sib)

    def ag_next(n, k):
        which = parts(n, near[k], core) if k < 3 else parts(n, near[3], core, k - 3)
        return [send(dst, dst, f_send.at[n, k], f_recv.at[n, k], sib) for _, dst in which]

    def ag_next_wait(n, k):
        ref = all_of(n, None if k < 3 else k - 3)
        return send(ref, ref, f_send.at[n, k], f_recv.at[n, k], sib)

    def ag_own(n):
        return [pltpu.make_async_copy(src, dst, loc.at[9 + n]) for src, dst in parts(n, chip, core)]

    def ag_own_wait(n):
        return pltpu.make_async_copy(all_of(n), all_of(n), loc.at[9 + n])

    def ag_start(n):
        for k in (1, 2, 0):
            for copy in ag(n, k):
                copy.start()
        for copy in ag_own(n):
            copy.start()

    def ag_turn(n):
        for k in (1, 2):
            ag_wait(n, k).wait_recv()
            for copy in ag(n, k + 2) + ag_next(n, k):
                copy.start()

    def ag_end(n):
        for k in (3, 4):
            ag_wait(n, k).wait_recv()
            for copy in ag_next(n, k):
                copy.start()

    def ag_close(n, sends=True, receives=True):
        if receives:
            ag_wait(n, 0).wait_recv()
            for k in range(1, 5):
                ag_next_wait(n, k).wait_recv()
        if sends:
            for k in range(5):
                ag_wait(n, k).wait_send()
            for k in range(1, 5):
                ag_next_wait(n, k).wait_send()
            ag_own_wait(n).wait()

    def reduce_z(own, arrived):
        total = own.astype(F32)
        for k in range(1, DEPTH):
            total = total + arrived[k - 1].astype(F32)
        return total

    @pl.when(i == 0)
    def _():
        greet([around(k) for k in range(1, TEAM)] + [under(k) for k in range(1, DEPTH)])
        for c in range(CHIPS):
            br_pair(c).start()
            load_own(c).start()
        for n in range(5):
            load(n).start()
        small_v[...] = jnp.zeros_like(small_v)
        dstate[...] = jnp.zeros_like(dstate)
        dcbuf[BLK : BLK + 8, :] = jnp.zeros((8, CONVC), F32)

    @pl.when(i < TEAM)
    def _():
        gate_backward(i, projz_ref[...].astype(F32), ssd_ref[...], dno_ref[...],
                      stat_ref[pl.ds(i, 1), :], par_ref[5:6, :CH], not_v, dy_v, dz_v, dzt_v, small_v)

    @pl.when(i == 1)
    def _():
        for c in range(CHIPS):
            load_own(c).wait()
            br_pair(c).wait_recv()
            ob_v[c] = (ob_v[c].astype(F32) + rb_v[c].astype(F32)).astype(BF)
        for role in (3, 1, 2):
            rs_first(0, role)
        pl.semaphore_signal(free, inc=1, device_id=sib, device_id_type=pl.DeviceIdType.MESH)

    @pl.when(i == TEAM)
    def _():
        pl.semaphore_wait(free, 1)
        for n in range(5):
            load(n).wait()

        @pl.loop(0, D // 256)
        def _(n):
            cols = pl.ds(pl.multiple_of(256 * n, 256), 256)
            wig_v[:, cols] = dot(dzt_v[...], nrm_v[:, cols]).astype(BF)

        for k in range(1, DEPTH):
            down(0, k).start()

        @pl.loop(0, D // 256)
        def _(n):
            cols = pl.ds(pl.multiple_of(256 * n, 256), 256)
            wog_v[:, cols] = dot(not_v[...], g_v[:, cols]).astype(BF)

        for k in range(1, DEPTH):
            down(3, k).start()

            @pl.when(extra(z + k))
            def _():
                down(4, k).start()

    def combine(c):
        dn_pair(c).wait_recv()
        hold(c)[...] = (hold(c)[...].astype(F32) + rb_v[c].astype(F32)).astype(BF)
        for role in (1, 2, 3):

            @pl.when(near[role] == c)
            def _():
                rs_first(1, role)

    def relay(c):
        for role in (1, 2):

            @pl.when(near[role] == c)
            def _():
                rs_second(1, role)

    for c in range(CHIPS - 1, 0, -1):

        @pl.when(i == TEAM + 1 + 2 * (CHIPS - c))
        def _():
            combine(c)
            if c < CHIPS - 1:
                relay(c + 1)

    @pl.when(i == TEAM + 2)
    def _():
        rs_second(0, 1)
        rs_second(0, 2)

    @pl.when((i > TEAM) & (i <= 2 * TEAM))
    def _():
        j = 2 * TEAM - i
        rows = block(j)
        d_rest = scan_backward(projc_ref[...], halo_ref[...], info_ref[...], idr_ref[0, 0:1, :], st_ref[0],
                               par_ref[...], dy_v[rows, :], cbuf, dcbuf, dstate, small_v)
        rest_v[:, rows] = d_rest.T.astype(BF)
        dn = dot(dz_v[rows, :], w_v[:NZ, :]) + dot(d_rest.astype(BF), w_v[NZ:, :])
        part = jnp.sum(dn * nrm_v[rows, :].astype(F32), axis=0, keepdims=True)
        for n in range(3):
            small_v[7 + n : 8 + n, :512] += part[:, 512 * n : 512 * n + 512]
        dn = dn.astype(BF)
        c = lax.div(j, 2)

        @pl.when(lax.rem(j, 2) == core)
        def _():
            hold(c)[...] = dn

        @pl.when(lax.rem(j, 2) != core)
        def _():
            give(c)[...] = dn
            dn_pair(c).start()

    @pl.when(i == 2 * TEAM - 1)
    def _():
        total = rs_total(0)
        stat = stat_ref[pl.ds(seq, 1), 0:BLK]
        stat = jnp.broadcast_to(stat, (128, BLK)).T
        s2 = lax.rsqrt(stat[:, 0:1] * (1.0 / DI) + EPSILON)
        out_ref[...] = (tok_v[...].astype(F32) + total * s2).astype(BF)

    @pl.when(i == 2 * TEAM)
    def _():
        for k in range(1, DEPTH):
            down(0, k).wait_recv()
        gz_v[...] = reduce_z(wig_v[:, lanes(z)], [zz_in[k - 1] for k in range(1, DEPTH)]).astype(BF)
        ag_start(0)

    @pl.when(i == 2 * TEAM + 1)
    def _():
        for n in range(3):
            small_v[7 + n : 8 + n, :512] = small_v[7 + n : 8 + n, :512] / par_ref[7 + n : 8 + n, :512]
        for k in range(1, DEPTH):
            down(5, k).start()
        combine(0)
        relay(1)

        @pl.loop(0, D // 256)
        def _(n):
            cols = pl.ds(pl.multiple_of(256 * n, 256), 256)
            bcd_v[:, cols] = dot(rest_v[NX:, :], nrm_v[:, cols]).astype(BF)

        bcd_pair().start()
        for k in range(1, DEPTH):
            down(0, k).wait_send()

        @pl.loop(0, D // 256)
        def _(n):
            cols = pl.ds(pl.multiple_of(256 * n, 256), 256)
            wig_v[:, cols] = dot(rest_v[:NX, :], nrm_v[:, cols]).astype(BF)

        for k in range(1, DEPTH):
            down(1, k).start()
        bcd_pair().wait_recv()
        bcd_v[half(core), :] = (bcd_v[half(core), :].astype(F32) + bcd_in[...].astype(F32)).astype(BF)
        for k in range(1, DEPTH):
            down(2, k).start()
        relay(0)
        ag_turn(0)
        for k in range(1, DEPTH):
            down(3, k).wait_recv()
        gw_v[0:HEADDIM, :] = reduce_z(wog_v[piece(z), :], [zw_in[k - 1, 0:HEADDIM] for k in range(1, DEPTH)]).astype(BF)
        ag_start(2)

        @pl.when(extra(z))
        def _():
            for k in range(1, DEPTH):
                down(4, k).wait_recv()
            gw_v[HEADDIM:, :] = reduce_z(
                wog_v[piece(DEPTH + lax.div(z, 2)), :], [zw_in[k - 1, HEADDIM:] for k in range(1, DEPTH)]).astype(BF)
            ag_start(3)

        for k in range(1, DEPTH):
            down(5, k).wait_recv()
        small_s[...] = reduce_z(small_v[...], [zs_in[k - 1] for k in range(1, DEPTH)])
        ag_start(4)
        ag_end(0)
        total = rs_total(1)
        uf = tok_v[...].astype(F32)
        along = total * norm_gain(par_ref[...])
        s1 = lax.rsqrt(jnp.mean(uf * uf, axis=1, keepdims=True) + EPSILON)
        tg_ref[...] = cot_v[...].astype(F32) + s1 * along - uf * (
            s1 * s1 * s1 * jnp.mean(along * uf, axis=1, keepdims=True))
        ag_turn(2)

        @pl.when(extra(z))
        def _():
            ag_turn(3)

        ag_turn(4)
        for k in range(1, DEPTH):
            down(1, k).wait_recv()
        gx_v[...] = reduce_z(wig_v[:, lanes(z)], [zx_in[k - 1] for k in range(1, DEPTH)]).astype(BF)
        ag_start(1)
        for k in range(1, DEPTH):
            down(2, k).wait_recv()
        gb_v[...] = reduce_z(bcd_v[half(core), lanes(z)], [zb_in[k - 1] for k in range(1, DEPTH)]).astype(BF)
        for k in range(1, CHIPS):
            bcd_push(k).start()
        ag_end(2)

        @pl.when(extra(z))
        def _():
            ag_end(3)

        ag_end(4)
        ag_turn(1)
        for k in range(1, CHIPS):
            bcd_push(k).wait_recv()
        total = gb_v[...].astype(F32)
        for k in range(1, CHIPS):
            total = total + gb_in[k - 1].astype(F32)
        gt_v[core] = total.astype(BF)
        bcd_back().start()
        ag_end(1)
        bcd_back().wait()
        last = [
            pltpu.make_async_copy(gt_v.at[0], wig_ref.at[pl.ds(2 * DI, HALF)], loc.at[15]),
            pltpu.make_async_copy(gt_v.at[1, 0 : WIDTH - 2 * DI - HALF],
                                  wig_ref.at[pl.ds(2 * DI + HALF, WIDTH - 2 * DI - HALF)], loc.at[16])]
        for copy in last:
            copy.start()
        for n in (0, 1, 2, 4):
            ag_close(n)

        @pl.when(extra(z))
        def _():
            ag_close(3, receives=False)

        @pl.when(jnp.logical_not(extra(z)))
        def _():
            ag_close(3, sends=False)

        for c in range(CHIPS):
            br_pair(c).wait_send()
            dn_pair(c).wait_send()
        for n in range(2):
            for kind in range(6):
                rs(n, kind).wait_send()
        for k in range(1, CHIPS):
            bcd_push(k).wait_send()
        for k in range(1, DEPTH):
            for n in (1, 2, 3, 5):
                down(n, k).wait_send()

            @pl.when(extra(z + k))
            def _():
                down(4, k).wait_send()

        bcd_pair().wait_send()
        for copy in last:
            copy.wait()


def backward_call(tok, cot, nrm, br, w, g, projz, ssd, dno, stat, par, projc, st, info, idr):
    n = nrm.shape[0]
    any_space = pl.BlockSpec(memory_space=pl.ANY)
    sds = jax.ShapeDtypeStruct
    dma = pltpu.SemaphoreType.DMA
    one = lambda i: jnp.minimum(i, TEAM - 1)
    two = lambda i: jnp.clip(2 * TEAM - i, 0, TEAM - 1)
    rows = lambda c, turn: pl.BlockSpec((BLK, c), lambda i: (turn(i), 0))
    cube = lambda a, b: pl.BlockSpec((1, a, b), lambda i: (two(i), 0, 0))
    fixed = lambda a, b: pl.BlockSpec((a, b), lambda i: (0, 0), pipeline_mode=pl.Buffered(1))
    vm = pltpu.VMEM
    return pl.pallas_call(
        backward_kernel,
        grid=(2 * TEAM + 2,),
        in_specs=[any_space] * 6 + [
            rows(NZ, one), rows(CH, one), rows(CH, one), fixed(TEAM, 2 * BLK), fixed(16, CONVC), rows(REST, two),
            pl.BlockSpec((16, REST), lambda i: (jnp.maximum(16 * two(i) - 1, 0), 0)),
            cube(STATE, CH), rows(128, two), cube(8, BLK)],
        out_specs=[fixed(BLK, D), fixed(BLK, D), any_space, any_space, any_space],
        out_shape=[sds((BLK, D), BF), sds((BLK, D), F32), sds((WIDTH, KROWS), BF),
                   sds((DI // DEPTH, D), BF), sds((TEAM, 16, CONVC), F32)],
        scratch_shapes=[
            vm((n, D), BF), vm((n, D), BF), vm((COLS, D), BF), vm((CH, n), BF), vm((n, CH), BF), vm((CH, n), BF),
            vm((n, CH), F32), vm((REST, n), BF), vm((CH, D), BF), vm((CH, D), BF), vm((BCD, D), BF),
            vm((HALF, D), BF),
            vm((DEPTH - 1, CH, KROWS), BF), vm((DEPTH - 1, CH, KROWS), BF), vm((DEPTH - 1, HALF, KROWS), BF),
            vm((DEPTH - 1, 2 * HEADDIM, D), BF), vm((DEPTH - 1, 16, CONVC), F32), vm((CH, KROWS), BF), vm((CH, KROWS), BF),
            vm((HALF, KROWS), BF), vm((2 * HEADDIM, D), BF), vm((CHIPS - 1, HALF, KROWS), BF), vm((2, HALF, KROWS), BF),
            vm((CHIPS, BLK, D), BF), vm((CHIPS, BLK, D), BF), vm((2, 2, BLK, D), BF), vm((2, 2, BLK // 2, D), BF),
            vm((BLK, D), BF), vm((BLK, D), BF), vm((16, CONVC), F32), vm((16, CONVC), F32),
            vm((BLK + 8, CONVC), F32), vm((BLK + 8, CONVC), F32), vm((STATE, CH), F32),
            dma((17,)), dma((CHIPS,)), dma((CHIPS,)), dma((2, 6)), dma((2, 6)), dma((CHIPS,)), dma((CHIPS,)),
            dma((CHIPS,)), dma((CHIPS,)), dma((6, DEPTH)), dma((6, DEPTH)),
            dma((5, 5)), dma((5, 5)), dma((5, 5)), dma((5, 5)), dma((2,)), dma((2,)),
            pltpu.SemaphoreType.REGULAR],
        compiler_params=pltpu.CompilerParams(
            collective_id=1, has_side_effects=True, vmem_limit_bytes=63 << 20),
    )(tok, cot, nrm, br, w, g, projz, ssd, dno, stat, par, projc, projc, st, info, idr)


def on_team(
    tokens, segment_ids, cotangent, w_in, w_out, conv_w, conv_b, a_log, dt_bias, d_skip,
    norm_w, gate_w,
):
    place = lax.axis_index("seq")
    chip, core = place // 2, place % 2
    depth = lax.axis_index("fsdp")
    shards = DEPTH
    n = tokens.shape[1] * TEAM
    w_t = w_in.T
    bcd = jnp.pad(w_t[2 * DI :], ((0, BCD - (WIDTH - 2 * DI)), (0, 0)))

    def put(a, whole_size):
        return lax.dynamic_update_slice_in_dim(
            jnp.zeros(a.shape[:-1] + (whole_size,), BF), a, depth * a.shape[-1], a.ndim - 1)

    def own_part(a):
        a = a.reshape(a.shape[0], 4, 12, HEADDIM)
        a = lax.dynamic_slice_in_dim(a, 3 * chip, 3, 2)
        first = lax.dynamic_index_in_dim(a, 2 * core, 2, keepdims=False)
        second = a[:, :, 1].reshape(-1, 2, 2, HEADDIM)
        second = lax.dynamic_index_in_dim(second, core, 2, keepdims=False)
        return jnp.concatenate([first, second], axis=1).reshape(a.shape[0], CH)

    wide = lambda a, size: jnp.pad(a, (0, size - a.shape[0]))
    conv_rows = put(jnp.concatenate([conv_w, conv_b[None]], axis=0), CHAN)
    chan_rows = own_part(jnp.concatenate(
        [conv_rows[:, :DI], put(gate_w, DI)[None], jnp.repeat(put(d_skip, HEADS), HEADDIM)[None]], axis=0))
    heads_row = jnp.concatenate([wide(put(dt_bias, HEADS), 128), wide(put(a_log, HEADS), 128)])
    side = jnp.concatenate([conv_rows[:, DI:], heads_row[None], jnp.zeros((1, NB), BF)], axis=0)
    gain_rows = jnp.pad(put(norm_w, D).reshape(3, D // 3), ((0, 0), (0, CONVC - D // 3)))
    small = jnp.concatenate(
        [jnp.concatenate([chan_rows, side], axis=1), gain_rows, jnp.zeros((6, CONVC), BF)], axis=0)
    tok, idr = token_info(segment_ids[0], 0, n)
    u_own, g_own = tokens[0], cotangent[0]
    nrm, projc, projz, st, ssd, dno, br, stat, par, w_loc, g = forward_call(
        u_own, g_own, w_t, bcd, w_out, small, tok, idr)
    layer_out, token_grad, wig, wog, smalls = backward_call(
        u_own, g_own, nrm, br, w_loc, g, projz, ssd, dno, stat, par, projc, st, tok, idr)
    w_in_grad = wig.astype(F32).T
    w_out_grad = wog.astype(F32)
    parts = smalls[:, :7, :CH].reshape(CHIPS, 2, 7, HPD, HEADDIM)
    first = parts[:, :, :, :4].transpose(1, 2, 3, 0, 4)
    second = parts[:, :, :, 4:].transpose(2, 3, 1, 0, 4).reshape(7, 4, CHIPS, HEADDIM)
    chang = jnp.stack([first[0], second, first[1]], axis=3).reshape(7, DI)
    sideg = jnp.sum(smalls[:, :6, CH:], axis=0)
    normg = jnp.sum(smalls[:, 7:10, :512], axis=0).reshape(D)
    convg = jnp.concatenate([chang[:5], sideg[:5]], axis=1)
    mine = lambda a: lax.dynamic_slice_in_dim(a, depth * (a.shape[-1] // shards), a.shape[-1] // shards, a.ndim - 1)
    convg = mine(convg)
    skipg = jnp.sum(chang[6].reshape(HEADS, HEADDIM), axis=1)
    return (layer_out[None], token_grad[None], w_in_grad, w_out_grad, convg[:4], convg[4],
            mine(sideg[5, :HEADS]), mine(sideg[5, 128 : 128 + HEADS]), mine(skipg), mine(normg), mine(chang[5]))


def solution(mesh):
    body = on_team if (mesh.shape["seq"], mesh.shape["fsdp"]) == (TEAM, DEPTH) else on_device
    return jax.shard_map(
        body,
        mesh=mesh,
        in_specs=(
            P("fsdp", "seq", None),
            P("fsdp", None),
            P("fsdp", "seq", None),
            P("fsdp", None),
            P("fsdp", None),
            P(None, "fsdp"),
            P("fsdp"),
            P("fsdp"),
            P("fsdp"),
            P("fsdp"),
            P("fsdp"),
            P("fsdp"),
        ),
        out_specs=(
            P("fsdp", "seq", None),
            P("fsdp", "seq", None),
            P("fsdp", None),
            P("fsdp", None),
            P(None, "fsdp"),
            P("fsdp"),
            P("fsdp"),
            P("fsdp"),
            P("fsdp"),
            P("fsdp"),
            P("fsdp"),
        ),
        check_vma=False,
    )
```

```python
import jax
import jax.numpy as jnp
from jax import lax
from jax.experimental import pallas as pl
from jax.experimental.pallas import tpu as pltpu
from jax.sharding import PartitionSpec as P

DI = 3072
HEADDIM = 64
STATE = 128
CONV = 4
SPAN = 256
HEADS = 48
D = 1536
WIDTH = 6448
DEPTH = 4
CHAN = 3328


EPSILON = 1e-05
HIGHEST = lax.Precision.HIGHEST


def passed_along(value, axis, steps):
    count = lax.axis_size(axis)
    first, last = (max(0, -steps), min(count, count - steps))
    return lax.ppermute(value, axis, [(source, source + steps) for source in range(first, last)])


def shortened(array):

    def short(part):
        return part.astype(jnp.bfloat16) if part.dtype == jnp.float32 else part

    return jax.tree.map(short, array)


def block_masks(ids_blocks, before_ids):
    block_len = ids_blocks.shape[1]
    places = jnp.arange(block_len)
    causal_mask = (places[:, None] >= places[None, :])[None] & (
        ids_blocks[:, :, None] == ids_blocks[:, None, :]
    )
    keep_flag = (ids_blocks == before_ids[:, None]).astype(jnp.float32)
    same_last = (ids_blocks == ids_blocks[:, -1:]).astype(jnp.float32)
    return (causal_mask, keep_flag, same_last)


def local_states(x_heads, b_rows, step_size, log_decay, same_last, keep_flag):
    cum_decay = jnp.cumsum(log_decay, axis=1)
    last_cum = cum_decay[:, -1]
    weights = jnp.exp(last_cum[:, None, :] - cum_decay) * step_size * same_last[:, :, None]
    fresh_state = jnp.einsum("csh,cshp,csn->chpn", weights, x_heads, b_rows, precision=HIGHEST)
    passing = keep_flag[:, -1:] * jnp.exp(last_cum)
    total_state = jnp.zeros_like(fresh_state[0])
    total_decay = jnp.ones_like(passing[0])
    total_state = fresh_state[0] + passing[0][:, None, None] * total_state
    total_decay = total_decay * passing[0]
    return (fresh_state, passing, total_state, total_decay)


def local_output(x_heads, b_rows, c_rows, step_size, log_decay, incoming, causal_mask, keep_flag):
    cum_decay = jnp.cumsum(log_decay, axis=1)
    cum_heads = jnp.swapaxes(cum_decay, 1, 2)
    gap_decay = cum_heads[:, :, :, None] - cum_heads[:, :, None, :]
    head_mask = causal_mask[:, None]
    decay_map = jnp.exp(jnp.where(head_mask, gap_decay, 0.0)) * head_mask.astype(jnp.float32)
    scores = jnp.einsum("ctn,csn->cts", c_rows, b_rows, precision=HIGHEST)
    mixing = scores[:, None] * decay_map * jnp.swapaxes(step_size, 1, 2)[:, :, None, :]
    inner_out = jnp.einsum("chts,cshp->cthp", mixing, x_heads, precision=HIGHEST)
    starts = [incoming]
    start_states = jnp.stack(starts)
    carried = jnp.einsum("ctn,chpn->cthp", c_rows, start_states, precision=HIGHEST)
    carried = carried * (keep_flag[:, :, None] * jnp.exp(cum_decay))[..., None]
    return inner_out + carried


def on_device(
    tokens,
    segment_ids,
    cotangent,
    w_in,
    w_out,
    conv_w,
    conv_b,
    a_log,
    dt_bias,
    d_skip,
    norm_w,
    gate_w,
):
    gathered = (
        lax.all_gather(w_in, "fsdp", axis=0, tiled=True),
        lax.all_gather(w_out, "fsdp", axis=0, tiled=True),
        lax.all_gather(conv_w, "fsdp", axis=1, tiled=True),
        lax.all_gather(conv_b, "fsdp", axis=0, tiled=True),
        lax.all_gather(a_log, "fsdp", axis=0, tiled=True),
        lax.all_gather(dt_bias, "fsdp", axis=0, tiled=True),
        lax.all_gather(d_skip, "fsdp", axis=0, tiled=True),
        lax.all_gather(norm_w, "fsdp", axis=0, tiled=True),
        lax.all_gather(gate_w, "fsdp", axis=0, tiled=True),
    )
    (
        w_in_full,
        w_out_full,
        conv_full,
        bias_full,
        a_log_full,
        dt_bias_full,
        skip_full,
        norm_full,
        gate_full,
    ) = gathered
    inputs = tokens[0].astype(jnp.float32)
    length = inputs.shape[0]
    norm_gain = norm_full.astype(jnp.float32)
    scale_in = lax.rsqrt(jnp.mean(inputs * inputs, axis=-1, keepdims=True) + EPSILON)
    normed = (inputs * scale_in * norm_gain).astype(jnp.bfloat16)
    projected = jnp.dot(normed, w_in_full, preferred_element_type=jnp.float32).astype(jnp.bfloat16)
    gate_z = projected[:, :DI].astype(jnp.float32)
    conv_in = projected[:, DI : DI + CHAN]
    dt_raw = projected[:, DI + CHAN :].astype(jnp.float32)
    first_row = lax.axis_index("seq") * length
    id_row = jnp.concatenate([jnp.full((CONV - 1,), -1, jnp.int32), segment_ids[0]], axis=0)
    ids_pad = lax.dynamic_slice_in_dim(id_row, first_row, length + CONV - 1)
    ids_own = ids_pad[CONV - 1 :]
    left_edge = passed_along(conv_in[length - (CONV - 1) :], "seq", 1)
    padded = jnp.concatenate([left_edge, conv_in], axis=0).astype(jnp.float32)
    kernel = conv_full.astype(jnp.float32)
    conv_out = jnp.zeros((length, CHAN), jnp.float32) + bias_full.astype(jnp.float32)
    same_docs = []
    for offset in range(CONV):
        same_doc = (ids_pad[offset : offset + length] == ids_own).astype(jnp.float32)
        same_docs.append(same_doc)
        conv_out = conv_out + kernel[offset] * padded[offset : offset + length] * same_doc[:, None]
    activated = jax.nn.silu(conv_out)
    blocks = length // SPAN
    x_heads = activated[:, :DI].reshape(blocks, SPAN, HEADS, HEADDIM)
    b_rows = activated[:, DI : DI + STATE].reshape(blocks, SPAN, STATE)
    c_rows = activated[:, DI + STATE :].reshape(blocks, SPAN, STATE)
    dt_bias_f = dt_bias_full.astype(jnp.float32)
    decay_rate = jnp.exp(a_log_full.astype(jnp.float32))
    step_flat = jax.nn.softplus(dt_raw + dt_bias_f)
    step_size = step_flat.reshape(blocks, SPAN, HEADS)
    log_decay = (-step_flat * decay_rate).reshape(blocks, SPAN, HEADS)
    ids_blocks = ids_own.reshape(blocks, SPAN)
    before_ids = ids_pad[CONV - 2 : CONV - 2 + length : SPAN]
    causal_mask, keep_flag, same_last = block_masks(ids_blocks, before_ids)

    def state_part(heads_in, rows_b, steps_in, decay_in):
        return local_states(heads_in, rows_b, steps_in, decay_in, same_last, keep_flag)

    (fresh_state, passing, total_state, total_decay), state_pull = jax.vjp(
        state_part, x_heads, b_rows, step_size, log_decay
    )

    def pass_forward(turn_index, received):
        return passed_along(
            (total_state + total_decay[:, None, None] * received).astype(jnp.bfloat16), "seq", 1
        ).astype(jnp.float32)

    incoming = lax.fori_loop(0, lax.axis_size("seq") - 1, pass_forward, jnp.zeros_like(total_state))

    def output_part(
        heads_in, rows_b, rows_c, steps_in, decay_in, fresh_in, passing_in, incoming_in
    ):
        return local_output(
            heads_in, rows_b, rows_c, steps_in, decay_in, incoming_in, causal_mask, keep_flag
        )

    ssd_out, output_pull = jax.vjp(
        output_part, x_heads, b_rows, c_rows, step_size, log_decay, fresh_state, passing, incoming
    )
    skip_heads = skip_full.astype(jnp.float32)
    y_full = (ssd_out + skip_heads[:, None] * x_heads).reshape(length, DI)
    silu_z = jax.nn.silu(gate_z)
    gated = y_full * silu_z
    scale_out = lax.rsqrt(jnp.mean(gated * gated, axis=-1, keepdims=True) + EPSILON)
    gate_gain = gate_full.astype(jnp.float32)
    normed_out = (gated * scale_out * gate_gain).astype(jnp.bfloat16)
    branch = jnp.dot(normed_out, w_out_full, preferred_element_type=jnp.float32)
    layer_out = (inputs + branch).astype(jnp.bfloat16)[None]
    grad_out = cotangent[0]
    d_w_out = lax.dot_general(
        normed_out, grad_out, (((0,), (0,)), ((), ())), preferred_element_type=jnp.float32
    )
    d_normed_out = lax.dot_general(
        grad_out, w_out_full, (((1,), (1,)), ((), ())), preferred_element_type=jnp.float32
    )
    d_gate_w = jnp.sum(d_normed_out * gated * scale_out, axis=0)
    along_out = d_normed_out * gate_gain
    cube_out = scale_out * scale_out * scale_out
    d_gated = scale_out * along_out - gated * cube_out * jnp.mean(
        along_out * gated, axis=-1, keepdims=True
    )
    d_y = d_gated * silu_z
    sig_z = jax.nn.sigmoid(gate_z)
    d_gate_z = d_gated * y_full * sig_z * (1.0 + gate_z * (1.0 - sig_z))
    d_ssd = d_y.reshape(blocks, SPAN, HEADS, HEADDIM)
    d_skip_grad = jnp.sum(d_ssd * x_heads, axis=(0, 1, 3))
    dx_out, db_out, dc_out, dstep_out, ddecay_out, d_fresh, d_passing, d_incoming = output_pull(
        d_ssd
    )

    def pass_backward(turn_index, received):
        return passed_along(d_incoming + total_decay[:, None, None] * received, "seq", -1)

    d_total = lax.fori_loop(0, lax.axis_size("seq") - 1, pass_backward, jnp.zeros_like(d_incoming))
    d_total_decay = jnp.sum(d_total * incoming, axis=(1, 2))
    dx_state, db_state, dstep_state, ddecay_state = state_pull(
        (d_fresh, d_passing, d_total, d_total_decay)
    )
    d_x = dx_out + dx_state + skip_heads[:, None] * d_ssd
    d_b = db_out + db_state
    d_log = (ddecay_out + ddecay_state).reshape(length, HEADS)
    d_step = (dstep_out + dstep_state).reshape(length, HEADS) - d_log * decay_rate
    d_a_log = -jnp.sum(d_log * step_flat, axis=0) * decay_rate
    d_dt_raw = d_step * jax.nn.sigmoid(dt_raw + dt_bias_f)
    d_dt_bias = jnp.sum(d_dt_raw, axis=0)
    d_act = jnp.concatenate(
        [d_x.reshape(length, DI), d_b.reshape(length, STATE), dc_out.reshape(length, STATE)], axis=1
    )
    sig_conv = jax.nn.sigmoid(conv_out)
    d_conv = d_act * sig_conv * (1.0 + conv_out * (1.0 - sig_conv))
    d_conv_b = jnp.sum(d_conv, axis=0)
    kernel_rows = []
    d_padded = jnp.zeros((length + CONV - 1, CHAN), jnp.float32)
    for offset in range(CONV):
        masked = d_conv * same_docs[offset][:, None]
        kernel_rows.append(jnp.sum(masked * padded[offset : offset + length], axis=0))
        d_padded = d_padded + jnp.pad(
            kernel[offset] * masked, ((offset, CONV - 1 - offset), (0, 0))
        )
    d_kernel = jnp.stack(kernel_rows)
    d_edge = passed_along(shortened(d_padded[: CONV - 1]), "seq", -1)
    d_conv_in = d_padded[CONV - 1 :] + jnp.pad(d_edge, ((length - (CONV - 1), 0), (0, 0)))
    d_projected = jnp.concatenate([d_gate_z, d_conv_in, d_dt_raw], axis=1).astype(jnp.bfloat16)
    d_normed = lax.dot_general(
        d_projected, w_in_full, (((1,), (1,)), ((), ())), preferred_element_type=jnp.float32
    )
    d_norm_w = jnp.sum(d_normed * inputs * scale_in, axis=0)
    along_in = d_normed * norm_gain
    cube_in = scale_in * scale_in * scale_in
    d_inputs = (
        scale_in * along_in
        - inputs * cube_in * jnp.mean(along_in * inputs, axis=-1, keepdims=True)
        + grad_out.astype(jnp.float32)
    )
    d_w_in = lax.dot_general(
        normed, d_projected, (((0,), (0,)), ((), ())), preferred_element_type=jnp.float32
    )
    weight_grads = (
        d_w_in,
        d_w_out,
        d_kernel,
        d_conv_b,
        d_a_log,
        d_dt_bias,
        d_skip_grad,
        d_norm_w,
        d_gate_w,
    )
    shares = tuple(
        (
            lax.psum_scatter(weight_grads[0], "fsdp", scatter_dimension=0, tiled=True),
            lax.psum_scatter(weight_grads[1], "fsdp", scatter_dimension=0, tiled=True),
            lax.psum_scatter(weight_grads[2], "fsdp", scatter_dimension=1, tiled=True),
            lax.psum_scatter(weight_grads[3], "fsdp", scatter_dimension=0, tiled=True),
            lax.psum_scatter(weight_grads[4], "fsdp", scatter_dimension=0, tiled=True),
            lax.psum_scatter(weight_grads[5], "fsdp", scatter_dimension=0, tiled=True),
            lax.psum_scatter(weight_grads[6], "fsdp", scatter_dimension=0, tiled=True),
            lax.psum_scatter(weight_grads[7], "fsdp", scatter_dimension=0, tiled=True),
            lax.psum_scatter(weight_grads[8], "fsdp", scatter_dimension=0, tiled=True),
        )
    )
    totals = lax.psum(shares, "seq")
    return (layer_out, d_inputs[None]) + tuple(totals)


F32 = jnp.float32
BF = jnp.bfloat16
BLK = 256
TEAM = 8
HPD = HEADS // TEAM
CH = HPD * HEADDIM
NZ, NX, NB, ND = CH, CH, 2 * STATE, 64
COLS = NZ + NX + NB + ND
REST = NX + NB + ND
CONVC = NX + NB
TAIL = CONV - 1


def dot(a, b):
    return lax.dot_general(a, b, (((1,), (0,)), ((), ())), preferred_element_type=F32)


def dot_nt(a, b):
    return lax.dot_general(a, b, (((1,), (1,)), ((), ())), preferred_element_type=F32)


def dot_tn(a, b):
    return lax.dot_general(a, b, (((0,), (0,)), ((), ())), preferred_element_type=F32)


def dot_exact(a, b):
    return lax.dot_general(
        a, b, (((1,), (0,)), ((), ())), precision=HIGHEST, preferred_element_type=F32
    )


def iota(shape, dim):
    return lax.broadcasted_iota(jnp.int32, shape, dim)


def split_dot(a, b):
    high = a.astype(BF)
    low = (a - high.astype(F32)).astype(BF)
    return dot(high, b) + dot(low, b)


def spread():
    return (iota((128, CH), 1) // HEADDIM == iota((128, CH), 0)).astype(BF)


def gather_heads():
    return (iota((CH, 128), 0) // HEADDIM == iota((CH, 128), 1)).astype(BF)


def lower_tri():
    return (iota((BLK, BLK), 0) >= iota((BLK, BLK), 1)).astype(F32)


def softplus(v):
    return jnp.maximum(v, 0.0) + jnp.log1p(jnp.exp(-jnp.abs(v)))


def sigmoid(v):
    return 1.0 / (1.0 + jnp.exp(-v))


def conv_taps(cbuf, cw, tok):
    out = cw[CONV : CONV + 1, :] + cw[CONV - 1 : CONV, :] * cbuf[8 : 8 + BLK, :]
    for back in range(1, CONV):
        term = cw[CONV - 1 - back : CONV - back, :] * cbuf[8 - back : 8 - back + BLK, :]
        out = out + term * tok[:, back : back + 1]
    return out


def pair_select(left, right):
    return jnp.where(iota(left.shape, 1) % 128 < HEADDIM, left, right)


def head_of(slot, chip, core):
    first = 12 * slot + 3 * chip + 2 * core
    second = 12 * (core + 2 * (slot - 4)) + 3 * chip + 1
    return first, second


def pick_heads():
    seq = lax.axis_index("seq")
    chip, core = lax.div(seq, 2), lax.rem(seq, 2)
    slot = iota((128, 128), 1)
    first, second = head_of(slot, chip, core)
    head = jnp.where(slot < 4, first, jnp.where(slot < HPD, second, -1))
    return (iota((128, 128), 0) == head).astype(BF)


def own_heads(par, dt_cols):
    pick = pick_heads()
    pair = jnp.concatenate([par[5:6, CH : CH + 128], par[5:6, CH + 128 :], jnp.zeros((6, 128), F32)], axis=0)
    pair = dot(pair.astype(BF), pick)
    wide = jnp.concatenate([dt_cols, jnp.zeros((BLK, 128 - ND), BF)], axis=1)
    return jnp.exp(pair[1:2, :]), dot(wide, pick) + pair[0:1, :], iota((BLK, 128), 1) < HPD, pick


def norm_gain(par):
    return jnp.concatenate([par[7 + i : 8 + i, :CH] for i in range(D // CH)], axis=1)


def row_sum(q):
    high = q.astype(BF)
    low = (q - high.astype(F32)).astype(BF)
    ones = jnp.ones((8, q.shape[1]), BF)
    return (dot_nt(ones, high) + dot_nt(ones, low))[0:1, :]


def scan_forward(j, nrm, w_v, par, tok, idr, cbuf, state, projc_ref, st_ref, ssd_v):
    rows = pl.ds(pl.multiple_of(BLK * j, BLK), BLK)
    proj = dot_nt(nrm, w_v[NZ:, :]).astype(BF)
    projc_ref[...] = proj
    cbuf[8 : 8 + BLK, :] = proj[:, :CONVC].astype(F32)
    conv_out = conv_taps(cbuf, par, tok)
    cbuf[0:8, :] = cbuf[BLK : BLK + 8, :]
    act = conv_out * sigmoid(conv_out)
    x = act[:, :CH]
    bm = act[:, CH : CH + STATE].astype(BF)
    cm = act[:, CH + STATE :].astype(BF)
    rate, dt_in, own, pick = own_heads(par, proj[:, CONVC:])
    step = jnp.where(own, softplus(dt_in), 0.0)
    cum = dot_exact(lower_tri(), -step * rate)
    cum_t = cum.T
    mask = (iota((BLK, BLK), 0) >= iota((BLK, BLK), 1)) & (tok[:, 0:1] == idr)
    gm = jnp.where(mask, dot_nt(cm, bm), 0.0)
    ex = spread()
    xs = (x * split_dot(step, ex)).astype(BF)
    parts = []
    for pair in range(HPD // 2):
        xp = xs[:, 128 * pair : 128 * pair + 128]
        both = []
        for h in (2 * pair, 2 * pair + 1):
            decay = jnp.exp(jnp.minimum(cum[:, h : h + 1] - cum_t[h : h + 1, :], 0.0))
            both.append(dot((gm * decay).astype(BF), xp))
        parts.append(pair_select(*both))
    inner = jnp.concatenate(parts, axis=1)
    old = state[...]
    st_ref[0] = old
    keep = tok[:, 7:8]
    carried = split_dot(keep * jnp.exp(cum), ex) * dot(cm, old.astype(BF))
    last = cum[BLK - 1 : BLK, :]
    weights = jnp.exp(last - cum) * step * tok[:, 8:9]
    through = split_dot(jnp.broadcast_to(keep[BLK - 1 :, :] * jnp.exp(last), (8, 128)), ex)[0:1, :]
    state[...] = dot_tn(bm, (x * split_dot(weights, ex)).astype(BF)) + through * old
    ssd_v[rows, :] = inner + carried + par[6:7, :CH] * x


def gate_forward(j, nrm_v, g_v, w_v, wo_v, par, ssd_v, projz_ref, ssd_ref, dno_ref, br_ref, stat_v):
    rows = pl.ds(pl.multiple_of(BLK * j, BLK), BLK)
    projz = dot_nt(nrm_v[rows, :], w_v[:NZ, :]).astype(BF)
    projz_ref[...] = projz
    ssd = ssd_v[rows, :]
    ssd_ref[...] = ssd
    z = projz.astype(F32)
    gate_w = par[5:6, :CH]
    gated = ssd * (z * sigmoid(z))
    br_ref[...] = dot((gated * gate_w).astype(BF), wo_v[...]).astype(BF)
    dno = dot_nt(g_v[rows, :], wo_v[...])
    dno_ref[...] = dno
    stat_v[pl.ds(j, 1), 0:BLK] = row_sum(gated * gated)
    stat_v[pl.ds(j, 1), BLK : 2 * BLK] = row_sum(dno * gate_w * gated)


def gate_backward(j, z, ssd, dno, stat, gate_w, not_v, dy_v, dz_v, dzt_v, small_v):
    rows = pl.ds(pl.multiple_of(BLK * j, BLK), BLK)
    sig_z = sigmoid(z)
    silu_z = z * sig_z
    stat = jnp.where(iota((128, BLK), 0) == 0, stat[:, :BLK], stat[:, BLK:]).T
    s2 = lax.rsqrt(stat[:, 0:1] * (1.0 / DI) + EPSILON)
    mean_ag = stat[:, 1:2] * (1.0 / DI)
    gated = ssd * silu_z
    gs = gated * s2
    not_v[:, rows] = (gs * gate_w).T.astype(BF)
    d_gated = s2 * (dno * gate_w) - gated * (s2 * s2 * s2 * mean_ag)
    dy_v[rows, :] = d_gated * silu_z
    dz = d_gated * ssd * sig_z * (1.0 + z * (1.0 - sig_z))
    dz_v[rows, :] = dz.astype(BF)
    dzt_v[:, rows] = dz.T.astype(BF)
    small_v[5:6, :CH] += jnp.sum(dno * gs, axis=0, keepdims=True)


def scan_backward(proj, halo, tok, idr, old, par, dy, cbuf, dcbuf, dstate, small_v):
    cbuf[0:8, :] = halo[8:16, :CONVC].astype(F32)
    cbuf[8 : 8 + BLK, :] = proj[:, :CONVC].astype(F32)
    conv_out = conv_taps(cbuf, par, tok)
    sig_c = sigmoid(conv_out)
    act = conv_out * sig_c
    x = act[:, :CH]
    bm = act[:, CH : CH + STATE].astype(BF)
    cm_f = act[:, CH + STATE :]
    cm = cm_f.astype(BF)
    rate, dt_in, own, pick = own_heads(par, proj[:, CONVC:])
    step = jnp.where(own, softplus(dt_in), 0.0)
    cum = dot_exact(lower_tri(), -step * rate)
    cum_t = cum.T
    mask = (iota((BLK, BLK), 0) >= iota((BLK, BLK), 1)) & (tok[:, 0:1] == idr)
    gm = jnp.where(mask, dot_nt(cm, bm), 0.0)
    ex = spread()
    gh = gather_heads()
    step_x = split_dot(step, ex)
    xs = (x * step_x).astype(BF)
    dyb = dy.astype(BF)
    dyt = dy.T.astype(BF)
    lane = iota((BLK, 128), 1)
    dg = jnp.zeros((BLK, BLK), F32)
    row_sums = jnp.zeros((BLK, 128), F32)
    col_sums = []
    e_rows = []
    for h in range(HPD):
        pair = h // 2
        decay = jnp.exp(jnp.minimum(cum[:, h : h + 1] - cum_t[h : h + 1, :], 0.0))
        mixed = gm * decay
        half = jnp.where((lane < HEADDIM) == (h % 2 == 0), dyb[:, 128 * pair : 128 * pair + 128], 0)
        dms = dot_nt(half.astype(BF), xs[:, 128 * pair : 128 * pair + 128])
        product = dms * mixed
        row_sums = jnp.where(lane == h, jnp.sum(product, axis=1, keepdims=True), row_sums)
        col_sums.append(jnp.sum(product, axis=0, keepdims=True))
        dg = dg + dms * decay
        e_rows.append(dot(dyt[HEADDIM * h : HEADDIM * h + HEADDIM, :], mixed.astype(BF)))
    dg = jnp.where(mask, dg, 0.0).astype(BF)
    e = jnp.concatenate(e_rows, axis=0).T
    col_sums.append(jnp.zeros((128 - HPD, BLK), F32))
    col = jnp.concatenate(col_sums, axis=0).T
    keep = tok[:, 7:8]
    old_b = old.astype(BF)
    dnew = dstate[...]
    dnew_b = dnew.astype(BF)
    carry_x = split_dot(keep * jnp.exp(cum), ex)
    dyk_f = dy * carry_x
    dyk = dyk_f.astype(BF)
    carried = dot(cm, old_b)
    last = cum[BLK - 1 : BLK, :]
    fade = jnp.exp(last - cum) * tok[:, 8:9]
    weights = fade * step
    weights_x = split_dot(weights, ex)
    zt = dot(bm, dnew_b)
    xw = (x * weights_x).astype(BF)
    through = keep[BLK - 1 :, :] * jnp.exp(last)
    through_x = split_dot(jnp.broadcast_to(through, (8, 128)), ex)[0:1, :]
    k_term = split_dot(dyk_f * carried, gh)
    r_term = split_dot(x * zt, gh)
    q_term = split_dot(x * e, gh)
    pass_term = jnp.sum(old * dnew, axis=0, keepdims=True) * through_x
    pass_h = split_dot(jnp.broadcast_to(pass_term, (8, CH)), gh)[0:1, :]
    wr = weights * r_term
    d_cum = row_sums - col + k_term - wr
    d_last = jnp.sum(wr, axis=0, keepdims=True) + pass_h
    d_cum = d_cum + jnp.where(iota((BLK, 128), 0) == BLK - 1, d_last, 0.0)
    upper = (iota((BLK, BLK), 0) <= iota((BLK, BLK), 1)).astype(F32)
    d_log = dot_exact(upper, d_cum)
    d_step = q_term + fade * r_term - d_log * rate
    d_a = -jnp.sum(d_log * step, axis=0, keepdims=True) * rate
    d_dt = jnp.where(own, d_step * sigmoid(dt_in), 0.0)
    d_skip = split_dot(jnp.broadcast_to(jnp.sum(dy * x, axis=0, keepdims=True), (8, CH)), gh)[0:1, :]
    d_skip = jnp.where(own[0:1, :], d_skip, 0.0)
    heads = jnp.concatenate(
        [d_a, jnp.sum(d_dt, axis=0, keepdims=True), d_skip, jnp.zeros((5, 128), F32)], axis=0)
    high = heads.astype(BF)
    heads = dot_nt(high, pick) + dot_nt((heads - high.astype(F32)).astype(BF), pick)
    d_dt = dot_nt(d_dt.astype(BF), pick)
    dstate[...] = dot_tn(cm, dyk) + through_x * dnew
    dx = step_x * e + weights_x * zt + par[6:7, :CH] * dy
    dc = dot(dg, bm) + dot_nt(dyk, old_b)
    db = dot(cm_f.T.astype(BF), dg).T + dot_nt(xw, dnew_b)
    d_act = jnp.concatenate([dx, db, dc], axis=1)
    d_conv = d_act * (sig_c * (1.0 + conv_out * (1.0 - sig_c)))
    dcbuf[0:BLK, :] = d_conv
    d_in = par[CONV - 1 : CONV, :] * d_conv
    cg = [None] * CONV
    cg[CONV - 1] = jnp.sum(d_conv * cbuf[8 : 8 + BLK, :], axis=0, keepdims=True)
    for back in range(1, CONV):
        tap = CONV - 1 - back
        cg[tap] = jnp.sum(
            d_conv * (cbuf[8 - back : 8 - back + BLK, :] * tok[:, back : back + 1]),
            axis=0, keepdims=True,
        )
        d_in = d_in + par[tap : tap + 1, :] * (
            dcbuf[back : back + BLK, :] * tok[:, 3 + back : 4 + back]
        )
    dcbuf[BLK : BLK + 8, :] = dcbuf[0:8, :]
    small_v[0:CONV, :] += jnp.concatenate(cg, axis=0)
    small_v[CONV : CONV + 1, :] += jnp.sum(d_conv, axis=0, keepdims=True)
    small_v[5:6, CH:] += jnp.concatenate([heads[0:1, :], heads[1:2, :]], axis=1)
    small_v[6:7, CH : CH + 128] += heads[2:3, :]
    return jnp.concatenate([d_in, d_dt[:, :ND]], axis=1)


def id_row(ids_ref, j):
    return ids_ref[0:1, pl.ds(pl.multiple_of(BLK * j, BLK), BLK)].astype(F32)


def token_info(ids_ref, j, blocks):
    row = id_row(ids_ref, j)
    left = jnp.where(j > 0, id_row(ids_ref, jnp.maximum(j - 1, 0)), -1.0)
    right = jnp.where(j < blocks - 1, id_row(ids_ref, jnp.minimum(j + 1, blocks - 1)), -2.0)
    lane = iota((1, BLK), 1)
    wide = lambda a: jnp.broadcast_to(a, (8, BLK))
    rows = [row]
    for back in range(1, CONV):
        shifted = jnp.where(lane < back, pltpu.roll(wide(left), back, 1)[0:1], pltpu.roll(wide(row), back, 1)[0:1])
        rows.append((shifted == row).astype(F32))
    for ahead in range(1, CONV):
        turn = BLK - ahead
        shifted = jnp.where(lane >= turn, pltpu.roll(wide(right), turn, 1)[0:1], pltpu.roll(wide(row), turn, 1)[0:1])
        rows.append((shifted == row).astype(F32))
    rows.append((row == left[:, BLK - 1 :]).astype(F32))
    rows.append((row == row[:, BLK - 1 :]).astype(F32))
    rows.append(jnp.zeros((128 - len(rows), BLK), F32))
    return row, jnp.concatenate(rows, axis=0).T


def pack_small(convw, convb, alog, dtb, dskip, normw, gatew, chip, core, z):
    def channel(m):
        slot = m // HEADDIM
        first, second = head_of(slot, chip, core)
        return jnp.where(slot < 4, first, second) * HEADDIM + m % HEADDIM

    row = lambda a: a.astype(F32).reshape(1, a.shape[0])
    pad = lambda a: jnp.concatenate([row(a), jnp.zeros((1, 128 - HEADS // DEPTH), F32)], axis=1)
    heads = jnp.concatenate([pad(dtb), pad(alog), pad(dskip), jnp.zeros((5, 128), F32)], axis=0).astype(BF)
    m = iota((CHAN // DEPTH, CONVC), 1)
    want = jnp.where(m < CH, channel(m), DI + m - CH)
    chosen = (iota((CHAN // DEPTH, CONVC), 0) + z * (CHAN // DEPTH) == want).astype(BF)
    conv = jnp.concatenate([convw.astype(F32), row(convb), jnp.zeros((3, CHAN // DEPTH), F32)], axis=0)
    conv = dot(conv.astype(BF), chosen)
    n = DI // DEPTH
    chosen = (iota((n, CH), 0) + z * n == channel(iota((n, CH), 1))).astype(BF)
    gate = dot(jnp.broadcast_to(row(gatew), (8, n)).astype(BF), chosen)[0:1]
    n = HEADS // DEPTH
    k = iota((128, CH), 0)
    chosen = ((k < n) & (k + z * n == channel(iota((128, CH), 1)) // HEADDIM)).astype(BF)
    skip = dot(heads, chosen)[2:3]
    k = iota((128, 128), 0)
    chosen = ((k < n) & (k + z * n == iota((128, 128), 1))).astype(BF)
    heads = dot(heads, chosen)
    gain = jnp.where(iota((DEPTH, CH), 0) == z, jnp.broadcast_to(row(normw), (DEPTH, CH)), 0.0)
    return jnp.concatenate([
        conv[0:5],
        jnp.concatenate([gate, heads[0:1], heads[1:2]], axis=1),
        jnp.concatenate([skip, jnp.zeros((1, NB), F32)], axis=1),
        jnp.concatenate([gain, jnp.zeros((DEPTH, NB), F32)], axis=1),
        jnp.zeros((5, CONVC), F32)], axis=0).astype(BF)


CHIPS = TEAM // 2
KROWS = D // DEPTH
BCD = NB + ND
HALF = BCD // 2


def places():
    seq = lax.axis_index("seq")
    return seq, lax.div(seq, 2), lax.rem(seq, 2), lax.axis_index("fsdp")


def neighbours(chip):
    return [chip, chip + 1 - 2 * lax.rem(chip, 2), lax.rem(chip + 2, CHIPS), CHIPS - 1 - chip]


def send(src, dst, send_sem, recv_sem, device):
    return pltpu.make_async_remote_copy(
        src_ref=src, dst_ref=dst, send_sem=send_sem, recv_sem=recv_sem,
        device_id=device, device_id_type=pl.DeviceIdType.MESH,
    )


def greet(devices):
    barrier = pltpu.get_barrier_semaphore()
    for device in devices:
        pl.semaphore_signal(
            barrier, inc=1, device_id=device, device_id_type=pl.DeviceIdType.MESH
        )
    pl.semaphore_wait(barrier, len(devices))


def forward_kernel(
    tok_ref, cot_ref, win_ref, wout_ref, ids_ref, convw_ref, convb_ref, alog_ref, dtb_ref, skip_ref, normw_ref, gatew_ref,
    nrm_ref, projc_ref, projz_ref, st_ref, ssd_ref, dno_ref, br_ref, info_ref, stat_ref, par_ref, w_ref, g_ref,
    u_v, g_v, w_v, wo_v, small_v, smalls, ssd_v, cbuf, state, stat_v, stat_in,
    loc, t_send, t_recv, y_send, y_recv, f_send, f_recv, z_send, z_recv, b_send, b_recv, s_send, s_recv, r_send, r_recv,
):
    i = pl.program_id(0)
    seq, chip, core, z = places()
    sib = {"seq": 2 * chip + 1 - core}
    near = neighbours(chip)
    peer = lambda k: {"seq": 2 * near[k] + core}
    under = lambda k: {"fsdp": lax.rem(z + k, DEPTH)}
    around = lambda k: {"seq": lax.rem(seq + k, TEAM)}
    block = lambda s: pl.ds(pl.multiple_of(BLK * s, BLK), BLK)
    lanes = lambda o: pl.ds(pl.multiple_of(KROWS * o, KROWS), KROWS)
    half = pl.ds(pl.multiple_of(NZ + NX + HALF * core, 16), HALF)
    has = [z < DEPTH - 1, z > 0]
    heads = [head_of(n, chip, core)[n // 4] for n in range(HPD)]
    piece = lambda n: pl.ds(pl.multiple_of(HEADDIM * n, HEADDIM), HEADDIM)

    def token_copy(n, k):
        src, dst = ((tok_ref, u_v), (cot_ref, g_v))[n]
        return send(src, dst.at[block(seq)], t_send.at[n, k], t_recv.at[n, k], sib if k == 0 else peer(k))

    def token_part(n, k, h):
        return (u_v, g_v)[n].at[pl.ds(pl.multiple_of(BLK * (2 * near[k] + core) + h * (BLK // 2), BLK // 2), BLK // 2)]

    def token_relay(n, h):
        part = token_part(n, 1 + h, h)
        return send(part, part, y_send.at[n, h], y_recv.at[n, h], peer(2 - h))

    def token_next(n, k):
        if k < 3:
            ref = (u_v, g_v)[n].at[block(2 * near[k] + core)]
        else:
            ref = token_part(n, 3, k - 3)
        return send(ref, ref, f_send.at[n, k], f_recv.at[n, k], sib)

    def token_start(n):
        for k in range(3):
            token_copy(n, k).start()

    def token_turn(n):
        for k in (1, 2):
            token_copy(n, k).wait_recv()
            token_relay(n, k - 1).start()
            token_next(n, k).start()

    def token_end(n):
        for h in range(2):
            token_relay(n, h).wait_recv()
            token_next(n, 3 + h).start()
        token_copy(n, 0).wait_recv()
        for k in range(1, 5):
            token_next(n, k).wait()
        for h in range(2):
            token_relay(n, h).wait_send()

    def place(p, o):
        if p < 3:
            return w_v.at[(pl.ds(NZ, NX), half, pl.ds(0, NZ))[p], lanes(o)]
        return wo_v.at[piece(o if p == 3 else DEPTH + lax.div(o, 2))]

    def hop(p, side, dist):
        o = z - dist if side == 0 else z + dist
        there = {"fsdp": z + 1} if side == 0 else {"fsdp": z - 1}
        return send(place(p, o), place(p, o), z_send.at[p, side, dist], z_recv.at[p, side, dist], there)

    def got(p, side, dist):
        o = z - dist - 1 if side == 0 else z + dist + 1
        there = {"fsdp": z + 1} if side == 0 else {"fsdp": z - 1}
        return send(place(p, o), place(p, o), z_send.at[p, side, dist], z_recv.at[p, side, dist], there)

    def share(side, dist):
        o = z - dist - 1 if side == 0 else z + dist + 1
        return send(place(1, o), place(1, o), b_send.at[side, dist], b_recv.at[side, dist], sib)

    def exists(p, side, hops):
        o = z - hops if side == 0 else z + hops
        there = (o >= 0) if side == 0 else (o < DEPTH)
        return there & (lax.rem(o + DEPTH, 2) == core) if p == 4 else there

    def small_copy(k):
        return send(small_v, smalls.at[k - 1], s_send.at[k], s_recv.at[k], under(k))

    def stat_copy(k):
        return send(stat_v, stat_in.at[k], r_send.at[k], r_recv.at[k], around(k))

    def local_copies():
        pairs = [(tok_ref, u_v.at[block(seq)]), (cot_ref, g_v.at[block(seq)])]
        return [pltpu.make_async_copy(src, dst, loc.at[n]) for n, (src, dst) in enumerate(pairs)]

    def own_weights():
        pairs = [(win_ref.at[pl.ds(2 * DI, WIDTH - 2 * DI)], w_v.at[pl.ds(NZ + NX, WIDTH - 2 * DI), lanes(z)], 3)]
        for n in range(HPD):
            row = HEADDIM * heads[n]
            pairs.append((win_ref.at[pl.ds(pl.multiple_of(row, HEADDIM), HEADDIM)],
                          w_v.at[piece(n), lanes(z)], 4 + n))
            pairs.append((win_ref.at[pl.ds(pl.multiple_of(DI + row, HEADDIM), HEADDIM)],
                          w_v.at[piece(HPD + n), lanes(z)], 10 + n))
        pairs.append((wout_ref.at[piece(3 * chip + 2 * core)], place(3, z), 16))
        return [pltpu.make_async_copy(src, dst, loc.at[n]) for src, dst, n in pairs]

    def own_extra():
        return pltpu.make_async_copy(wout_ref.at[piece(3 * chip + 1)], place(4, z), loc.at[17])

    def pass_on(parts, dist):
        for p in parts:
            for side in range(2):

                @pl.when(exists(p, side, dist + 1))
                def _():
                    got(p, side, dist).wait_recv()
                    if p == 1:
                        share(side, dist).start()

                if dist < DEPTH - 2:

                    @pl.when(exists(p, side, dist + 1) & has[side])
                    def _():
                        hop(p, side, dist + 1).start()

    def start_own(parts):
        for p in parts:
            for side in range(2):

                @pl.when(exists(p, side, 0) & has[side])
                def _():
                    hop(p, side, 0).start()

    @pl.when(i == 0)
    def _():
        greet([around(k) for k in range(1, TEAM)] + [under(k) for k in range(1, DEPTH)])
        token_start(0)
        for copy in own_weights() + local_copies():
            copy.start()

        @pl.when(lax.rem(z, 2) == core)
        def _():
            own_extra().start()

        w_v[NZ + NX + WIDTH - 2 * DI :, lanes(z)] = jnp.zeros((BCD - (WIDTH - 2 * DI), KROWS), BF)
        for copy in own_weights():
            copy.wait()
        start_own((0, 1))
        small_v[...] = pack_small(convw_ref[...], convb_ref[...], alog_ref[...], dtb_ref[...], skip_ref[...],
                                  normw_ref[...], gatew_ref[...], chip, core, z)
        for k in range(1, DEPTH):
            small_copy(k).start()
        state[...] = jnp.zeros_like(state)
        cbuf[0:8, :] = jnp.zeros((8, CONVC), F32)
        pass_on((0, 1), 0)
        token_turn(0)
        token_start(1)
        pass_on((0, 1), 1)
        start_own((2,))
        token_end(0)
        pass_on((0, 1), 2)
        for k in range(1, DEPTH):
            small_copy(k).wait()
        for copy in local_copies():
            copy.wait()
        for side in range(2):
            for dist in range(DEPTH - 1):

                @pl.when(exists(1, side, dist + 1))
                def _():
                    share(side, dist).wait()

        total = small_v[...].astype(F32)
        for k in range(1, DEPTH):
            total = total + smalls[k - 1].astype(F32)
        par_ref[...] = total

    @pl.when(i == 1)
    def _():
        @pl.when(lax.rem(z, 2) == core)
        def _():
            own_extra().wait()

        pass_on((2,), 0)
        start_own((3, 4))

    @pl.when(i == 3)
    def _():
        pass_on((2,), 1)

    @pl.when(i == 4)
    def _():
        token_turn(1)

    @pl.when(i == 5)
    def _():
        pass_on((3, 4), 0)

    @pl.when(i == 7)
    def _():
        pass_on((3, 4), 1)

    @pl.when(i == TEAM)
    def _():
        pass_on((2, 3, 4), 2)
        token_end(1)
        pltpu.make_async_copy(w_v, w_ref, loc.at[18]).start()
        pltpu.make_async_copy(g_v, g_ref, loc.at[19]).start()

    par = par_ref[...]

    @pl.when(i < TEAM)
    def _():
        u = u_v[block(i), :].astype(F32)
        scale = lax.rsqrt(jnp.mean(u * u, axis=1, keepdims=True) + EPSILON)
        nrm = (u * scale * norm_gain(par)).astype(BF)
        nrm_ref[...] = nrm
        u_v[block(i), :] = nrm
        row, info = token_info(ids_ref, i, TEAM)
        info_ref[...] = info
        scan_forward(i, nrm, w_v, par, info, row, cbuf, state,
                     projc_ref, st_ref, ssd_v)

    @pl.when(i >= TEAM)
    def _():
        gate_forward(i - TEAM, u_v, g_v, w_v, wo_v, par, ssd_v, projz_ref, ssd_ref, dno_ref,
                     br_ref, stat_v)

    @pl.when(i == 2 * TEAM - 1)
    def _():
        for k in range(1, TEAM):
            stat_copy(k).start()
        total = stat_v[...]
        for k in range(1, TEAM):
            stat_copy(k).wait_recv()
            total = total + stat_in[k]
        stat_ref[...] = total
        for k in range(1, TEAM):
            stat_copy(k).wait_send()
        for n in range(2):
            for k in range(3):
                token_copy(n, k).wait_send()
        for side in range(2):
            for dist in range(DEPTH - 1):
                for p in range(5):

                    @pl.when(exists(p, side, dist) & has[side])
                    def _():
                        hop(p, side, dist).wait_send()

        pltpu.make_async_copy(w_v, w_ref, loc.at[18]).wait()
        pltpu.make_async_copy(g_v, g_ref, loc.at[19]).wait()


def forward_call(tok, cot, win, wout, ids, small):
    n = tok.shape[0] * TEAM
    any_space = pl.BlockSpec(memory_space=pl.ANY)
    sds = jax.ShapeDtypeStruct
    dma = pltpu.SemaphoreType.DMA
    one = lambda i: jnp.minimum(i, TEAM - 1)
    two = lambda i: jnp.maximum(i - TEAM, 0)
    rows = lambda c, turn: pl.BlockSpec((BLK, c), lambda i: (turn(i), 0))
    cube = lambda a, b: pl.BlockSpec((1, a, b), lambda i: (one(i), 0, 0))
    fixed = lambda a, b: pl.BlockSpec((a, b), lambda i: (0, 0))
    return pl.pallas_call(
        forward_kernel,
        grid=(2 * TEAM,),
        in_specs=[any_space] * 4 + [
            pl.BlockSpec(a.shape, lambda i, n=a.ndim: (0,) * n, pipeline_mode=pl.Buffered(1)) for a in (ids, *small)],
        out_specs=[rows(D, one), rows(REST, one), rows(NZ, two), cube(STATE, CH), rows(CH, two),
                   rows(CH, two), rows(D, two), rows(128, one), fixed(TEAM, 2 * BLK), fixed(16, CONVC),
                   any_space, any_space],
        out_shape=[sds((n, D), BF), sds((n, REST), BF), sds((n, NZ), BF), sds((TEAM, STATE, CH), F32),
                   sds((n, CH), F32), sds((n, CH), F32), sds((n, D), BF), sds((n, 128), F32), sds((TEAM, 2 * BLK), F32),
                   sds((16, CONVC), F32), sds((COLS, D), BF), sds((n, D), BF)],
        scratch_shapes=[pltpu.VMEM((n, D), BF), pltpu.VMEM((n, D), BF), pltpu.VMEM((COLS, D), BF),
                        pltpu.VMEM((CH, D), BF), pltpu.VMEM((16, CONVC), BF), pltpu.VMEM((DEPTH - 1, 16, CONVC), BF),
                        pltpu.VMEM((n, CH), F32), pltpu.VMEM((BLK + 8, CONVC), F32),
                        pltpu.VMEM((STATE, CH), F32), pltpu.VMEM((TEAM, 2 * BLK), F32),
                        pltpu.VMEM((TEAM, TEAM, 2 * BLK), F32),
                        dma((20,)), dma((2, 3)), dma((2, 3)), dma((2, 2)), dma((2, 2)), dma((2, 5)),
                        dma((2, 5)), dma((5, 2, DEPTH - 1)), dma((5, 2, DEPTH - 1)),
                        dma((2, DEPTH - 1)), dma((2, DEPTH - 1)),
                        dma((DEPTH,)), dma((DEPTH,)), dma((TEAM,)), dma((TEAM,))],
        compiler_params=pltpu.CompilerParams(
            collective_id=0, has_side_effects=True, vmem_limit_bytes=60 << 20),
    )(tok, cot, win, wout, ids, *small)


def backward_kernel(
    tok_ref, cot_ref, nrm_ref, br_ref, w_ref, g_ref,
    projz_ref, ssd_ref, dno_ref, stat_ref, par_ref, projc_ref, halo_ref, st_ref, info_ref, ids_ref,
    out_ref, tg_ref, wig_ref, wog_ref, smalls_ref,
    nrm_v, g_v, w_v, not_v, dz_v, dzt_v, dy_v, rest_v, wig_v, wog_v, bcd_v, bcd_in,
    zz_in, zx_in, zb_in, zw_in, zs_in, gz_v, gx_v, gb_v, gw_v, gb_in, gt_v, ob_v, rb_v, in_v, rel_v,
    tok_v, cot_v, small_v, small_s, cbuf, dcbuf, dstate,
    loc, b_send, b_recv, p_send, p_recv, d_send, d_recv, q_send, q_recv, z_send, z_recv,
    a_send, a_recv, f_send, f_recv, h_send, h_recv, free,
):
    i = pl.program_id(0)
    seq, chip, core, z = places()
    sib = {"seq": 2 * chip + 1 - core}
    near = neighbours(chip)
    peer = lambda k: {"seq": 2 * near[k] + core}
    under = lambda k: {"fsdp": lax.rem(z + k, DEPTH)}
    around = lambda k: {"seq": lax.rem(seq + k, TEAM)}
    block = lambda s: pl.ds(pl.multiple_of(BLK * s, BLK), BLK)
    lanes = lambda o: pl.ds(pl.multiple_of(KROWS * o, KROWS), KROWS)
    piece = lambda n: pl.ds(pl.multiple_of(HEADDIM * n, HEADDIM), HEADDIM)
    half = lambda c: pl.ds(pl.multiple_of(HALF * c, 16), HALF)
    extra = lambda o: lax.rem(o, 2) == core
    n_all = HEADDIM * HPD
    give = lambda c: g_v.at[block(c)]
    hold = lambda c: g_v.at[block(CHIPS + c)]

    def load(n):
        pairs = [(nrm_ref, nrm_v), (g_ref, g_v), (w_ref, w_v), (tok_ref, tok_v), (cot_ref, cot_v)]
        return pltpu.make_async_copy(pairs[n][0], pairs[n][1], loc.at[n])

    def load_own(c):
        return pltpu.make_async_copy(br_ref.at[block(2 * c + core)], ob_v.at[c], loc.at[5 + c])

    def br_pair(c):
        return send(br_ref.at[block(2 * c + 1 - core)], rb_v.at[c], b_send.at[c], b_recv.at[c], sib)

    def block_of(n, c):
        return ob_v.at[c] if n == 0 else hold(c)

    def rs(n, kind):
        h = pl.ds((0, BLK // 2, BLK // 2, 0, 0, BLK // 2)[kind], BLK // 2)
        src = block_of(n, near[(1, 1, 2, 2, 3, 3)[kind]]).at[h]
        if kind < 4:
            dst = in_v.at[n, kind // 2, h]
        else:
            dst = rel_v.at[n, 5 - kind]
        return send(src, dst, p_send.at[n, kind], p_recv.at[n, kind], peer((1, 1, 2, 2, 1, 2)[kind]))

    def rs_first(n, role):
        for kind in ((), (0,), (2,), (4, 5))[role]:
            rs(n, kind).start()

    def rs_second(n, role):
        kind, came = ((1, 5), (3, 4))[role - 1]
        rs(n, came).wait_recv()
        h = pl.ds((BLK // 2, 0)[role - 1], BLK // 2)
        ref = block_of(n, near[role]).at[h]
        ref[...] = (ref[...].astype(F32) + rel_v[n, role - 1].astype(F32)).astype(BF)
        rs(n, kind).start()

    def rs_total(n):
        for kind in range(4):
            rs(n, kind).wait_recv()
        return block_of(n, chip)[...].astype(F32) + in_v[n, 0].astype(F32) + in_v[n, 1].astype(F32)

    def dn_pair(c):
        return send(give(c), rb_v.at[c], d_send.at[c], d_recv.at[c], sib)

    def down(n, k):
        o = lax.rem(z + k, DEPTH)
        src, dst = [
            (wig_v.at[:, lanes(o)], zz_in.at[k - 1]),
            (wig_v.at[:, lanes(o)], zx_in.at[k - 1]),
            (bcd_v.at[half(core), lanes(o)], zb_in.at[k - 1]),
            (wog_v.at[piece(o)], zw_in.at[k - 1, 0:HEADDIM]),
            (wog_v.at[piece(DEPTH + lax.div(o, 2))], zw_in.at[k - 1, HEADDIM:]),
            (small_v, zs_in.at[k - 1]),
        ][n]
        return send(src, dst, z_send.at[n, k], z_recv.at[n, k], under(k))

    def bcd_pair():
        return send(bcd_v.at[half(1 - core)], bcd_in, h_send.at[0], h_recv.at[0], sib)

    def bcd_push(k):
        return send(gb_v, gb_in.at[k - 1], q_send.at[k], q_recv.at[k], peer(k))

    def bcd_back():
        return send(gt_v.at[core], gt_v.at[core], h_send.at[1], h_recv.at[1], sib)

    def parts(n, c, cr, h=None):
        if n < 2:
            base = n * DI // HEADDIM
            src = (gz_v, gx_v)[n]
            slots = range(HPD) if h is None else range(3 * h, 3 * h + 3)
            return [(src.at[piece(s)], wig_ref.at[piece(base + head_of(s, c, cr)[s // 4])]) for s in slots]
        if n < 4:
            row = HEADDIM * (3 * c + 2 * cr if n == 2 else 3 * c + 1)
            first, size = (0, HEADDIM) if h is None else (h * HEADDIM // 2, HEADDIM // 2)
            return [(gw_v.at[pl.ds(HEADDIM * (n - 2) + first, size)],
                     wog_ref.at[pl.ds(pl.multiple_of(row + first, HEADDIM // 2), size)])]
        if h is None:
            return [(small_s, smalls_ref.at[2 * c + cr])]
        return [(small_s.at[8 * h : 8 * h + 8], smalls_ref.at[2 * c + cr, 8 * h : 8 * h + 8])]

    def all_of(n, h=None):
        if n < 2:
            return wig_ref.at[pl.ds(n * DI, n_all if h is None else n_all // 2)]
        return parts(n, 0, 0, h)[0][1]

    def ag(n, k):
        if k < 3:
            return [send(src, dst, a_send.at[n, k], a_recv.at[n, k], sib if k == 0 else peer(k))
                    for src, dst in parts(n, chip, core)]
        return [send(dst, dst, a_send.at[n, k], a_recv.at[n, k], peer(5 - k))
                for _, dst in parts(n, near[k - 2], core, k - 3)]

    def ag_wait(n, k):
        ref = all_of(n, None if k < 3 else k - 3)
        return send(ref, ref, a_send.at[n, k], a_recv.at[n, k], sib)

    def ag_next(n, k):
        which = parts(n, near[k], core) if k < 3 else parts(n, near[3], core, k - 3)
        return [send(dst, dst, f_send.at[n, k], f_recv.at[n, k], sib) for _, dst in which]

    def ag_next_wait(n, k):
        ref = all_of(n, None if k < 3 else k - 3)
        return send(ref, ref, f_send.at[n, k], f_recv.at[n, k], sib)

    def ag_own(n):
        return [pltpu.make_async_copy(src, dst, loc.at[9 + n]) for src, dst in parts(n, chip, core)]

    def ag_own_wait(n):
        return pltpu.make_async_copy(all_of(n), all_of(n), loc.at[9 + n])

    def ag_start(n):
        for k in (1, 2, 0):
            for copy in ag(n, k):
                copy.start()
        for copy in ag_own(n):
            copy.start()

    def ag_turn(n):
        for k in (1, 2):
            ag_wait(n, k).wait_recv()
            for copy in ag(n, k + 2) + ag_next(n, k):
                copy.start()

    def ag_end(n):
        for k in (3, 4):
            ag_wait(n, k).wait_recv()
            for copy in ag_next(n, k):
                copy.start()

    def ag_close(n, sends=True, receives=True):
        if receives:
            ag_wait(n, 0).wait_recv()
            for k in range(1, 5):
                ag_next_wait(n, k).wait_recv()
        if sends:
            for k in range(5):
                ag_wait(n, k).wait_send()
            for k in range(1, 5):
                ag_next_wait(n, k).wait_send()
            ag_own_wait(n).wait()

    def reduce_z(own, arrived):
        total = own.astype(F32)
        for k in range(1, DEPTH):
            total = total + arrived[k - 1].astype(F32)
        return total

    @pl.when(i == 0)
    def _():
        greet([around(k) for k in range(1, TEAM)] + [under(k) for k in range(1, DEPTH)])
        for c in range(CHIPS):
            br_pair(c).start()
            load_own(c).start()
        for n in range(5):
            load(n).start()
        small_v[...] = jnp.zeros_like(small_v)
        dstate[...] = jnp.zeros_like(dstate)
        dcbuf[BLK : BLK + 8, :] = jnp.zeros((8, CONVC), F32)

    @pl.when(i < TEAM)
    def _():
        gate_backward(i, projz_ref[...].astype(F32), ssd_ref[...], dno_ref[...],
                      stat_ref[pl.ds(i, 1), :], par_ref[5:6, :CH], not_v, dy_v, dz_v, dzt_v, small_v)

    @pl.when(i == 1)
    def _():
        for c in range(CHIPS):
            load_own(c).wait()
            br_pair(c).wait_recv()
            ob_v[c] = (ob_v[c].astype(F32) + rb_v[c].astype(F32)).astype(BF)
        for role in (3, 1, 2):
            rs_first(0, role)
        pl.semaphore_signal(free, inc=1, device_id=sib, device_id_type=pl.DeviceIdType.MESH)

    @pl.when(i == TEAM)
    def _():
        pl.semaphore_wait(free, 1)
        for n in range(5):
            load(n).wait()

        @pl.loop(0, D // 256)
        def _(n):
            cols = pl.ds(pl.multiple_of(256 * n, 256), 256)
            wig_v[:, cols] = dot(dzt_v[...], nrm_v[:, cols]).astype(BF)

        for k in range(1, DEPTH):
            down(0, k).start()

        @pl.loop(0, D // 256)
        def _(n):
            cols = pl.ds(pl.multiple_of(256 * n, 256), 256)
            wog_v[:, cols] = dot(not_v[...], g_v[:, cols]).astype(BF)

        for k in range(1, DEPTH):
            down(3, k).start()

            @pl.when(extra(z + k))
            def _():
                down(4, k).start()

    def combine(c):
        dn_pair(c).wait_recv()
        hold(c)[...] = (hold(c)[...].astype(F32) + rb_v[c].astype(F32)).astype(BF)
        for role in (1, 2, 3):

            @pl.when(near[role] == c)
            def _():
                rs_first(1, role)

    def relay(c):
        for role in (1, 2):

            @pl.when(near[role] == c)
            def _():
                rs_second(1, role)

    for c in range(CHIPS - 1, 0, -1):

        @pl.when(i == TEAM + 1 + 2 * (CHIPS - c))
        def _():
            combine(c)
            if c < CHIPS - 1:
                relay(c + 1)

    @pl.when(i == TEAM + 2)
    def _():
        rs_second(0, 1)
        rs_second(0, 2)

    @pl.when((i > TEAM) & (i <= 2 * TEAM))
    def _():
        j = 2 * TEAM - i
        rows = block(j)
        d_rest = scan_backward(projc_ref[...], halo_ref[...], info_ref[...], id_row(ids_ref, j), st_ref[0],
                               par_ref[...], dy_v[rows, :], cbuf, dcbuf, dstate, small_v)
        rest_v[:, rows] = d_rest.T.astype(BF)
        dn = dot(dz_v[rows, :], w_v[:NZ, :]) + dot(d_rest.astype(BF), w_v[NZ:, :])
        part = jnp.sum(dn * nrm_v[rows, :].astype(F32), axis=0, keepdims=True)
        for n in range(D // CH):
            small_v[7 + n : 8 + n, :CH] += part[:, CH * n : CH * n + CH]
        dn = dn.astype(BF)
        c = lax.div(j, 2)

        @pl.when(lax.rem(j, 2) == core)
        def _():
            hold(c)[...] = dn

        @pl.when(lax.rem(j, 2) != core)
        def _():
            give(c)[...] = dn
            dn_pair(c).start()

    @pl.when(i == 2 * TEAM - 1)
    def _():
        total = rs_total(0)
        stat = stat_ref[pl.ds(seq, 1), 0:BLK]
        stat = jnp.broadcast_to(stat, (128, BLK)).T
        s2 = lax.rsqrt(stat[:, 0:1] * (1.0 / DI) + EPSILON)
        out_ref[...] = (tok_v[...].astype(F32) + total * s2).astype(BF)

    @pl.when(i == 2 * TEAM)
    def _():
        for k in range(1, DEPTH):
            down(0, k).wait_recv()
        gz_v[...] = reduce_z(wig_v[:, lanes(z)], [zz_in[k - 1] for k in range(1, DEPTH)]).astype(BF)
        ag_start(0)

    @pl.when(i == 2 * TEAM + 1)
    def _():
        for n in range(D // CH):
            small_v[7 + n : 8 + n, :CH] = small_v[7 + n : 8 + n, :CH] / par_ref[7 + n : 8 + n, :CH]
        for k in range(1, DEPTH):
            down(5, k).start()
        combine(0)
        relay(1)

        @pl.loop(0, D // 256)
        def _(n):
            cols = pl.ds(pl.multiple_of(256 * n, 256), 256)
            bcd_v[:, cols] = dot(rest_v[NX:, :], nrm_v[:, cols]).astype(BF)

        bcd_pair().start()
        for k in range(1, DEPTH):
            down(0, k).wait_send()

        @pl.loop(0, D // 256)
        def _(n):
            cols = pl.ds(pl.multiple_of(256 * n, 256), 256)
            wig_v[:, cols] = dot(rest_v[:NX, :], nrm_v[:, cols]).astype(BF)

        for k in range(1, DEPTH):
            down(1, k).start()
        bcd_pair().wait_recv()
        bcd_v[half(core), :] = (bcd_v[half(core), :].astype(F32) + bcd_in[...].astype(F32)).astype(BF)
        for k in range(1, DEPTH):
            down(2, k).start()
        relay(0)
        ag_turn(0)
        for k in range(1, DEPTH):
            down(3, k).wait_recv()
        gw_v[0:HEADDIM, :] = reduce_z(wog_v[piece(z), :], [zw_in[k - 1, 0:HEADDIM] for k in range(1, DEPTH)]).astype(BF)
        ag_start(2)

        @pl.when(extra(z))
        def _():
            for k in range(1, DEPTH):
                down(4, k).wait_recv()
            gw_v[HEADDIM:, :] = reduce_z(
                wog_v[piece(DEPTH + lax.div(z, 2)), :], [zw_in[k - 1, HEADDIM:] for k in range(1, DEPTH)]).astype(BF)
            ag_start(3)

        for k in range(1, DEPTH):
            down(5, k).wait_recv()
        small_s[...] = reduce_z(small_v[...], [zs_in[k - 1] for k in range(1, DEPTH)])
        ag_start(4)
        ag_end(0)
        total = rs_total(1)
        uf = tok_v[...].astype(F32)
        along = total * norm_gain(par_ref[...])
        s1 = lax.rsqrt(jnp.mean(uf * uf, axis=1, keepdims=True) + EPSILON)
        tg_ref[...] = cot_v[...].astype(F32) + s1 * along - uf * (
            s1 * s1 * s1 * jnp.mean(along * uf, axis=1, keepdims=True))
        ag_turn(2)

        @pl.when(extra(z))
        def _():
            ag_turn(3)

        ag_turn(4)
        for k in range(1, DEPTH):
            down(1, k).wait_recv()
        gx_v[...] = reduce_z(wig_v[:, lanes(z)], [zx_in[k - 1] for k in range(1, DEPTH)]).astype(BF)
        ag_start(1)
        for k in range(1, DEPTH):
            down(2, k).wait_recv()
        gb_v[...] = reduce_z(bcd_v[half(core), lanes(z)], [zb_in[k - 1] for k in range(1, DEPTH)]).astype(BF)
        for k in range(1, CHIPS):
            bcd_push(k).start()
        ag_end(2)

        @pl.when(extra(z))
        def _():
            ag_end(3)

        ag_end(4)
        ag_turn(1)
        for k in range(1, CHIPS):
            bcd_push(k).wait_recv()
        total = gb_v[...].astype(F32)
        for k in range(1, CHIPS):
            total = total + gb_in[k - 1].astype(F32)
        gt_v[core] = total.astype(BF)
        bcd_back().start()
        ag_end(1)
        bcd_back().wait()
        last = [
            pltpu.make_async_copy(gt_v.at[0], wig_ref.at[pl.ds(2 * DI, HALF)], loc.at[15]),
            pltpu.make_async_copy(gt_v.at[1, 0 : WIDTH - 2 * DI - HALF],
                                  wig_ref.at[pl.ds(2 * DI + HALF, WIDTH - 2 * DI - HALF)], loc.at[16])]
        for copy in last:
            copy.start()
        for n in (0, 1, 2, 4):
            ag_close(n)

        @pl.when(extra(z))
        def _():
            ag_close(3, receives=False)

        @pl.when(jnp.logical_not(extra(z)))
        def _():
            ag_close(3, sends=False)

        for c in range(CHIPS):
            br_pair(c).wait_send()
            dn_pair(c).wait_send()
        for n in range(2):
            for kind in range(6):
                rs(n, kind).wait_send()
        for k in range(1, CHIPS):
            bcd_push(k).wait_send()
        for k in range(1, DEPTH):
            for n in (1, 2, 3, 5):
                down(n, k).wait_send()

            @pl.when(extra(z + k))
            def _():
                down(4, k).wait_send()

        bcd_pair().wait_send()
        for copy in last:
            copy.wait()


def backward_call(tok, cot, nrm, br, w, g, projz, ssd, dno, stat, par, projc, st, info, ids):
    n = nrm.shape[0]
    any_space = pl.BlockSpec(memory_space=pl.ANY)
    sds = jax.ShapeDtypeStruct
    dma = pltpu.SemaphoreType.DMA
    one = lambda i: jnp.minimum(i, TEAM - 1)
    two = lambda i: jnp.clip(2 * TEAM - i, 0, TEAM - 1)
    rows = lambda c, turn: pl.BlockSpec((BLK, c), lambda i: (turn(i), 0))
    cube = lambda a, b: pl.BlockSpec((1, a, b), lambda i: (two(i), 0, 0))
    fixed = lambda a, b: pl.BlockSpec((a, b), lambda i: (0, 0), pipeline_mode=pl.Buffered(1))
    vm = pltpu.VMEM
    return pl.pallas_call(
        backward_kernel,
        grid=(2 * TEAM + 2,),
        in_specs=[any_space] * 6 + [
            rows(NZ, one), rows(CH, one), rows(CH, one), fixed(TEAM, 2 * BLK), fixed(16, CONVC), rows(REST, two),
            pl.BlockSpec((16, REST), lambda i: (jnp.maximum(16 * two(i) - 1, 0), 0)),
            cube(STATE, CH), rows(128, two), fixed(1, n)],
        out_specs=[fixed(BLK, D), fixed(BLK, D), any_space, any_space, any_space],
        out_shape=[sds((BLK, D), BF), sds((BLK, D), F32), sds((WIDTH, KROWS), BF),
                   sds((DI // DEPTH, D), BF), sds((TEAM, 16, CONVC), F32)],
        scratch_shapes=[
            vm((n, D), BF), vm((n, D), BF), vm((COLS, D), BF), vm((CH, n), BF), vm((n, CH), BF), vm((CH, n), BF),
            vm((n, CH), F32), vm((REST, n), BF), vm((CH, D), BF), vm((CH, D), BF), vm((BCD, D), BF),
            vm((HALF, D), BF),
            vm((DEPTH - 1, CH, KROWS), BF), vm((DEPTH - 1, CH, KROWS), BF), vm((DEPTH - 1, HALF, KROWS), BF),
            vm((DEPTH - 1, 2 * HEADDIM, D), BF), vm((DEPTH - 1, 16, CONVC), F32), vm((CH, KROWS), BF), vm((CH, KROWS), BF),
            vm((HALF, KROWS), BF), vm((2 * HEADDIM, D), BF), vm((CHIPS - 1, HALF, KROWS), BF), vm((2, HALF, KROWS), BF),
            vm((CHIPS, BLK, D), BF), vm((CHIPS, BLK, D), BF), vm((2, 2, BLK, D), BF), vm((2, 2, BLK // 2, D), BF),
            vm((BLK, D), BF), vm((BLK, D), BF), vm((16, CONVC), F32), vm((16, CONVC), F32),
            vm((BLK + 8, CONVC), F32), vm((BLK + 8, CONVC), F32), vm((STATE, CH), F32),
            dma((17,)), dma((CHIPS,)), dma((CHIPS,)), dma((2, 6)), dma((2, 6)), dma((CHIPS,)), dma((CHIPS,)),
            dma((CHIPS,)), dma((CHIPS,)), dma((6, DEPTH)), dma((6, DEPTH)),
            dma((5, 5)), dma((5, 5)), dma((5, 5)), dma((5, 5)), dma((2,)), dma((2,)),
            pltpu.SemaphoreType.REGULAR],
        compiler_params=pltpu.CompilerParams(
            collective_id=1, has_side_effects=True, vmem_limit_bytes=63 << 20),
    )(tok, cot, nrm, br, w, g, projz, ssd, dno, stat, par, projc, projc, st, info, ids)


def finish_kernel(
    lo_ref, tg_ref, wig_ref, wog_ref, smalls_ref,
    out_ref, grad_ref, win_ref, wout_ref, convw_ref, convb_ref, alog_ref, dtb_ref, skip_ref, normw_ref, gatew_ref,
    all_v, in_v, in_f, wo_v, wo_f, lo_v, tg_v, sems,
):
    rows_in, rows_wo = WIDTH // 13, DI // DEPTH // 4
    chunks = [(wig_ref, in_v, in_f, win_ref, slice(rows_in * n, rows_in * n + rows_in)) for n in range(13)]
    chunks += [(wog_ref, wo_v, wo_f, wout_ref, slice(rows_wo * n, rows_wo * n + rows_wo)) for n in range(4)]
    come = [pltpu.make_async_copy(a.at[r], b.at[r], sems.at[0, n]) for n, (a, b, _, _, r) in enumerate(chunks)]
    go = [pltpu.make_async_copy(a.at[r], b.at[r], sems.at[1, n]) for n, (_, _, a, b, r) in enumerate(chunks)]
    last = len(chunks)
    enter = [pltpu.make_async_copy(lo_ref, lo_v, sems.at[0, last]), pltpu.make_async_copy(tg_ref, tg_v, sems.at[0, last + 1])]
    leave = [pltpu.make_async_copy(lo_v, out_ref, sems.at[1, last]), pltpu.make_async_copy(tg_v, grad_ref, sems.at[1, last + 1])]
    for copy in come + enter:
        copy.start()
    for n, (_, src, dst, _, r) in enumerate(chunks):
        come[n].wait()
        dst[r] = src[r].astype(F32)
        go[n].start()
    for n in range(2):
        enter[n].wait()
        leave[n].start()
    for d in range(TEAM):
        for slot in range(HPD):
            head = head_of(slot, d // 2, d % 2)[slot // 4]
            all_v[:, HEADDIM * head : HEADDIM * head + HEADDIM] = smalls_ref[
                d, 0:8, HEADDIM * slot : HEADDIM * slot + HEADDIM]
    side = smalls_ref[0, :, CH:]
    gain = smalls_ref[0, :, :CH]
    for d in range(1, TEAM):
        side = side + smalls_ref[d, :, CH:]
        gain = gain + smalls_ref[d, :, :CH]
    all_v[:, DI:] = side[0:8]
    z = lax.axis_index("fsdp")
    nc, ng, nh = CHAN // DEPTH, DI // DEPTH, HEADS // DEPTH
    for o in range(DEPTH):

        @pl.when(z == o)
        def _():
            convw_ref[...] = all_v[0:CONV, nc * o : nc * o + nc]
            convb_ref[...] = all_v[CONV : CONV + 1, nc * o : nc * o + nc].reshape(nc)
            gatew_ref[...] = all_v[5:6, ng * o : ng * o + ng].reshape(ng)
            alog_ref[...] = side[5:6, nh * o : nh * o + nh].reshape(nh)
            dtb_ref[...] = side[5:6, 128 + nh * o : 128 + nh * o + nh].reshape(nh)
            skip_ref[...] = side[6:7, nh * o : nh * o + nh].reshape(nh)
            normw_ref[...] = gain[7 + o : 8 + o, :].reshape(KROWS)

    for copy in go + leave:
        copy.wait()


def finish_call(lo, tg, wig, wog, smalls):
    any_space = pl.BlockSpec(memory_space=pl.ANY)
    vmem = pl.BlockSpec(memory_space=pltpu.VMEM)
    sizes = [(CONV, CHAN // DEPTH), (CHAN // DEPTH,)] + [(HEADS // DEPTH,)] * 3 + [(KROWS,), (DI // DEPTH,)]
    sds = jax.ShapeDtypeStruct
    rows = DI // DEPTH
    return pl.pallas_call(
        finish_kernel,
        in_specs=[any_space] * 4 + [vmem],
        out_specs=[any_space] * 4 + [vmem] * len(sizes),
        out_shape=[sds((BLK, D), BF), sds((BLK, D), F32), sds((WIDTH, KROWS), F32), sds((rows, D), F32)]
        + [sds(s, F32) for s in sizes],
        scratch_shapes=[pltpu.VMEM((8, CHAN), F32), pltpu.VMEM((WIDTH, KROWS), BF), pltpu.VMEM((WIDTH, KROWS), F32),
                        pltpu.VMEM((rows, D), BF), pltpu.VMEM((rows, D), F32), pltpu.VMEM((BLK, D), BF), pltpu.VMEM((BLK, D), F32),
                        pltpu.SemaphoreType.DMA((2, 19))],
        compiler_params=pltpu.CompilerParams(vmem_limit_bytes=62 << 20),
    )(lo, tg, wig, wog, smalls)


def on_team(
    tokens, segment_ids, cotangent, w_in, w_out, conv_w, conv_b, a_log, dt_bias, d_skip,
    norm_w, gate_w,
):
    tok, cot = tokens[0], cotangent[0]
    small = (conv_w, conv_b, a_log, dt_bias, d_skip, norm_w, gate_w)
    nrm, projc, projz, st, ssd, dno, br, info, stat, par, w_loc, g = forward_call(
        tok, cot, w_in.T, w_out, segment_ids, small)
    lo, tg, wig, wog, smalls = backward_call(
        tok, cot, nrm, br, w_loc, g, projz, ssd, dno, stat, par, projc, st, info, segment_ids)
    lo, tg, wig, wog, convw, convb, alog, dtb, skip, normw, gatew = finish_call(lo, tg, wig, wog, smalls)
    return (lo[None], tg[None], wig.T, wog, convw, convb, alog, dtb, skip, normw, gatew)


def solution(mesh):
    body = on_team if (mesh.shape["seq"], mesh.shape["fsdp"]) == (TEAM, DEPTH) else on_device
    return jax.shard_map(
        body,
        mesh=mesh,
        in_specs=(
            P("fsdp", "seq", None),
            P("fsdp", None),
            P("fsdp", "seq", None),
            P("fsdp", None),
            P("fsdp", None),
            P(None, "fsdp"),
            P("fsdp"),
            P("fsdp"),
            P("fsdp"),
            P("fsdp"),
            P("fsdp"),
            P("fsdp"),
        ),
        out_specs=(
            P("fsdp", "seq", None),
            P("fsdp", "seq", None),
            P("fsdp", None),
            P("fsdp", None),
            P(None, "fsdp"),
            P("fsdp"),
            P("fsdp"),
            P("fsdp"),
            P("fsdp"),
            P("fsdp"),
            P("fsdp"),
        ),
        check_vma=False,
    )
```

```python
import jax
import jax.numpy as jnp
from jax import lax
from jax.experimental import pallas as pl
from jax.experimental.pallas import tpu as pltpu
from jax.sharding import PartitionSpec as P

DI = 3072
HEADDIM = 64
STATE = 128
CONV = 4
SPAN = 256
HEADS = 48
D = 1536
WIDTH = 6448
DEPTH = 4
CHAN = 3328


EPSILON = 1e-05
HIGHEST = lax.Precision.HIGHEST


def passed_along(value, axis, steps):
    count = lax.axis_size(axis)
    first, last = (max(0, -steps), min(count, count - steps))
    return lax.ppermute(value, axis, [(source, source + steps) for source in range(first, last)])


def shortened(array):

    def short(part):
        return part.astype(jnp.bfloat16) if part.dtype == jnp.float32 else part

    return jax.tree.map(short, array)


def block_masks(ids_blocks, before_ids):
    block_len = ids_blocks.shape[1]
    places = jnp.arange(block_len)
    causal_mask = (places[:, None] >= places[None, :])[None] & (
        ids_blocks[:, :, None] == ids_blocks[:, None, :]
    )
    keep_flag = (ids_blocks == before_ids[:, None]).astype(jnp.float32)
    same_last = (ids_blocks == ids_blocks[:, -1:]).astype(jnp.float32)
    return (causal_mask, keep_flag, same_last)


def local_states(x_heads, b_rows, step_size, log_decay, same_last, keep_flag):
    cum_decay = jnp.cumsum(log_decay, axis=1)
    last_cum = cum_decay[:, -1]
    weights = jnp.exp(last_cum[:, None, :] - cum_decay) * step_size * same_last[:, :, None]
    fresh_state = jnp.einsum("csh,cshp,csn->chpn", weights, x_heads, b_rows, precision=HIGHEST)
    passing = keep_flag[:, -1:] * jnp.exp(last_cum)
    total_state = jnp.zeros_like(fresh_state[0])
    total_decay = jnp.ones_like(passing[0])
    total_state = fresh_state[0] + passing[0][:, None, None] * total_state
    total_decay = total_decay * passing[0]
    return (fresh_state, passing, total_state, total_decay)


def local_output(x_heads, b_rows, c_rows, step_size, log_decay, incoming, causal_mask, keep_flag):
    cum_decay = jnp.cumsum(log_decay, axis=1)
    cum_heads = jnp.swapaxes(cum_decay, 1, 2)
    gap_decay = cum_heads[:, :, :, None] - cum_heads[:, :, None, :]
    head_mask = causal_mask[:, None]
    decay_map = jnp.exp(jnp.where(head_mask, gap_decay, 0.0)) * head_mask.astype(jnp.float32)
    scores = jnp.einsum("ctn,csn->cts", c_rows, b_rows, precision=HIGHEST)
    mixing = scores[:, None] * decay_map * jnp.swapaxes(step_size, 1, 2)[:, :, None, :]
    inner_out = jnp.einsum("chts,cshp->cthp", mixing, x_heads, precision=HIGHEST)
    starts = [incoming]
    start_states = jnp.stack(starts)
    carried = jnp.einsum("ctn,chpn->cthp", c_rows, start_states, precision=HIGHEST)
    carried = carried * (keep_flag[:, :, None] * jnp.exp(cum_decay))[..., None]
    return inner_out + carried


def on_device(
    tokens,
    segment_ids,
    cotangent,
    w_in,
    w_out,
    conv_w,
    conv_b,
    a_log,
    dt_bias,
    d_skip,
    norm_w,
    gate_w,
):
    gathered = (
        lax.all_gather(w_in, "fsdp", axis=0, tiled=True),
        lax.all_gather(w_out, "fsdp", axis=0, tiled=True),
        lax.all_gather(conv_w, "fsdp", axis=1, tiled=True),
        lax.all_gather(conv_b, "fsdp", axis=0, tiled=True),
        lax.all_gather(a_log, "fsdp", axis=0, tiled=True),
        lax.all_gather(dt_bias, "fsdp", axis=0, tiled=True),
        lax.all_gather(d_skip, "fsdp", axis=0, tiled=True),
        lax.all_gather(norm_w, "fsdp", axis=0, tiled=True),
        lax.all_gather(gate_w, "fsdp", axis=0, tiled=True),
    )
    (
        w_in_full,
        w_out_full,
        conv_full,
        bias_full,
        a_log_full,
        dt_bias_full,
        skip_full,
        norm_full,
        gate_full,
    ) = gathered
    inputs = tokens[0].astype(jnp.float32)
    length = inputs.shape[0]
    norm_gain = norm_full.astype(jnp.float32)
    scale_in = lax.rsqrt(jnp.mean(inputs * inputs, axis=-1, keepdims=True) + EPSILON)
    normed = (inputs * scale_in * norm_gain).astype(jnp.bfloat16)
    projected = jnp.dot(normed, w_in_full, preferred_element_type=jnp.float32).astype(jnp.bfloat16)
    gate_z = projected[:, :DI].astype(jnp.float32)
    conv_in = projected[:, DI : DI + CHAN]
    dt_raw = projected[:, DI + CHAN :].astype(jnp.float32)
    first_row = lax.axis_index("seq") * length
    id_row = jnp.concatenate([jnp.full((CONV - 1,), -1, jnp.int32), segment_ids[0]], axis=0)
    ids_pad = lax.dynamic_slice_in_dim(id_row, first_row, length + CONV - 1)
    ids_own = ids_pad[CONV - 1 :]
    left_edge = passed_along(conv_in[length - (CONV - 1) :], "seq", 1)
    padded = jnp.concatenate([left_edge, conv_in], axis=0).astype(jnp.float32)
    kernel = conv_full.astype(jnp.float32)
    conv_out = jnp.zeros((length, CHAN), jnp.float32) + bias_full.astype(jnp.float32)
    same_docs = []
    for offset in range(CONV):
        same_doc = (ids_pad[offset : offset + length] == ids_own).astype(jnp.float32)
        same_docs.append(same_doc)
        conv_out = conv_out + kernel[offset] * padded[offset : offset + length] * same_doc[:, None]
    activated = jax.nn.silu(conv_out)
    blocks = length // SPAN
    x_heads = activated[:, :DI].reshape(blocks, SPAN, HEADS, HEADDIM)
    b_rows = activated[:, DI : DI + STATE].reshape(blocks, SPAN, STATE)
    c_rows = activated[:, DI + STATE :].reshape(blocks, SPAN, STATE)
    dt_bias_f = dt_bias_full.astype(jnp.float32)
    decay_rate = jnp.exp(a_log_full.astype(jnp.float32))
    step_flat = jax.nn.softplus(dt_raw + dt_bias_f)
    step_size = step_flat.reshape(blocks, SPAN, HEADS)
    log_decay = (-step_flat * decay_rate).reshape(blocks, SPAN, HEADS)
    ids_blocks = ids_own.reshape(blocks, SPAN)
    before_ids = ids_pad[CONV - 2 : CONV - 2 + length : SPAN]
    causal_mask, keep_flag, same_last = block_masks(ids_blocks, before_ids)

    def state_part(heads_in, rows_b, steps_in, decay_in):
        return local_states(heads_in, rows_b, steps_in, decay_in, same_last, keep_flag)

    (fresh_state, passing, total_state, total_decay), state_pull = jax.vjp(
        state_part, x_heads, b_rows, step_size, log_decay
    )

    def pass_forward(turn_index, received):
        return passed_along(
            (total_state + total_decay[:, None, None] * received).astype(jnp.bfloat16), "seq", 1
        ).astype(jnp.float32)

    incoming = lax.fori_loop(0, lax.axis_size("seq") - 1, pass_forward, jnp.zeros_like(total_state))

    def output_part(
        heads_in, rows_b, rows_c, steps_in, decay_in, fresh_in, passing_in, incoming_in
    ):
        return local_output(
            heads_in, rows_b, rows_c, steps_in, decay_in, incoming_in, causal_mask, keep_flag
        )

    ssd_out, output_pull = jax.vjp(
        output_part, x_heads, b_rows, c_rows, step_size, log_decay, fresh_state, passing, incoming
    )
    skip_heads = skip_full.astype(jnp.float32)
    y_full = (ssd_out + skip_heads[:, None] * x_heads).reshape(length, DI)
    silu_z = jax.nn.silu(gate_z)
    gated = y_full * silu_z
    scale_out = lax.rsqrt(jnp.mean(gated * gated, axis=-1, keepdims=True) + EPSILON)
    gate_gain = gate_full.astype(jnp.float32)
    normed_out = (gated * scale_out * gate_gain).astype(jnp.bfloat16)
    branch = jnp.dot(normed_out, w_out_full, preferred_element_type=jnp.float32)
    layer_out = (inputs + branch).astype(jnp.bfloat16)[None]
    grad_out = cotangent[0]
    d_w_out = lax.dot_general(
        normed_out, grad_out, (((0,), (0,)), ((), ())), preferred_element_type=jnp.float32
    )
    d_normed_out = lax.dot_general(
        grad_out, w_out_full, (((1,), (1,)), ((), ())), preferred_element_type=jnp.float32
    )
    d_gate_w = jnp.sum(d_normed_out * gated * scale_out, axis=0)
    along_out = d_normed_out * gate_gain
    cube_out = scale_out * scale_out * scale_out
    d_gated = scale_out * along_out - gated * cube_out * jnp.mean(
        along_out * gated, axis=-1, keepdims=True
    )
    d_y = d_gated * silu_z
    sig_z = jax.nn.sigmoid(gate_z)
    d_gate_z = d_gated * y_full * sig_z * (1.0 + gate_z * (1.0 - sig_z))
    d_ssd = d_y.reshape(blocks, SPAN, HEADS, HEADDIM)
    d_skip_grad = jnp.sum(d_ssd * x_heads, axis=(0, 1, 3))
    dx_out, db_out, dc_out, dstep_out, ddecay_out, d_fresh, d_passing, d_incoming = output_pull(
        d_ssd
    )

    def pass_backward(turn_index, received):
        return passed_along(d_incoming + total_decay[:, None, None] * received, "seq", -1)

    d_total = lax.fori_loop(0, lax.axis_size("seq") - 1, pass_backward, jnp.zeros_like(d_incoming))
    d_total_decay = jnp.sum(d_total * incoming, axis=(1, 2))
    dx_state, db_state, dstep_state, ddecay_state = state_pull(
        (d_fresh, d_passing, d_total, d_total_decay)
    )
    d_x = dx_out + dx_state + skip_heads[:, None] * d_ssd
    d_b = db_out + db_state
    d_log = (ddecay_out + ddecay_state).reshape(length, HEADS)
    d_step = (dstep_out + dstep_state).reshape(length, HEADS) - d_log * decay_rate
    d_a_log = -jnp.sum(d_log * step_flat, axis=0) * decay_rate
    d_dt_raw = d_step * jax.nn.sigmoid(dt_raw + dt_bias_f)
    d_dt_bias = jnp.sum(d_dt_raw, axis=0)
    d_act = jnp.concatenate(
        [d_x.reshape(length, DI), d_b.reshape(length, STATE), dc_out.reshape(length, STATE)], axis=1
    )
    sig_conv = jax.nn.sigmoid(conv_out)
    d_conv = d_act * sig_conv * (1.0 + conv_out * (1.0 - sig_conv))
    d_conv_b = jnp.sum(d_conv, axis=0)
    kernel_rows = []
    d_padded = jnp.zeros((length + CONV - 1, CHAN), jnp.float32)
    for offset in range(CONV):
        masked = d_conv * same_docs[offset][:, None]
        kernel_rows.append(jnp.sum(masked * padded[offset : offset + length], axis=0))
        d_padded = d_padded + jnp.pad(
            kernel[offset] * masked, ((offset, CONV - 1 - offset), (0, 0))
        )
    d_kernel = jnp.stack(kernel_rows)
    d_edge = passed_along(shortened(d_padded[: CONV - 1]), "seq", -1)
    d_conv_in = d_padded[CONV - 1 :] + jnp.pad(d_edge, ((length - (CONV - 1), 0), (0, 0)))
    d_projected = jnp.concatenate([d_gate_z, d_conv_in, d_dt_raw], axis=1).astype(jnp.bfloat16)
    d_normed = lax.dot_general(
        d_projected, w_in_full, (((1,), (1,)), ((), ())), preferred_element_type=jnp.float32
    )
    d_norm_w = jnp.sum(d_normed * inputs * scale_in, axis=0)
    along_in = d_normed * norm_gain
    cube_in = scale_in * scale_in * scale_in
    d_inputs = (
        scale_in * along_in
        - inputs * cube_in * jnp.mean(along_in * inputs, axis=-1, keepdims=True)
        + grad_out.astype(jnp.float32)
    )
    d_w_in = lax.dot_general(
        normed, d_projected, (((0,), (0,)), ((), ())), preferred_element_type=jnp.float32
    )
    weight_grads = (
        d_w_in,
        d_w_out,
        d_kernel,
        d_conv_b,
        d_a_log,
        d_dt_bias,
        d_skip_grad,
        d_norm_w,
        d_gate_w,
    )
    shares = tuple(
        (
            lax.psum_scatter(weight_grads[0], "fsdp", scatter_dimension=0, tiled=True),
            lax.psum_scatter(weight_grads[1], "fsdp", scatter_dimension=0, tiled=True),
            lax.psum_scatter(weight_grads[2], "fsdp", scatter_dimension=1, tiled=True),
            lax.psum_scatter(weight_grads[3], "fsdp", scatter_dimension=0, tiled=True),
            lax.psum_scatter(weight_grads[4], "fsdp", scatter_dimension=0, tiled=True),
            lax.psum_scatter(weight_grads[5], "fsdp", scatter_dimension=0, tiled=True),
            lax.psum_scatter(weight_grads[6], "fsdp", scatter_dimension=0, tiled=True),
            lax.psum_scatter(weight_grads[7], "fsdp", scatter_dimension=0, tiled=True),
            lax.psum_scatter(weight_grads[8], "fsdp", scatter_dimension=0, tiled=True),
        )
    )
    totals = lax.psum(shares, "seq")
    return (layer_out, d_inputs[None]) + tuple(totals)


F32 = jnp.float32
BF = jnp.bfloat16
BLK = 256
TEAM = 8
HPD = HEADS // TEAM
CH = HPD * HEADDIM
NZ, NX, NB, ND = CH, CH, 2 * STATE, 64
COLS = NZ + NX + NB + ND
REST = NX + NB + ND
CONVC = NX + NB
TAIL = CONV - 1


def dot(a, b):
    return lax.dot_general(a, b, (((1,), (0,)), ((), ())), preferred_element_type=F32)


def dot_nt(a, b):
    return lax.dot_general(a, b, (((1,), (1,)), ((), ())), preferred_element_type=F32)


def dot_tn(a, b):
    return lax.dot_general(a, b, (((0,), (0,)), ((), ())), preferred_element_type=F32)


def dot_exact(a, b):
    high = b.astype(BF)
    left = b - high.astype(F32)
    middle = left.astype(BF)
    low = (left - middle.astype(F32)).astype(BF)
    n = b.shape[1]
    p = dot(a.astype(BF), jnp.concatenate([high, middle, low], axis=1))
    return p[:, :n] + p[:, n : 2 * n] + p[:, 2 * n :]


def iota(shape, dim):
    return lax.broadcasted_iota(jnp.int32, shape, dim)


def split_dot(a, b):
    high = a.astype(BF)
    low = (a - high.astype(F32)).astype(BF)
    return dot(high, b) + dot(low, b)


def spread():
    return (iota((128, CH), 1) // HEADDIM == iota((128, CH), 0)).astype(BF)


def gather_heads():
    return (iota((CH, 128), 0) // HEADDIM == iota((CH, 128), 1)).astype(BF)


def lower_tri():
    return (iota((BLK, BLK), 0) >= iota((BLK, BLK), 1)).astype(F32)


def softplus(v):
    return jnp.maximum(v, 0.0) + jnp.log1p(jnp.exp(-jnp.abs(v)))


def sigmoid(v):
    return 1.0 / (1.0 + jnp.exp(-v))


def conv_taps(cbuf, cw, tok):
    out = cw[CONV : CONV + 1, :] + cw[CONV - 1 : CONV, :] * cbuf[8 : 8 + BLK, :]
    for back in range(1, CONV):
        term = cw[CONV - 1 - back : CONV - back, :] * cbuf[8 - back : 8 - back + BLK, :]
        out = out + term * tok[:, back : back + 1]
    return out


def pair_select(left, right):
    return jnp.where(iota(left.shape, 1) % 128 < HEADDIM, left, right)


def head_of(slot, chip, core):
    first = 12 * slot + 3 * chip + 2 * core
    second = 12 * (core + 2 * (slot - 4)) + 3 * chip + 1
    return first, second


def pick_heads():
    seq = lax.axis_index("seq")
    chip, core = lax.div(seq, 2), lax.rem(seq, 2)
    slot = iota((128, 128), 1)
    first, second = head_of(slot, chip, core)
    head = jnp.where(slot < 4, first, jnp.where(slot < HPD, second, -1))
    return (iota((128, 128), 0) == head).astype(BF)


def own_heads(par, dt_cols):
    pick = pick_heads()
    pair = jnp.concatenate([par[5:6, CH : CH + 128], par[5:6, CH + 128 :], jnp.zeros((6, 128), F32)], axis=0)
    pair = dot(pair.astype(BF), pick)
    wide = jnp.concatenate([dt_cols, jnp.zeros((BLK, 128 - ND), BF)], axis=1)
    return jnp.exp(pair[1:2, :]), dot(wide, pick) + pair[0:1, :], iota((BLK, 128), 1) < HPD, pick


def norm_gain(par):
    return jnp.concatenate([par[7 + i : 8 + i, :CH] for i in range(D // CH)], axis=1)


def row_sum(q):
    high = q.astype(BF)
    low = (q - high.astype(F32)).astype(BF)
    ones = jnp.ones((8, q.shape[1]), BF)
    return (dot_nt(ones, high) + dot_nt(ones, low))[0:1, :]


def scan_forward(j, nrm, w_v, par, tok, idr, cbuf, state, projc_ref, st_ref, ssd_v):
    rows = pl.ds(pl.multiple_of(BLK * j, BLK), BLK)
    proj = dot_nt(nrm, w_v[NZ:, :]).astype(BF)
    projc_ref[...] = proj
    cbuf[8 : 8 + BLK, :] = proj[:, :CONVC].astype(F32)
    conv_out = conv_taps(cbuf, par, tok)
    cbuf[0:8, :] = cbuf[BLK : BLK + 8, :]
    act = conv_out * sigmoid(conv_out)
    x = act[:, :CH]
    bm = act[:, CH : CH + STATE].astype(BF)
    cm = act[:, CH + STATE :].astype(BF)
    rate, dt_in, own, pick = own_heads(par, proj[:, CONVC:])
    step = jnp.where(own, softplus(dt_in), 0.0)
    cum = dot_exact(lower_tri(), -step * rate)
    cum_t = cum.T
    mask = (iota((BLK, BLK), 0) >= iota((BLK, BLK), 1)) & (tok[:, 0:1] == idr)
    gm = jnp.where(mask, dot_nt(cm, bm), 0.0)
    ex = spread()
    xs = (x * split_dot(step, ex)).astype(BF)
    parts = []
    for pair in range(HPD // 2):
        xp = xs[:, 128 * pair : 128 * pair + 128]
        both = []
        for h in (2 * pair, 2 * pair + 1):
            decay = jnp.exp(jnp.minimum(cum[:, h : h + 1] - cum_t[h : h + 1, :], 0.0))
            both.append(dot((gm * decay).astype(BF), xp))
        parts.append(pair_select(*both))
    inner = jnp.concatenate(parts, axis=1)
    old = state[...]
    st_ref[0] = old
    keep = tok[:, 7:8]
    carried = split_dot(keep * jnp.exp(cum), ex) * dot(cm, old.astype(BF))
    last = cum[BLK - 1 : BLK, :]
    weights = jnp.exp(last - cum) * step * tok[:, 8:9]
    through = split_dot(jnp.broadcast_to(keep[BLK - 1 :, :] * jnp.exp(last), (8, 128)), ex)[0:1, :]
    state[...] = dot_tn(bm, (x * split_dot(weights, ex)).astype(BF)) + through * old
    ssd_v[rows, :] = inner + carried + par[6:7, :CH] * x


def gate_forward(j, nrm_v, g_v, w_v, wo_v, par, ssd_v, projz_ref, ssd_ref, dno_ref, br_ref, stat_v):
    rows = pl.ds(pl.multiple_of(BLK * j, BLK), BLK)
    projz = dot_nt(nrm_v[rows, :], w_v[:NZ, :]).astype(BF)
    projz_ref[...] = projz
    ssd = ssd_v[rows, :]
    ssd_ref[...] = ssd
    z = projz.astype(F32)
    gate_w = par[5:6, :CH]
    gated = ssd * (z * sigmoid(z))
    br_ref[...] = dot((gated * gate_w).astype(BF), wo_v[...]).astype(BF)
    dno = dot_nt(g_v[rows, :], wo_v[...])
    dno_ref[...] = dno
    stat_v[pl.ds(j, 1), 0:BLK] = row_sum(gated * gated)
    stat_v[pl.ds(j, 1), BLK : 2 * BLK] = row_sum(dno * gate_w * gated)


def gate_backward(j, z, ssd, dno, stat, gate_w, not_v, dy_v, dz_v, dzt_v, small_v):
    rows = pl.ds(pl.multiple_of(BLK * j, BLK), BLK)
    sig_z = sigmoid(z)
    silu_z = z * sig_z
    stat = jnp.where(iota((128, BLK), 0) == 0, stat[:, :BLK], stat[:, BLK:]).T
    s2 = lax.rsqrt(stat[:, 0:1] * (1.0 / DI) + EPSILON)
    mean_ag = stat[:, 1:2] * (1.0 / DI)
    gated = ssd * silu_z
    gs = gated * s2
    not_v[:, rows] = (gs * gate_w).T.astype(BF)
    d_gated = s2 * (dno * gate_w) - gated * (s2 * s2 * s2 * mean_ag)
    dy_v[rows, :] = d_gated * silu_z
    dz = d_gated * ssd * sig_z * (1.0 + z * (1.0 - sig_z))
    dz_v[rows, :] = dz.astype(BF)
    dzt_v[:, rows] = dz.T.astype(BF)
    small_v[5:6, :CH] += jnp.sum(dno * gs, axis=0, keepdims=True)


def scan_backward(proj, halo, tok, idr, old, par, dy, cbuf, dcbuf, dstate, small_v):
    cbuf[0:8, :] = halo[8:16, :CONVC].astype(F32)
    cbuf[8 : 8 + BLK, :] = proj[:, :CONVC].astype(F32)
    conv_out = conv_taps(cbuf, par, tok)
    sig_c = sigmoid(conv_out)
    act = conv_out * sig_c
    x = act[:, :CH]
    bm = act[:, CH : CH + STATE].astype(BF)
    cm_f = act[:, CH + STATE :]
    cm = cm_f.astype(BF)
    rate, dt_in, own, pick = own_heads(par, proj[:, CONVC:])
    step = jnp.where(own, softplus(dt_in), 0.0)
    cum = dot_exact(lower_tri(), -step * rate)
    cum_t = cum.T
    mask = (iota((BLK, BLK), 0) >= iota((BLK, BLK), 1)) & (tok[:, 0:1] == idr)
    gm = jnp.where(mask, dot_nt(cm, bm), 0.0)
    ex = spread()
    gh = gather_heads()
    step_x = split_dot(step, ex)
    xs = (x * step_x).astype(BF)
    dyb = dy.astype(BF)
    dyt = dy.T.astype(BF)
    lane = iota((BLK, 128), 1)
    dg = jnp.zeros((BLK, BLK), F32)
    row_sums = jnp.zeros((BLK, 128), F32)
    col_sums = []
    e_rows = []
    for h in range(HPD):
        pair = h // 2
        decay = jnp.exp(jnp.minimum(cum[:, h : h + 1] - cum_t[h : h + 1, :], 0.0))
        mixed = gm * decay
        half = jnp.where((lane < HEADDIM) == (h % 2 == 0), dyb[:, 128 * pair : 128 * pair + 128], 0)
        dms = dot_nt(half.astype(BF), xs[:, 128 * pair : 128 * pair + 128])
        product = dms * mixed
        row_sums = jnp.where(lane == h, jnp.sum(product, axis=1, keepdims=True), row_sums)
        col_sums.append(jnp.sum(product, axis=0, keepdims=True))
        dg = dg + dms * decay
        e_rows.append(dot(dyt[HEADDIM * h : HEADDIM * h + HEADDIM, :], mixed.astype(BF)))
    dg = jnp.where(mask, dg, 0.0).astype(BF)
    e = jnp.concatenate(e_rows, axis=0).T
    col_sums.append(jnp.zeros((128 - HPD, BLK), F32))
    col = jnp.concatenate(col_sums, axis=0).T
    keep = tok[:, 7:8]
    old_b = old.astype(BF)
    dnew = dstate[...]
    dnew_b = dnew.astype(BF)
    carry_x = split_dot(keep * jnp.exp(cum), ex)
    dyk_f = dy * carry_x
    dyk = dyk_f.astype(BF)
    carried = dot(cm, old_b)
    last = cum[BLK - 1 : BLK, :]
    fade = jnp.exp(last - cum) * tok[:, 8:9]
    weights = fade * step
    weights_x = split_dot(weights, ex)
    zt = dot(bm, dnew_b)
    xw = (x * weights_x).astype(BF)
    through = keep[BLK - 1 :, :] * jnp.exp(last)
    through_x = split_dot(jnp.broadcast_to(through, (8, 128)), ex)[0:1, :]
    k_term = split_dot(dyk_f * carried, gh)
    r_term = split_dot(x * zt, gh)
    q_term = split_dot(x * e, gh)
    pass_term = jnp.sum(old * dnew, axis=0, keepdims=True) * through_x
    pass_h = split_dot(jnp.broadcast_to(pass_term, (8, CH)), gh)[0:1, :]
    wr = weights * r_term
    d_cum = row_sums - col + k_term - wr
    d_last = jnp.sum(wr, axis=0, keepdims=True) + pass_h
    d_cum = d_cum + jnp.where(iota((BLK, 128), 0) == BLK - 1, d_last, 0.0)
    upper = (iota((BLK, BLK), 0) <= iota((BLK, BLK), 1)).astype(F32)
    d_log = dot_exact(upper, d_cum)
    d_step = q_term + fade * r_term - d_log * rate
    d_a = -jnp.sum(d_log * step, axis=0, keepdims=True) * rate
    d_dt = jnp.where(own, d_step * sigmoid(dt_in), 0.0)
    d_skip = split_dot(jnp.broadcast_to(jnp.sum(dy * x, axis=0, keepdims=True), (8, CH)), gh)[0:1, :]
    d_skip = jnp.where(own[0:1, :], d_skip, 0.0)
    heads = jnp.concatenate(
        [d_a, jnp.sum(d_dt, axis=0, keepdims=True), d_skip, jnp.zeros((5, 128), F32)], axis=0)
    high = heads.astype(BF)
    heads = dot_nt(high, pick) + dot_nt((heads - high.astype(F32)).astype(BF), pick)
    d_dt = dot_nt(d_dt.astype(BF), pick)
    dstate[...] = dot_tn(cm, dyk) + through_x * dnew
    dx = step_x * e + weights_x * zt + par[6:7, :CH] * dy
    dc = dot(dg, bm) + dot_nt(dyk, old_b)
    db = dot(cm_f.T.astype(BF), dg).T + dot_nt(xw, dnew_b)
    d_act = jnp.concatenate([dx, db, dc], axis=1)
    d_conv = d_act * (sig_c * (1.0 + conv_out * (1.0 - sig_c)))
    dcbuf[0:BLK, :] = d_conv
    d_in = par[CONV - 1 : CONV, :] * d_conv
    cg = [None] * CONV
    cg[CONV - 1] = jnp.sum(d_conv * cbuf[8 : 8 + BLK, :], axis=0, keepdims=True)
    for back in range(1, CONV):
        tap = CONV - 1 - back
        cg[tap] = jnp.sum(
            d_conv * (cbuf[8 - back : 8 - back + BLK, :] * tok[:, back : back + 1]),
            axis=0, keepdims=True,
        )
        d_in = d_in + par[tap : tap + 1, :] * (
            dcbuf[back : back + BLK, :] * tok[:, 3 + back : 4 + back]
        )
    dcbuf[BLK : BLK + 8, :] = dcbuf[0:8, :]
    small_v[0:CONV, :] += jnp.concatenate(cg, axis=0)
    small_v[CONV : CONV + 1, :] += jnp.sum(d_conv, axis=0, keepdims=True)
    small_v[5:6, CH:] += jnp.concatenate([heads[0:1, :], heads[1:2, :]], axis=1)
    small_v[6:7, CH : CH + 128] += heads[2:3, :]
    return jnp.concatenate([d_in, d_dt[:, :ND]], axis=1)


def id_row(ids_ref, j):
    return ids_ref[0:1, pl.ds(pl.multiple_of(BLK * j, BLK), BLK)].astype(F32)


def token_info(ids_ref, j, blocks):
    row = id_row(ids_ref, j)
    left = jnp.where(j > 0, id_row(ids_ref, jnp.maximum(j - 1, 0)), -1.0)
    right = jnp.where(j < blocks - 1, id_row(ids_ref, jnp.minimum(j + 1, blocks - 1)), -2.0)
    lane = iota((1, BLK), 1)
    wide = lambda a: jnp.broadcast_to(a, (8, BLK))
    rows = [row]
    for back in range(1, CONV):
        shifted = jnp.where(lane < back, pltpu.roll(wide(left), back, 1)[0:1], pltpu.roll(wide(row), back, 1)[0:1])
        rows.append((shifted == row).astype(F32))
    for ahead in range(1, CONV):
        turn = BLK - ahead
        shifted = jnp.where(lane >= turn, pltpu.roll(wide(right), turn, 1)[0:1], pltpu.roll(wide(row), turn, 1)[0:1])
        rows.append((shifted == row).astype(F32))
    rows.append((row == left[:, BLK - 1 :]).astype(F32))
    rows.append((row == row[:, BLK - 1 :]).astype(F32))
    rows.append(jnp.zeros((128 - len(rows), BLK), F32))
    return row, jnp.concatenate(rows, axis=0).T


def pack_small(convw, convb, alog, dtb, dskip, normw, gatew, chip, core, z):
    def channel(m):
        slot = m // HEADDIM
        first, second = head_of(slot, chip, core)
        return jnp.where(slot < 4, first, second) * HEADDIM + m % HEADDIM

    row = lambda a: a.astype(F32).reshape(1, a.shape[0])
    pad = lambda a: jnp.concatenate([row(a), jnp.zeros((1, 128 - HEADS // DEPTH), F32)], axis=1)
    heads = jnp.concatenate([pad(dtb), pad(alog), pad(dskip), jnp.zeros((5, 128), F32)], axis=0).astype(BF)
    m = iota((CHAN // DEPTH, CONVC), 1)
    want = jnp.where(m < CH, channel(m), DI + m - CH)
    chosen = (iota((CHAN // DEPTH, CONVC), 0) + z * (CHAN // DEPTH) == want).astype(BF)
    conv = jnp.concatenate([convw.astype(F32), row(convb), jnp.zeros((3, CHAN // DEPTH), F32)], axis=0)
    conv = dot(conv.astype(BF), chosen)
    n = DI // DEPTH
    chosen = (iota((n, CH), 0) + z * n == channel(iota((n, CH), 1))).astype(BF)
    gate = dot(jnp.broadcast_to(row(gatew), (8, n)).astype(BF), chosen)[0:1]
    n = HEADS // DEPTH
    k = iota((128, CH), 0)
    chosen = ((k < n) & (k + z * n == channel(iota((128, CH), 1)) // HEADDIM)).astype(BF)
    skip = dot(heads, chosen)[2:3]
    k = iota((128, 128), 0)
    chosen = ((k < n) & (k + z * n == iota((128, 128), 1))).astype(BF)
    heads = dot(heads, chosen)
    gain = jnp.where(iota((DEPTH, CH), 0) == z, jnp.broadcast_to(row(normw), (DEPTH, CH)), 0.0)
    return jnp.concatenate([
        conv[0:5],
        jnp.concatenate([gate, heads[0:1], heads[1:2]], axis=1),
        jnp.concatenate([skip, jnp.zeros((1, NB), F32)], axis=1),
        jnp.concatenate([gain, jnp.zeros((DEPTH, NB), F32)], axis=1),
        jnp.zeros((5, CONVC), F32)], axis=0).astype(BF)


CHIPS = TEAM // 2
KROWS = D // DEPTH
BCD = NB + ND
HALF = BCD // 2


def places():
    seq = lax.axis_index("seq")
    return seq, lax.div(seq, 2), lax.rem(seq, 2), lax.axis_index("fsdp")


def neighbours(chip):
    return [chip, chip + 1 - 2 * lax.rem(chip, 2), lax.rem(chip + 2, CHIPS), CHIPS - 1 - chip]


def send(src, dst, send_sem, recv_sem, device):
    return pltpu.make_async_remote_copy(
        src_ref=src, dst_ref=dst, send_sem=send_sem, recv_sem=recv_sem,
        device_id=device, device_id_type=pl.DeviceIdType.MESH,
    )


def greet(devices):
    barrier = pltpu.get_barrier_semaphore()
    for device in devices:
        pl.semaphore_signal(
            barrier, inc=1, device_id=device, device_id_type=pl.DeviceIdType.MESH
        )
    pl.semaphore_wait(barrier, len(devices))


def forward_kernel(
    tok_ref, cot_ref, win_ref, wout_ref, ids_ref, convw_ref, convb_ref, alog_ref, dtb_ref, skip_ref, normw_ref, gatew_ref,
    nrm_ref, projc_ref, projz_ref, st_ref, ssd_ref, dno_ref, br_ref, info_ref, stat_ref, par_ref, w_ref, g_ref,
    u_v, g_v, w_v, wo_v, small_v, smalls, ssd_v, cbuf, state, stat_v, stat_in,
    loc, t_send, t_recv, y_send, y_recv, f_send, f_recv, z_send, z_recv, b_send, b_recv, s_send, s_recv, r_send, r_recv,
):
    i = pl.program_id(0)
    seq, chip, core, z = places()
    sib = {"seq": 2 * chip + 1 - core}
    near = neighbours(chip)
    peer = lambda k: {"seq": 2 * near[k] + core}
    under = lambda k: {"fsdp": lax.rem(z + k, DEPTH)}
    around = lambda k: {"seq": lax.rem(seq + k, TEAM)}
    block = lambda s: pl.ds(pl.multiple_of(BLK * s, BLK), BLK)
    lanes = lambda o: pl.ds(pl.multiple_of(KROWS * o, KROWS), KROWS)
    half = pl.ds(pl.multiple_of(NZ + NX + HALF * core, 16), HALF)
    has = [z < DEPTH - 1, z > 0]
    heads = [head_of(n, chip, core)[n // 4] for n in range(HPD)]
    piece = lambda n: pl.ds(pl.multiple_of(HEADDIM * n, HEADDIM), HEADDIM)

    def token_copy(n, k):
        src, dst = ((tok_ref, u_v), (cot_ref, g_v))[n]
        return send(src, dst.at[block(seq)], t_send.at[n, k], t_recv.at[n, k], sib if k == 0 else peer(k))

    def token_part(n, k, h):
        return (u_v, g_v)[n].at[pl.ds(pl.multiple_of(BLK * (2 * near[k] + core) + h * (BLK // 2), BLK // 2), BLK // 2)]

    def token_relay(n, h):
        part = token_part(n, 1 + h, h)
        return send(part, part, y_send.at[n, h], y_recv.at[n, h], peer(2 - h))

    def token_next(n, k):
        if k < 3:
            ref = (u_v, g_v)[n].at[block(2 * near[k] + core)]
        else:
            ref = token_part(n, 3, k - 3)
        return send(ref, ref, f_send.at[n, k], f_recv.at[n, k], sib)

    def token_start(n):
        for k in range(3):
            token_copy(n, k).start()

    def token_turn(n):
        for k in (1, 2):
            token_copy(n, k).wait_recv()
            token_relay(n, k - 1).start()
            token_next(n, k).start()

    def token_end(n):
        for h in range(2):
            token_relay(n, h).wait_recv()
            token_next(n, 3 + h).start()
        token_copy(n, 0).wait_recv()
        for k in range(1, 5):
            token_next(n, k).wait()
        for h in range(2):
            token_relay(n, h).wait_send()

    def place(p, o):
        if p < 3:
            return w_v.at[(pl.ds(NZ, NX), half, pl.ds(0, NZ))[p], lanes(o)]
        return wo_v.at[piece(o if p == 3 else DEPTH + lax.div(o, 2))]

    def hop(p, side, dist):
        o = z - dist if side == 0 else z + dist
        there = {"fsdp": z + 1} if side == 0 else {"fsdp": z - 1}
        return send(place(p, o), place(p, o), z_send.at[p, side, dist], z_recv.at[p, side, dist], there)

    def got(p, side, dist):
        o = z - dist - 1 if side == 0 else z + dist + 1
        there = {"fsdp": z + 1} if side == 0 else {"fsdp": z - 1}
        return send(place(p, o), place(p, o), z_send.at[p, side, dist], z_recv.at[p, side, dist], there)

    def share(side, dist):
        o = z - dist - 1 if side == 0 else z + dist + 1
        return send(place(1, o), place(1, o), b_send.at[side, dist], b_recv.at[side, dist], sib)

    def exists(p, side, hops):
        o = z - hops if side == 0 else z + hops
        there = (o >= 0) if side == 0 else (o < DEPTH)
        return there & (lax.rem(o + DEPTH, 2) == core) if p == 4 else there

    def small_copy(k):
        return send(small_v, smalls.at[k - 1], s_send.at[k], s_recv.at[k], under(k))

    def stat_copy(k):
        return send(stat_v, stat_in.at[k], r_send.at[k], r_recv.at[k], around(k))

    def local_copies():
        pairs = [(tok_ref, u_v.at[block(seq)]), (cot_ref, g_v.at[block(seq)])]
        return [pltpu.make_async_copy(src, dst, loc.at[n]) for n, (src, dst) in enumerate(pairs)]

    def own_weights():
        pairs = [(win_ref.at[pl.ds(2 * DI, WIDTH - 2 * DI)], w_v.at[pl.ds(NZ + NX, WIDTH - 2 * DI), lanes(z)], 3)]
        for n in range(HPD):
            row = HEADDIM * heads[n]
            pairs.append((win_ref.at[pl.ds(pl.multiple_of(row, HEADDIM), HEADDIM)],
                          w_v.at[piece(n), lanes(z)], 4 + n))
            pairs.append((win_ref.at[pl.ds(pl.multiple_of(DI + row, HEADDIM), HEADDIM)],
                          w_v.at[piece(HPD + n), lanes(z)], 10 + n))
        pairs.append((wout_ref.at[piece(3 * chip + 2 * core)], place(3, z), 16))
        return [pltpu.make_async_copy(src, dst, loc.at[n]) for src, dst, n in pairs]

    def own_extra():
        return pltpu.make_async_copy(wout_ref.at[piece(3 * chip + 1)], place(4, z), loc.at[17])

    def pass_on(parts, dist):
        for p in parts:
            for side in range(2):

                @pl.when(exists(p, side, dist + 1))
                def _():
                    got(p, side, dist).wait_recv()
                    if p == 1:
                        share(side, dist).start()

                if dist < DEPTH - 2:

                    @pl.when(exists(p, side, dist + 1) & has[side])
                    def _():
                        hop(p, side, dist + 1).start()

    def start_own(parts):
        for p in parts:
            for side in range(2):

                @pl.when(exists(p, side, 0) & has[side])
                def _():
                    hop(p, side, 0).start()

    @pl.when(i == 0)
    def _():
        greet([around(k) for k in range(1, TEAM)] + [under(k) for k in range(1, DEPTH)])
        token_start(0)
        for copy in own_weights() + local_copies():
            copy.start()

        @pl.when(lax.rem(z, 2) == core)
        def _():
            own_extra().start()

        w_v[NZ + NX + WIDTH - 2 * DI :, lanes(z)] = jnp.zeros((BCD - (WIDTH - 2 * DI), KROWS), BF)
        for copy in own_weights():
            copy.wait()
        start_own((0, 1))
        small_v[...] = pack_small(convw_ref[...], convb_ref[...], alog_ref[...], dtb_ref[...], skip_ref[...],
                                  normw_ref[...], gatew_ref[...], chip, core, z)
        for k in range(1, DEPTH):
            small_copy(k).start()
        state[...] = jnp.zeros_like(state)
        cbuf[0:8, :] = jnp.zeros((8, CONVC), F32)
        pass_on((0, 1), 0)
        token_turn(0)
        token_start(1)
        pass_on((0, 1), 1)
        start_own((2,))
        token_end(0)
        pass_on((0, 1), 2)
        for k in range(1, DEPTH):
            small_copy(k).wait()
        for copy in local_copies():
            copy.wait()
        for side in range(2):
            for dist in range(DEPTH - 1):

                @pl.when(exists(1, side, dist + 1))
                def _():
                    share(side, dist).wait()

        total = small_v[...].astype(F32)
        for k in range(1, DEPTH):
            total = total + smalls[k - 1].astype(F32)
        par_ref[...] = total

    @pl.when(i == 1)
    def _():
        @pl.when(lax.rem(z, 2) == core)
        def _():
            own_extra().wait()

        pass_on((2,), 0)
        start_own((3, 4))

    @pl.when(i == 3)
    def _():
        pass_on((2,), 1)

    @pl.when(i == 4)
    def _():
        token_turn(1)

    @pl.when(i == 5)
    def _():
        pass_on((3, 4), 0)

    @pl.when(i == 7)
    def _():
        pass_on((3, 4), 1)

    @pl.when(i == TEAM)
    def _():
        pass_on((2, 3, 4), 2)
        token_end(1)
        pltpu.make_async_copy(w_v, w_ref, loc.at[18]).start()
        pltpu.make_async_copy(g_v, g_ref, loc.at[19]).start()

    par = par_ref[...]

    @pl.when(i < TEAM)
    def _():
        u = u_v[block(i), :].astype(F32)
        scale = lax.rsqrt(jnp.mean(u * u, axis=1, keepdims=True) + EPSILON)
        nrm = (u * scale * norm_gain(par)).astype(BF)
        nrm_ref[...] = nrm
        u_v[block(i), :] = nrm
        row, info = token_info(ids_ref, i, TEAM)
        info_ref[...] = info
        scan_forward(i, nrm, w_v, par, info, row, cbuf, state,
                     projc_ref, st_ref, ssd_v)

    @pl.when(i >= TEAM)
    def _():
        gate_forward(i - TEAM, u_v, g_v, w_v, wo_v, par, ssd_v, projz_ref, ssd_ref, dno_ref,
                     br_ref, stat_v)

    @pl.when(i == 2 * TEAM - 1)
    def _():
        for k in range(1, TEAM):
            stat_copy(k).start()
        total = stat_v[...]
        for k in range(1, TEAM):
            stat_copy(k).wait_recv()
            total = total + stat_in[k]
        stat_ref[...] = total
        for k in range(1, TEAM):
            stat_copy(k).wait_send()
        for n in range(2):
            for k in range(3):
                token_copy(n, k).wait_send()
        for side in range(2):
            for dist in range(DEPTH - 1):
                for p in range(5):

                    @pl.when(exists(p, side, dist) & has[side])
                    def _():
                        hop(p, side, dist).wait_send()

        pltpu.make_async_copy(w_v, w_ref, loc.at[18]).wait()
        pltpu.make_async_copy(g_v, g_ref, loc.at[19]).wait()


def forward_call(tok, cot, win, wout, ids, small):
    n = tok.shape[0] * TEAM
    any_space = pl.BlockSpec(memory_space=pl.ANY)
    sds = jax.ShapeDtypeStruct
    dma = pltpu.SemaphoreType.DMA
    one = lambda i: jnp.minimum(i, TEAM - 1)
    two = lambda i: jnp.maximum(i - TEAM, 0)
    rows = lambda c, turn: pl.BlockSpec((BLK, c), lambda i: (turn(i), 0))
    cube = lambda a, b: pl.BlockSpec((1, a, b), lambda i: (one(i), 0, 0))
    fixed = lambda a, b: pl.BlockSpec((a, b), lambda i: (0, 0))
    return pl.pallas_call(
        forward_kernel,
        grid=(2 * TEAM,),
        in_specs=[any_space] * 4 + [
            pl.BlockSpec(a.shape, lambda i, n=a.ndim: (0,) * n, pipeline_mode=pl.Buffered(1)) for a in (ids, *small)],
        out_specs=[rows(D, one), rows(REST, one), rows(NZ, two), cube(STATE, CH), rows(CH, two),
                   rows(CH, two), rows(D, two), rows(128, one), fixed(TEAM, 2 * BLK), fixed(16, CONVC),
                   any_space, any_space],
        out_shape=[sds((n, D), BF), sds((n, REST), BF), sds((n, NZ), BF), sds((TEAM, STATE, CH), F32),
                   sds((n, CH), F32), sds((n, CH), F32), sds((n, D), BF), sds((n, 128), F32), sds((TEAM, 2 * BLK), F32),
                   sds((16, CONVC), F32), sds((COLS, D), BF), sds((n, D), BF)],
        scratch_shapes=[pltpu.VMEM((n, D), BF), pltpu.VMEM((n, D), BF), pltpu.VMEM((COLS, D), BF),
                        pltpu.VMEM((CH, D), BF), pltpu.VMEM((16, CONVC), BF), pltpu.VMEM((DEPTH - 1, 16, CONVC), BF),
                        pltpu.VMEM((n, CH), F32), pltpu.VMEM((BLK + 8, CONVC), F32),
                        pltpu.VMEM((STATE, CH), F32), pltpu.VMEM((TEAM, 2 * BLK), F32),
                        pltpu.VMEM((TEAM, TEAM, 2 * BLK), F32),
                        dma((20,)), dma((2, 3)), dma((2, 3)), dma((2, 2)), dma((2, 2)), dma((2, 5)),
                        dma((2, 5)), dma((5, 2, DEPTH - 1)), dma((5, 2, DEPTH - 1)),
                        dma((2, DEPTH - 1)), dma((2, DEPTH - 1)),
                        dma((DEPTH,)), dma((DEPTH,)), dma((TEAM,)), dma((TEAM,))],
        compiler_params=pltpu.CompilerParams(
            collective_id=0, has_side_effects=True, vmem_limit_bytes=60 << 20),
    )(tok, cot, win, wout, ids, *small)


def backward_kernel(
    tok_ref, cot_ref, nrm_ref, br_ref, w_ref, g_ref,
    projz_ref, ssd_ref, dno_ref, stat_ref, par_ref, projc_ref, halo_ref, st_ref, info_ref, ids_ref,
    out_ref, tg_ref, wig_ref, wog_ref, smalls_ref,
    nrm_v, g_v, w_v, not_v, dz_v, dzt_v, dy_v, rest_v, wig_v, wog_v, bcd_v, bcd_in,
    zz_in, zx_in, zb_in, zw_in, zs_in, zz_rel, zx_rel, zb_rel, zw_rel, gz_v, gx_v, gb_v, gw_v, gb_in, gt_v, ob_v, rb_v, in_v, rel_v,
    tok_v, cot_v, small_v, small_s, cbuf, dcbuf, dstate,
    loc, b_send, b_recv, p_send, p_recv, d_send, d_recv, q_send, q_recv, z_send, z_recv, s_send, s_recv,
    a_send, a_recv, f_send, f_recv, h_send, h_recv, free,
):
    i = pl.program_id(0)
    seq, chip, core, z = places()
    sib = {"seq": 2 * chip + 1 - core}
    near = neighbours(chip)
    peer = lambda k: {"seq": 2 * near[k] + core}
    under = lambda k: {"fsdp": lax.rem(z + k, DEPTH)}
    around = lambda k: {"seq": lax.rem(seq + k, TEAM)}
    block = lambda s: pl.ds(pl.multiple_of(BLK * s, BLK), BLK)
    lanes = lambda o: pl.ds(pl.multiple_of(KROWS * o, KROWS), KROWS)
    piece = lambda n: pl.ds(pl.multiple_of(HEADDIM * n, HEADDIM), HEADDIM)
    half = lambda c: pl.ds(pl.multiple_of(HALF * c, 16), HALF)
    extra = lambda o: lax.rem(o, 2) == core
    n_all = HEADDIM * HPD
    give = lambda c: g_v.at[block(c)]
    hold = lambda c: g_v.at[block(CHIPS + c)]

    def load(n):
        pairs = [(nrm_ref, nrm_v), (g_ref, g_v), (w_ref, w_v), (tok_ref, tok_v), (cot_ref, cot_v)]
        return pltpu.make_async_copy(pairs[n][0], pairs[n][1], loc.at[n])

    def load_own(c):
        return pltpu.make_async_copy(br_ref.at[block(2 * c + core)], ob_v.at[c], loc.at[5 + c])

    def br_pair(c):
        return send(br_ref.at[block(2 * c + 1 - core)], rb_v.at[c], b_send.at[c], b_recv.at[c], sib)

    def block_of(n, c):
        return ob_v.at[c] if n == 0 else hold(c)

    def rs(n, kind):
        h = pl.ds((0, BLK // 2, BLK // 2, 0, 0, BLK // 2)[kind], BLK // 2)
        src = block_of(n, near[(1, 1, 2, 2, 3, 3)[kind]]).at[h]
        if kind < 4:
            dst = in_v.at[n, kind // 2, h]
        else:
            dst = rel_v.at[n, 5 - kind]
        return send(src, dst, p_send.at[n, kind], p_recv.at[n, kind], peer((1, 1, 2, 2, 1, 2)[kind]))

    def rs_first(n, role):
        for kind in ((), (0,), (2,), (4, 5))[role]:
            rs(n, kind).start()

    def rs_second(n, role):
        kind, came = ((1, 5), (3, 4))[role - 1]
        rs(n, came).wait_recv()
        h = pl.ds((BLK // 2, 0)[role - 1], BLK // 2)
        ref = block_of(n, near[role]).at[h]
        ref[...] = (ref[...].astype(F32) + rel_v[n, role - 1].astype(F32)).astype(BF)
        rs(n, kind).start()

    def rs_total(n):
        for kind in range(4):
            rs(n, kind).wait_recv()
        return block_of(n, chip)[...].astype(F32) + in_v[n, 0].astype(F32) + in_v[n, 1].astype(F32)

    def dn_pair(c):
        return send(give(c), rb_v.at[c], d_send.at[c], d_recv.at[c], sib)

    mate = z + 1 - 2 * lax.rem(z, 2)
    outer = (z == 0) | (z == DEPTH - 1)
    far = lambda j: (2 + j) - lax.div(z, 2) * (1 + 2 * j)
    rest = [slice(None)] * 3 + [slice(0, HEADDIM), slice(HEADDIM, 2 * HEADDIM)]
    z_in = [zz_in, zx_in, zb_in, zw_in, zw_in]
    z_rel = [zz_rel, zx_rel, zb_rel, zw_rel, zw_rel]

    def z_part(n, o):
        if n < 2:
            return wig_v.at[:, lanes(o)]
        if n == 2:
            return bcd_v.at[half(core), lanes(o)]
        return wog_v.at[piece(o if n == 3 else DEPTH + lax.div(o, 2))]

    def z_mate(n):
        return send(z_part(n, mate), z_in[n].at[0, rest[n]], z_send.at[n, 0], z_recv.at[n, 0], {"fsdp": mate})

    def z_hand(n, j):
        return send(z_part(n, far(j)), z_rel[n].at[j, rest[n]], z_send.at[n, 2 + j], z_recv.at[n, 2 + j], {"fsdp": mate})

    def z_far(n, j):
        return send(z_part(n, far(j)), z_in[n].at[1, rest[n]], z_send.at[n, 2 + j], z_recv.at[n, 1], {"fsdp": far(j)})

    def held(n, o, also=None):
        if n == 4:
            return extra(o) if also is None else extra(o) & also
        return also

    def under_cond(cond, body):
        if cond is None:
            body()
        else:
            pl.when(cond)(body)

    def z_start(n):
        for j in (1, 0):
            under_cond(held(n, far(j), outer), lambda: z_hand(n, j).start())

    def z_start_mate(n):
        under_cond(held(n, mate), lambda: z_mate(n).start())

    def z_relay(n):
        for j in (1, 0):

            def body():
                z_hand(n, j).wait_recv()
                ref = z_part(n, far(j))
                ref[...] = (ref[...].astype(F32) + z_rel[n][j, rest[n]].astype(F32)).astype(BF)
                z_far(n, j).start()

            under_cond(held(n, far(j), jnp.logical_not(outer)), body)

    def z_total(n):
        z_mate(n).wait_recv()
        z_far(n, 0).wait_recv()
        return z_part(n, z)[...].astype(F32) + z_in[n][0, rest[n]].astype(F32) + z_in[n][1, rest[n]].astype(F32)

    def z_close(n):
        under_cond(held(n, mate), lambda: z_mate(n).wait_send())
        for j in range(2):
            under_cond(held(n, far(j)), lambda: z_far(n, j).wait_send())

    def small_copy(k):
        return send(small_v, zs_in.at[k - 1], s_send.at[k], s_recv.at[k], under(k))

    def bcd_pair():
        return send(bcd_v.at[half(1 - core)], bcd_in, h_send.at[0], h_recv.at[0], sib)

    def bcd_push(k):
        return send(gb_v, gb_in.at[k - 1], q_send.at[k], q_recv.at[k], peer(k))

    def bcd_back():
        return send(gt_v.at[core], gt_v.at[core], h_send.at[1], h_recv.at[1], sib)

    def parts(n, c, cr, h=None):
        if n < 2:
            base = n * DI // HEADDIM
            src = (gz_v, gx_v)[n]
            slots = range(HPD) if h is None else range(3 * h, 3 * h + 3)
            return [(src.at[piece(s)], wig_ref.at[piece(base + head_of(s, c, cr)[s // 4])]) for s in slots]
        if n < 4:
            row = HEADDIM * (3 * c + 2 * cr if n == 2 else 3 * c + 1)
            first, size = (0, HEADDIM) if h is None else (h * HEADDIM // 2, HEADDIM // 2)
            return [(gw_v.at[pl.ds(HEADDIM * (n - 2) + first, size)],
                     wog_ref.at[pl.ds(pl.multiple_of(row + first, HEADDIM // 2), size)])]
        if h is None:
            return [(small_s, smalls_ref.at[2 * c + cr])]
        return [(small_s.at[8 * h : 8 * h + 8], smalls_ref.at[2 * c + cr, 8 * h : 8 * h + 8])]

    def all_of(n, h=None):
        if n < 2:
            return wig_ref.at[pl.ds(n * DI, n_all if h is None else n_all // 2)]
        return parts(n, 0, 0, h)[0][1]

    def ag(n, k):
        if k < 3:
            return [send(src, dst, a_send.at[n, k], a_recv.at[n, k], sib if k == 0 else peer(k))
                    for src, dst in parts(n, chip, core)]
        return [send(dst, dst, a_send.at[n, k], a_recv.at[n, k], peer(5 - k))
                for _, dst in parts(n, near[k - 2], core, k - 3)]

    def ag_wait(n, k):
        ref = all_of(n, None if k < 3 else k - 3)
        return send(ref, ref, a_send.at[n, k], a_recv.at[n, k], sib)

    def ag_next(n, k):
        which = parts(n, near[k], core) if k < 3 else parts(n, near[3], core, k - 3)
        return [send(dst, dst, f_send.at[n, k], f_recv.at[n, k], sib) for _, dst in which]

    def ag_next_wait(n, k):
        ref = all_of(n, None if k < 3 else k - 3)
        return send(ref, ref, f_send.at[n, k], f_recv.at[n, k], sib)

    def ag_own(n):
        return [pltpu.make_async_copy(src, dst, loc.at[9 + n]) for src, dst in parts(n, chip, core)]

    def ag_own_wait(n):
        return pltpu.make_async_copy(all_of(n), all_of(n), loc.at[9 + n])

    def ag_start(n):
        for k in (1, 2, 0):
            for copy in ag(n, k):
                copy.start()
        for copy in ag_own(n):
            copy.start()

    def ag_turn(n):
        for k in (1, 2):
            ag_wait(n, k).wait_recv()
            for copy in ag(n, k + 2) + ag_next(n, k):
                copy.start()

    def ag_end(n):
        for k in (3, 4):
            ag_wait(n, k).wait_recv()
            for copy in ag_next(n, k):
                copy.start()

    def ag_close(n, sends=True, receives=True):
        if receives:
            ag_wait(n, 0).wait_recv()
            for k in range(1, 5):
                ag_next_wait(n, k).wait_recv()
        if sends:
            for k in range(5):
                ag_wait(n, k).wait_send()
            for k in range(1, 5):
                ag_next_wait(n, k).wait_send()
            ag_own_wait(n).wait()

    @pl.when(i == 0)
    def _():
        greet([around(k) for k in range(1, TEAM)] + [under(k) for k in range(1, DEPTH)])
        for c in range(CHIPS):
            br_pair(c).start()
            load_own(c).start()
        for n in range(5):
            load(n).start()
        small_v[...] = jnp.zeros_like(small_v)
        dstate[...] = jnp.zeros_like(dstate)
        dcbuf[BLK : BLK + 8, :] = jnp.zeros((8, CONVC), F32)

    @pl.when(i < TEAM)
    def _():
        gate_backward(i, projz_ref[...].astype(F32), ssd_ref[...], dno_ref[...],
                      stat_ref[pl.ds(i, 1), :], par_ref[5:6, :CH], not_v, dy_v, dz_v, dzt_v, small_v)

    @pl.when(i == 1)
    def _():
        for c in range(CHIPS):
            load_own(c).wait()
            br_pair(c).wait_recv()
            ob_v[c] = (ob_v[c].astype(F32) + rb_v[c].astype(F32)).astype(BF)
        for role in (3, 1, 2):
            rs_first(0, role)
        pl.semaphore_signal(free, inc=1, device_id=sib, device_id_type=pl.DeviceIdType.MESH)

    @pl.when(i == TEAM)
    def _():
        pl.semaphore_wait(free, 1)
        for n in range(5):
            load(n).wait()

        @pl.loop(0, D // 256)
        def _(n):
            cols = pl.ds(pl.multiple_of(256 * n, 256), 256)
            wig_v[:, cols] = dot(dzt_v[...], nrm_v[:, cols]).astype(BF)

        z_start(0)

        @pl.loop(0, D // 256)
        def _(n):
            cols = pl.ds(pl.multiple_of(256 * n, 256), 256)
            wog_v[:, cols] = dot(not_v[...], g_v[:, cols]).astype(BF)

        z_start(3)
        z_start(4)
        for n in (0, 3, 4):
            z_start_mate(n)

    def combine(c):
        dn_pair(c).wait_recv()
        hold(c)[...] = (hold(c)[...].astype(F32) + rb_v[c].astype(F32)).astype(BF)
        for role in (1, 2, 3):

            @pl.when(near[role] == c)
            def _():
                rs_first(1, role)

    def relay(c):
        for role in (1, 2):

            @pl.when(near[role] == c)
            def _():
                rs_second(1, role)

    for c in range(CHIPS - 1, 0, -1):

        @pl.when(i == TEAM + 1 + 2 * (CHIPS - c))
        def _():
            combine(c)
            if c < CHIPS - 1:
                relay(c + 1)

    @pl.when(i == TEAM + 2)
    def _():
        rs_second(0, 1)
        rs_second(0, 2)

    @pl.when(i == 2 * TEAM)
    def _():
        gz_v[...] = z_total(0).astype(BF)
        ag_start(0)

    @pl.when((i > TEAM) & (i <= 2 * TEAM))
    def _():
        j = 2 * TEAM - i
        rows = block(j)
        d_rest = scan_backward(projc_ref[...], halo_ref[...], info_ref[...], id_row(ids_ref, j), st_ref[0],
                               par_ref[...], dy_v[rows, :], cbuf, dcbuf, dstate, small_v)
        rest_v[:, rows] = d_rest.T.astype(BF)
        dn = dot(dz_v[rows, :], w_v[:NZ, :]) + dot(d_rest.astype(BF), w_v[NZ:, :])
        part = jnp.sum(dn * nrm_v[rows, :].astype(F32), axis=0, keepdims=True)
        for n in range(D // CH):
            small_v[7 + n : 8 + n, :CH] += part[:, CH * n : CH * n + CH]
        dn = dn.astype(BF)
        c = lax.div(j, 2)

        @pl.when(lax.rem(j, 2) == core)
        def _():
            hold(c)[...] = dn

        @pl.when(lax.rem(j, 2) != core)
        def _():
            give(c)[...] = dn
            dn_pair(c).start()

    @pl.when(i == 2 * TEAM - 1)
    def _():
        total = rs_total(0)
        stat = stat_ref[pl.ds(seq, 1), 0:BLK]
        stat = jnp.broadcast_to(stat, (128, BLK)).T
        s2 = lax.rsqrt(stat[:, 0:1] * (1.0 / DI) + EPSILON)
        out_ref[...] = (tok_v[...].astype(F32) + total * s2).astype(BF)

    @pl.when(i == TEAM + 4)
    def _():
        z_relay(0)

    @pl.when(i == TEAM + 6)
    def _():
        z_relay(3)
        z_relay(4)

    @pl.when(i == 2 * TEAM + 1)
    def _():
        for n in range(D // CH):
            small_v[7 + n : 8 + n, :CH] = small_v[7 + n : 8 + n, :CH] / par_ref[7 + n : 8 + n, :CH]
        for k in range(1, DEPTH):
            small_copy(k).start()
        combine(0)

        @pl.loop(0, D // 256)
        def _(n):
            cols = pl.ds(pl.multiple_of(256 * n, 256), 256)
            bcd_v[:, cols] = dot(rest_v[NX:, :], nrm_v[:, cols]).astype(BF)

        bcd_pair().start()
        relay(1)
        z_close(0)

        @pl.loop(0, D // 256)
        def _(n):
            cols = pl.ds(pl.multiple_of(256 * n, 256), 256)
            wig_v[:, cols] = dot(rest_v[:NX, :], nrm_v[:, cols]).astype(BF)

        z_start(1)
        z_start_mate(1)
        bcd_pair().wait_recv()
        bcd_v[half(core), :] = (bcd_v[half(core), :].astype(F32) + bcd_in[...].astype(F32)).astype(BF)
        z_start(2)
        z_start_mate(2)
        gw_v[0:HEADDIM, :] = z_total(3).astype(BF)
        ag_start(2)

        @pl.when(extra(z))
        def _():
            gw_v[HEADDIM:, :] = z_total(4).astype(BF)
            ag_start(3)

        relay(0)
        total = small_v[...]
        for k in range(1, DEPTH):
            small_copy(k).wait_recv()
            total = total + zs_in[k - 1]
        small_s[...] = total
        ag_start(4)
        ag_turn(0)
        z_relay(1)
        z_relay(2)
        ag_turn(2)

        @pl.when(extra(z))
        def _():
            ag_turn(3)

        ag_turn(4)
        ag_end(0)
        total = rs_total(1)
        uf = tok_v[...].astype(F32)
        along = total * norm_gain(par_ref[...])
        s1 = lax.rsqrt(jnp.mean(uf * uf, axis=1, keepdims=True) + EPSILON)
        tg_ref[...] = cot_v[...].astype(F32) + s1 * along - uf * (
            s1 * s1 * s1 * jnp.mean(along * uf, axis=1, keepdims=True))
        gx_v[...] = z_total(1).astype(BF)
        ag_start(1)
        ag_end(2)

        @pl.when(extra(z))
        def _():
            ag_end(3)

        ag_end(4)
        gb_v[...] = z_total(2).astype(BF)
        for k in range(1, CHIPS):
            bcd_push(k).start()
        ag_turn(1)
        for k in range(1, CHIPS):
            bcd_push(k).wait_recv()
        total = gb_v[...].astype(F32)
        for k in range(1, CHIPS):
            total = total + gb_in[k - 1].astype(F32)
        gt_v[core] = total.astype(BF)
        bcd_back().start()
        ag_end(1)
        bcd_back().wait()
        last = [
            pltpu.make_async_copy(gt_v.at[0], wig_ref.at[pl.ds(2 * DI, HALF)], loc.at[15]),
            pltpu.make_async_copy(gt_v.at[1, 0 : WIDTH - 2 * DI - HALF],
                                  wig_ref.at[pl.ds(2 * DI + HALF, WIDTH - 2 * DI - HALF)], loc.at[16])]
        for copy in last:
            copy.start()
        for n in (0, 1, 2, 4):
            ag_close(n)

        @pl.when(extra(z))
        def _():
            ag_close(3, receives=False)

        @pl.when(jnp.logical_not(extra(z)))
        def _():
            ag_close(3, sends=False)

        for c in range(CHIPS):
            br_pair(c).wait_send()
            dn_pair(c).wait_send()
        for n in range(2):
            for kind in range(6):
                rs(n, kind).wait_send()
        for k in range(1, CHIPS):
            bcd_push(k).wait_send()
        for k in range(1, DEPTH):
            small_copy(k).wait_send()
        for n in (1, 2, 3, 4):
            z_close(n)
        bcd_pair().wait_send()
        for copy in last:
            copy.wait()


def backward_call(tok, cot, nrm, br, w, g, projz, ssd, dno, stat, par, projc, st, info, ids):
    n = nrm.shape[0]
    any_space = pl.BlockSpec(memory_space=pl.ANY)
    sds = jax.ShapeDtypeStruct
    dma = pltpu.SemaphoreType.DMA
    one = lambda i: jnp.minimum(i, TEAM - 1)
    two = lambda i: jnp.clip(2 * TEAM - i, 0, TEAM - 1)
    rows = lambda c, turn: pl.BlockSpec((BLK, c), lambda i: (turn(i), 0))
    cube = lambda a, b: pl.BlockSpec((1, a, b), lambda i: (two(i), 0, 0))
    fixed = lambda a, b: pl.BlockSpec((a, b), lambda i: (0, 0), pipeline_mode=pl.Buffered(1))
    vm = pltpu.VMEM
    return pl.pallas_call(
        backward_kernel,
        grid=(2 * TEAM + 2,),
        in_specs=[any_space] * 6 + [
            rows(NZ, one), rows(CH, one), rows(CH, one), fixed(TEAM, 2 * BLK), fixed(16, CONVC), rows(REST, two),
            pl.BlockSpec((16, REST), lambda i: (jnp.maximum(16 * two(i) - 1, 0), 0)),
            cube(STATE, CH), rows(128, two), fixed(1, n)],
        out_specs=[fixed(BLK, D), fixed(BLK, D), any_space, any_space, any_space],
        out_shape=[sds((BLK, D), BF), sds((BLK, D), F32), sds((WIDTH, KROWS), BF),
                   sds((DI // DEPTH, D), BF), sds((TEAM, 16, CONVC), F32)],
        scratch_shapes=[
            vm((n, D), BF), vm((n, D), BF), vm((COLS, D), BF), vm((CH, n), BF), vm((n, CH), BF), vm((CH, n), BF),
            vm((n, CH), F32), vm((REST, n), BF), vm((CH, D), BF), vm((CH, D), BF), vm((BCD, D), BF),
            vm((HALF, D), BF),
            vm((2, CH, KROWS), BF), vm((2, CH, KROWS), BF), vm((2, HALF, KROWS), BF), vm((2, 2 * HEADDIM, D), BF),
            vm((DEPTH - 1, 16, CONVC), F32),
            vm((2, CH, KROWS), BF), vm((2, CH, KROWS), BF), vm((2, HALF, KROWS), BF), vm((2, 2 * HEADDIM, D), BF), vm((CH, KROWS), BF), vm((CH, KROWS), BF),
            vm((HALF, KROWS), BF), vm((2 * HEADDIM, D), BF), vm((CHIPS - 1, HALF, KROWS), BF), vm((2, HALF, KROWS), BF),
            vm((CHIPS, BLK, D), BF), vm((CHIPS, BLK, D), BF), vm((2, 2, BLK, D), BF), vm((2, 2, BLK // 2, D), BF),
            vm((BLK, D), BF), vm((BLK, D), BF), vm((16, CONVC), F32), vm((16, CONVC), F32),
            vm((BLK + 8, CONVC), F32), vm((BLK + 8, CONVC), F32), vm((STATE, CH), F32),
            dma((17,)), dma((CHIPS,)), dma((CHIPS,)), dma((2, 6)), dma((2, 6)), dma((CHIPS,)), dma((CHIPS,)),
            dma((CHIPS,)), dma((CHIPS,)), dma((5, 4)), dma((5, 4)), dma((DEPTH,)), dma((DEPTH,)),
            dma((5, 5)), dma((5, 5)), dma((5, 5)), dma((5, 5)), dma((2,)), dma((2,)),
            pltpu.SemaphoreType.REGULAR],
        compiler_params=pltpu.CompilerParams(
            collective_id=1, has_side_effects=True, vmem_limit_bytes=63 << 20),
    )(tok, cot, nrm, br, w, g, projz, ssd, dno, stat, par, projc, projc, st, info, ids)


def finish_kernel(
    lo_ref, tg_ref, wig_ref, wog_ref, smalls_ref,
    out_ref, grad_ref, win_ref, wout_ref, convw_ref, convb_ref, alog_ref, dtb_ref, skip_ref, normw_ref, gatew_ref,
    all_v, in_v, in_f, wo_v, wo_f, lo_v, tg_v, sems,
):
    rows_in, rows_wo = WIDTH // 13, DI // DEPTH // 4
    chunks = [(wig_ref, in_v, in_f, win_ref, slice(rows_in * n, rows_in * n + rows_in)) for n in range(13)]
    chunks += [(wog_ref, wo_v, wo_f, wout_ref, slice(rows_wo * n, rows_wo * n + rows_wo)) for n in range(4)]
    come = [pltpu.make_async_copy(a.at[r], b.at[r], sems.at[0, n]) for n, (a, b, _, _, r) in enumerate(chunks)]
    go = [pltpu.make_async_copy(a.at[r], b.at[r], sems.at[1, n]) for n, (_, _, a, b, r) in enumerate(chunks)]
    last = len(chunks)
    enter = [pltpu.make_async_copy(lo_ref, lo_v, sems.at[0, last]), pltpu.make_async_copy(tg_ref, tg_v, sems.at[0, last + 1])]
    leave = [pltpu.make_async_copy(lo_v, out_ref, sems.at[1, last]), pltpu.make_async_copy(tg_v, grad_ref, sems.at[1, last + 1])]
    for copy in come + enter:
        copy.start()
    for n, (_, src, dst, _, r) in enumerate(chunks):
        come[n].wait()
        dst[r] = src[r].astype(F32)
        go[n].start()
    for n in range(2):
        enter[n].wait()
        leave[n].start()
    for d in range(TEAM):
        for slot in range(HPD):
            head = head_of(slot, d // 2, d % 2)[slot // 4]
            all_v[:, HEADDIM * head : HEADDIM * head + HEADDIM] = smalls_ref[
                d, 0:8, HEADDIM * slot : HEADDIM * slot + HEADDIM]
    side = smalls_ref[0, :, CH:]
    gain = smalls_ref[0, :, :CH]
    for d in range(1, TEAM):
        side = side + smalls_ref[d, :, CH:]
        gain = gain + smalls_ref[d, :, :CH]
    all_v[:, DI:] = side[0:8]
    z = lax.axis_index("fsdp")
    nc, ng, nh = CHAN // DEPTH, DI // DEPTH, HEADS // DEPTH
    for o in range(DEPTH):

        @pl.when(z == o)
        def _():
            convw_ref[...] = all_v[0:CONV, nc * o : nc * o + nc]
            convb_ref[...] = all_v[CONV : CONV + 1, nc * o : nc * o + nc].reshape(nc)
            gatew_ref[...] = all_v[5:6, ng * o : ng * o + ng].reshape(ng)
            alog_ref[...] = side[5:6, nh * o : nh * o + nh].reshape(nh)
            dtb_ref[...] = side[5:6, 128 + nh * o : 128 + nh * o + nh].reshape(nh)
            skip_ref[...] = side[6:7, nh * o : nh * o + nh].reshape(nh)
            normw_ref[...] = gain[7 + o : 8 + o, :].reshape(KROWS)

    for copy in go + leave:
        copy.wait()


def finish_call(lo, tg, wig, wog, smalls):
    any_space = pl.BlockSpec(memory_space=pl.ANY)
    vmem = pl.BlockSpec(memory_space=pltpu.VMEM)
    sizes = [(CONV, CHAN // DEPTH), (CHAN // DEPTH,)] + [(HEADS // DEPTH,)] * 3 + [(KROWS,), (DI // DEPTH,)]
    sds = jax.ShapeDtypeStruct
    rows = DI // DEPTH
    return pl.pallas_call(
        finish_kernel,
        in_specs=[any_space] * 4 + [vmem],
        out_specs=[any_space] * 4 + [vmem] * len(sizes),
        out_shape=[sds((BLK, D), BF), sds((BLK, D), F32), sds((WIDTH, KROWS), F32), sds((rows, D), F32)]
        + [sds(s, F32) for s in sizes],
        scratch_shapes=[pltpu.VMEM((8, CHAN), F32), pltpu.VMEM((WIDTH, KROWS), BF), pltpu.VMEM((WIDTH, KROWS), F32),
                        pltpu.VMEM((rows, D), BF), pltpu.VMEM((rows, D), F32), pltpu.VMEM((BLK, D), BF), pltpu.VMEM((BLK, D), F32),
                        pltpu.SemaphoreType.DMA((2, 19))],
        compiler_params=pltpu.CompilerParams(vmem_limit_bytes=62 << 20),
    )(lo, tg, wig, wog, smalls)


def on_team(
    tokens, segment_ids, cotangent, w_in, w_out, conv_w, conv_b, a_log, dt_bias, d_skip,
    norm_w, gate_w,
):
    tok, cot = tokens[0], cotangent[0]
    small = (conv_w, conv_b, a_log, dt_bias, d_skip, norm_w, gate_w)
    nrm, projc, projz, st, ssd, dno, br, info, stat, par, w_loc, g = forward_call(
        tok, cot, w_in.T, w_out, segment_ids, small)
    lo, tg, wig, wog, smalls = backward_call(
        tok, cot, nrm, br, w_loc, g, projz, ssd, dno, stat, par, projc, st, info, segment_ids)
    lo, tg, wig, wog, convw, convb, alog, dtb, skip, normw, gatew = finish_call(lo, tg, wig, wog, smalls)
    return (lo[None], tg[None], wig.T, wog, convw, convb, alog, dtb, skip, normw, gatew)


def solution(mesh):
    body = on_team if (mesh.shape["seq"], mesh.shape["fsdp"]) == (TEAM, DEPTH) else on_device
    return jax.shard_map(
        body,
        mesh=mesh,
        in_specs=(
            P("fsdp", "seq", None),
            P("fsdp", None),
            P("fsdp", "seq", None),
            P("fsdp", None),
            P("fsdp", None),
            P(None, "fsdp"),
            P("fsdp"),
            P("fsdp"),
            P("fsdp"),
            P("fsdp"),
            P("fsdp"),
            P("fsdp"),
        ),
        out_specs=(
            P("fsdp", "seq", None),
            P("fsdp", "seq", None),
            P("fsdp", None),
            P("fsdp", None),
            P(None, "fsdp"),
            P("fsdp"),
            P("fsdp"),
            P("fsdp"),
            P("fsdp"),
            P("fsdp"),
            P("fsdp"),
        ),
        check_vma=False,
    )
```

```python
import jax
import jax.numpy as jnp
from jax import lax
from jax.experimental import pallas as pl
from jax.experimental.pallas import tpu as pltpu
from jax.sharding import PartitionSpec as P

DI = 3072
HEADDIM = 64
STATE = 128
CONV = 4
SPAN = 256
HEADS = 48
D = 1536
WIDTH = 6448
DEPTH = 4
CHAN = 3328


EPSILON = 1e-05
HIGHEST = lax.Precision.HIGHEST


def passed_along(value, axis, steps):
    count = lax.axis_size(axis)
    first, last = (max(0, -steps), min(count, count - steps))
    return lax.ppermute(value, axis, [(source, source + steps) for source in range(first, last)])


def shortened(array):

    def short(part):
        return part.astype(jnp.bfloat16) if part.dtype == jnp.float32 else part

    return jax.tree.map(short, array)


def block_masks(ids_blocks, before_ids):
    block_len = ids_blocks.shape[1]
    places = jnp.arange(block_len)
    causal_mask = (places[:, None] >= places[None, :])[None] & (
        ids_blocks[:, :, None] == ids_blocks[:, None, :]
    )
    keep_flag = (ids_blocks == before_ids[:, None]).astype(jnp.float32)
    same_last = (ids_blocks == ids_blocks[:, -1:]).astype(jnp.float32)
    return (causal_mask, keep_flag, same_last)


def local_states(x_heads, b_rows, step_size, log_decay, same_last, keep_flag):
    cum_decay = jnp.cumsum(log_decay, axis=1)
    last_cum = cum_decay[:, -1]
    weights = jnp.exp(last_cum[:, None, :] - cum_decay) * step_size * same_last[:, :, None]
    fresh_state = jnp.einsum("csh,cshp,csn->chpn", weights, x_heads, b_rows, precision=HIGHEST)
    passing = keep_flag[:, -1:] * jnp.exp(last_cum)
    total_state = jnp.zeros_like(fresh_state[0])
    total_decay = jnp.ones_like(passing[0])
    total_state = fresh_state[0] + passing[0][:, None, None] * total_state
    total_decay = total_decay * passing[0]
    return (fresh_state, passing, total_state, total_decay)


def local_output(x_heads, b_rows, c_rows, step_size, log_decay, incoming, causal_mask, keep_flag):
    cum_decay = jnp.cumsum(log_decay, axis=1)
    cum_heads = jnp.swapaxes(cum_decay, 1, 2)
    gap_decay = cum_heads[:, :, :, None] - cum_heads[:, :, None, :]
    head_mask = causal_mask[:, None]
    decay_map = jnp.exp(jnp.where(head_mask, gap_decay, 0.0)) * head_mask.astype(jnp.float32)
    scores = jnp.einsum("ctn,csn->cts", c_rows, b_rows, precision=HIGHEST)
    mixing = scores[:, None] * decay_map * jnp.swapaxes(step_size, 1, 2)[:, :, None, :]
    inner_out = jnp.einsum("chts,cshp->cthp", mixing, x_heads, precision=HIGHEST)
    starts = [incoming]
    start_states = jnp.stack(starts)
    carried = jnp.einsum("ctn,chpn->cthp", c_rows, start_states, precision=HIGHEST)
    carried = carried * (keep_flag[:, :, None] * jnp.exp(cum_decay))[..., None]
    return inner_out + carried


def on_device(
    tokens,
    segment_ids,
    cotangent,
    w_in,
    w_out,
    conv_w,
    conv_b,
    a_log,
    dt_bias,
    d_skip,
    norm_w,
    gate_w,
):
    gathered = (
        lax.all_gather(w_in, "fsdp", axis=0, tiled=True),
        lax.all_gather(w_out, "fsdp", axis=0, tiled=True),
        lax.all_gather(conv_w, "fsdp", axis=1, tiled=True),
        lax.all_gather(conv_b, "fsdp", axis=0, tiled=True),
        lax.all_gather(a_log, "fsdp", axis=0, tiled=True),
        lax.all_gather(dt_bias, "fsdp", axis=0, tiled=True),
        lax.all_gather(d_skip, "fsdp", axis=0, tiled=True),
        lax.all_gather(norm_w, "fsdp", axis=0, tiled=True),
        lax.all_gather(gate_w, "fsdp", axis=0, tiled=True),
    )
    (
        w_in_full,
        w_out_full,
        conv_full,
        bias_full,
        a_log_full,
        dt_bias_full,
        skip_full,
        norm_full,
        gate_full,
    ) = gathered
    inputs = tokens[0].astype(jnp.float32)
    length = inputs.shape[0]
    norm_gain = norm_full.astype(jnp.float32)
    scale_in = lax.rsqrt(jnp.mean(inputs * inputs, axis=-1, keepdims=True) + EPSILON)
    normed = (inputs * scale_in * norm_gain).astype(jnp.bfloat16)
    projected = jnp.dot(normed, w_in_full, preferred_element_type=jnp.float32).astype(jnp.bfloat16)
    gate_z = projected[:, :DI].astype(jnp.float32)
    conv_in = projected[:, DI : DI + CHAN]
    dt_raw = projected[:, DI + CHAN :].astype(jnp.float32)
    first_row = lax.axis_index("seq") * length
    id_row = jnp.concatenate([jnp.full((CONV - 1,), -1, jnp.int32), segment_ids[0]], axis=0)
    ids_pad = lax.dynamic_slice_in_dim(id_row, first_row, length + CONV - 1)
    ids_own = ids_pad[CONV - 1 :]
    left_edge = passed_along(conv_in[length - (CONV - 1) :], "seq", 1)
    padded = jnp.concatenate([left_edge, conv_in], axis=0).astype(jnp.float32)
    kernel = conv_full.astype(jnp.float32)
    conv_out = jnp.zeros((length, CHAN), jnp.float32) + bias_full.astype(jnp.float32)
    same_docs = []
    for offset in range(CONV):
        same_doc = (ids_pad[offset : offset + length] == ids_own).astype(jnp.float32)
        same_docs.append(same_doc)
        conv_out = conv_out + kernel[offset] * padded[offset : offset + length] * same_doc[:, None]
    activated = jax.nn.silu(conv_out)
    blocks = length // SPAN
    x_heads = activated[:, :DI].reshape(blocks, SPAN, HEADS, HEADDIM)
    b_rows = activated[:, DI : DI + STATE].reshape(blocks, SPAN, STATE)
    c_rows = activated[:, DI + STATE :].reshape(blocks, SPAN, STATE)
    dt_bias_f = dt_bias_full.astype(jnp.float32)
    decay_rate = jnp.exp(a_log_full.astype(jnp.float32))
    step_flat = jax.nn.softplus(dt_raw + dt_bias_f)
    step_size = step_flat.reshape(blocks, SPAN, HEADS)
    log_decay = (-step_flat * decay_rate).reshape(blocks, SPAN, HEADS)
    ids_blocks = ids_own.reshape(blocks, SPAN)
    before_ids = ids_pad[CONV - 2 : CONV - 2 + length : SPAN]
    causal_mask, keep_flag, same_last = block_masks(ids_blocks, before_ids)

    def state_part(heads_in, rows_b, steps_in, decay_in):
        return local_states(heads_in, rows_b, steps_in, decay_in, same_last, keep_flag)

    (fresh_state, passing, total_state, total_decay), state_pull = jax.vjp(
        state_part, x_heads, b_rows, step_size, log_decay
    )

    def pass_forward(turn_index, received):
        return passed_along(
            (total_state + total_decay[:, None, None] * received).astype(jnp.bfloat16), "seq", 1
        ).astype(jnp.float32)

    incoming = lax.fori_loop(0, lax.axis_size("seq") - 1, pass_forward, jnp.zeros_like(total_state))

    def output_part(
        heads_in, rows_b, rows_c, steps_in, decay_in, fresh_in, passing_in, incoming_in
    ):
        return local_output(
            heads_in, rows_b, rows_c, steps_in, decay_in, incoming_in, causal_mask, keep_flag
        )

    ssd_out, output_pull = jax.vjp(
        output_part, x_heads, b_rows, c_rows, step_size, log_decay, fresh_state, passing, incoming
    )
    skip_heads = skip_full.astype(jnp.float32)
    y_full = (ssd_out + skip_heads[:, None] * x_heads).reshape(length, DI)
    silu_z = jax.nn.silu(gate_z)
    gated = y_full * silu_z
    scale_out = lax.rsqrt(jnp.mean(gated * gated, axis=-1, keepdims=True) + EPSILON)
    gate_gain = gate_full.astype(jnp.float32)
    normed_out = (gated * scale_out * gate_gain).astype(jnp.bfloat16)
    branch = jnp.dot(normed_out, w_out_full, preferred_element_type=jnp.float32)
    layer_out = (inputs + branch).astype(jnp.bfloat16)[None]
    grad_out = cotangent[0]
    d_w_out = lax.dot_general(
        normed_out, grad_out, (((0,), (0,)), ((), ())), preferred_element_type=jnp.float32
    )
    d_normed_out = lax.dot_general(
        grad_out, w_out_full, (((1,), (1,)), ((), ())), preferred_element_type=jnp.float32
    )
    d_gate_w = jnp.sum(d_normed_out * gated * scale_out, axis=0)
    along_out = d_normed_out * gate_gain
    cube_out = scale_out * scale_out * scale_out
    d_gated = scale_out * along_out - gated * cube_out * jnp.mean(
        along_out * gated, axis=-1, keepdims=True
    )
    d_y = d_gated * silu_z
    sig_z = jax.nn.sigmoid(gate_z)
    d_gate_z = d_gated * y_full * sig_z * (1.0 + gate_z * (1.0 - sig_z))
    d_ssd = d_y.reshape(blocks, SPAN, HEADS, HEADDIM)
    d_skip_grad = jnp.sum(d_ssd * x_heads, axis=(0, 1, 3))
    dx_out, db_out, dc_out, dstep_out, ddecay_out, d_fresh, d_passing, d_incoming = output_pull(
        d_ssd
    )

    def pass_backward(turn_index, received):
        return passed_along(d_incoming + total_decay[:, None, None] * received, "seq", -1)

    d_total = lax.fori_loop(0, lax.axis_size("seq") - 1, pass_backward, jnp.zeros_like(d_incoming))
    d_total_decay = jnp.sum(d_total * incoming, axis=(1, 2))
    dx_state, db_state, dstep_state, ddecay_state = state_pull(
        (d_fresh, d_passing, d_total, d_total_decay)
    )
    d_x = dx_out + dx_state + skip_heads[:, None] * d_ssd
    d_b = db_out + db_state
    d_log = (ddecay_out + ddecay_state).reshape(length, HEADS)
    d_step = (dstep_out + dstep_state).reshape(length, HEADS) - d_log * decay_rate
    d_a_log = -jnp.sum(d_log * step_flat, axis=0) * decay_rate
    d_dt_raw = d_step * jax.nn.sigmoid(dt_raw + dt_bias_f)
    d_dt_bias = jnp.sum(d_dt_raw, axis=0)
    d_act = jnp.concatenate(
        [d_x.reshape(length, DI), d_b.reshape(length, STATE), dc_out.reshape(length, STATE)], axis=1
    )
    sig_conv = jax.nn.sigmoid(conv_out)
    d_conv = d_act * sig_conv * (1.0 + conv_out * (1.0 - sig_conv))
    d_conv_b = jnp.sum(d_conv, axis=0)
    kernel_rows = []
    d_padded = jnp.zeros((length + CONV - 1, CHAN), jnp.float32)
    for offset in range(CONV):
        masked = d_conv * same_docs[offset][:, None]
        kernel_rows.append(jnp.sum(masked * padded[offset : offset + length], axis=0))
        d_padded = d_padded + jnp.pad(
            kernel[offset] * masked, ((offset, CONV - 1 - offset), (0, 0))
        )
    d_kernel = jnp.stack(kernel_rows)
    d_edge = passed_along(shortened(d_padded[: CONV - 1]), "seq", -1)
    d_conv_in = d_padded[CONV - 1 :] + jnp.pad(d_edge, ((length - (CONV - 1), 0), (0, 0)))
    d_projected = jnp.concatenate([d_gate_z, d_conv_in, d_dt_raw], axis=1).astype(jnp.bfloat16)
    d_normed = lax.dot_general(
        d_projected, w_in_full, (((1,), (1,)), ((), ())), preferred_element_type=jnp.float32
    )
    d_norm_w = jnp.sum(d_normed * inputs * scale_in, axis=0)
    along_in = d_normed * norm_gain
    cube_in = scale_in * scale_in * scale_in
    d_inputs = (
        scale_in * along_in
        - inputs * cube_in * jnp.mean(along_in * inputs, axis=-1, keepdims=True)
        + grad_out.astype(jnp.float32)
    )
    d_w_in = lax.dot_general(
        normed, d_projected, (((0,), (0,)), ((), ())), preferred_element_type=jnp.float32
    )
    weight_grads = (
        d_w_in,
        d_w_out,
        d_kernel,
        d_conv_b,
        d_a_log,
        d_dt_bias,
        d_skip_grad,
        d_norm_w,
        d_gate_w,
    )
    shares = tuple(
        (
            lax.psum_scatter(weight_grads[0], "fsdp", scatter_dimension=0, tiled=True),
            lax.psum_scatter(weight_grads[1], "fsdp", scatter_dimension=0, tiled=True),
            lax.psum_scatter(weight_grads[2], "fsdp", scatter_dimension=1, tiled=True),
            lax.psum_scatter(weight_grads[3], "fsdp", scatter_dimension=0, tiled=True),
            lax.psum_scatter(weight_grads[4], "fsdp", scatter_dimension=0, tiled=True),
            lax.psum_scatter(weight_grads[5], "fsdp", scatter_dimension=0, tiled=True),
            lax.psum_scatter(weight_grads[6], "fsdp", scatter_dimension=0, tiled=True),
            lax.psum_scatter(weight_grads[7], "fsdp", scatter_dimension=0, tiled=True),
            lax.psum_scatter(weight_grads[8], "fsdp", scatter_dimension=0, tiled=True),
        )
    )
    totals = lax.psum(shares, "seq")
    return (layer_out, d_inputs[None]) + tuple(totals)


F32 = jnp.float32
BF = jnp.bfloat16
BLK = 256
TEAM = 8
HPD = HEADS // TEAM
CH = HPD * HEADDIM
NZ, NX, NB, ND = CH, CH, 2 * STATE, 64
COLS = NZ + NX + NB + ND
REST = NX + NB + ND
CONVC = NX + NB
TAIL = CONV - 1


def dot(a, b):
    return lax.dot_general(a, b, (((1,), (0,)), ((), ())), preferred_element_type=F32)


def dot_nt(a, b):
    return lax.dot_general(a, b, (((1,), (1,)), ((), ())), preferred_element_type=F32)


def dot_tn(a, b):
    return lax.dot_general(a, b, (((0,), (0,)), ((), ())), preferred_element_type=F32)


def dot_exact(a, b):
    high = b.astype(BF)
    left = b - high.astype(F32)
    middle = left.astype(BF)
    low = (left - middle.astype(F32)).astype(BF)
    n = b.shape[1]
    p = dot(a.astype(BF), jnp.concatenate([high, middle, low], axis=1))
    return p[:, :n] + p[:, n : 2 * n] + p[:, 2 * n :]


def iota(shape, dim):
    return lax.broadcasted_iota(jnp.int32, shape, dim)


def split_dot(a, b):
    high = a.astype(BF)
    low = (a - high.astype(F32)).astype(BF)
    return dot(high, b) + dot(low, b)


def spread():
    return (iota((128, CH), 1) // HEADDIM == iota((128, CH), 0)).astype(BF)


def gather_heads():
    return (iota((CH, 128), 0) // HEADDIM == iota((CH, 128), 1)).astype(BF)


def lower_tri():
    return (iota((BLK, BLK), 0) >= iota((BLK, BLK), 1)).astype(F32)


def softplus(v):
    return jnp.maximum(v, 0.0) + jnp.log1p(jnp.exp(-jnp.abs(v)))


def sigmoid(v):
    return 1.0 / (1.0 + jnp.exp(-v))


def conv_taps(cbuf, cw, tok):
    out = cw[CONV : CONV + 1, :] + cw[CONV - 1 : CONV, :] * cbuf[8 : 8 + BLK, :]
    for back in range(1, CONV):
        term = cw[CONV - 1 - back : CONV - back, :] * cbuf[8 - back : 8 - back + BLK, :]
        out = out + term * tok[:, back : back + 1]
    return out


def pair_select(left, right):
    return jnp.where(iota(left.shape, 1) % 128 < HEADDIM, left, right)


def head_of(slot, chip, core):
    first = 12 * slot + 3 * chip + 2 * core
    second = 12 * (core + 2 * (slot - 4)) + 3 * chip + 1
    return first, second


def pick_heads():
    seq = lax.axis_index("seq")
    chip, core = lax.div(seq, 2), lax.rem(seq, 2)
    slot = iota((128, 128), 1)
    first, second = head_of(slot, chip, core)
    head = jnp.where(slot < 4, first, jnp.where(slot < HPD, second, -1))
    return (iota((128, 128), 0) == head).astype(BF)


def own_heads(par, dt_cols):
    pick = pick_heads()
    pair = jnp.concatenate([par[5:6, CH : CH + 128], par[5:6, CH + 128 :], jnp.zeros((6, 128), F32)], axis=0)
    pair = dot(pair.astype(BF), pick)
    wide = jnp.concatenate([dt_cols, jnp.zeros((BLK, 128 - ND), BF)], axis=1)
    return jnp.exp(pair[1:2, :]), dot(wide, pick) + pair[0:1, :], iota((BLK, 128), 1) < HPD, pick


def norm_gain(par):
    return jnp.concatenate([par[7 + i : 8 + i, :CH] for i in range(D // CH)], axis=1)


def row_sum(q):
    high = q.astype(BF)
    low = (q - high.astype(F32)).astype(BF)
    ones = jnp.ones((8, q.shape[1]), BF)
    return (dot_nt(ones, high) + dot_nt(ones, low))[0:1, :]


def scan_forward(j, nrm, w_v, par, tok, idr, cbuf, state, projc_ref, st_ref, ssd_v):
    rows = pl.ds(pl.multiple_of(BLK * j, BLK), BLK)
    proj = dot_nt(nrm, w_v[NZ:, :]).astype(BF)
    projc_ref[...] = proj
    cbuf[8 : 8 + BLK, :] = proj[:, :CONVC].astype(F32)
    conv_out = conv_taps(cbuf, par, tok)
    cbuf[0:8, :] = cbuf[BLK : BLK + 8, :]
    act = conv_out * sigmoid(conv_out)
    x = act[:, :CH]
    bm = act[:, CH : CH + STATE].astype(BF)
    cm = act[:, CH + STATE :].astype(BF)
    rate, dt_in, own, pick = own_heads(par, proj[:, CONVC:])
    step = jnp.where(own, softplus(dt_in), 0.0)
    cum = dot_exact(lower_tri(), -step * rate)
    cum_t = cum.T
    mask = (iota((BLK, BLK), 0) >= iota((BLK, BLK), 1)) & (tok[:, 0:1] == idr)
    gm = jnp.where(mask, dot_nt(cm, bm), 0.0)
    ex = spread()
    xs = (x * split_dot(step, ex)).astype(BF)
    parts = []
    for pair in range(HPD // 2):
        xp = xs[:, 128 * pair : 128 * pair + 128]
        both = []
        for h in (2 * pair, 2 * pair + 1):
            decay = jnp.exp(jnp.minimum(cum[:, h : h + 1] - cum_t[h : h + 1, :], 0.0))
            both.append(dot((gm * decay).astype(BF), xp))
        parts.append(pair_select(*both))
    inner = jnp.concatenate(parts, axis=1)
    old = state[...]
    st_ref[0] = old
    keep = tok[:, 7:8]
    carried = split_dot(keep * jnp.exp(cum), ex) * dot(cm, old.astype(BF))
    last = cum[BLK - 1 : BLK, :]
    weights = jnp.exp(last - cum) * step * tok[:, 8:9]
    through = split_dot(jnp.broadcast_to(keep[BLK - 1 :, :] * jnp.exp(last), (8, 128)), ex)[0:1, :]
    state[...] = dot_tn(bm, (x * split_dot(weights, ex)).astype(BF)) + through * old
    ssd_v[rows, :] = inner + carried + par[6:7, :CH] * x


def gate_forward(j, nrm_v, g_v, w_v, wo_v, par, ssd_v, projz_ref, ssd_ref, dno_ref, br_ref, stat_v):
    rows = pl.ds(pl.multiple_of(BLK * j, BLK), BLK)
    projz = dot_nt(nrm_v[rows, :], w_v[:NZ, :]).astype(BF)
    projz_ref[...] = projz
    ssd = ssd_v[rows, :]
    ssd_ref[...] = ssd
    z = projz.astype(F32)
    gate_w = par[5:6, :CH]
    gated = ssd * (z * sigmoid(z))
    br_ref[...] = dot((gated * gate_w).astype(BF), wo_v[...]).astype(BF)
    dno = dot_nt(g_v[rows, :], wo_v[...])
    dno_ref[...] = dno
    stat_v[pl.ds(j, 1), 0:BLK] = row_sum(gated * gated)
    stat_v[pl.ds(j, 1), BLK : 2 * BLK] = row_sum(dno * gate_w * gated)


def gate_backward(j, z, ssd, dno, stat, gate_w, not_v, dy_v, dz_v, dzt_v, small_v):
    rows = pl.ds(pl.multiple_of(BLK * j, BLK), BLK)
    sig_z = sigmoid(z)
    silu_z = z * sig_z
    stat = jnp.where(iota((128, BLK), 0) == 0, stat[:, :BLK], stat[:, BLK:]).T
    s2 = lax.rsqrt(stat[:, 0:1] * (1.0 / DI) + EPSILON)
    mean_ag = stat[:, 1:2] * (1.0 / DI)
    gated = ssd * silu_z
    gs = gated * s2
    not_v[:, rows] = (gs * gate_w).T.astype(BF)
    d_gated = s2 * (dno * gate_w) - gated * (s2 * s2 * s2 * mean_ag)
    dy_v[rows, :] = d_gated * silu_z
    dz = d_gated * ssd * sig_z * (1.0 + z * (1.0 - sig_z))
    dz_v[rows, :] = dz.astype(BF)
    dzt_v[:, rows] = dz.T.astype(BF)
    small_v[5:6, :CH] += jnp.sum(dno * gs, axis=0, keepdims=True)


def scan_backward(proj, halo, tok, idr, old, par, dy, cbuf, dcbuf, dstate, small_v):
    cbuf[0:8, :] = halo[8:16, :CONVC].astype(F32)
    cbuf[8 : 8 + BLK, :] = proj[:, :CONVC].astype(F32)
    conv_out = conv_taps(cbuf, par, tok)
    sig_c = sigmoid(conv_out)
    act = conv_out * sig_c
    x = act[:, :CH]
    bm = act[:, CH : CH + STATE].astype(BF)
    cm_f = act[:, CH + STATE :]
    cm = cm_f.astype(BF)
    rate, dt_in, own, pick = own_heads(par, proj[:, CONVC:])
    step = jnp.where(own, softplus(dt_in), 0.0)
    cum = dot_exact(lower_tri(), -step * rate)
    cum_t = cum.T
    mask = (iota((BLK, BLK), 0) >= iota((BLK, BLK), 1)) & (tok[:, 0:1] == idr)
    gm = jnp.where(mask, dot_nt(cm, bm), 0.0)
    ex = spread()
    gh = gather_heads()
    step_x = split_dot(step, ex)
    xs = (x * step_x).astype(BF)
    dyb = dy.astype(BF)
    dyt = dy.T.astype(BF)
    lane = iota((BLK, 128), 1)
    dg = jnp.zeros((BLK, BLK), F32)
    row_sums = jnp.zeros((BLK, 128), F32)
    col_sums = []
    e_rows = []
    for h in range(HPD):
        pair = h // 2
        decay = jnp.exp(jnp.minimum(cum[:, h : h + 1] - cum_t[h : h + 1, :], 0.0))
        mixed = gm * decay
        half = jnp.where((lane < HEADDIM) == (h % 2 == 0), dyb[:, 128 * pair : 128 * pair + 128], 0)
        dms = dot_nt(half.astype(BF), xs[:, 128 * pair : 128 * pair + 128])
        product = dms * mixed
        row_sums = jnp.where(lane == h, jnp.sum(product, axis=1, keepdims=True), row_sums)
        col_sums.append(jnp.sum(product, axis=0, keepdims=True))
        dg = dg + dms * decay
        e_rows.append(dot(dyt[HEADDIM * h : HEADDIM * h + HEADDIM, :], mixed.astype(BF)))
    dg = jnp.where(mask, dg, 0.0).astype(BF)
    e = jnp.concatenate(e_rows, axis=0).T
    col_sums.append(jnp.zeros((128 - HPD, BLK), F32))
    col = jnp.concatenate(col_sums, axis=0).T
    keep = tok[:, 7:8]
    old_b = old.astype(BF)
    dnew = dstate[...]
    dnew_b = dnew.astype(BF)
    carry_x = split_dot(keep * jnp.exp(cum), ex)
    dyk_f = dy * carry_x
    dyk = dyk_f.astype(BF)
    carried = dot(cm, old_b)
    last = cum[BLK - 1 : BLK, :]
    fade = jnp.exp(last - cum) * tok[:, 8:9]
    weights = fade * step
    weights_x = split_dot(weights, ex)
    zt = dot(bm, dnew_b)
    xw = (x * weights_x).astype(BF)
    through = keep[BLK - 1 :, :] * jnp.exp(last)
    through_x = split_dot(jnp.broadcast_to(through, (8, 128)), ex)[0:1, :]
    k_term = split_dot(dyk_f * carried, gh)
    r_term = split_dot(x * zt, gh)
    q_term = split_dot(x * e, gh)
    pass_term = jnp.sum(old * dnew, axis=0, keepdims=True) * through_x
    pass_h = split_dot(jnp.broadcast_to(pass_term, (8, CH)), gh)[0:1, :]
    wr = weights * r_term
    d_cum = row_sums - col + k_term - wr
    d_last = jnp.sum(wr, axis=0, keepdims=True) + pass_h
    d_cum = d_cum + jnp.where(iota((BLK, 128), 0) == BLK - 1, d_last, 0.0)
    upper = (iota((BLK, BLK), 0) <= iota((BLK, BLK), 1)).astype(F32)
    d_log = dot_exact(upper, d_cum)
    d_step = q_term + fade * r_term - d_log * rate
    d_a = -jnp.sum(d_log * step, axis=0, keepdims=True) * rate
    d_dt = jnp.where(own, d_step * sigmoid(dt_in), 0.0)
    d_skip = split_dot(jnp.broadcast_to(jnp.sum(dy * x, axis=0, keepdims=True), (8, CH)), gh)[0:1, :]
    d_skip = jnp.where(own[0:1, :], d_skip, 0.0)
    heads = jnp.concatenate(
        [d_a, jnp.sum(d_dt, axis=0, keepdims=True), d_skip, jnp.zeros((5, 128), F32)], axis=0)
    high = heads.astype(BF)
    heads = dot_nt(high, pick) + dot_nt((heads - high.astype(F32)).astype(BF), pick)
    d_dt = dot_nt(d_dt.astype(BF), pick)
    dstate[...] = dot_tn(cm, dyk) + through_x * dnew
    dx = step_x * e + weights_x * zt + par[6:7, :CH] * dy
    dc = dot(dg, bm) + dot_nt(dyk, old_b)
    db = dot(cm_f.T.astype(BF), dg).T + dot_nt(xw, dnew_b)
    d_act = jnp.concatenate([dx, db, dc], axis=1)
    d_conv = d_act * (sig_c * (1.0 + conv_out * (1.0 - sig_c)))
    dcbuf[0:BLK, :] = d_conv
    d_in = par[CONV - 1 : CONV, :] * d_conv
    cg = [None] * CONV
    cg[CONV - 1] = jnp.sum(d_conv * cbuf[8 : 8 + BLK, :], axis=0, keepdims=True)
    for back in range(1, CONV):
        tap = CONV - 1 - back
        cg[tap] = jnp.sum(
            d_conv * (cbuf[8 - back : 8 - back + BLK, :] * tok[:, back : back + 1]),
            axis=0, keepdims=True,
        )
        d_in = d_in + par[tap : tap + 1, :] * (
            dcbuf[back : back + BLK, :] * tok[:, 3 + back : 4 + back]
        )
    dcbuf[BLK : BLK + 8, :] = dcbuf[0:8, :]
    small_v[0:CONV, :] += jnp.concatenate(cg, axis=0)
    small_v[CONV : CONV + 1, :] += jnp.sum(d_conv, axis=0, keepdims=True)
    small_v[5:6, CH:] += jnp.concatenate([heads[0:1, :], heads[1:2, :]], axis=1)
    small_v[6:7, CH : CH + 128] += heads[2:3, :]
    return jnp.concatenate([d_in, d_dt[:, :ND]], axis=1)


def id_row(ids_ref, j):
    return ids_ref[0:1, pl.ds(pl.multiple_of(BLK * j, BLK), BLK)].astype(F32)


def token_info(ids_ref, j, blocks):
    row = id_row(ids_ref, j)
    left = jnp.where(j > 0, id_row(ids_ref, jnp.maximum(j - 1, 0)), -1.0)
    right = jnp.where(j < blocks - 1, id_row(ids_ref, jnp.minimum(j + 1, blocks - 1)), -2.0)
    lane = iota((1, BLK), 1)
    wide = lambda a: jnp.broadcast_to(a, (8, BLK))
    rows = [row]
    for back in range(1, CONV):
        shifted = jnp.where(lane < back, pltpu.roll(wide(left), back, 1)[0:1], pltpu.roll(wide(row), back, 1)[0:1])
        rows.append((shifted == row).astype(F32))
    for ahead in range(1, CONV):
        turn = BLK - ahead
        shifted = jnp.where(lane >= turn, pltpu.roll(wide(right), turn, 1)[0:1], pltpu.roll(wide(row), turn, 1)[0:1])
        rows.append((shifted == row).astype(F32))
    rows.append((row == left[:, BLK - 1 :]).astype(F32))
    rows.append((row == row[:, BLK - 1 :]).astype(F32))
    rows.append(jnp.zeros((128 - len(rows), BLK), F32))
    return row, jnp.concatenate(rows, axis=0).T


def pack_small(convw, convb, alog, dtb, dskip, normw, gatew, chip, core, z):
    def channel(m):
        slot = m // HEADDIM
        first, second = head_of(slot, chip, core)
        return jnp.where(slot < 4, first, second) * HEADDIM + m % HEADDIM

    row = lambda a: a.astype(F32).reshape(1, a.shape[0])
    pad = lambda a: jnp.concatenate([row(a), jnp.zeros((1, 128 - HEADS // DEPTH), F32)], axis=1)
    heads = jnp.concatenate([pad(dtb), pad(alog), pad(dskip), jnp.zeros((5, 128), F32)], axis=0).astype(BF)
    m = iota((CHAN // DEPTH, CONVC), 1)
    want = jnp.where(m < CH, channel(m), DI + m - CH)
    chosen = (iota((CHAN // DEPTH, CONVC), 0) + z * (CHAN // DEPTH) == want).astype(BF)
    conv = jnp.concatenate([convw.astype(F32), row(convb), jnp.zeros((3, CHAN // DEPTH), F32)], axis=0)
    conv = dot(conv.astype(BF), chosen)
    n = DI // DEPTH
    chosen = (iota((n, CH), 0) + z * n == channel(iota((n, CH), 1))).astype(BF)
    gate = dot(jnp.broadcast_to(row(gatew), (8, n)).astype(BF), chosen)[0:1]
    n = HEADS // DEPTH
    k = iota((128, CH), 0)
    chosen = ((k < n) & (k + z * n == channel(iota((128, CH), 1)) // HEADDIM)).astype(BF)
    skip = dot(heads, chosen)[2:3]
    k = iota((128, 128), 0)
    chosen = ((k < n) & (k + z * n == iota((128, 128), 1))).astype(BF)
    heads = dot(heads, chosen)
    gain = jnp.where(iota((DEPTH, CH), 0) == z, jnp.broadcast_to(row(normw), (DEPTH, CH)), 0.0)
    return jnp.concatenate([
        conv[0:5],
        jnp.concatenate([gate, heads[0:1], heads[1:2]], axis=1),
        jnp.concatenate([skip, jnp.zeros((1, NB), F32)], axis=1),
        jnp.concatenate([gain, jnp.zeros((DEPTH, NB), F32)], axis=1),
        jnp.zeros((5, CONVC), F32)], axis=0).astype(BF)


CHIPS = TEAM // 2
KROWS = D // DEPTH
BCD = NB + ND
HALF = BCD // 2


def places():
    seq = lax.axis_index("seq")
    return seq, lax.div(seq, 2), lax.rem(seq, 2), lax.axis_index("fsdp")


def neighbours(chip):
    return [chip, chip + 1 - 2 * lax.rem(chip, 2), lax.rem(chip + 2, CHIPS), CHIPS - 1 - chip]


def send(src, dst, send_sem, recv_sem, device):
    return pltpu.make_async_remote_copy(
        src_ref=src, dst_ref=dst, send_sem=send_sem, recv_sem=recv_sem,
        device_id=device, device_id_type=pl.DeviceIdType.MESH,
    )


def greet(devices):
    barrier = pltpu.get_barrier_semaphore()
    for device in devices:
        pl.semaphore_signal(
            barrier, inc=1, device_id=device, device_id_type=pl.DeviceIdType.MESH
        )
    pl.semaphore_wait(barrier, len(devices))


def forward_kernel(
    tok_ref, cot_ref, win_ref, wout_ref, ids_ref, convw_ref, convb_ref, alog_ref, dtb_ref, skip_ref, normw_ref, gatew_ref,
    nrm_ref, projc_ref, projz_ref, st_ref, ssd_ref, dno_ref, br_ref, info_ref, stat_ref, par_ref, w_ref, g_ref,
    u_v, g_v, w_v, wo_v, small_v, smalls, ssd_v, cbuf, state, stat_v, stat_in,
    loc, t_send, t_recv, y_send, y_recv, f_send, f_recv, z_send, z_recv, b_send, b_recv, s_send, s_recv, r_send, r_recv,
):
    i = pl.program_id(0)
    seq, chip, core, z = places()
    sib = {"seq": 2 * chip + 1 - core}
    near = neighbours(chip)
    peer = lambda k: {"seq": 2 * near[k] + core}
    under = lambda k: {"fsdp": lax.rem(z + k, DEPTH)}
    around = lambda k: {"seq": lax.rem(seq + k, TEAM)}
    block = lambda s: pl.ds(pl.multiple_of(BLK * s, BLK), BLK)
    lanes = lambda o: pl.ds(pl.multiple_of(KROWS * o, KROWS), KROWS)
    half = pl.ds(pl.multiple_of(NZ + NX + HALF * core, 16), HALF)
    has = [z < DEPTH - 1, z > 0]
    heads = [head_of(n, chip, core)[n // 4] for n in range(HPD)]
    piece = lambda n: pl.ds(pl.multiple_of(HEADDIM * n, HEADDIM), HEADDIM)

    def token_copy(n, k):
        src, dst = ((tok_ref, u_v), (cot_ref, g_v))[n]
        return send(src, dst.at[block(seq)], t_send.at[n, k], t_recv.at[n, k], sib if k == 0 else peer(k))

    def token_part(n, k, h):
        return (u_v, g_v)[n].at[pl.ds(pl.multiple_of(BLK * (2 * near[k] + core) + h * (BLK // 2), BLK // 2), BLK // 2)]

    def token_relay(n, h):
        part = token_part(n, 1 + h, h)
        return send(part, part, y_send.at[n, h], y_recv.at[n, h], peer(2 - h))

    def token_next(n, k):
        if k < 3:
            ref = (u_v, g_v)[n].at[block(2 * near[k] + core)]
        else:
            ref = token_part(n, 3, k - 3)
        return send(ref, ref, f_send.at[n, k], f_recv.at[n, k], sib)

    def token_start(n):
        for k in range(3):
            token_copy(n, k).start()

    def token_turn(n):
        for k in (1, 2):
            token_copy(n, k).wait_recv()
            token_relay(n, k - 1).start()
            token_next(n, k).start()

    def token_end(n):
        for h in range(2):
            token_relay(n, h).wait_recv()
            token_next(n, 3 + h).start()
        token_copy(n, 0).wait_recv()
        for k in range(1, 5):
            token_next(n, k).wait()
        for h in range(2):
            token_relay(n, h).wait_send()

    def place(p, o):
        if p < 3:
            return w_v.at[(pl.ds(NZ, NX), half, pl.ds(0, NZ))[p], lanes(o)]
        return wo_v.at[piece(o if p == 3 else DEPTH + lax.div(o, 2))]

    def hop(p, side, dist):
        o = z - dist if side == 0 else z + dist
        there = {"fsdp": z + 1} if side == 0 else {"fsdp": z - 1}
        return send(place(p, o), place(p, o), z_send.at[p, side, dist], z_recv.at[p, side, dist], there)

    def got(p, side, dist):
        o = z - dist - 1 if side == 0 else z + dist + 1
        there = {"fsdp": z + 1} if side == 0 else {"fsdp": z - 1}
        return send(place(p, o), place(p, o), z_send.at[p, side, dist], z_recv.at[p, side, dist], there)

    def share(side, dist):
        o = z - dist - 1 if side == 0 else z + dist + 1
        return send(place(1, o), place(1, o), b_send.at[side, dist], b_recv.at[side, dist], sib)

    def exists(p, side, hops):
        o = z - hops if side == 0 else z + hops
        there = (o >= 0) if side == 0 else (o < DEPTH)
        return there & (lax.rem(o + DEPTH, 2) == core) if p == 4 else there

    def small_copy(k):
        return send(small_v, smalls.at[k - 1], s_send.at[k], s_recv.at[k], under(k))

    def stat_copy(k):
        return send(stat_v, stat_in.at[k], r_send.at[k], r_recv.at[k], around(k))

    def local_copies():
        pairs = [(tok_ref, u_v.at[block(seq)]), (cot_ref, g_v.at[block(seq)])]
        return [pltpu.make_async_copy(src, dst, loc.at[n]) for n, (src, dst) in enumerate(pairs)]

    def own_weights():
        pairs = [(win_ref.at[pl.ds(2 * DI, WIDTH - 2 * DI)], w_v.at[pl.ds(NZ + NX, WIDTH - 2 * DI), lanes(z)], 3)]
        for n in range(HPD):
            row = HEADDIM * heads[n]
            pairs.append((win_ref.at[pl.ds(pl.multiple_of(row, HEADDIM), HEADDIM)],
                          w_v.at[piece(n), lanes(z)], 4 + n))
            pairs.append((win_ref.at[pl.ds(pl.multiple_of(DI + row, HEADDIM), HEADDIM)],
                          w_v.at[piece(HPD + n), lanes(z)], 10 + n))
        pairs.append((wout_ref.at[piece(3 * chip + 2 * core)], place(3, z), 16))
        return [pltpu.make_async_copy(src, dst, loc.at[n]) for src, dst, n in pairs]

    def own_extra():
        return pltpu.make_async_copy(wout_ref.at[piece(3 * chip + 1)], place(4, z), loc.at[17])

    def pass_on(parts, dist):
        for p in parts:
            for side in range(2):

                @pl.when(exists(p, side, dist + 1))
                def _():
                    got(p, side, dist).wait_recv()
                    if p == 1:
                        share(side, dist).start()

                if dist < DEPTH - 2:

                    @pl.when(exists(p, side, dist + 1) & has[side])
                    def _():
                        hop(p, side, dist + 1).start()

    def start_own(parts):
        for p in parts:
            for side in range(2):

                @pl.when(exists(p, side, 0) & has[side])
                def _():
                    hop(p, side, 0).start()

    @pl.when(i == 0)
    def _():
        greet([around(k) for k in range(1, TEAM)] + [under(k) for k in range(1, DEPTH)])
        token_start(0)
        for copy in own_weights() + local_copies():
            copy.start()

        @pl.when(lax.rem(z, 2) == core)
        def _():
            own_extra().start()

        w_v[NZ + NX + WIDTH - 2 * DI :, lanes(z)] = jnp.zeros((BCD - (WIDTH - 2 * DI), KROWS), BF)
        for copy in own_weights():
            copy.wait()
        start_own((0, 1))
        small_v[...] = pack_small(convw_ref[...], convb_ref[...], alog_ref[...], dtb_ref[...], skip_ref[...],
                                  normw_ref[...], gatew_ref[...], chip, core, z)
        for k in range(1, DEPTH):
            small_copy(k).start()
        state[...] = jnp.zeros_like(state)
        cbuf[0:8, :] = jnp.zeros((8, CONVC), F32)
        pass_on((0, 1), 0)
        token_turn(0)
        token_start(1)
        pass_on((0, 1), 1)
        start_own((2,))
        token_end(0)
        pass_on((0, 1), 2)
        for k in range(1, DEPTH):
            small_copy(k).wait()
        for copy in local_copies():
            copy.wait()
        for side in range(2):
            for dist in range(DEPTH - 1):

                @pl.when(exists(1, side, dist + 1))
                def _():
                    share(side, dist).wait()

        total = small_v[...].astype(F32)
        for k in range(1, DEPTH):
            total = total + smalls[k - 1].astype(F32)
        par_ref[...] = total

    @pl.when(i == 1)
    def _():
        @pl.when(lax.rem(z, 2) == core)
        def _():
            own_extra().wait()

        pass_on((2,), 0)
        start_own((3, 4))

    @pl.when(i == 3)
    def _():
        pass_on((2,), 1)

    @pl.when(i == 4)
    def _():
        token_turn(1)

    @pl.when(i == 5)
    def _():
        pass_on((3, 4), 0)

    @pl.when(i == 7)
    def _():
        pass_on((3, 4), 1)

    @pl.when(i == TEAM)
    def _():
        pass_on((2, 3, 4), 2)
        token_end(1)
        pltpu.make_async_copy(w_v, w_ref, loc.at[18]).start()
        pltpu.make_async_copy(g_v, g_ref, loc.at[19]).start()

    par = par_ref[...]

    @pl.when(i < TEAM)
    def _():
        u = u_v[block(i), :].astype(F32)
        scale = lax.rsqrt(jnp.mean(u * u, axis=1, keepdims=True) + EPSILON)
        nrm = (u * scale * norm_gain(par)).astype(BF)
        nrm_ref[...] = nrm
        u_v[block(i), :] = nrm
        row, info = token_info(ids_ref, i, TEAM)
        info_ref[...] = info
        scan_forward(i, nrm, w_v, par, info, row, cbuf, state,
                     projc_ref, st_ref, ssd_v)

    @pl.when(i >= TEAM)
    def _():
        gate_forward(i - TEAM, u_v, g_v, w_v, wo_v, par, ssd_v, projz_ref, ssd_ref, dno_ref,
                     br_ref, stat_v)

    @pl.when(i == 2 * TEAM - 1)
    def _():
        for k in range(1, TEAM):
            stat_copy(k).start()
        total = stat_v[...]
        for k in range(1, TEAM):
            stat_copy(k).wait_recv()
            total = total + stat_in[k]
        stat_ref[...] = total
        for k in range(1, TEAM):
            stat_copy(k).wait_send()
        for n in range(2):
            for k in range(3):
                token_copy(n, k).wait_send()
        for side in range(2):
            for dist in range(DEPTH - 1):
                for p in range(5):

                    @pl.when(exists(p, side, dist) & has[side])
                    def _():
                        hop(p, side, dist).wait_send()

        pltpu.make_async_copy(w_v, w_ref, loc.at[18]).wait()
        pltpu.make_async_copy(g_v, g_ref, loc.at[19]).wait()


def forward_call(tok, cot, win, wout, ids, small):
    n = tok.shape[0] * TEAM
    any_space = pl.BlockSpec(memory_space=pl.ANY)
    sds = jax.ShapeDtypeStruct
    dma = pltpu.SemaphoreType.DMA
    one = lambda i: jnp.minimum(i, TEAM - 1)
    two = lambda i: jnp.maximum(i - TEAM, 0)
    rows = lambda c, turn: pl.BlockSpec((BLK, c), lambda i: (turn(i), 0))
    cube = lambda a, b: pl.BlockSpec((1, a, b), lambda i: (one(i), 0, 0))
    fixed = lambda a, b: pl.BlockSpec((a, b), lambda i: (0, 0))
    return pl.pallas_call(
        forward_kernel,
        grid=(2 * TEAM,),
        in_specs=[any_space] * 4 + [
            pl.BlockSpec(a.shape, lambda i, n=a.ndim: (0,) * n, pipeline_mode=pl.Buffered(1)) for a in (ids, *small)],
        out_specs=[rows(D, one), rows(REST, one), rows(NZ, two), cube(STATE, CH), rows(CH, two),
                   rows(CH, two), rows(D, two), rows(128, one), fixed(TEAM, 2 * BLK), fixed(16, CONVC),
                   any_space, any_space],
        out_shape=[sds((n, D), BF), sds((n, REST), BF), sds((n, NZ), BF), sds((TEAM, STATE, CH), F32),
                   sds((n, CH), F32), sds((n, CH), F32), sds((n, D), BF), sds((n, 128), F32), sds((TEAM, 2 * BLK), F32),
                   sds((16, CONVC), F32), sds((COLS, D), BF), sds((n, D), BF)],
        scratch_shapes=[pltpu.VMEM((n, D), BF), pltpu.VMEM((n, D), BF), pltpu.VMEM((COLS, D), BF),
                        pltpu.VMEM((CH, D), BF), pltpu.VMEM((16, CONVC), BF), pltpu.VMEM((DEPTH - 1, 16, CONVC), BF),
                        pltpu.VMEM((n, CH), F32), pltpu.VMEM((BLK + 8, CONVC), F32),
                        pltpu.VMEM((STATE, CH), F32), pltpu.VMEM((TEAM, 2 * BLK), F32),
                        pltpu.VMEM((TEAM, TEAM, 2 * BLK), F32),
                        dma((20,)), dma((2, 3)), dma((2, 3)), dma((2, 2)), dma((2, 2)), dma((2, 5)),
                        dma((2, 5)), dma((5, 2, DEPTH - 1)), dma((5, 2, DEPTH - 1)),
                        dma((2, DEPTH - 1)), dma((2, DEPTH - 1)),
                        dma((DEPTH,)), dma((DEPTH,)), dma((TEAM,)), dma((TEAM,))],
        compiler_params=pltpu.CompilerParams(
            collective_id=0, has_side_effects=True, vmem_limit_bytes=60 << 20),
    )(tok, cot, win, wout, ids, *small)


def backward_kernel(
    tok_ref, cot_ref, nrm_ref, br_ref, w_ref, g_ref,
    projz_ref, ssd_ref, dno_ref, stat_ref, par_ref, projc_ref, halo_ref, st_ref, info_ref, ids_ref,
    out_ref, tg_ref, wig_ref, wog_ref, smalls_ref,
    nrm_v, g_v, w_v, not_v, dz_v, dzt_v, dy_v, rest_v, wig_v, wog_v, bcd_v, bcd_in,
    zz_in, zx_in, zb_in, zw_in, zs_in, zz_rel, zx_rel, zb_rel, zw_rel, gz_v, gx_v, gb_v, gw_v, gb_in, gt_v, ob_v, rb_v, in_v, rel_v,
    tok_v, cot_v, small_v, small_s, cbuf, dcbuf, dstate,
    loc, b_send, b_recv, p_send, p_recv, d_send, d_recv, q_send, q_recv, z_send, z_recv, s_send, s_recv,
    a_send, a_recv, f_send, f_recv, h_send, h_recv, free,
):
    i = pl.program_id(0)
    seq, chip, core, z = places()
    sib = {"seq": 2 * chip + 1 - core}
    near = neighbours(chip)
    peer = lambda k: {"seq": 2 * near[k] + core}
    under = lambda k: {"fsdp": lax.rem(z + k, DEPTH)}
    around = lambda k: {"seq": lax.rem(seq + k, TEAM)}
    block = lambda s: pl.ds(pl.multiple_of(BLK * s, BLK), BLK)
    lanes = lambda o: pl.ds(pl.multiple_of(KROWS * o, KROWS), KROWS)
    piece = lambda n: pl.ds(pl.multiple_of(HEADDIM * n, HEADDIM), HEADDIM)
    half = lambda c: pl.ds(pl.multiple_of(HALF * c, 16), HALF)
    extra = lambda o: lax.rem(o, 2) == core
    n_all = HEADDIM * HPD
    give = lambda c: g_v.at[block(c)]
    hold = lambda c: g_v.at[block(CHIPS + c)]

    def load(n):
        pairs = [(nrm_ref, nrm_v), (g_ref, g_v), (w_ref, w_v), (tok_ref, tok_v), (cot_ref, cot_v)]
        return pltpu.make_async_copy(pairs[n][0], pairs[n][1], loc.at[n])

    def load_own(c):
        return pltpu.make_async_copy(br_ref.at[block(2 * c + core)], ob_v.at[c], loc.at[5 + c])

    def br_pair(c):
        return send(br_ref.at[block(2 * c + 1 - core)], rb_v.at[c], b_send.at[c], b_recv.at[c], sib)

    def block_of(n, c):
        return ob_v.at[c] if n == 0 else hold(c)

    def rs(n, kind):
        h = pl.ds((0, BLK // 2, BLK // 2, 0, 0, BLK // 2)[kind], BLK // 2)
        src = block_of(n, near[(1, 1, 2, 2, 3, 3)[kind]]).at[h]
        if kind < 4:
            dst = in_v.at[n, kind // 2, h]
        else:
            dst = rel_v.at[n, 5 - kind]
        return send(src, dst, p_send.at[n, kind], p_recv.at[n, kind], peer((1, 1, 2, 2, 1, 2)[kind]))

    def rs_first(n, role):
        for kind in ((), (0,), (2,), (4, 5))[role]:
            rs(n, kind).start()

    def rs_second(n, role):
        kind, came = ((1, 5), (3, 4))[role - 1]
        rs(n, came).wait_recv()
        h = pl.ds((BLK // 2, 0)[role - 1], BLK // 2)
        ref = block_of(n, near[role]).at[h]
        ref[...] = ref[...] + rel_v[n, role - 1]
        rs(n, kind).start()

    def rs_total(n):
        for kind in range(4):
            rs(n, kind).wait_recv()
        return block_of(n, chip)[...].astype(F32) + in_v[n, 0].astype(F32) + in_v[n, 1].astype(F32)

    def dn_pair(c):
        return send(give(c), rb_v.at[c], d_send.at[c], d_recv.at[c], sib)

    mate = z + 1 - 2 * lax.rem(z, 2)
    outer = (z == 0) | (z == DEPTH - 1)
    far = lambda j: (2 + j) - lax.div(z, 2) * (1 + 2 * j)
    rest = [slice(None)] * 3 + [slice(0, HEADDIM), slice(HEADDIM, 2 * HEADDIM)]
    z_in = [zz_in, zx_in, zb_in, zw_in, zw_in]
    z_rel = [zz_rel, zx_rel, zb_rel, zw_rel, zw_rel]

    def z_part(n, o):
        if n < 2:
            return wig_v.at[:, lanes(o)]
        if n == 2:
            return bcd_v.at[half(core), lanes(o)]
        return wog_v.at[piece(o if n == 3 else DEPTH + lax.div(o, 2))]

    def z_mate(n):
        return send(z_part(n, mate), z_in[n].at[0, rest[n]], z_send.at[n, 0], z_recv.at[n, 0], {"fsdp": mate})

    def z_hand(n, j):
        return send(z_part(n, far(j)), z_rel[n].at[j, rest[n]], z_send.at[n, 2 + j], z_recv.at[n, 2 + j], {"fsdp": mate})

    def z_far(n, j):
        return send(z_part(n, far(j)), z_in[n].at[1, rest[n]], z_send.at[n, 2 + j], z_recv.at[n, 1], {"fsdp": far(j)})

    def held(n, o, also=None):
        if n == 4:
            return extra(o) if also is None else extra(o) & also
        return also

    def under_cond(cond, body):
        if cond is None:
            body()
        else:
            pl.when(cond)(body)

    def z_start(n):
        for j in (1, 0):
            under_cond(held(n, far(j), outer), lambda: z_hand(n, j).start())

    def z_start_mate(n):
        under_cond(held(n, mate), lambda: z_mate(n).start())

    def z_relay(n):
        for j in (1, 0):

            def body():
                z_hand(n, j).wait_recv()
                ref = z_part(n, far(j))
                ref[...] = ref[...] + z_rel[n][j, rest[n]]
                z_far(n, j).start()

            under_cond(held(n, far(j), jnp.logical_not(outer)), body)

    def z_total(n):
        z_mate(n).wait_recv()
        z_far(n, 0).wait_recv()
        return z_part(n, z)[...].astype(F32) + z_in[n][0, rest[n]].astype(F32) + z_in[n][1, rest[n]].astype(F32)

    def z_close(n):
        under_cond(held(n, mate), lambda: z_mate(n).wait_send())
        for j in range(2):
            under_cond(held(n, far(j)), lambda: z_far(n, j).wait_send())

    def small_copy(k):
        return send(small_v, zs_in.at[k - 1], s_send.at[k], s_recv.at[k], under(k))

    def bcd_pair():
        return send(bcd_v.at[half(1 - core)], bcd_in, h_send.at[0], h_recv.at[0], sib)

    def bcd_push(k):
        return send(gb_v, gb_in.at[k - 1], q_send.at[k], q_recv.at[k], peer(k))

    def bcd_back():
        return send(gt_v.at[core], gt_v.at[core], h_send.at[1], h_recv.at[1], sib)

    def parts(n, c, cr, h=None):
        if n < 2:
            base = n * DI // HEADDIM
            src = (gz_v, gx_v)[n]
            slots = range(HPD) if h is None else range(3 * h, 3 * h + 3)
            return [(src.at[piece(s)], wig_ref.at[piece(base + head_of(s, c, cr)[s // 4])]) for s in slots]
        if n < 4:
            row = HEADDIM * (3 * c + 2 * cr if n == 2 else 3 * c + 1)
            first, size = (0, HEADDIM) if h is None else (h * HEADDIM // 2, HEADDIM // 2)
            return [(gw_v.at[pl.ds(HEADDIM * (n - 2) + first, size)],
                     wog_ref.at[pl.ds(pl.multiple_of(row + first, HEADDIM // 2), size)])]
        if h is None:
            return [(small_s, smalls_ref.at[2 * c + cr])]
        return [(small_s.at[8 * h : 8 * h + 8], smalls_ref.at[2 * c + cr, 8 * h : 8 * h + 8])]

    def all_of(n, h=None):
        if n < 2:
            return wig_ref.at[pl.ds(n * DI, n_all if h is None else n_all // 2)]
        return parts(n, 0, 0, h)[0][1]

    def ag(n, k):
        if k < 3:
            return [send(src, dst, a_send.at[n, k], a_recv.at[n, k], sib if k == 0 else peer(k))
                    for src, dst in parts(n, chip, core)]
        return [send(dst, dst, a_send.at[n, k], a_recv.at[n, k], peer(5 - k))
                for _, dst in parts(n, near[k - 2], core, k - 3)]

    def ag_wait(n, k):
        ref = all_of(n, None if k < 3 else k - 3)
        return send(ref, ref, a_send.at[n, k], a_recv.at[n, k], sib)

    def ag_next(n, k):
        which = parts(n, near[k], core) if k < 3 else parts(n, near[3], core, k - 3)
        return [send(dst, dst, f_send.at[n, k], f_recv.at[n, k], sib) for _, dst in which]

    def ag_next_wait(n, k):
        ref = all_of(n, None if k < 3 else k - 3)
        return send(ref, ref, f_send.at[n, k], f_recv.at[n, k], sib)

    def ag_own(n):
        return [pltpu.make_async_copy(src, dst, loc.at[9 + n]) for src, dst in parts(n, chip, core)]

    def ag_own_wait(n):
        return pltpu.make_async_copy(all_of(n), all_of(n), loc.at[9 + n])

    def ag_start(n):
        for k in (1, 2, 0):
            for copy in ag(n, k):
                copy.start()
        for copy in ag_own(n):
            copy.start()

    def ag_turn(n):
        for k in (1, 2):
            ag_wait(n, k).wait_recv()
            for copy in ag(n, k + 2) + ag_next(n, k):
                copy.start()

    def ag_end(n):
        for k in (3, 4):
            ag_wait(n, k).wait_recv()
            for copy in ag_next(n, k):
                copy.start()

    def ag_close(n, sends=True, receives=True):
        if receives:
            ag_wait(n, 0).wait_recv()
            for k in range(1, 5):
                ag_next_wait(n, k).wait_recv()
        if sends:
            for k in range(5):
                ag_wait(n, k).wait_send()
            for k in range(1, 5):
                ag_next_wait(n, k).wait_send()
            ag_own_wait(n).wait()

    @pl.when(i == 0)
    def _():
        greet([around(k) for k in range(1, TEAM)] + [under(k) for k in range(1, DEPTH)])
        for c in range(CHIPS):
            br_pair(c).start()
            load_own(c).start()
        for n in range(5):
            load(n).start()
        small_v[...] = jnp.zeros_like(small_v)
        dstate[...] = jnp.zeros_like(dstate)
        dcbuf[BLK : BLK + 8, :] = jnp.zeros((8, CONVC), F32)

    @pl.when(i < TEAM)
    def _():
        gate_backward(i, projz_ref[...].astype(F32), ssd_ref[...], dno_ref[...],
                      stat_ref[pl.ds(i, 1), :], par_ref[5:6, :CH], not_v, dy_v, dz_v, dzt_v, small_v)

    @pl.when(i == 1)
    def _():
        for c in range(CHIPS):
            load_own(c).wait()
            br_pair(c).wait_recv()
            ob_v[c] = ob_v[c] + rb_v[c]
        for role in (3, 1, 2):
            rs_first(0, role)
        pl.semaphore_signal(free, inc=1, device_id=sib, device_id_type=pl.DeviceIdType.MESH)

    @pl.when(i == TEAM)
    def _():
        pl.semaphore_wait(free, 1)
        for n in range(5):
            load(n).wait()

        @pl.loop(0, D // 512)
        def _(n):
            cols = pl.ds(pl.multiple_of(512 * n, 512), 512)
            wig_v[:, cols] = dot(dzt_v[...], nrm_v[:, cols]).astype(BF)

        z_start(0)

        @pl.loop(0, D // 512)
        def _(n):
            cols = pl.ds(pl.multiple_of(512 * n, 512), 512)
            wog_v[:, cols] = dot(not_v[...], g_v[:, cols]).astype(BF)

        z_start(3)
        z_start(4)
        for n in (0, 3, 4):
            z_start_mate(n)

    def combine(c):
        dn_pair(c).wait_recv()
        hold(c)[...] = hold(c)[...] + rb_v[c]
        for role in (1, 2, 3):

            @pl.when(near[role] == c)
            def _():
                rs_first(1, role)

    def relay(c):
        for role in (1, 2):

            @pl.when(near[role] == c)
            def _():
                rs_second(1, role)

    for c in range(CHIPS - 1, 0, -1):

        @pl.when(i == TEAM + 1 + 2 * (CHIPS - c))
        def _():
            combine(c)
            if c < CHIPS - 1:
                relay(c + 1)

    @pl.when(i == TEAM + 2)
    def _():
        rs_second(0, 1)
        rs_second(0, 2)

    @pl.when(i == 2 * TEAM)
    def _():
        gz_v[...] = z_total(0).astype(BF)
        ag_start(0)

    @pl.when((i > TEAM) & (i <= 2 * TEAM))
    def _():
        j = 2 * TEAM - i
        rows = block(j)
        d_rest = scan_backward(projc_ref[...], halo_ref[...], info_ref[...], id_row(ids_ref, j), st_ref[0],
                               par_ref[...], dy_v[rows, :], cbuf, dcbuf, dstate, small_v)
        rest_v[:, rows] = d_rest.T.astype(BF)
        dn = dot(jnp.concatenate([dz_v[rows, :], d_rest.astype(BF)], axis=1), w_v[...])
        part = jnp.sum(dn * nrm_v[rows, :].astype(F32), axis=0, keepdims=True)
        for n in range(D // CH):
            small_v[7 + n : 8 + n, :CH] += part[:, CH * n : CH * n + CH]
        dn = dn.astype(BF)
        c = lax.div(j, 2)

        @pl.when(lax.rem(j, 2) == core)
        def _():
            hold(c)[...] = dn

        @pl.when(lax.rem(j, 2) != core)
        def _():
            give(c)[...] = dn
            dn_pair(c).start()

    @pl.when(i == 2 * TEAM - 1)
    def _():
        total = rs_total(0)
        stat = stat_ref[pl.ds(seq, 1), 0:BLK]
        stat = jnp.broadcast_to(stat, (128, BLK)).T
        s2 = lax.rsqrt(stat[:, 0:1] * (1.0 / DI) + EPSILON)
        out_ref[...] = (tok_v[...].astype(F32) + total * s2).astype(BF)

    @pl.when(i == TEAM + 4)
    def _():
        z_relay(0)

    @pl.when(i == TEAM + 6)
    def _():
        z_relay(3)
        z_relay(4)

    @pl.when(i == 2 * TEAM + 1)
    def _():
        for n in range(D // CH):
            small_v[7 + n : 8 + n, :CH] = small_v[7 + n : 8 + n, :CH] / par_ref[7 + n : 8 + n, :CH]
        for k in range(1, DEPTH):
            small_copy(k).start()
        combine(0)

        relay(1)
        z_close(0)

        @pl.loop(0, D // 512)
        def _(n):
            cols = pl.ds(pl.multiple_of(512 * n, 512), 512)
            both = dot(rest_v[...], nrm_v[:, cols]).astype(BF)
            wig_v[:, cols] = both[:NX]
            bcd_v[:, cols] = both[NX:]

        bcd_pair().start()
        z_start(1)
        z_start_mate(1)
        bcd_pair().wait_recv()
        bcd_v[half(core), :] = bcd_v[half(core), :] + bcd_in[...]
        z_start(2)
        z_start_mate(2)
        gw_v[0:HEADDIM, :] = z_total(3).astype(BF)
        ag_start(2)

        @pl.when(extra(z))
        def _():
            gw_v[HEADDIM:, :] = z_total(4).astype(BF)
            ag_start(3)

        relay(0)
        total = small_v[...]
        for k in range(1, DEPTH):
            small_copy(k).wait_recv()
            total = total + zs_in[k - 1]
        small_s[...] = total
        ag_start(4)
        ag_turn(0)
        z_relay(1)
        z_relay(2)
        ag_turn(2)

        @pl.when(extra(z))
        def _():
            ag_turn(3)

        ag_turn(4)
        ag_end(0)
        total = rs_total(1)
        uf = tok_v[...].astype(F32)
        along = total * norm_gain(par_ref[...])
        s1 = lax.rsqrt(jnp.mean(uf * uf, axis=1, keepdims=True) + EPSILON)
        tg_ref[...] = cot_v[...].astype(F32) + s1 * along - uf * (
            s1 * s1 * s1 * jnp.mean(along * uf, axis=1, keepdims=True))
        gx_v[...] = z_total(1).astype(BF)
        ag_start(1)
        ag_end(2)

        @pl.when(extra(z))
        def _():
            ag_end(3)

        ag_end(4)
        gb_v[...] = z_total(2).astype(BF)
        for k in range(1, CHIPS):
            bcd_push(k).start()
        ag_turn(1)
        for k in range(1, CHIPS):
            bcd_push(k).wait_recv()
        total = gb_v[...].astype(F32)
        for k in range(1, CHIPS):
            total = total + gb_in[k - 1].astype(F32)
        gt_v[core] = total.astype(BF)
        bcd_back().start()
        ag_end(1)
        bcd_back().wait()
        last = [
            pltpu.make_async_copy(gt_v.at[0], wig_ref.at[pl.ds(2 * DI, HALF)], loc.at[15]),
            pltpu.make_async_copy(gt_v.at[1, 0 : WIDTH - 2 * DI - HALF],
                                  wig_ref.at[pl.ds(2 * DI + HALF, WIDTH - 2 * DI - HALF)], loc.at[16])]
        for copy in last:
            copy.start()
        for n in (0, 1, 2, 4):
            ag_close(n)

        @pl.when(extra(z))
        def _():
            ag_close(3, receives=False)

        @pl.when(jnp.logical_not(extra(z)))
        def _():
            ag_close(3, sends=False)

        for c in range(CHIPS):
            br_pair(c).wait_send()
            dn_pair(c).wait_send()
        for n in range(2):
            for kind in range(6):
                rs(n, kind).wait_send()
        for k in range(1, CHIPS):
            bcd_push(k).wait_send()
        for k in range(1, DEPTH):
            small_copy(k).wait_send()
        for n in (1, 2, 3, 4):
            z_close(n)
        bcd_pair().wait_send()
        for copy in last:
            copy.wait()


def backward_call(tok, cot, nrm, br, w, g, projz, ssd, dno, stat, par, projc, st, info, ids):
    n = nrm.shape[0]
    any_space = pl.BlockSpec(memory_space=pl.ANY)
    sds = jax.ShapeDtypeStruct
    dma = pltpu.SemaphoreType.DMA
    one = lambda i: jnp.minimum(i, TEAM - 1)
    two = lambda i: jnp.clip(2 * TEAM - i, 0, TEAM - 1)
    rows = lambda c, turn: pl.BlockSpec((BLK, c), lambda i: (turn(i), 0))
    cube = lambda a, b: pl.BlockSpec((1, a, b), lambda i: (two(i), 0, 0))
    fixed = lambda a, b: pl.BlockSpec((a, b), lambda i: (0, 0), pipeline_mode=pl.Buffered(1))
    vm = pltpu.VMEM
    return pl.pallas_call(
        backward_kernel,
        grid=(2 * TEAM + 2,),
        in_specs=[any_space] * 6 + [
            rows(NZ, one), rows(CH, one), rows(CH, one), fixed(TEAM, 2 * BLK), fixed(16, CONVC), rows(REST, two),
            pl.BlockSpec((16, REST), lambda i: (jnp.maximum(16 * two(i) - 1, 0), 0)),
            cube(STATE, CH), rows(128, two), fixed(1, n)],
        out_specs=[fixed(BLK, D), fixed(BLK, D), any_space, any_space, any_space],
        out_shape=[sds((BLK, D), BF), sds((BLK, D), F32), sds((WIDTH, KROWS), BF),
                   sds((DI // DEPTH, D), BF), sds((TEAM, 16, CONVC), F32)],
        scratch_shapes=[
            vm((n, D), BF), vm((n, D), BF), vm((COLS, D), BF), vm((CH, n), BF), vm((n, CH), BF), vm((CH, n), BF),
            vm((n, CH), F32), vm((REST, n), BF), vm((CH, D), BF), vm((CH, D), BF), vm((BCD, D), BF),
            vm((HALF, D), BF),
            vm((2, CH, KROWS), BF), vm((2, CH, KROWS), BF), vm((2, HALF, KROWS), BF), vm((2, 2 * HEADDIM, D), BF),
            vm((DEPTH - 1, 16, CONVC), F32),
            vm((2, CH, KROWS), BF), vm((2, CH, KROWS), BF), vm((2, HALF, KROWS), BF), vm((2, 2 * HEADDIM, D), BF), vm((CH, KROWS), BF), vm((CH, KROWS), BF),
            vm((HALF, KROWS), BF), vm((2 * HEADDIM, D), BF), vm((CHIPS - 1, HALF, KROWS), BF), vm((2, HALF, KROWS), BF),
            vm((CHIPS, BLK, D), BF), vm((CHIPS, BLK, D), BF), vm((2, 2, BLK, D), BF), vm((2, 2, BLK // 2, D), BF),
            vm((BLK, D), BF), vm((BLK, D), BF), vm((16, CONVC), F32), vm((16, CONVC), F32),
            vm((BLK + 8, CONVC), F32), vm((BLK + 8, CONVC), F32), vm((STATE, CH), F32),
            dma((17,)), dma((CHIPS,)), dma((CHIPS,)), dma((2, 6)), dma((2, 6)), dma((CHIPS,)), dma((CHIPS,)),
            dma((CHIPS,)), dma((CHIPS,)), dma((5, 4)), dma((5, 4)), dma((DEPTH,)), dma((DEPTH,)),
            dma((5, 5)), dma((5, 5)), dma((5, 5)), dma((5, 5)), dma((2,)), dma((2,)),
            pltpu.SemaphoreType.REGULAR],
        compiler_params=pltpu.CompilerParams(
            collective_id=1, has_side_effects=True, vmem_limit_bytes=63 << 20),
    )(tok, cot, nrm, br, w, g, projz, ssd, dno, stat, par, projc, projc, st, info, ids)


def finish_kernel(
    lo_ref, tg_ref, wig_ref, wog_ref, smalls_ref,
    out_ref, grad_ref, win_ref, wout_ref, convw_ref, convb_ref, alog_ref, dtb_ref, skip_ref, normw_ref, gatew_ref,
    all_v, in_v, in_f, wo_v, wo_f, lo_v, tg_v, sems,
):
    rows_in, rows_wo = WIDTH // 13, DI // DEPTH // 4
    chunks = [(wig_ref, in_v, in_f, win_ref, slice(rows_in * n, rows_in * n + rows_in)) for n in range(13)]
    chunks += [(wog_ref, wo_v, wo_f, wout_ref, slice(rows_wo * n, rows_wo * n + rows_wo)) for n in range(4)]
    come = [pltpu.make_async_copy(a.at[r], b.at[r], sems.at[0, n]) for n, (a, b, _, _, r) in enumerate(chunks)]
    go = [pltpu.make_async_copy(a.at[r], b.at[r], sems.at[1, n]) for n, (_, _, a, b, r) in enumerate(chunks)]
    last = len(chunks)
    enter = [pltpu.make_async_copy(lo_ref, lo_v, sems.at[0, last]), pltpu.make_async_copy(tg_ref, tg_v, sems.at[0, last + 1])]
    leave = [pltpu.make_async_copy(lo_v, out_ref, sems.at[1, last]), pltpu.make_async_copy(tg_v, grad_ref, sems.at[1, last + 1])]
    for copy in come + enter:
        copy.start()
    for n, (_, src, dst, _, r) in enumerate(chunks):
        come[n].wait()
        dst[r] = src[r].astype(F32)
        go[n].start()
    for n in range(2):
        enter[n].wait()
        leave[n].start()
    for d in range(TEAM):
        for slot in range(HPD):
            head = head_of(slot, d // 2, d % 2)[slot // 4]
            all_v[:, HEADDIM * head : HEADDIM * head + HEADDIM] = smalls_ref[
                d, 0:8, HEADDIM * slot : HEADDIM * slot + HEADDIM]
    side = smalls_ref[0, :, CH:]
    gain = smalls_ref[0, :, :CH]
    for d in range(1, TEAM):
        side = side + smalls_ref[d, :, CH:]
        gain = gain + smalls_ref[d, :, :CH]
    all_v[:, DI:] = side[0:8]
    z = lax.axis_index("fsdp")
    nc, ng, nh = CHAN // DEPTH, DI // DEPTH, HEADS // DEPTH
    for o in range(DEPTH):

        @pl.when(z == o)
        def _():
            convw_ref[...] = all_v[0:CONV, nc * o : nc * o + nc]
            convb_ref[...] = all_v[CONV : CONV + 1, nc * o : nc * o + nc].reshape(nc)
            gatew_ref[...] = all_v[5:6, ng * o : ng * o + ng].reshape(ng)
            alog_ref[...] = side[5:6, nh * o : nh * o + nh].reshape(nh)
            dtb_ref[...] = side[5:6, 128 + nh * o : 128 + nh * o + nh].reshape(nh)
            skip_ref[...] = side[6:7, nh * o : nh * o + nh].reshape(nh)
            normw_ref[...] = gain[7 + o : 8 + o, :].reshape(KROWS)

    for copy in go + leave:
        copy.wait()


def finish_call(lo, tg, wig, wog, smalls):
    any_space = pl.BlockSpec(memory_space=pl.ANY)
    vmem = pl.BlockSpec(memory_space=pltpu.VMEM)
    sizes = [(CONV, CHAN // DEPTH), (CHAN // DEPTH,)] + [(HEADS // DEPTH,)] * 3 + [(KROWS,), (DI // DEPTH,)]
    sds = jax.ShapeDtypeStruct
    rows = DI // DEPTH
    return pl.pallas_call(
        finish_kernel,
        in_specs=[any_space] * 4 + [vmem],
        out_specs=[any_space] * 4 + [vmem] * len(sizes),
        out_shape=[sds((BLK, D), BF), sds((BLK, D), F32), sds((WIDTH, KROWS), F32), sds((rows, D), F32)]
        + [sds(s, F32) for s in sizes],
        scratch_shapes=[pltpu.VMEM((8, CHAN), F32), pltpu.VMEM((WIDTH, KROWS), BF), pltpu.VMEM((WIDTH, KROWS), F32),
                        pltpu.VMEM((rows, D), BF), pltpu.VMEM((rows, D), F32), pltpu.VMEM((BLK, D), BF), pltpu.VMEM((BLK, D), F32),
                        pltpu.SemaphoreType.DMA((2, 19))],
        compiler_params=pltpu.CompilerParams(vmem_limit_bytes=62 << 20),
    )(lo, tg, wig, wog, smalls)


def on_team(
    tokens, segment_ids, cotangent, w_in, w_out, conv_w, conv_b, a_log, dt_bias, d_skip,
    norm_w, gate_w,
):
    tok, cot = tokens[0], cotangent[0]
    small = (conv_w, conv_b, a_log, dt_bias, d_skip, norm_w, gate_w)
    nrm, projc, projz, st, ssd, dno, br, info, stat, par, w_loc, g = forward_call(
        tok, cot, w_in.T, w_out, segment_ids, small)
    lo, tg, wig, wog, smalls = backward_call(
        tok, cot, nrm, br, w_loc, g, projz, ssd, dno, stat, par, projc, st, info, segment_ids)
    lo, tg, wig, wog, convw, convb, alog, dtb, skip, normw, gatew = finish_call(lo, tg, wig, wog, smalls)
    return (lo[None], tg[None], wig.T, wog, convw, convb, alog, dtb, skip, normw, gatew)


def solution(mesh):
    body = on_team if (mesh.shape["seq"], mesh.shape["fsdp"]) == (TEAM, DEPTH) else on_device
    return jax.shard_map(
        body,
        mesh=mesh,
        in_specs=(
            P("fsdp", "seq", None),
            P("fsdp", None),
            P("fsdp", "seq", None),
            P("fsdp", None),
            P("fsdp", None),
            P(None, "fsdp"),
            P("fsdp"),
            P("fsdp"),
            P("fsdp"),
            P("fsdp"),
            P("fsdp"),
            P("fsdp"),
        ),
        out_specs=(
            P("fsdp", "seq", None),
            P("fsdp", "seq", None),
            P("fsdp", None),
            P("fsdp", None),
            P(None, "fsdp"),
            P("fsdp"),
            P("fsdp"),
            P("fsdp"),
            P("fsdp"),
            P("fsdp"),
            P("fsdp"),
        ),
        check_vma=False,
    )
```

```python
import jax
import jax.numpy as jnp
from jax import lax
from jax.experimental import pallas as pl
from jax.experimental.pallas import tpu as pltpu
from jax.sharding import PartitionSpec as P

DI = 3072
HEADDIM = 64
STATE = 128
CONV = 4
SPAN = 256
HEADS = 48
D = 1536
WIDTH = 6448
DEPTH = 4
CHAN = 3328


EPSILON = 1e-05
HIGHEST = lax.Precision.HIGHEST


def passed_along(value, axis, steps):
    count = lax.axis_size(axis)
    first, last = (max(0, -steps), min(count, count - steps))
    return lax.ppermute(value, axis, [(source, source + steps) for source in range(first, last)])


def shortened(array):

    def short(part):
        return part.astype(jnp.bfloat16) if part.dtype == jnp.float32 else part

    return jax.tree.map(short, array)


def block_masks(ids_blocks, before_ids):
    block_len = ids_blocks.shape[1]
    places = jnp.arange(block_len)
    causal_mask = (places[:, None] >= places[None, :])[None] & (
        ids_blocks[:, :, None] == ids_blocks[:, None, :]
    )
    keep_flag = (ids_blocks == before_ids[:, None]).astype(jnp.float32)
    same_last = (ids_blocks == ids_blocks[:, -1:]).astype(jnp.float32)
    return (causal_mask, keep_flag, same_last)


def local_states(x_heads, b_rows, step_size, log_decay, same_last, keep_flag):
    cum_decay = jnp.cumsum(log_decay, axis=1)
    last_cum = cum_decay[:, -1]
    weights = jnp.exp(last_cum[:, None, :] - cum_decay) * step_size * same_last[:, :, None]
    fresh_state = jnp.einsum("csh,cshp,csn->chpn", weights, x_heads, b_rows, precision=HIGHEST)
    passing = keep_flag[:, -1:] * jnp.exp(last_cum)
    total_state = jnp.zeros_like(fresh_state[0])
    total_decay = jnp.ones_like(passing[0])
    total_state = fresh_state[0] + passing[0][:, None, None] * total_state
    total_decay = total_decay * passing[0]
    return (fresh_state, passing, total_state, total_decay)


def local_output(x_heads, b_rows, c_rows, step_size, log_decay, incoming, causal_mask, keep_flag):
    cum_decay = jnp.cumsum(log_decay, axis=1)
    cum_heads = jnp.swapaxes(cum_decay, 1, 2)
    gap_decay = cum_heads[:, :, :, None] - cum_heads[:, :, None, :]
    head_mask = causal_mask[:, None]
    decay_map = jnp.exp(jnp.where(head_mask, gap_decay, 0.0)) * head_mask.astype(jnp.float32)
    scores = jnp.einsum("ctn,csn->cts", c_rows, b_rows, precision=HIGHEST)
    mixing = scores[:, None] * decay_map * jnp.swapaxes(step_size, 1, 2)[:, :, None, :]
    inner_out = jnp.einsum("chts,cshp->cthp", mixing, x_heads, precision=HIGHEST)
    starts = [incoming]
    start_states = jnp.stack(starts)
    carried = jnp.einsum("ctn,chpn->cthp", c_rows, start_states, precision=HIGHEST)
    carried = carried * (keep_flag[:, :, None] * jnp.exp(cum_decay))[..., None]
    return inner_out + carried


def on_device(
    tokens,
    segment_ids,
    cotangent,
    w_in,
    w_out,
    conv_w,
    conv_b,
    a_log,
    dt_bias,
    d_skip,
    norm_w,
    gate_w,
):
    gathered = (
        lax.all_gather(w_in, "fsdp", axis=0, tiled=True),
        lax.all_gather(w_out, "fsdp", axis=0, tiled=True),
        lax.all_gather(conv_w, "fsdp", axis=1, tiled=True),
        lax.all_gather(conv_b, "fsdp", axis=0, tiled=True),
        lax.all_gather(a_log, "fsdp", axis=0, tiled=True),
        lax.all_gather(dt_bias, "fsdp", axis=0, tiled=True),
        lax.all_gather(d_skip, "fsdp", axis=0, tiled=True),
        lax.all_gather(norm_w, "fsdp", axis=0, tiled=True),
        lax.all_gather(gate_w, "fsdp", axis=0, tiled=True),
    )
    (
        w_in_full,
        w_out_full,
        conv_full,
        bias_full,
        a_log_full,
        dt_bias_full,
        skip_full,
        norm_full,
        gate_full,
    ) = gathered
    inputs = tokens[0].astype(jnp.float32)
    length = inputs.shape[0]
    norm_gain = norm_full.astype(jnp.float32)
    scale_in = lax.rsqrt(jnp.mean(inputs * inputs, axis=-1, keepdims=True) + EPSILON)
    normed = (inputs * scale_in * norm_gain).astype(jnp.bfloat16)
    projected = jnp.dot(normed, w_in_full, preferred_element_type=jnp.float32).astype(jnp.bfloat16)
    gate_z = projected[:, :DI].astype(jnp.float32)
    conv_in = projected[:, DI : DI + CHAN]
    dt_raw = projected[:, DI + CHAN :].astype(jnp.float32)
    first_row = lax.axis_index("seq") * length
    id_row = jnp.concatenate([jnp.full((CONV - 1,), -1, jnp.int32), segment_ids[0]], axis=0)
    ids_pad = lax.dynamic_slice_in_dim(id_row, first_row, length + CONV - 1)
    ids_own = ids_pad[CONV - 1 :]
    left_edge = passed_along(conv_in[length - (CONV - 1) :], "seq", 1)
    padded = jnp.concatenate([left_edge, conv_in], axis=0).astype(jnp.float32)
    kernel = conv_full.astype(jnp.float32)
    conv_out = jnp.zeros((length, CHAN), jnp.float32) + bias_full.astype(jnp.float32)
    same_docs = []
    for offset in range(CONV):
        same_doc = (ids_pad[offset : offset + length] == ids_own).astype(jnp.float32)
        same_docs.append(same_doc)
        conv_out = conv_out + kernel[offset] * padded[offset : offset + length] * same_doc[:, None]
    activated = jax.nn.silu(conv_out)
    blocks = length // SPAN
    x_heads = activated[:, :DI].reshape(blocks, SPAN, HEADS, HEADDIM)
    b_rows = activated[:, DI : DI + STATE].reshape(blocks, SPAN, STATE)
    c_rows = activated[:, DI + STATE :].reshape(blocks, SPAN, STATE)
    dt_bias_f = dt_bias_full.astype(jnp.float32)
    decay_rate = jnp.exp(a_log_full.astype(jnp.float32))
    step_flat = jax.nn.softplus(dt_raw + dt_bias_f)
    step_size = step_flat.reshape(blocks, SPAN, HEADS)
    log_decay = (-step_flat * decay_rate).reshape(blocks, SPAN, HEADS)
    ids_blocks = ids_own.reshape(blocks, SPAN)
    before_ids = ids_pad[CONV - 2 : CONV - 2 + length : SPAN]
    causal_mask, keep_flag, same_last = block_masks(ids_blocks, before_ids)

    def state_part(heads_in, rows_b, steps_in, decay_in):
        return local_states(heads_in, rows_b, steps_in, decay_in, same_last, keep_flag)

    (fresh_state, passing, total_state, total_decay), state_pull = jax.vjp(
        state_part, x_heads, b_rows, step_size, log_decay
    )

    def pass_forward(turn_index, received):
        return passed_along(
            (total_state + total_decay[:, None, None] * received).astype(jnp.bfloat16), "seq", 1
        ).astype(jnp.float32)

    incoming = lax.fori_loop(0, lax.axis_size("seq") - 1, pass_forward, jnp.zeros_like(total_state))

    def output_part(
        heads_in, rows_b, rows_c, steps_in, decay_in, fresh_in, passing_in, incoming_in
    ):
        return local_output(
            heads_in, rows_b, rows_c, steps_in, decay_in, incoming_in, causal_mask, keep_flag
        )

    ssd_out, output_pull = jax.vjp(
        output_part, x_heads, b_rows, c_rows, step_size, log_decay, fresh_state, passing, incoming
    )
    skip_heads = skip_full.astype(jnp.float32)
    y_full = (ssd_out + skip_heads[:, None] * x_heads).reshape(length, DI)
    silu_z = jax.nn.silu(gate_z)
    gated = y_full * silu_z
    scale_out = lax.rsqrt(jnp.mean(gated * gated, axis=-1, keepdims=True) + EPSILON)
    gate_gain = gate_full.astype(jnp.float32)
    normed_out = (gated * scale_out * gate_gain).astype(jnp.bfloat16)
    branch = jnp.dot(normed_out, w_out_full, preferred_element_type=jnp.float32)
    layer_out = (inputs + branch).astype(jnp.bfloat16)[None]
    grad_out = cotangent[0]
    d_w_out = lax.dot_general(
        normed_out, grad_out, (((0,), (0,)), ((), ())), preferred_element_type=jnp.float32
    )
    d_normed_out = lax.dot_general(
        grad_out, w_out_full, (((1,), (1,)), ((), ())), preferred_element_type=jnp.float32
    )
    d_gate_w = jnp.sum(d_normed_out * gated * scale_out, axis=0)
    along_out = d_normed_out * gate_gain
    cube_out = scale_out * scale_out * scale_out
    d_gated = scale_out * along_out - gated * cube_out * jnp.mean(
        along_out * gated, axis=-1, keepdims=True
    )
    d_y = d_gated * silu_z
    sig_z = jax.nn.sigmoid(gate_z)
    d_gate_z = d_gated * y_full * sig_z * (1.0 + gate_z * (1.0 - sig_z))
    d_ssd = d_y.reshape(blocks, SPAN, HEADS, HEADDIM)
    d_skip_grad = jnp.sum(d_ssd * x_heads, axis=(0, 1, 3))
    dx_out, db_out, dc_out, dstep_out, ddecay_out, d_fresh, d_passing, d_incoming = output_pull(
        d_ssd
    )

    def pass_backward(turn_index, received):
        return passed_along(d_incoming + total_decay[:, None, None] * received, "seq", -1)

    d_total = lax.fori_loop(0, lax.axis_size("seq") - 1, pass_backward, jnp.zeros_like(d_incoming))
    d_total_decay = jnp.sum(d_total * incoming, axis=(1, 2))
    dx_state, db_state, dstep_state, ddecay_state = state_pull(
        (d_fresh, d_passing, d_total, d_total_decay)
    )
    d_x = dx_out + dx_state + skip_heads[:, None] * d_ssd
    d_b = db_out + db_state
    d_log = (ddecay_out + ddecay_state).reshape(length, HEADS)
    d_step = (dstep_out + dstep_state).reshape(length, HEADS) - d_log * decay_rate
    d_a_log = -jnp.sum(d_log * step_flat, axis=0) * decay_rate
    d_dt_raw = d_step * jax.nn.sigmoid(dt_raw + dt_bias_f)
    d_dt_bias = jnp.sum(d_dt_raw, axis=0)
    d_act = jnp.concatenate(
        [d_x.reshape(length, DI), d_b.reshape(length, STATE), dc_out.reshape(length, STATE)], axis=1
    )
    sig_conv = jax.nn.sigmoid(conv_out)
    d_conv = d_act * sig_conv * (1.0 + conv_out * (1.0 - sig_conv))
    d_conv_b = jnp.sum(d_conv, axis=0)
    kernel_rows = []
    d_padded = jnp.zeros((length + CONV - 1, CHAN), jnp.float32)
    for offset in range(CONV):
        masked = d_conv * same_docs[offset][:, None]
        kernel_rows.append(jnp.sum(masked * padded[offset : offset + length], axis=0))
        d_padded = d_padded + jnp.pad(
            kernel[offset] * masked, ((offset, CONV - 1 - offset), (0, 0))
        )
    d_kernel = jnp.stack(kernel_rows)
    d_edge = passed_along(shortened(d_padded[: CONV - 1]), "seq", -1)
    d_conv_in = d_padded[CONV - 1 :] + jnp.pad(d_edge, ((length - (CONV - 1), 0), (0, 0)))
    d_projected = jnp.concatenate([d_gate_z, d_conv_in, d_dt_raw], axis=1).astype(jnp.bfloat16)
    d_normed = lax.dot_general(
        d_projected, w_in_full, (((1,), (1,)), ((), ())), preferred_element_type=jnp.float32
    )
    d_norm_w = jnp.sum(d_normed * inputs * scale_in, axis=0)
    along_in = d_normed * norm_gain
    cube_in = scale_in * scale_in * scale_in
    d_inputs = (
        scale_in * along_in
        - inputs * cube_in * jnp.mean(along_in * inputs, axis=-1, keepdims=True)
        + grad_out.astype(jnp.float32)
    )
    d_w_in = lax.dot_general(
        normed, d_projected, (((0,), (0,)), ((), ())), preferred_element_type=jnp.float32
    )
    weight_grads = (
        d_w_in,
        d_w_out,
        d_kernel,
        d_conv_b,
        d_a_log,
        d_dt_bias,
        d_skip_grad,
        d_norm_w,
        d_gate_w,
    )
    shares = tuple(
        (
            lax.psum_scatter(weight_grads[0], "fsdp", scatter_dimension=0, tiled=True),
            lax.psum_scatter(weight_grads[1], "fsdp", scatter_dimension=0, tiled=True),
            lax.psum_scatter(weight_grads[2], "fsdp", scatter_dimension=1, tiled=True),
            lax.psum_scatter(weight_grads[3], "fsdp", scatter_dimension=0, tiled=True),
            lax.psum_scatter(weight_grads[4], "fsdp", scatter_dimension=0, tiled=True),
            lax.psum_scatter(weight_grads[5], "fsdp", scatter_dimension=0, tiled=True),
            lax.psum_scatter(weight_grads[6], "fsdp", scatter_dimension=0, tiled=True),
            lax.psum_scatter(weight_grads[7], "fsdp", scatter_dimension=0, tiled=True),
            lax.psum_scatter(weight_grads[8], "fsdp", scatter_dimension=0, tiled=True),
        )
    )
    totals = lax.psum(shares, "seq")
    return (layer_out, d_inputs[None]) + tuple(totals)


F32 = jnp.float32
BF = jnp.bfloat16
BLK = 256
TEAM = 8
HPD = HEADS // TEAM
CH = HPD * HEADDIM
NZ, NX, NB, ND = CH, CH, 2 * STATE, 64
COLS = NZ + NX + NB + ND
REST = NX + NB + ND
CONVC = NX + NB
TAIL = CONV - 1


def dot(a, b):
    return lax.dot_general(a, b, (((1,), (0,)), ((), ())), preferred_element_type=F32)


def dot_nt(a, b):
    return lax.dot_general(a, b, (((1,), (1,)), ((), ())), preferred_element_type=F32)


def dot_tn(a, b):
    return lax.dot_general(a, b, (((0,), (0,)), ((), ())), preferred_element_type=F32)


def dot_exact(a, b):
    high = b.astype(BF)
    left = b - high.astype(F32)
    middle = left.astype(BF)
    low = (left - middle.astype(F32)).astype(BF)
    n = b.shape[1]
    p = dot(a.astype(BF), jnp.concatenate([high, middle, low], axis=1))
    return p[:, :n] + p[:, n : 2 * n] + p[:, 2 * n :]


def iota(shape, dim):
    return lax.broadcasted_iota(jnp.int32, shape, dim)


def split_dot(a, b):
    high = a.astype(BF)
    low = (a - high.astype(F32)).astype(BF)
    return dot(high, b) + dot(low, b)


def spread():
    return (iota((128, CH), 1) // HEADDIM == iota((128, CH), 0)).astype(BF)


def gather_heads():
    return (iota((CH, 128), 0) // HEADDIM == iota((CH, 128), 1)).astype(BF)


def lower_tri():
    return (iota((BLK, BLK), 0) >= iota((BLK, BLK), 1)).astype(F32)


def softplus(v):
    return jnp.maximum(v, 0.0) + jnp.log1p(jnp.exp(-jnp.abs(v)))


def sigmoid(v):
    return 1.0 / (1.0 + jnp.exp(-v))


def conv_taps(cbuf, cw, tok):
    out = cw[CONV : CONV + 1, :] + cw[CONV - 1 : CONV, :] * cbuf[8 : 8 + BLK, :]
    for back in range(1, CONV):
        term = cw[CONV - 1 - back : CONV - back, :] * cbuf[8 - back : 8 - back + BLK, :]
        out = out + term * tok[:, back : back + 1]
    return out


def pair_select(left, right):
    return jnp.where(iota(left.shape, 1) % 128 < HEADDIM, left, right)


def head_of(slot, chip, core):
    first = 12 * slot + 3 * chip + 2 * core
    second = 12 * (core + 2 * (slot - 4)) + 3 * chip + 1
    return first, second


def pick_heads():
    seq = lax.axis_index("seq")
    chip, core = lax.div(seq, 2), lax.rem(seq, 2)
    slot = iota((128, 128), 1)
    first, second = head_of(slot, chip, core)
    head = jnp.where(slot < 4, first, jnp.where(slot < HPD, second, -1))
    return (iota((128, 128), 0) == head).astype(BF)


def own_heads(par, dt_cols):
    pick = pick_heads()
    pair = jnp.concatenate([par[5:6, CH : CH + 128], par[5:6, CH + 128 :], jnp.zeros((6, 128), F32)], axis=0)
    pair = dot(pair.astype(BF), pick)
    wide = jnp.concatenate([dt_cols, jnp.zeros((BLK, 128 - ND), BF)], axis=1)
    return jnp.exp(pair[1:2, :]), dot(wide, pick) + pair[0:1, :], iota((BLK, 128), 1) < HPD, pick


def norm_gain(par):
    return jnp.concatenate([par[7 + i : 8 + i, :CH] for i in range(D // CH)], axis=1)


def row_sum(q):
    high = q.astype(BF)
    low = (q - high.astype(F32)).astype(BF)
    ones = jnp.ones((8, q.shape[1]), BF)
    return (dot_nt(ones, high) + dot_nt(ones, low))[0:1, :]


def scan_forward(j, nrm, w_v, par, tok, idr, cbuf, state, projc_ref, st_ref, ssd_v):
    rows = pl.ds(pl.multiple_of(BLK * j, BLK), BLK)
    proj = dot_nt(nrm, w_v[NZ:, :]).astype(BF)
    projc_ref[...] = proj
    cbuf[8 : 8 + BLK, :] = proj[:, :CONVC].astype(F32)
    conv_out = conv_taps(cbuf, par, tok)
    cbuf[0:8, :] = cbuf[BLK : BLK + 8, :]
    act = conv_out * sigmoid(conv_out)
    x = act[:, :CH]
    bm = act[:, CH : CH + STATE].astype(BF)
    cm = act[:, CH + STATE :].astype(BF)
    rate, dt_in, own, pick = own_heads(par, proj[:, CONVC:])
    step = jnp.where(own, softplus(dt_in), 0.0)
    cum = dot_exact(lower_tri(), -step * rate)
    cum_t = cum.T
    mask = (iota((BLK, BLK), 0) >= iota((BLK, BLK), 1)) & (tok[:, 0:1] == idr)
    gm = jnp.where(mask, dot_nt(cm, bm), 0.0)
    ex = spread()
    xs = (x * split_dot(step, ex)).astype(BF)
    parts = []
    for pair in range(HPD // 2):
        xp = xs[:, 128 * pair : 128 * pair + 128]
        both = []
        for h in (2 * pair, 2 * pair + 1):
            decay = jnp.exp(jnp.minimum(cum[:, h : h + 1] - cum_t[h : h + 1, :], 0.0))
            both.append(dot((gm * decay).astype(BF), xp))
        parts.append(pair_select(*both))
    inner = jnp.concatenate(parts, axis=1)
    old = state[...]
    st_ref[0] = old
    keep = tok[:, 7:8]
    carried = split_dot(keep * jnp.exp(cum), ex) * dot(cm, old.astype(BF))
    last = cum[BLK - 1 : BLK, :]
    weights = jnp.exp(last - cum) * step * tok[:, 8:9]
    through = split_dot(jnp.broadcast_to(keep[BLK - 1 :, :] * jnp.exp(last), (8, 128)), ex)[0:1, :]
    state[...] = dot_tn(bm, (x * split_dot(weights, ex)).astype(BF)) + through * old
    ssd_v[rows, :] = inner + carried + par[6:7, :CH] * x


def gate_forward(j, nrm_v, g_v, w_v, wo_v, par, ssd_v, projz_ref, ssd_ref, dno_ref, br_ref, stat_v):
    rows = pl.ds(pl.multiple_of(BLK * j, BLK), BLK)
    projz = dot_nt(nrm_v[rows, :], w_v[:NZ, :]).astype(BF)
    projz_ref[...] = projz
    ssd = ssd_v[rows, :]
    ssd_ref[...] = ssd
    z = projz.astype(F32)
    gate_w = par[5:6, :CH]
    gated = ssd * (z * sigmoid(z))
    br_ref[...] = dot((gated * gate_w).astype(BF), wo_v[...]).astype(BF)
    dno = dot_nt(g_v[rows, :], wo_v[...])
    dno_ref[...] = dno
    stat_v[pl.ds(j, 1), 0:BLK] = row_sum(gated * gated)
    stat_v[pl.ds(j, 1), BLK : 2 * BLK] = row_sum(dno * gate_w * gated)


def gate_backward(j, z, ssd, dno, stat, gate_w, not_v, dy_v, dz_v, dzt_v, small_v):
    rows = pl.ds(pl.multiple_of(BLK * j, BLK), BLK)
    sig_z = sigmoid(z)
    silu_z = z * sig_z
    stat = jnp.where(iota((128, BLK), 0) == 0, stat[:, :BLK], stat[:, BLK:]).T
    s2 = lax.rsqrt(stat[:, 0:1] * (1.0 / DI) + EPSILON)
    mean_ag = stat[:, 1:2] * (1.0 / DI)
    gated = ssd * silu_z
    gs = gated * s2
    not_v[:, rows] = (gs * gate_w).T.astype(BF)
    d_gated = s2 * (dno * gate_w) - gated * (s2 * s2 * s2 * mean_ag)
    dy_v[rows, :] = d_gated * silu_z
    dz = d_gated * ssd * sig_z * (1.0 + z * (1.0 - sig_z))
    dz_v[rows, :] = dz.astype(BF)
    dzt_v[:, rows] = dz.T.astype(BF)
    small_v[5:6, :CH] += jnp.sum(dno * gs, axis=0, keepdims=True)


def scan_backward(proj, halo, tok, idr, old, par, dy, cbuf, dcbuf, dstate, small_v):
    cbuf[0:8, :] = halo[8:16, :CONVC].astype(F32)
    cbuf[8 : 8 + BLK, :] = proj[:, :CONVC].astype(F32)
    conv_out = conv_taps(cbuf, par, tok)
    sig_c = sigmoid(conv_out)
    act = conv_out * sig_c
    x = act[:, :CH]
    bm = act[:, CH : CH + STATE].astype(BF)
    cm_f = act[:, CH + STATE :]
    cm = cm_f.astype(BF)
    rate, dt_in, own, pick = own_heads(par, proj[:, CONVC:])
    step = jnp.where(own, softplus(dt_in), 0.0)
    cum = dot_exact(lower_tri(), -step * rate)
    cum_t = cum.T
    mask = (iota((BLK, BLK), 0) >= iota((BLK, BLK), 1)) & (tok[:, 0:1] == idr)
    gm = jnp.where(mask, dot_nt(cm, bm), 0.0)
    ex = spread()
    gh = gather_heads()
    step_x = dot(step.astype(BF), ex)
    xs = (x * step_x).astype(BF)
    dyb = dy.astype(BF)
    dyt = dy.T.astype(BF)
    lane = iota((BLK, 128), 1)
    dg = jnp.zeros((BLK, BLK), F32)
    row_sums = jnp.zeros((BLK, 128), F32)
    col_sums = []
    e_rows = []
    for h in range(HPD):
        pair = h // 2
        decay = jnp.exp(jnp.minimum(cum[:, h : h + 1] - cum_t[h : h + 1, :], 0.0))
        mixed = gm * decay
        half = jnp.where((lane < HEADDIM) == (h % 2 == 0), dyb[:, 128 * pair : 128 * pair + 128], 0)
        dms = dot_nt(half.astype(BF), xs[:, 128 * pair : 128 * pair + 128])
        product = dms * mixed
        row_sums = jnp.where(lane == h, jnp.sum(product, axis=1, keepdims=True), row_sums)
        col_sums.append(jnp.sum(product, axis=0, keepdims=True))
        dg = dg + dms * decay
        e_rows.append(dot(dyt[HEADDIM * h : HEADDIM * h + HEADDIM, :], mixed.astype(BF)))
    dg = jnp.where(mask, dg, 0.0).astype(BF)
    e = jnp.concatenate(e_rows, axis=0).T
    col_sums.append(jnp.zeros((128 - HPD, BLK), F32))
    col = jnp.concatenate(col_sums, axis=0).T
    keep = tok[:, 7:8]
    old_b = old.astype(BF)
    dnew = dstate[...]
    dnew_b = dnew.astype(BF)
    carry_x = dot((keep * jnp.exp(cum)).astype(BF), ex)
    dyk_f = dy * carry_x
    dyk = dyk_f.astype(BF)
    carried = dot(cm, old_b)
    last = cum[BLK - 1 : BLK, :]
    fade = jnp.exp(last - cum) * tok[:, 8:9]
    weights = fade * step
    weights_x = dot(weights.astype(BF), ex)
    zt = dot(bm, dnew_b)
    xw = (x * weights_x).astype(BF)
    through = keep[BLK - 1 :, :] * jnp.exp(last)
    through_x = split_dot(jnp.broadcast_to(through, (8, 128)), ex)[0:1, :]
    k_term = dot((dyk_f * carried).astype(BF), gh)
    r_term = dot((x * zt).astype(BF), gh)
    q_term = dot((x * e).astype(BF), gh)
    pass_term = jnp.sum(old * dnew, axis=0, keepdims=True) * through_x
    pass_h = split_dot(jnp.broadcast_to(pass_term, (8, CH)), gh)[0:1, :]
    wr = weights * r_term
    d_cum = row_sums - col + k_term - wr
    d_last = jnp.sum(wr, axis=0, keepdims=True) + pass_h
    d_cum = d_cum + jnp.where(iota((BLK, 128), 0) == BLK - 1, d_last, 0.0)
    upper = (iota((BLK, BLK), 0) <= iota((BLK, BLK), 1)).astype(F32)
    d_log = dot_exact(upper, d_cum)
    d_step = q_term + fade * r_term - d_log * rate
    d_a = -jnp.sum(d_log * step, axis=0, keepdims=True) * rate
    d_dt = jnp.where(own, d_step * sigmoid(dt_in), 0.0)
    d_skip = split_dot(jnp.broadcast_to(jnp.sum(dy * x, axis=0, keepdims=True), (8, CH)), gh)[0:1, :]
    d_skip = jnp.where(own[0:1, :], d_skip, 0.0)
    heads = jnp.concatenate(
        [d_a, jnp.sum(d_dt, axis=0, keepdims=True), d_skip, jnp.zeros((5, 128), F32)], axis=0)
    high = heads.astype(BF)
    heads = dot_nt(high, pick) + dot_nt((heads - high.astype(F32)).astype(BF), pick)
    d_dt = dot_nt(d_dt.astype(BF), pick)
    dstate[...] = dot_tn(cm, dyk) + through_x * dnew
    dx = step_x * e + weights_x * zt + par[6:7, :CH] * dy
    dc = dot(dg, bm) + dot_nt(dyk, old_b)
    db = dot(cm_f.T.astype(BF), dg).T + dot_nt(xw, dnew_b)
    d_act = jnp.concatenate([dx, db, dc], axis=1)
    d_conv = d_act * (sig_c * (1.0 + conv_out * (1.0 - sig_c)))
    dcbuf[0:BLK, :] = d_conv
    d_in = par[CONV - 1 : CONV, :] * d_conv
    cg = [None] * CONV
    cg[CONV - 1] = jnp.sum(d_conv * cbuf[8 : 8 + BLK, :], axis=0, keepdims=True)
    for back in range(1, CONV):
        tap = CONV - 1 - back
        cg[tap] = jnp.sum(
            d_conv * (cbuf[8 - back : 8 - back + BLK, :] * tok[:, back : back + 1]),
            axis=0, keepdims=True,
        )
        d_in = d_in + par[tap : tap + 1, :] * (
            dcbuf[back : back + BLK, :] * tok[:, 3 + back : 4 + back]
        )
    dcbuf[BLK : BLK + 8, :] = dcbuf[0:8, :]
    small_v[0:CONV, :] += jnp.concatenate(cg, axis=0)
    small_v[CONV : CONV + 1, :] += jnp.sum(d_conv, axis=0, keepdims=True)
    small_v[5:6, CH:] += jnp.concatenate([heads[0:1, :], heads[1:2, :]], axis=1)
    small_v[6:7, CH : CH + 128] += heads[2:3, :]
    return jnp.concatenate([d_in, d_dt[:, :ND]], axis=1)


def id_row(ids_ref, j):
    return ids_ref[0:1, pl.ds(pl.multiple_of(BLK * j, BLK), BLK)].astype(F32)


def token_info(ids_ref, j, blocks):
    row = id_row(ids_ref, j)
    left = jnp.where(j > 0, id_row(ids_ref, jnp.maximum(j - 1, 0)), -1.0)
    right = jnp.where(j < blocks - 1, id_row(ids_ref, jnp.minimum(j + 1, blocks - 1)), -2.0)
    lane = iota((1, BLK), 1)
    wide = lambda a: jnp.broadcast_to(a, (8, BLK))
    rows = [row]
    for back in range(1, CONV):
        shifted = jnp.where(lane < back, pltpu.roll(wide(left), back, 1)[0:1], pltpu.roll(wide(row), back, 1)[0:1])
        rows.append((shifted == row).astype(F32))
    for ahead in range(1, CONV):
        turn = BLK - ahead
        shifted = jnp.where(lane >= turn, pltpu.roll(wide(right), turn, 1)[0:1], pltpu.roll(wide(row), turn, 1)[0:1])
        rows.append((shifted == row).astype(F32))
    rows.append((row == left[:, BLK - 1 :]).astype(F32))
    rows.append((row == row[:, BLK - 1 :]).astype(F32))
    rows.append(jnp.zeros((128 - len(rows), BLK), F32))
    return row, jnp.concatenate(rows, axis=0).T


def pack_small(convw, convb, alog, dtb, dskip, normw, gatew, chip, core, z):
    def channel(m):
        slot = m // HEADDIM
        first, second = head_of(slot, chip, core)
        return jnp.where(slot < 4, first, second) * HEADDIM + m % HEADDIM

    row = lambda a: a.astype(F32).reshape(1, a.shape[0])
    pad = lambda a: jnp.concatenate([row(a), jnp.zeros((1, 128 - HEADS // DEPTH), F32)], axis=1)
    heads = jnp.concatenate([pad(dtb), pad(alog), pad(dskip), jnp.zeros((5, 128), F32)], axis=0).astype(BF)
    m = iota((CHAN // DEPTH, CONVC), 1)
    want = jnp.where(m < CH, channel(m), DI + m - CH)
    chosen = (iota((CHAN // DEPTH, CONVC), 0) + z * (CHAN // DEPTH) == want).astype(BF)
    conv = jnp.concatenate([convw.astype(F32), row(convb), jnp.zeros((3, CHAN // DEPTH), F32)], axis=0)
    conv = dot(conv.astype(BF), chosen)
    n = DI // DEPTH
    chosen = (iota((n, CH), 0) + z * n == channel(iota((n, CH), 1))).astype(BF)
    gate = dot(jnp.broadcast_to(row(gatew), (8, n)).astype(BF), chosen)[0:1]
    n = HEADS // DEPTH
    k = iota((128, CH), 0)
    chosen = ((k < n) & (k + z * n == channel(iota((128, CH), 1)) // HEADDIM)).astype(BF)
    skip = dot(heads, chosen)[2:3]
    k = iota((128, 128), 0)
    chosen = ((k < n) & (k + z * n == iota((128, 128), 1))).astype(BF)
    heads = dot(heads, chosen)
    gain = jnp.where(iota((DEPTH, CH), 0) == z, jnp.broadcast_to(row(normw), (DEPTH, CH)), 0.0)
    return jnp.concatenate([
        conv[0:5],
        jnp.concatenate([gate, heads[0:1], heads[1:2]], axis=1),
        jnp.concatenate([skip, jnp.zeros((1, NB), F32)], axis=1),
        jnp.concatenate([gain, jnp.zeros((DEPTH, NB), F32)], axis=1),
        jnp.zeros((5, CONVC), F32)], axis=0).astype(BF)


CHIPS = TEAM // 2
KROWS = D // DEPTH
BCD = NB + ND
HALF = BCD // 2


def places():
    seq = lax.axis_index("seq")
    return seq, lax.div(seq, 2), lax.rem(seq, 2), lax.axis_index("fsdp")


def neighbours(chip):
    return [chip, chip + 1 - 2 * lax.rem(chip, 2), lax.rem(chip + 2, CHIPS), CHIPS - 1 - chip]


def send(src, dst, send_sem, recv_sem, device):
    return pltpu.make_async_remote_copy(
        src_ref=src, dst_ref=dst, send_sem=send_sem, recv_sem=recv_sem,
        device_id=device, device_id_type=pl.DeviceIdType.MESH,
    )


def greet(devices):
    barrier = pltpu.get_barrier_semaphore()
    for device in devices:
        pl.semaphore_signal(
            barrier, inc=1, device_id=device, device_id_type=pl.DeviceIdType.MESH
        )
    pl.semaphore_wait(barrier, len(devices))


def forward_kernel(
    tok_ref, cot_ref, win_ref, wout_ref, ids_ref, convw_ref, convb_ref, alog_ref, dtb_ref, skip_ref, normw_ref, gatew_ref,
    nrm_ref, projc_ref, projz_ref, st_ref, ssd_ref, dno_ref, br_ref, info_ref, stat_ref, par_ref, w_ref, g_ref,
    u_v, g_v, w_v, wo_v, small_v, smalls, ssd_v, cbuf, state, stat_v, stat_in,
    loc, t_send, t_recv, y_send, y_recv, f_send, f_recv, z_send, z_recv, b_send, b_recv, s_send, s_recv, r_send, r_recv,
):
    i = pl.program_id(0)
    seq, chip, core, z = places()
    sib = {"seq": 2 * chip + 1 - core}
    near = neighbours(chip)
    peer = lambda k: {"seq": 2 * near[k] + core}
    under = lambda k: {"fsdp": lax.rem(z + k, DEPTH)}
    around = lambda k: {"seq": lax.rem(seq + k, TEAM)}
    block = lambda s: pl.ds(pl.multiple_of(BLK * s, BLK), BLK)
    lanes = lambda o: pl.ds(pl.multiple_of(KROWS * o, KROWS), KROWS)
    half = pl.ds(pl.multiple_of(NZ + NX + HALF * core, 16), HALF)
    has = [z < DEPTH - 1, z > 0]
    heads = [head_of(n, chip, core)[n // 4] for n in range(HPD)]
    piece = lambda n: pl.ds(pl.multiple_of(HEADDIM * n, HEADDIM), HEADDIM)

    def token_copy(n, k):
        src, dst = ((tok_ref, u_v), (cot_ref, g_v))[n]
        return send(src, dst.at[block(seq)], t_send.at[n, k], t_recv.at[n, k], sib if k == 0 else peer(k))

    def token_part(n, k, h):
        return (u_v, g_v)[n].at[pl.ds(pl.multiple_of(BLK * (2 * near[k] + core) + h * (BLK // 2), BLK // 2), BLK // 2)]

    def token_relay(n, h):
        part = token_part(n, 1 + h, h)
        return send(part, part, y_send.at[n, h], y_recv.at[n, h], peer(2 - h))

    def token_next(n, k):
        if k < 3:
            ref = (u_v, g_v)[n].at[block(2 * near[k] + core)]
        else:
            ref = token_part(n, 3, k - 3)
        return send(ref, ref, f_send.at[n, k], f_recv.at[n, k], sib)

    def token_start(n):
        for k in range(3):
            token_copy(n, k).start()

    def token_turn(n):
        for k in (1, 2):
            token_copy(n, k).wait_recv()
            token_relay(n, k - 1).start()
            token_next(n, k).start()

    def token_end(n):
        for h in range(2):
            token_relay(n, h).wait_recv()
            token_next(n, 3 + h).start()
        token_copy(n, 0).wait_recv()
        for k in range(1, 5):
            token_next(n, k).wait()
        for h in range(2):
            token_relay(n, h).wait_send()

    def place(p, o):
        if p < 3:
            return w_v.at[(pl.ds(NZ, NX), half, pl.ds(0, NZ))[p], lanes(o)]
        return wo_v.at[piece(o if p == 3 else DEPTH + lax.div(o, 2))]

    def hop(p, side, dist):
        o = z - dist if side == 0 else z + dist
        there = {"fsdp": z + 1} if side == 0 else {"fsdp": z - 1}
        return send(place(p, o), place(p, o), z_send.at[p, side, dist], z_recv.at[p, side, dist], there)

    def got(p, side, dist):
        o = z - dist - 1 if side == 0 else z + dist + 1
        there = {"fsdp": z + 1} if side == 0 else {"fsdp": z - 1}
        return send(place(p, o), place(p, o), z_send.at[p, side, dist], z_recv.at[p, side, dist], there)

    def share(side, dist):
        o = z - dist - 1 if side == 0 else z + dist + 1
        return send(place(1, o), place(1, o), b_send.at[side, dist], b_recv.at[side, dist], sib)

    def exists(p, side, hops):
        o = z - hops if side == 0 else z + hops
        there = (o >= 0) if side == 0 else (o < DEPTH)
        return there & (lax.rem(o + DEPTH, 2) == core) if p == 4 else there

    def small_copy(k):
        return send(small_v, smalls.at[k - 1], s_send.at[k], s_recv.at[k], under(k))

    def stat_copy(k):
        return send(stat_v, stat_in.at[k], r_send.at[k], r_recv.at[k], around(k))

    def local_copies():
        pairs = [(tok_ref, u_v.at[block(seq)]), (cot_ref, g_v.at[block(seq)])]
        return [pltpu.make_async_copy(src, dst, loc.at[n]) for n, (src, dst) in enumerate(pairs)]

    def own_weights():
        pairs = [(win_ref.at[pl.ds(2 * DI, WIDTH - 2 * DI)], w_v.at[pl.ds(NZ + NX, WIDTH - 2 * DI), lanes(z)], 3)]
        for n in range(HPD):
            row = HEADDIM * heads[n]
            pairs.append((win_ref.at[pl.ds(pl.multiple_of(row, HEADDIM), HEADDIM)],
                          w_v.at[piece(n), lanes(z)], 4 + n))
            pairs.append((win_ref.at[pl.ds(pl.multiple_of(DI + row, HEADDIM), HEADDIM)],
                          w_v.at[piece(HPD + n), lanes(z)], 10 + n))
        pairs.append((wout_ref.at[piece(3 * chip + 2 * core)], place(3, z), 16))
        return [pltpu.make_async_copy(src, dst, loc.at[n]) for src, dst, n in pairs]

    def own_extra():
        return pltpu.make_async_copy(wout_ref.at[piece(3 * chip + 1)], place(4, z), loc.at[17])

    def pass_on(parts, dist):
        for p in parts:
            for side in range(2):

                @pl.when(exists(p, side, dist + 1))
                def _():
                    got(p, side, dist).wait_recv()
                    if p == 1:
                        share(side, dist).start()

                if dist < DEPTH - 2:

                    @pl.when(exists(p, side, dist + 1) & has[side])
                    def _():
                        hop(p, side, dist + 1).start()

    def start_own(parts):
        for p in parts:
            for side in range(2):

                @pl.when(exists(p, side, 0) & has[side])
                def _():
                    hop(p, side, 0).start()

    @pl.when(i == 0)
    def _():
        greet([around(k) for k in range(1, TEAM)] + [under(k) for k in range(1, DEPTH)])
        token_start(0)
        for copy in own_weights() + local_copies():
            copy.start()

        @pl.when(lax.rem(z, 2) == core)
        def _():
            own_extra().start()

        w_v[NZ + NX + WIDTH - 2 * DI :, lanes(z)] = jnp.zeros((BCD - (WIDTH - 2 * DI), KROWS), BF)
        for copy in own_weights():
            copy.wait()
        start_own((0, 1))
        small_v[...] = pack_small(convw_ref[...], convb_ref[...], alog_ref[...], dtb_ref[...], skip_ref[...],
                                  normw_ref[...], gatew_ref[...], chip, core, z)
        for k in range(1, DEPTH):
            small_copy(k).start()
        state[...] = jnp.zeros_like(state)
        cbuf[0:8, :] = jnp.zeros((8, CONVC), F32)
        pass_on((0, 1), 0)
        token_turn(0)
        token_start(1)
        pass_on((0, 1), 1)
        start_own((2,))
        token_end(0)
        pass_on((0, 1), 2)
        for k in range(1, DEPTH):
            small_copy(k).wait()
        for copy in local_copies():
            copy.wait()
        for side in range(2):
            for dist in range(DEPTH - 1):

                @pl.when(exists(1, side, dist + 1))
                def _():
                    share(side, dist).wait()

        total = small_v[...].astype(F32)
        for k in range(1, DEPTH):
            total = total + smalls[k - 1].astype(F32)
        par_ref[...] = total

    @pl.when(i == 1)
    def _():
        @pl.when(lax.rem(z, 2) == core)
        def _():
            own_extra().wait()

        pass_on((2,), 0)
        start_own((3, 4))

    @pl.when(i == 3)
    def _():
        pass_on((2,), 1)

    @pl.when(i == 4)
    def _():
        token_turn(1)

    @pl.when(i == 5)
    def _():
        pass_on((3, 4), 0)

    @pl.when(i == 7)
    def _():
        pass_on((3, 4), 1)

    @pl.when(i == TEAM)
    def _():
        pass_on((2, 3, 4), 2)
        token_end(1)
        pltpu.make_async_copy(w_v, w_ref, loc.at[18]).start()
        pltpu.make_async_copy(g_v, g_ref, loc.at[19]).start()

    par = par_ref[...]

    @pl.when(i < TEAM)
    def _():
        u = u_v[block(i), :].astype(F32)
        scale = lax.rsqrt(jnp.mean(u * u, axis=1, keepdims=True) + EPSILON)
        nrm = (u * scale * norm_gain(par)).astype(BF)
        nrm_ref[...] = nrm
        u_v[block(i), :] = nrm
        row, info = token_info(ids_ref, i, TEAM)
        info_ref[...] = info
        scan_forward(i, nrm, w_v, par, info, row, cbuf, state,
                     projc_ref, st_ref, ssd_v)

    @pl.when(i >= TEAM)
    def _():
        gate_forward(i - TEAM, u_v, g_v, w_v, wo_v, par, ssd_v, projz_ref, ssd_ref, dno_ref,
                     br_ref, stat_v)

    @pl.when(i == 2 * TEAM - 1)
    def _():
        for k in range(1, TEAM):
            stat_copy(k).start()
        total = stat_v[...]
        for k in range(1, TEAM):
            stat_copy(k).wait_recv()
            total = total + stat_in[k]
        stat_ref[...] = total
        for k in range(1, TEAM):
            stat_copy(k).wait_send()
        for n in range(2):
            for k in range(3):
                token_copy(n, k).wait_send()
        for side in range(2):
            for dist in range(DEPTH - 1):
                for p in range(5):

                    @pl.when(exists(p, side, dist) & has[side])
                    def _():
                        hop(p, side, dist).wait_send()

        pltpu.make_async_copy(w_v, w_ref, loc.at[18]).wait()
        pltpu.make_async_copy(g_v, g_ref, loc.at[19]).wait()


def forward_call(tok, cot, win, wout, ids, small):
    n = tok.shape[0] * TEAM
    any_space = pl.BlockSpec(memory_space=pl.ANY)
    sds = jax.ShapeDtypeStruct
    dma = pltpu.SemaphoreType.DMA
    one = lambda i: jnp.minimum(i, TEAM - 1)
    two = lambda i: jnp.maximum(i - TEAM, 0)
    rows = lambda c, turn: pl.BlockSpec((BLK, c), lambda i: (turn(i), 0))
    cube = lambda a, b: pl.BlockSpec((1, a, b), lambda i: (one(i), 0, 0))
    fixed = lambda a, b: pl.BlockSpec((a, b), lambda i: (0, 0))
    return pl.pallas_call(
        forward_kernel,
        grid=(2 * TEAM,),
        in_specs=[any_space] * 4 + [
            pl.BlockSpec(a.shape, lambda i, n=a.ndim: (0,) * n, pipeline_mode=pl.Buffered(1)) for a in (ids, *small)],
        out_specs=[rows(D, one), rows(REST, one), rows(NZ, two), cube(STATE, CH), rows(CH, two),
                   rows(CH, two), rows(D, two), rows(128, one), fixed(TEAM, 2 * BLK), fixed(16, CONVC),
                   any_space, any_space],
        out_shape=[sds((n, D), BF), sds((n, REST), BF), sds((n, NZ), BF), sds((TEAM, STATE, CH), F32),
                   sds((n, CH), F32), sds((n, CH), F32), sds((n, D), BF), sds((n, 128), F32), sds((TEAM, 2 * BLK), F32),
                   sds((16, CONVC), F32), sds((COLS, D), BF), sds((n, D), BF)],
        scratch_shapes=[pltpu.VMEM((n, D), BF), pltpu.VMEM((n, D), BF), pltpu.VMEM((COLS, D), BF),
                        pltpu.VMEM((CH, D), BF), pltpu.VMEM((16, CONVC), BF), pltpu.VMEM((DEPTH - 1, 16, CONVC), BF),
                        pltpu.VMEM((n, CH), F32), pltpu.VMEM((BLK + 8, CONVC), F32),
                        pltpu.VMEM((STATE, CH), F32), pltpu.VMEM((TEAM, 2 * BLK), F32),
                        pltpu.VMEM((TEAM, TEAM, 2 * BLK), F32),
                        dma((20,)), dma((2, 3)), dma((2, 3)), dma((2, 2)), dma((2, 2)), dma((2, 5)),
                        dma((2, 5)), dma((5, 2, DEPTH - 1)), dma((5, 2, DEPTH - 1)),
                        dma((2, DEPTH - 1)), dma((2, DEPTH - 1)),
                        dma((DEPTH,)), dma((DEPTH,)), dma((TEAM,)), dma((TEAM,))],
        compiler_params=pltpu.CompilerParams(
            collective_id=0, has_side_effects=True, vmem_limit_bytes=60 << 20),
    )(tok, cot, win, wout, ids, *small)


def backward_kernel(
    tok_ref, cot_ref, nrm_ref, br_ref, w_ref, g_ref,
    projz_ref, ssd_ref, dno_ref, stat_ref, par_ref, projc_ref, halo_ref, st_ref, info_ref, ids_ref,
    out_ref, tg_ref, wig_ref, wog_ref, smalls_ref,
    nrm_v, g_v, w_v, not_v, dz_v, dzt_v, dy_v, rest_v, wig_v, wog_v, bcd_v, bcd_in,
    zz_in, zx_in, zb_in, zw_in, zs_in, zz_rel, zx_rel, zb_rel, zw_rel, gz_v, gx_v, gb_v, gw_v, gb_in, gt_v, ob_v, rb_v, in_v, rel_v,
    tok_v, cot_v, small_v, small_s, cbuf, dcbuf, dstate,
    loc, b_send, b_recv, p_send, p_recv, d_send, d_recv, q_send, q_recv, z_send, z_recv, s_send, s_recv,
    a_send, a_recv, f_send, f_recv, h_send, h_recv, free,
):
    i = pl.program_id(0)
    seq, chip, core, z = places()
    sib = {"seq": 2 * chip + 1 - core}
    near = neighbours(chip)
    peer = lambda k: {"seq": 2 * near[k] + core}
    under = lambda k: {"fsdp": lax.rem(z + k, DEPTH)}
    around = lambda k: {"seq": lax.rem(seq + k, TEAM)}
    block = lambda s: pl.ds(pl.multiple_of(BLK * s, BLK), BLK)
    lanes = lambda o: pl.ds(pl.multiple_of(KROWS * o, KROWS), KROWS)
    piece = lambda n: pl.ds(pl.multiple_of(HEADDIM * n, HEADDIM), HEADDIM)
    half = lambda c: pl.ds(pl.multiple_of(HALF * c, 16), HALF)
    extra = lambda o: lax.rem(o, 2) == core
    n_all = HEADDIM * HPD
    give = lambda c: g_v.at[block(c)]
    hold = lambda c: g_v.at[block(CHIPS + c)]

    def load(n):
        pairs = [(nrm_ref, nrm_v), (g_ref, g_v), (w_ref, w_v), (tok_ref, tok_v), (cot_ref, cot_v)]
        return pltpu.make_async_copy(pairs[n][0], pairs[n][1], loc.at[n])

    def load_own(c):
        return pltpu.make_async_copy(br_ref.at[block(2 * c + core)], ob_v.at[c], loc.at[5 + c])

    def br_pair(c):
        return send(br_ref.at[block(2 * c + 1 - core)], rb_v.at[c], b_send.at[c], b_recv.at[c], sib)

    def block_of(n, c):
        return ob_v.at[c] if n == 0 else hold(c)

    def rs(n, kind):
        h = pl.ds((0, BLK // 2, BLK // 2, 0, 0, BLK // 2)[kind], BLK // 2)
        src = block_of(n, near[(1, 1, 2, 2, 3, 3)[kind]]).at[h]
        if kind < 4:
            dst = in_v.at[n, kind // 2, h]
        else:
            dst = rel_v.at[n, 5 - kind]
        return send(src, dst, p_send.at[n, kind], p_recv.at[n, kind], peer((1, 1, 2, 2, 1, 2)[kind]))

    def rs_first(n, role):
        for kind in ((), (0,), (2,), (4, 5))[role]:
            rs(n, kind).start()

    def rs_second(n, role):
        kind, came = ((1, 5), (3, 4))[role - 1]
        rs(n, came).wait_recv()
        h = pl.ds((BLK // 2, 0)[role - 1], BLK // 2)
        ref = block_of(n, near[role]).at[h]
        ref[...] = ref[...] + rel_v[n, role - 1]
        rs(n, kind).start()

    def rs_total(n):
        for kind in range(4):
            rs(n, kind).wait_recv()
        return block_of(n, chip)[...].astype(F32) + in_v[n, 0].astype(F32) + in_v[n, 1].astype(F32)

    def dn_pair(c):
        return send(give(c), rb_v.at[c], d_send.at[c], d_recv.at[c], sib)

    mate = z + 1 - 2 * lax.rem(z, 2)
    outer = (z == 0) | (z == DEPTH - 1)
    far = lambda j: (2 + j) - lax.div(z, 2) * (1 + 2 * j)
    rest = [slice(None)] * 3 + [slice(0, HEADDIM), slice(HEADDIM, 2 * HEADDIM)]
    z_in = [zz_in, zx_in, zb_in, zw_in, zw_in]
    z_rel = [zz_rel, zx_rel, zb_rel, zw_rel, zw_rel]

    def z_part(n, o):
        if n < 2:
            return wig_v.at[:, lanes(o)]
        if n == 2:
            return bcd_v.at[half(core), lanes(o)]
        return wog_v.at[piece(o if n == 3 else DEPTH + lax.div(o, 2))]

    def z_mate(n):
        return send(z_part(n, mate), z_in[n].at[0, rest[n]], z_send.at[n, 0], z_recv.at[n, 0], {"fsdp": mate})

    def z_hand(n, j):
        return send(z_part(n, far(j)), z_rel[n].at[j, rest[n]], z_send.at[n, 2 + j], z_recv.at[n, 2 + j], {"fsdp": mate})

    def z_far(n, j):
        return send(z_part(n, far(j)), z_in[n].at[1, rest[n]], z_send.at[n, 2 + j], z_recv.at[n, 1], {"fsdp": far(j)})

    def held(n, o, also=None):
        if n == 4:
            return extra(o) if also is None else extra(o) & also
        return also

    def under_cond(cond, body):
        if cond is None:
            body()
        else:
            pl.when(cond)(body)

    def z_start(n):
        for j in (1, 0):
            under_cond(held(n, far(j), outer), lambda: z_hand(n, j).start())

    def z_start_mate(n):
        under_cond(held(n, mate), lambda: z_mate(n).start())

    def z_relay(n):
        for j in (1, 0):

            def body():
                z_hand(n, j).wait_recv()
                ref = z_part(n, far(j))
                ref[...] = ref[...] + z_rel[n][j, rest[n]]
                z_far(n, j).start()

            under_cond(held(n, far(j), jnp.logical_not(outer)), body)

    def z_total(n):
        z_mate(n).wait_recv()
        z_far(n, 0).wait_recv()
        return z_part(n, z)[...].astype(F32) + z_in[n][0, rest[n]].astype(F32) + z_in[n][1, rest[n]].astype(F32)

    def z_close(n):
        under_cond(held(n, mate), lambda: z_mate(n).wait_send())
        for j in range(2):
            under_cond(held(n, far(j)), lambda: z_far(n, j).wait_send())

    def small_copy(k):
        return send(small_v, zs_in.at[k - 1], s_send.at[k], s_recv.at[k], under(k))

    def bcd_pair():
        return send(bcd_v.at[half(1 - core)], bcd_in, h_send.at[0], h_recv.at[0], sib)

    def bcd_push(k):
        return send(gb_v, gb_in.at[k - 1], q_send.at[k], q_recv.at[k], peer(k))

    def bcd_back():
        return send(gt_v.at[core], gt_v.at[core], h_send.at[1], h_recv.at[1], sib)

    def parts(n, c, cr, h=None):
        if n < 2:
            base = n * DI // HEADDIM
            src = (gz_v, gx_v)[n]
            slots = range(HPD) if h is None else range(3 * h, 3 * h + 3)
            return [(src.at[piece(s)], wig_ref.at[piece(base + head_of(s, c, cr)[s // 4])]) for s in slots]
        if n < 4:
            row = HEADDIM * (3 * c + 2 * cr if n == 2 else 3 * c + 1)
            first, size = (0, HEADDIM) if h is None else (h * HEADDIM // 2, HEADDIM // 2)
            return [(gw_v.at[pl.ds(HEADDIM * (n - 2) + first, size)],
                     wog_ref.at[pl.ds(pl.multiple_of(row + first, HEADDIM // 2), size)])]
        if h is None:
            return [(small_s, smalls_ref.at[2 * c + cr])]
        return [(small_s.at[8 * h : 8 * h + 8], smalls_ref.at[2 * c + cr, 8 * h : 8 * h + 8])]

    def all_of(n, h=None):
        if n < 2:
            return wig_ref.at[pl.ds(n * DI, n_all if h is None else n_all // 2)]
        return parts(n, 0, 0, h)[0][1]

    def ag(n, k):
        if k < 3:
            return [send(src, dst, a_send.at[n, k], a_recv.at[n, k], sib if k == 0 else peer(k))
                    for src, dst in parts(n, chip, core)]
        return [send(dst, dst, a_send.at[n, k], a_recv.at[n, k], peer(5 - k))
                for _, dst in parts(n, near[k - 2], core, k - 3)]

    def ag_wait(n, k):
        ref = all_of(n, None if k < 3 else k - 3)
        return send(ref, ref, a_send.at[n, k], a_recv.at[n, k], sib)

    def ag_next(n, k):
        which = parts(n, near[k], core) if k < 3 else parts(n, near[3], core, k - 3)
        return [send(dst, dst, f_send.at[n, k], f_recv.at[n, k], sib) for _, dst in which]

    def ag_next_wait(n, k):
        ref = all_of(n, None if k < 3 else k - 3)
        return send(ref, ref, f_send.at[n, k], f_recv.at[n, k], sib)

    def ag_own(n):
        return [pltpu.make_async_copy(src, dst, loc.at[9 + n]) for src, dst in parts(n, chip, core)]

    def ag_own_wait(n):
        return pltpu.make_async_copy(all_of(n), all_of(n), loc.at[9 + n])

    def ag_start(n):
        for k in (1, 2, 0):
            for copy in ag(n, k):
                copy.start()
        for copy in ag_own(n):
            copy.start()

    def ag_turn(n):
        for k in (1, 2):
            ag_wait(n, k).wait_recv()
            for copy in ag(n, k + 2) + ag_next(n, k):
                copy.start()

    def ag_end(n):
        for k in (3, 4):
            ag_wait(n, k).wait_recv()
            for copy in ag_next(n, k):
                copy.start()

    def ag_close(n, sends=True, receives=True):
        if receives:
            ag_wait(n, 0).wait_recv()
            for k in range(1, 5):
                ag_next_wait(n, k).wait_recv()
        if sends:
            for k in range(5):
                ag_wait(n, k).wait_send()
            for k in range(1, 5):
                ag_next_wait(n, k).wait_send()
            ag_own_wait(n).wait()

    @pl.when(i == 0)
    def _():
        greet([around(k) for k in range(1, TEAM)] + [under(k) for k in range(1, DEPTH)])
        for c in range(CHIPS):
            br_pair(c).start()
            load_own(c).start()
        for n in range(5):
            load(n).start()
        small_v[...] = jnp.zeros_like(small_v)
        dstate[...] = jnp.zeros_like(dstate)
        dcbuf[BLK : BLK + 8, :] = jnp.zeros((8, CONVC), F32)

    @pl.when(i < TEAM)
    def _():
        gate_backward(i, projz_ref[...].astype(F32), ssd_ref[...], dno_ref[...],
                      stat_ref[pl.ds(i, 1), :], par_ref[5:6, :CH], not_v, dy_v, dz_v, dzt_v, small_v)

    @pl.when(i == 1)
    def _():
        for c in range(CHIPS):
            load_own(c).wait()
            br_pair(c).wait_recv()
            ob_v[c] = ob_v[c] + rb_v[c]
        for role in (3, 1, 2):
            rs_first(0, role)
        pl.semaphore_signal(free, inc=1, device_id=sib, device_id_type=pl.DeviceIdType.MESH)

    @pl.when(i == TEAM)
    def _():
        pl.semaphore_wait(free, 1)
        for n in range(5):
            load(n).wait()

        @pl.loop(0, D // 512)
        def _(n):
            cols = pl.ds(pl.multiple_of(512 * n, 512), 512)
            wig_v[:, cols] = dot(dzt_v[...], nrm_v[:, cols]).astype(BF)

        z_start(0)

        @pl.loop(0, D // 512)
        def _(n):
            cols = pl.ds(pl.multiple_of(512 * n, 512), 512)
            wog_v[:, cols] = dot(not_v[...], g_v[:, cols]).astype(BF)

        z_start(3)
        z_start(4)
        for n in (0, 3, 4):
            z_start_mate(n)

    def combine(c):
        dn_pair(c).wait_recv()
        hold(c)[...] = hold(c)[...] + rb_v[c]
        for role in (1, 2, 3):

            @pl.when(near[role] == c)
            def _():
                rs_first(1, role)

    def relay(c):
        for role in (1, 2):

            @pl.when(near[role] == c)
            def _():
                rs_second(1, role)

    for c in range(CHIPS - 1, 0, -1):

        @pl.when(i == TEAM + 1 + 2 * (CHIPS - c))
        def _():
            combine(c)
            if c < CHIPS - 1:
                relay(c + 1)

    @pl.when(i == TEAM + 2)
    def _():
        rs_second(0, 1)
        rs_second(0, 2)

    @pl.when(i == 2 * TEAM)
    def _():
        gz_v[...] = z_total(0).astype(BF)
        ag_start(0)

    @pl.when((i > TEAM) & (i <= 2 * TEAM))
    def _():
        j = 2 * TEAM - i
        rows = block(j)
        d_rest = scan_backward(projc_ref[...], halo_ref[...], info_ref[...], id_row(ids_ref, j), st_ref[0],
                               par_ref[...], dy_v[rows, :], cbuf, dcbuf, dstate, small_v)
        rest_v[:, rows] = d_rest.T.astype(BF)
        dn = dot(jnp.concatenate([dz_v[rows, :], d_rest.astype(BF)], axis=1), w_v[...])
        part = jnp.sum(dn * nrm_v[rows, :].astype(F32), axis=0, keepdims=True)
        for n in range(D // CH):
            small_v[7 + n : 8 + n, :CH] += part[:, CH * n : CH * n + CH]
        dn = dn.astype(BF)
        c = lax.div(j, 2)

        @pl.when(lax.rem(j, 2) == core)
        def _():
            hold(c)[...] = dn

        @pl.when(lax.rem(j, 2) != core)
        def _():
            give(c)[...] = dn
            dn_pair(c).start()

    @pl.when(i == 2 * TEAM - 1)
    def _():
        total = rs_total(0)
        stat = stat_ref[pl.ds(seq, 1), 0:BLK]
        stat = jnp.broadcast_to(stat, (128, BLK)).T
        s2 = lax.rsqrt(stat[:, 0:1] * (1.0 / DI) + EPSILON)
        out_ref[...] = (tok_v[...].astype(F32) + total * s2).astype(BF)

    @pl.when(i == TEAM + 4)
    def _():
        z_relay(0)

    @pl.when(i == TEAM + 6)
    def _():
        z_relay(3)
        z_relay(4)

    @pl.when(i == 2 * TEAM + 1)
    def _():
        for n in range(D // CH):
            small_v[7 + n : 8 + n, :CH] = small_v[7 + n : 8 + n, :CH] / par_ref[7 + n : 8 + n, :CH]
        for k in range(1, DEPTH):
            small_copy(k).start()
        combine(0)

        relay(1)
        z_close(0)

        @pl.loop(0, D // 512)
        def _(n):
            cols = pl.ds(pl.multiple_of(512 * n, 512), 512)
            both = dot(rest_v[...], nrm_v[:, cols]).astype(BF)
            wig_v[:, cols] = both[:NX]
            bcd_v[:, cols] = both[NX:]

        bcd_pair().start()
        z_start(1)
        z_start_mate(1)
        bcd_pair().wait_recv()
        bcd_v[half(core), :] = bcd_v[half(core), :] + bcd_in[...]
        z_start(2)
        z_start_mate(2)
        gw_v[0:HEADDIM, :] = z_total(3).astype(BF)
        ag_start(2)

        @pl.when(extra(z))
        def _():
            gw_v[HEADDIM:, :] = z_total(4).astype(BF)
            ag_start(3)

        relay(0)
        total = small_v[...]
        for k in range(1, DEPTH):
            small_copy(k).wait_recv()
            total = total + zs_in[k - 1]
        small_s[...] = total
        ag_start(4)
        ag_turn(0)
        z_relay(1)
        z_relay(2)
        ag_turn(2)

        @pl.when(extra(z))
        def _():
            ag_turn(3)

        ag_turn(4)
        ag_end(0)
        total = rs_total(1)
        uf = tok_v[...].astype(F32)
        along = total * norm_gain(par_ref[...])
        s1 = lax.rsqrt(jnp.mean(uf * uf, axis=1, keepdims=True) + EPSILON)
        tg_ref[...] = cot_v[...].astype(F32) + s1 * along - uf * (
            s1 * s1 * s1 * jnp.mean(along * uf, axis=1, keepdims=True))
        gx_v[...] = z_total(1).astype(BF)
        ag_start(1)
        ag_end(2)

        @pl.when(extra(z))
        def _():
            ag_end(3)

        ag_end(4)
        gb_v[...] = z_total(2).astype(BF)
        for k in range(1, CHIPS):
            bcd_push(k).start()
        ag_turn(1)
        for k in range(1, CHIPS):
            bcd_push(k).wait_recv()
        total = gb_v[...].astype(F32)
        for k in range(1, CHIPS):
            total = total + gb_in[k - 1].astype(F32)
        gt_v[core] = total.astype(BF)
        bcd_back().start()
        ag_end(1)
        bcd_back().wait()
        last = [
            pltpu.make_async_copy(gt_v.at[0], wig_ref.at[pl.ds(2 * DI, HALF)], loc.at[15]),
            pltpu.make_async_copy(gt_v.at[1, 0 : WIDTH - 2 * DI - HALF],
                                  wig_ref.at[pl.ds(2 * DI + HALF, WIDTH - 2 * DI - HALF)], loc.at[16])]
        for copy in last:
            copy.start()
        for n in (0, 1, 2, 4):
            ag_close(n)

        @pl.when(extra(z))
        def _():
            ag_close(3, receives=False)

        @pl.when(jnp.logical_not(extra(z)))
        def _():
            ag_close(3, sends=False)

        for c in range(CHIPS):
            br_pair(c).wait_send()
            dn_pair(c).wait_send()
        for n in range(2):
            for kind in range(6):
                rs(n, kind).wait_send()
        for k in range(1, CHIPS):
            bcd_push(k).wait_send()
        for k in range(1, DEPTH):
            small_copy(k).wait_send()
        for n in (1, 2, 3, 4):
            z_close(n)
        bcd_pair().wait_send()
        for copy in last:
            copy.wait()


def backward_call(tok, cot, nrm, br, w, g, projz, ssd, dno, stat, par, projc, st, info, ids):
    n = nrm.shape[0]
    any_space = pl.BlockSpec(memory_space=pl.ANY)
    sds = jax.ShapeDtypeStruct
    dma = pltpu.SemaphoreType.DMA
    one = lambda i: jnp.minimum(i, TEAM - 1)
    two = lambda i: jnp.clip(2 * TEAM - i, 0, TEAM - 1)
    rows = lambda c, turn: pl.BlockSpec((BLK, c), lambda i: (turn(i), 0))
    cube = lambda a, b: pl.BlockSpec((1, a, b), lambda i: (two(i), 0, 0))
    fixed = lambda a, b: pl.BlockSpec((a, b), lambda i: (0, 0), pipeline_mode=pl.Buffered(1))
    vm = pltpu.VMEM
    return pl.pallas_call(
        backward_kernel,
        grid=(2 * TEAM + 2,),
        in_specs=[any_space] * 6 + [
            rows(NZ, one), rows(CH, one), rows(CH, one), fixed(TEAM, 2 * BLK), fixed(16, CONVC), rows(REST, two),
            pl.BlockSpec((16, REST), lambda i: (jnp.maximum(16 * two(i) - 1, 0), 0)),
            cube(STATE, CH), rows(128, two), fixed(1, n)],
        out_specs=[fixed(BLK, D), fixed(BLK, D), any_space, any_space, any_space],
        out_shape=[sds((BLK, D), BF), sds((BLK, D), F32), sds((WIDTH, KROWS), BF),
                   sds((DI // DEPTH, D), BF), sds((TEAM, 16, CONVC), F32)],
        scratch_shapes=[
            vm((n, D), BF), vm((n, D), BF), vm((COLS, D), BF), vm((CH, n), BF), vm((n, CH), BF), vm((CH, n), BF),
            vm((n, CH), F32), vm((REST, n), BF), vm((CH, D), BF), vm((CH, D), BF), vm((BCD, D), BF),
            vm((HALF, D), BF),
            vm((2, CH, KROWS), BF), vm((2, CH, KROWS), BF), vm((2, HALF, KROWS), BF), vm((2, 2 * HEADDIM, D), BF),
            vm((DEPTH - 1, 16, CONVC), F32),
            vm((2, CH, KROWS), BF), vm((2, CH, KROWS), BF), vm((2, HALF, KROWS), BF), vm((2, 2 * HEADDIM, D), BF), vm((CH, KROWS), BF), vm((CH, KROWS), BF),
            vm((HALF, KROWS), BF), vm((2 * HEADDIM, D), BF), vm((CHIPS - 1, HALF, KROWS), BF), vm((2, HALF, KROWS), BF),
            vm((CHIPS, BLK, D), BF), vm((CHIPS, BLK, D), BF), vm((2, 2, BLK, D), BF), vm((2, 2, BLK // 2, D), BF),
            vm((BLK, D), BF), vm((BLK, D), BF), vm((16, CONVC), F32), vm((16, CONVC), F32),
            vm((BLK + 8, CONVC), F32), vm((BLK + 8, CONVC), F32), vm((STATE, CH), F32),
            dma((17,)), dma((CHIPS,)), dma((CHIPS,)), dma((2, 6)), dma((2, 6)), dma((CHIPS,)), dma((CHIPS,)),
            dma((CHIPS,)), dma((CHIPS,)), dma((5, 4)), dma((5, 4)), dma((DEPTH,)), dma((DEPTH,)),
            dma((5, 5)), dma((5, 5)), dma((5, 5)), dma((5, 5)), dma((2,)), dma((2,)),
            pltpu.SemaphoreType.REGULAR],
        compiler_params=pltpu.CompilerParams(
            collective_id=1, has_side_effects=True, vmem_limit_bytes=63 << 20),
    )(tok, cot, nrm, br, w, g, projz, ssd, dno, stat, par, projc, projc, st, info, ids)


def finish_kernel(
    lo_ref, tg_ref, wig_ref, wog_ref, smalls_ref,
    out_ref, grad_ref, win_ref, wout_ref, convw_ref, convb_ref, alog_ref, dtb_ref, skip_ref, normw_ref, gatew_ref,
    all_v, in_v, in_f, wo_v, wo_f, lo_v, tg_v, sems,
):
    rows_in, rows_wo = WIDTH // 13, DI // DEPTH // 4
    chunks = [(wig_ref, in_v, in_f, win_ref, slice(rows_in * n, rows_in * n + rows_in)) for n in range(13)]
    chunks += [(wog_ref, wo_v, wo_f, wout_ref, slice(rows_wo * n, rows_wo * n + rows_wo)) for n in range(4)]
    come = [pltpu.make_async_copy(a.at[r], b.at[r], sems.at[0, n]) for n, (a, b, _, _, r) in enumerate(chunks)]
    go = [pltpu.make_async_copy(a.at[r], b.at[r], sems.at[1, n]) for n, (_, _, a, b, r) in enumerate(chunks)]
    last = len(chunks)
    enter = [pltpu.make_async_copy(lo_ref, lo_v, sems.at[0, last]), pltpu.make_async_copy(tg_ref, tg_v, sems.at[0, last + 1])]
    leave = [pltpu.make_async_copy(lo_v, out_ref, sems.at[1, last]), pltpu.make_async_copy(tg_v, grad_ref, sems.at[1, last + 1])]
    for copy in come + enter:
        copy.start()
    for n, (_, src, dst, _, r) in enumerate(chunks):
        come[n].wait()
        dst[r] = src[r].astype(F32)
        go[n].start()
    for n in range(2):
        enter[n].wait()
        leave[n].start()
    for d in range(TEAM):
        for slot in range(HPD):
            head = head_of(slot, d // 2, d % 2)[slot // 4]
            all_v[:, HEADDIM * head : HEADDIM * head + HEADDIM] = smalls_ref[
                d, 0:8, HEADDIM * slot : HEADDIM * slot + HEADDIM]
    side = smalls_ref[0, :, CH:]
    gain = smalls_ref[0, :, :CH]
    for d in range(1, TEAM):
        side = side + smalls_ref[d, :, CH:]
        gain = gain + smalls_ref[d, :, :CH]
    all_v[:, DI:] = side[0:8]
    z = lax.axis_index("fsdp")
    nc, ng, nh = CHAN // DEPTH, DI // DEPTH, HEADS // DEPTH
    for o in range(DEPTH):

        @pl.when(z == o)
        def _():
            convw_ref[...] = all_v[0:CONV, nc * o : nc * o + nc]
            convb_ref[...] = all_v[CONV : CONV + 1, nc * o : nc * o + nc].reshape(nc)
            gatew_ref[...] = all_v[5:6, ng * o : ng * o + ng].reshape(ng)
            alog_ref[...] = side[5:6, nh * o : nh * o + nh].reshape(nh)
            dtb_ref[...] = side[5:6, 128 + nh * o : 128 + nh * o + nh].reshape(nh)
            skip_ref[...] = side[6:7, nh * o : nh * o + nh].reshape(nh)
            normw_ref[...] = gain[7 + o : 8 + o, :].reshape(KROWS)

    for copy in go + leave:
        copy.wait()


def finish_call(lo, tg, wig, wog, smalls):
    any_space = pl.BlockSpec(memory_space=pl.ANY)
    vmem = pl.BlockSpec(memory_space=pltpu.VMEM)
    sizes = [(CONV, CHAN // DEPTH), (CHAN // DEPTH,)] + [(HEADS // DEPTH,)] * 3 + [(KROWS,), (DI // DEPTH,)]
    sds = jax.ShapeDtypeStruct
    rows = DI // DEPTH
    return pl.pallas_call(
        finish_kernel,
        in_specs=[any_space] * 4 + [vmem],
        out_specs=[any_space] * 4 + [vmem] * len(sizes),
        out_shape=[sds((BLK, D), BF), sds((BLK, D), F32), sds((WIDTH, KROWS), F32), sds((rows, D), F32)]
        + [sds(s, F32) for s in sizes],
        scratch_shapes=[pltpu.VMEM((8, CHAN), F32), pltpu.VMEM((WIDTH, KROWS), BF), pltpu.VMEM((WIDTH, KROWS), F32),
                        pltpu.VMEM((rows, D), BF), pltpu.VMEM((rows, D), F32), pltpu.VMEM((BLK, D), BF), pltpu.VMEM((BLK, D), F32),
                        pltpu.SemaphoreType.DMA((2, 19))],
        compiler_params=pltpu.CompilerParams(vmem_limit_bytes=62 << 20),
    )(lo, tg, wig, wog, smalls)


def on_team(
    tokens, segment_ids, cotangent, w_in, w_out, conv_w, conv_b, a_log, dt_bias, d_skip,
    norm_w, gate_w,
):
    tok, cot = tokens[0], cotangent[0]
    small = (conv_w, conv_b, a_log, dt_bias, d_skip, norm_w, gate_w)
    nrm, projc, projz, st, ssd, dno, br, info, stat, par, w_loc, g = forward_call(
        tok, cot, w_in.T, w_out, segment_ids, small)
    lo, tg, wig, wog, smalls = backward_call(
        tok, cot, nrm, br, w_loc, g, projz, ssd, dno, stat, par, projc, st, info, segment_ids)
    lo, tg, wig, wog, convw, convb, alog, dtb, skip, normw, gatew = finish_call(lo, tg, wig, wog, smalls)
    return (lo[None], tg[None], wig.T, wog, convw, convb, alog, dtb, skip, normw, gatew)


def solution(mesh):
    body = on_team if (mesh.shape["seq"], mesh.shape["fsdp"]) == (TEAM, DEPTH) else on_device
    return jax.shard_map(
        body,
        mesh=mesh,
        in_specs=(
            P("fsdp", "seq", None),
            P("fsdp", None),
            P("fsdp", "seq", None),
            P("fsdp", None),
            P("fsdp", None),
            P(None, "fsdp"),
            P("fsdp"),
            P("fsdp"),
            P("fsdp"),
            P("fsdp"),
            P("fsdp"),
            P("fsdp"),
        ),
        out_specs=(
            P("fsdp", "seq", None),
            P("fsdp", "seq", None),
            P("fsdp", None),
            P("fsdp", None),
            P(None, "fsdp"),
            P("fsdp"),
            P("fsdp"),
            P("fsdp"),
            P("fsdp"),
            P("fsdp"),
            P("fsdp"),
        ),
        check_vma=False,
    )
```
